128 devices in a mesh: dp: 4 (over y), ctx: 32 (over z, x, core).
Axes of the slice: x: 4, y: 4, z: 4, core: 2. Of those that a mesh axis runs over, the one named last changes fastest.
Arguments:
- tokens: bfloat16 [16384, 1536], P(('dp', 'ctx')), may hold values from -6 to 6
- segment_ids: int32 [4, 4096], P('dp', 'ctx'), may hold values from 0 to 15, never falling along the last dimension, each value on 1 to 3072 neighbouring positions
- expert_ids: int32 [16384, 2], P(('dp', 'ctx')), may hold values from 0 to 15, all different within a row
- w_query: bfloat16 [1536, 1536], P(('dp', 'ctx')), may hold values from -0.15625 to 0.15625
- w_key: bfloat16 [1536, 512], P(('dp', 'ctx')), may hold values from -0.3125 to 0.3125
- w_value: bfloat16 [1536, 512], P(('dp', 'ctx')), may hold values from -0.3125 to 0.3125
- w_out: bfloat16 [1536, 1536], P(None, ('dp', 'ctx')), may hold values from -0.625 to 0.625
- w_router: bfloat16 [1536, 16], P(('dp', 'ctx')), may hold values from -0.15625 to 0.15625
- gain_attn: bfloat16 [1536], P(('dp', 'ctx')), may hold values from 0.5 to 1.5
- gain_moe: bfloat16 [1536], P(('dp', 'ctx')), may hold values from 0.5 to 1.5
- w_gate: bfloat16 [1536, 16384], P('dp', 'ctx'), may hold values from -0.15625 to 0.15625
- w_up: bfloat16 [1536, 16384], P('dp', 'ctx'), may hold values from -0.15625 to 0.15625
- w_down: bfloat16 [16384, 1536], P('ctx', 'dp'), may hold values from -0.1875 to 0.1875
- cotangent: bfloat16 [16384, 1536], P(('dp', 'ctx')), may hold values from -6 to 6
Outputs:
- block_out: bfloat16 [16384, 1536], P(('dp', 'ctx'))
- grad_tokens: float32 [16384, 1536], P(('dp', 'ctx'))
- grad_w_query: float32 [1536, 1536], P(('dp', 'ctx'))
- grad_w_key: float32 [1536, 512], P(('dp', 'ctx'))
- grad_w_value: float32 [1536, 512], P(('dp', 'ctx'))
- grad_w_out: float32 [1536, 1536], P(None, ('dp', 'ctx'))
- grad_w_router: float32 [1536, 16], P(('dp', 'ctx'))
- grad_gain_attn: float32 [1536], P(('dp', 'ctx'))
- grad_gain_moe: float32 [1536], P(('dp', 'ctx'))
- grad_w_gate: float32 [1536, 16384], P('dp', 'ctx')
- grad_w_up: float32 [1536, 16384], P('dp', 'ctx')
- grad_w_down: float32 [16384, 1536], P('ctx', 'dp')
The draws below stay inside these ranges and needn't reach their ends.
Inputs may be any that keep to these rules, and one draw needn't show every extreme that they name: `expert_ids`: each token names two different experts. `segment_ids`: within a sequence the ids never fall.
All inputs are finite; a program needn't handle non-finite values.
Results may differ from the reference program's by a relative error of at most 0.017.
The reference program's roundings to bfloat16 on the way count: a program that leaves them out, or rounds other values in their place, can miss the bound.
Values may be sent and summed in bfloat16 or wider, within the bound.
A program may use at most 192 MiB of HBM per device.

```python
import math
import jax
import jax.numpy as jnp
import numpy as np
from jax import lax

MODEL_WIDTH = 1536
HEADS = 24
KV = 8
HD = 64
EXPERT_COUNT = 16
FF = 1024
DEVICE_TOKENS = 128
SEQ = 4096
TOKENS = 16384
EXPERT_CAPACITY = 20
N_DP = 4
N_CTX = 32


def shard_levels(stream_key, dims, split, smallest, high):
    loudness = 1.0
    for position, shards_of in split:
        heights = jax.random.uniform(jax.random.fold_in(jax.random.fold_in(stream_key, 6), position), (shards_of,), jnp.float32, smallest / len(split), high / len(split))
        loudness = loudness * jnp.repeat(jnp.exp(heights), dims[position] // shards_of).reshape((-1,) + (1,) * (len(dims) - 1 - position))
    return loudness


def different_ones(stream_key, rows, count, top, lift):
    order = jax.random.permutation(jax.random.fold_in(stream_key, 1), count)
    boost = order
    for power in range(3):
        boost = boost * boost // count
    boost = boost * lift // count
    lots = jax.random.randint(jax.random.fold_in(stream_key, 2), (rows, count), 0, 4096) + boost
    fixed_rows = jax.random.permutation(jax.random.fold_in(stream_key, 3), rows)[jnp.arange(count) % rows]
    lots = jnp.where(jnp.arange(rows)[:, None] == fixed_rows[None, :], 1 << 14, lots)
    priority = lots * count + jnp.arange(count)
    return lax.top_k(priority.astype(jnp.int32), top)[1].astype(jnp.int32)


def length_profile(count, total, most, skew):
    portions = [(1 << 20) // math.isqrt(grade ** skew) + 1 for grade in range(2, count + 1)]
    rest, holding = total - most - (count - 1), [1] * (count - 1)
    while rest > 0:
        free = [i for i in range(count - 1) if holding[i] < most]
        mass, remaining = sum([portions[i] for i in free]), rest
        for i in free:
            extra = min(most - holding[i], max(1, remaining * portions[i] // mass), rest)
            holding[i] = holding[i] + extra
            rest = rest - extra
    return np.array([most] + holding)


def ragged(rng, amount, total, most, lean):
    if amount == 2:
        one = jax.random.randint(rng, (), max(1, total - most), min(most, total - 1) + 1)
        return jnp.stack([one, total - one])
    lengths = jnp.asarray(length_profile(amount, total, most, lean), jnp.int32)
    twos = (amount - 1) // 2
    source_of, sink = lengths[1:1 + 2 * twos:2], lengths[2:2 + 2 * twos:2]
    room = jnp.minimum(source_of - 1, most - sink)
    shifted = jax.random.randint(jax.random.fold_in(rng, 1), (twos,), 0, 1 << 20) % (room + 1)
    lengths = lengths.at[1:1 + 2 * twos:2].set(source_of - shifted).at[2:2 + 2 * twos:2].set(sink + shifted)
    return lengths[jax.random.permutation(jax.random.fold_in(rng, 2), amount)]


def normal_values(rng, dims, width, limit, cuts=(), held_as=jnp.bfloat16):
    values = width * jax.random.normal(rng, dims, jnp.float32)
    if cuts:
        values = values * shard_levels(rng, dims, cuts, -0.22, 0.18)
    return jnp.clip(values, -limit, limit).astype(held_as)


def setup_inputs(seed: int = 0) -> dict:
    streams_of = jax.random.split(jax.random.key(seed), 15)
    return {
        "tokens": normal_values(streams_of[0], (TOKENS, MODEL_WIDTH), 1.0, 6.0, ((0, 128),)),
        "segment_ids": jax.vmap(lambda own: jnp.searchsorted(jnp.cumsum(ragged(own, max(4, SEQ // 256), SEQ, 3 * SEQ // 4, 2)), jnp.arange(SEQ), side="right"))(jax.random.split(streams_of[1], N_DP)).reshape((N_DP, SEQ)).astype(jnp.int32),
        "expert_ids": different_ones(streams_of[2], TOKENS, EXPERT_COUNT, 2, 1024),
        "w_query": normal_values(streams_of[3], (MODEL_WIDTH, HEADS * HD), MODEL_WIDTH ** -0.5, 0.15625, ((0, 128),)),
        "w_key": normal_values(streams_of[4], (MODEL_WIDTH, KV * HD), (MODEL_WIDTH // 4) ** -0.5, 0.3125, ((0, 128),)),
        "w_value": normal_values(streams_of[5], (MODEL_WIDTH, KV * HD), (MODEL_WIDTH // 4) ** -0.5, 0.3125, ((0, 128),)),
        "w_out": normal_values(streams_of[6], (HEADS * HD, MODEL_WIDTH), (HEADS * HD // 16) ** -0.5, 0.625, ((1, 128),)),
        "w_router": normal_values(streams_of[7], (MODEL_WIDTH, EXPERT_COUNT), MODEL_WIDTH ** -0.5, 0.15625, ((0, 128),)),
        "gain_attn": jnp.clip(1.0 + 0.1 * jax.random.normal(streams_of[8], (MODEL_WIDTH,), jnp.float32), 0.5, 1.5).astype(jnp.bfloat16),
        "gain_moe": jnp.clip(1.0 + 0.1 * jax.random.normal(streams_of[9], (MODEL_WIDTH,), jnp.float32), 0.5, 1.5).astype(jnp.bfloat16),
        "w_gate": normal_values(streams_of[10], (MODEL_WIDTH, EXPERT_COUNT * FF), MODEL_WIDTH ** -0.5, 0.15625, ((0, 4), (1, 32))),
        "w_up": normal_values(streams_of[11], (MODEL_WIDTH, EXPERT_COUNT * FF), MODEL_WIDTH ** -0.5, 0.15625, ((0, 4), (1, 32))),
        "w_down": normal_values(streams_of[12], (EXPERT_COUNT * FF, MODEL_WIDTH), FF ** -0.5, 0.1875, ((0, 32), (1, 4))),
        "cotangent": normal_values(streams_of[13], (TOKENS, MODEL_WIDTH), 1.0, 6.0, ((0, 128),)),
    }


EPS = 1e-05
SCALE_QK = 0.125
HIGH_PRECISION = lax.Precision.HIGHEST

@jax.custom_vjp
def low(v):
    return lax.optimization_barrier(v.astype(jnp.bfloat16)).astype(jnp.float32)

@jax.custom_vjp
def low_back(v):
    return v

def low_keep(v):
    return (low(v), None)

def low_pass(kept, grad):
    return (grad,)

def back_keep(v):
    return (v, None)

def back_low(kept, grad):
    return (low(grad),)
low.defvjp(low_keep, low_pass)
low_back.defvjp(back_keep, back_low)

def hi_dot(left, right):
    return jnp.dot(left, right, precision=HIGH_PRECISION)

def rms_norm(values, gain):
    inverse = lax.rsqrt(lax.optimization_barrier(jnp.mean(values * values, axis=-1, keepdims=True)) + EPS)
    return values * inverse * gain

def attend_one(queries, keys, values, segments):
    length = queries.shape[0]
    block_rows = math.gcd(length, 512)
    per_group = HEADS // KV
    key_heads = keys.reshape(length, KV, HD)
    value_heads = values.reshape(length, KV, HD)
    positions = jnp.arange(length, dtype=jnp.int32)

    def one_block(offset):
        rows = lax.dynamic_slice_in_dim(queries, offset, block_rows, 0).reshape(block_rows, KV, per_group, HD)
        row_pos = offset + jnp.arange(block_rows, dtype=jnp.int32)
        row_seg = lax.dynamic_slice_in_dim(segments, offset, block_rows, 0)
        scores = jnp.einsum('qkgd,skd->kgqs', rows, key_heads, precision=HIGH_PRECISION) * SCALE_QK
        scores = low_back(scores)
        allowed = (row_pos[:, None] >= positions[None, :]) & (row_seg[:, None] == segments[None, :])
        scores = jnp.where(allowed, scores, -1e+30)
        prob_low = low(jax.nn.softmax(scores, axis=-1))
        mixed = jnp.einsum('kgqs,skd->qkgd', prob_low, value_heads, precision=HIGH_PRECISION)
        return mixed.reshape(block_rows, HEADS * HD)
    offsets = (jnp.arange(length // block_rows) * block_rows).astype(jnp.int32)
    return lax.map(jax.checkpoint(one_block), offsets).reshape(length, HEADS * HD)

def block_forward(tokens, w_query, w_key, w_value, w_out, w_router, gain_attn, gain_moe, w_gate, w_up, w_down, segment_ids, expert_ids):
    normed = low(rms_norm(tokens, gain_attn))
    queries = low(low_back(hi_dot(normed, w_query)))
    keys = low(low_back(hi_dot(normed, w_key)))
    values = low(low_back(hi_dot(normed, w_value)))
    attn = lax.map(lambda group_in: attend_one(*group_in), (queries.reshape(N_DP, SEQ, HEADS * HD), keys.reshape(N_DP, SEQ, KV * HD), values.reshape(N_DP, SEQ, KV * HD), segment_ids))
    attn = low(low_back(attn.reshape(TOKENS, HEADS * HD)))
    middle = tokens + low_back(hi_dot(attn, w_out))
    mixture_input = low(rms_norm(middle, gain_moe))
    logits = hi_dot(mixture_input, w_router)
    block_list = N_DP * N_CTX
    chosen = expert_ids[:, :, None] == jnp.arange(EXPERT_COUNT, dtype=jnp.int32)[None, None, :]
    chosen_f = chosen.astype(jnp.float32)
    picked = lax.optimization_barrier(jnp.sum(chosen_f * logits[:, None, :], axis=-1))
    gates = jax.nn.softmax(picked, axis=-1)
    gate_e = lax.optimization_barrier(jnp.sum(chosen_f * gates[:, :, None], axis=1))
    used = lax.optimization_barrier(jnp.sum(chosen.astype(jnp.int32), axis=1)).reshape(block_list, DEVICE_TOKENS, EXPERT_COUNT)
    before = jnp.cumsum(used, axis=1) - used
    slot_hit = (used[..., None] == 1) & (before[..., None] == jnp.arange(EXPERT_CAPACITY, dtype=jnp.int32))
    routing_choice = slot_hit.astype(jnp.float32).reshape(block_list, DEVICE_TOKENS, EXPERT_COUNT * EXPERT_CAPACITY)
    weight_tokens = routing_choice * jnp.repeat(gate_e.reshape(block_list, DEVICE_TOKENS, EXPERT_COUNT), EXPERT_CAPACITY, axis=2)
    expert_input = jnp.einsum('rmz,rmf->rzf', routing_choice, mixture_input.reshape(block_list, DEVICE_TOKENS, MODEL_WIDTH), precision=HIGH_PRECISION)
    expert_input = expert_input.reshape(block_list, EXPERT_COUNT, EXPERT_CAPACITY, MODEL_WIDTH)
    gate_val = low_back(jnp.einsum('becd,def->becf', expert_input, w_gate.reshape(MODEL_WIDTH, EXPERT_COUNT, FF), precision=HIGH_PRECISION))
    up_val = low_back(jnp.einsum('becd,def->becf', expert_input, w_up.reshape(MODEL_WIDTH, EXPERT_COUNT, FF), precision=HIGH_PRECISION))
    hidden = low(jax.nn.silu(gate_val) * up_val)
    expert_output = low_back(jnp.einsum('becf,efd->becd', hidden, w_down.reshape(EXPERT_COUNT, FF, MODEL_WIDTH), precision=HIGH_PRECISION))
    mixture_experts = jnp.einsum('ioc,icj->ioj', weight_tokens, expert_output.reshape(block_list, EXPERT_COUNT * EXPERT_CAPACITY, MODEL_WIDTH), precision=HIGH_PRECISION)
    return middle + mixture_experts.reshape(TOKENS, MODEL_WIDTH)

def reference(tokens, segment_ids, expert_ids, w_query, w_key, w_value, w_out, w_router, gain_attn, gain_moe, w_gate, w_up, w_down, cotangent):
    floats = tuple((array.astype(jnp.float32) for array in (tokens, w_query, w_key, w_value, w_out, w_router, gain_attn, gain_moe, w_gate, w_up, w_down)))

    def forward(*inputs):
        return block_forward(*inputs, segment_ids, expert_ids)
    output, pullback = jax.vjp(forward, *floats)
    grads = pullback(cotangent.astype(jnp.float32))
    return (output.astype(jnp.bfloat16), grads[0], grads[1], grads[2], grads[3], grads[4], grads[5], grads[6], grads[7], grads[8], grads[9], grads[10])
```

```python
import functools

import jax
import jax.numpy as jnp
from jax import lax
from jax.experimental import pallas as pl
from jax.experimental.pallas import tpu as pltpu
from jax.sharding import PartitionSpec as P

MODEL_WIDTH = 1536
HEADS = 24
KV = 8
HD = 64
EXPERT_COUNT = 16
FF = 1024
EXPERT_CAPACITY = 20
SLOTS = 24
ROWS = 128
PAIR = 256
HEAD_Q = 192
Q_HALF = 768
KV_HALF = 512
EXTRA = 128
PACK = Q_HALF + KV_HALF + EXTRA + Q_HALF

EPS = 1e-05
SCALE_QK = 0.125
NEGATIVE = -1e30
HIGH_PRECISION = lax.Precision.HIGHEST
MESH = pl.DeviceIdType.MESH
ANY = pl.BlockSpec(memory_space=pl.ANY)
IN_VMEM = pl.BlockSpec(memory_space=pltpu.VMEM)
BF = jnp.bfloat16
F32 = jnp.float32


def coords():
    i = lax.axis_index("ctx")
    return lax.axis_index("dp"), i // 8, (i // 2) % 4, i % 2


def dev(y, z, x, c):
    return (y, z * 8 + x * 2 + c)


def signal(target):
    pl.semaphore_signal(
        pltpu.get_barrier_semaphore(), inc=1, device_id=target, device_id_type=MESH
    )


def remote(src, dst, send, recv, target):
    return pltpu.make_async_remote_copy(
        src_ref=src, dst_ref=dst, send_sem=send, recv_sem=recv, device_id=target, device_id_type=MESH
    )


def params(cid, vmem=None):
    return pltpu.CompilerParams(collective_id=cid, has_side_effects=True, vmem_limit_bytes=vmem)


def axis_peer(axis, step):
    y, z, x, c = coords()
    if axis == "y":
        return dev((y + step) % 4, z, x, c)
    if axis == "z":
        return dev(y, (z + step) % 4, x, c)
    return dev(y, z, (x + step) % 4, c)


ORDERS = (("x", "z", "y"), ("y", "x", "z"), ("z", "y", "x"), ("y", "x", "z"))
WIDTHS = (Q_HALF, KV_HALF, Q_HALF, EXTRA)
STARTS = (0, Q_HALF, Q_HALF + KV_HALF, 2 * Q_HALF + KV_HALF)
PARTS = 4
STEPS = (1, 3, 2)


def slab(ref, done, y, z, x):
    return ref.at[
        slice(None) if "y" in done else y,
        slice(None) if "z" in done else z,
        slice(None) if "x" in done else x,
    ]


def gather_kernel(
    pack, tokens, segs, out0, out1, out2, out3, pair, seg_all,
    sib, block, p_send, p_recv, l_sem, s_send, s_recv, sib_send, sib_recv,
):
    y, z, x, c = coords()
    outs = (out0, out1, out2, out3)
    me = z * 8 + x * 2 + c
    sibling = dev(y, z, x, 1 - c)

    def greet(k, carry):
        signal((y, (me + k) % 32))
        return carry

    lax.fori_loop(1, 32, greet, 0)
    for step in STEPS:
        signal(axis_peer("y", step))
    pl.semaphore_wait(pltpu.get_barrier_semaphore(), 34)

    first = remote(pack.at[1 - c], sib, sib_send.at[0], sib_recv.at[0], sibling)
    first.start()
    second = remote(tokens, pair.at[c], sib_send.at[1], sib_recv.at[1], sibling)
    second.start()
    own_rows = pltpu.make_async_copy(tokens, pair.at[c], l_sem.at[4])
    own_rows.start()
    own_segs = pltpu.make_async_copy(segs, seg_all.at[me], l_sem.at[5])
    own_segs.start()

    def spread(k, carry):
        remote(segs, seg_all.at[me], s_send, s_recv, (y, (me + k) % 32)).start()
        return carry

    lax.fori_loop(1, 32, spread, 0)

    first.wait()
    own = pack[c, :12].astype(F32)
    other = sib[:12].astype(F32)
    low = jnp.where(c == 0, own, other)
    high = jnp.where(c == 0, other, own)
    block[...] = jnp.concatenate([low, high], axis=0).astype(BF)

    locals_ = []
    for part in range(PARTS):
        cols = pl.ds(STARTS[part], WIDTHS[part])
        here = pltpu.make_async_copy(block.at[:, cols], outs[part].at[y, z, x], l_sem.at[part])
        here.start()
        locals_.append(here)
    for phase in range(3):
        copies = []
        for part in range(PARTS):
            axis = ORDERS[part][phase]
            done = ORDERS[part][:phase]
            for n, step in enumerate(STEPS):
                dst = slab(outs[part], done, y, z, x)
                src = block.at[:, pl.ds(STARTS[part], WIDTHS[part])] if phase == 0 else dst
                copy = remote(
                    src, dst, p_send.at[phase, part, n], p_recv.at[phase, part, n], axis_peer(axis, step)
                )
                copy.start()
                copies.append(copy)
        if phase == 0:
            for here in locals_:
                here.wait()
        for copy in copies:
            copy.wait()
    second.wait()
    own_rows.wait()
    own_segs.wait()
    drain = remote(
        seg_all.at[pl.ds(0, 31)], seg_all.at[pl.ds(0, 31)], s_send, s_recv, sibling
    )
    drain.wait_send()
    drain.wait_recv()


def gather_weights(pack, tokens, segs):
    return pl.pallas_call(
        gather_kernel,
        out_shape=[jax.ShapeDtypeStruct((4, 4, 4, 24, width), BF) for width in WIDTHS]
        + [
            jax.ShapeDtypeStruct((2, ROWS, MODEL_WIDTH), BF),
            jax.ShapeDtypeStruct((32, 1, 128), jnp.int32),
        ],
        in_specs=[IN_VMEM, ANY, ANY],
        out_specs=[ANY] * 6,
        scratch_shapes=[
            pltpu.VMEM((16, PACK), BF),
            pltpu.VMEM((24, PACK), BF),
            pltpu.SemaphoreType.DMA((3, PARTS, 3)),
            pltpu.SemaphoreType.DMA((3, PARTS, 3)),
            pltpu.SemaphoreType.DMA((6,)),
            pltpu.SemaphoreType.DMA,
            pltpu.SemaphoreType.DMA,
            pltpu.SemaphoreType.DMA((2,)),
            pltpu.SemaphoreType.DMA((2,)),
        ],
        compiler_params=params(1),
        name="gather_weights",
    )(pack, tokens, segs)


def plane_greet(y, me, c, sibling):
    def greet(k, carry):
        t = (me + k) % 16
        signal(dev(y, t // 4, t % 4, c))
        return carry

    lax.fori_loop(1, 16, greet, 0)
    if sibling is not None:
        signal(sibling)
        pl.semaphore_wait(pltpu.get_barrier_semaphore(), 16)
    else:
        pl.semaphore_wait(pltpu.get_barrier_semaphore(), 15)


def heads_out_kernel(q4, kv4, half, q_in, kv_in, half_sib, l_sem, q_send, q_recv, k_send, k_recv, o_send, o_recv):
    y, z, x, c = coords()
    me = z * 4 + x
    sibling = dev(y, z, x, 1 - c)
    plane_greet(y, me, c, sibling)

    def send_kv(k, carry):
        t = (me + k) % 16
        remote(kv4.at[t // 4], kv_in.at[me], k_send, k_recv, dev(y, t // 4, t % 4, c)).start()
        return carry

    q_copies = []
    for n, step in enumerate(STEPS):
        to = (z + step) % 4
        copy = remote(q4.at[to], q_in.at[z], q_send.at[n], q_recv.at[n], dev(y, to, x, c))
        copy.start()
        q_copies.append(copy)
    lax.fori_loop(1, 16, send_kv, 0)
    swap = remote(half, half_sib, o_send, o_recv, sibling)
    swap.start()
    here = [
        pltpu.make_async_copy(q4.at[z], q_in.at[z], l_sem.at[0]),
        pltpu.make_async_copy(kv4.at[z], kv_in.at[me], l_sem.at[1]),
    ]
    for copy in here:
        copy.start()
    for copy in here:
        copy.wait()
    for copy in q_copies:
        copy.wait()
    drain = remote(kv_in.at[pl.ds(0, 15)], kv_in.at[pl.ds(0, 15)], k_send, k_recv, sibling)
    drain.wait_send()
    drain.wait_recv()
    swap.wait()


def heads_out(q4, kv4, half):
    return pl.pallas_call(
        heads_out_kernel,
        out_shape=[
            jax.ShapeDtypeStruct((4, PAIR, HEAD_Q), BF),
            jax.ShapeDtypeStruct((16, PAIR, 128), BF),
            jax.ShapeDtypeStruct((MODEL_WIDTH, Q_HALF), BF),
        ],
        in_specs=[ANY] * 3,
        out_specs=[ANY] * 3,
        scratch_shapes=[
            pltpu.SemaphoreType.DMA((3,)),
            pltpu.SemaphoreType.DMA((3,)),
            pltpu.SemaphoreType.DMA((3,)),
            pltpu.SemaphoreType.DMA,
            pltpu.SemaphoreType.DMA,
            pltpu.SemaphoreType.DMA,
            pltpu.SemaphoreType.DMA,
        ],
        compiler_params=params(2),
        name="heads_out",
    )(q4, kv4, half)


def heads_back_kernel(dq4, dkv, dq_in, dkv_in, l_sem, q_send, q_recv, k_send, k_recv):
    y, z, x, c = coords()
    me = z * 4 + x
    plane_greet(y, me, c, None)

    def send_kv(k, carry):
        t = (me + k) % 16
        remote(dkv.at[t], dkv_in.at[me], k_send, k_recv, dev(y, t // 4, t % 4, c)).start()
        return carry

    q_copies = []
    for n, step in enumerate(STEPS):
        to = (z + step) % 4
        copy = remote(dq4.at[to], dq_in.at[z], q_send.at[n], q_recv.at[n], dev(y, to, x, c))
        copy.start()
        q_copies.append(copy)
    lax.fori_loop(1, 16, send_kv, 0)
    here = [
        pltpu.make_async_copy(dq4.at[z], dq_in.at[z], l_sem.at[0]),
        pltpu.make_async_copy(dkv.at[me], dkv_in.at[me], l_sem.at[1]),
    ]
    for copy in here:
        copy.start()
    for copy in here:
        copy.wait()
    for copy in q_copies:
        copy.wait()
    neighbour = dev(y, (z + 1) % 4, x, c)
    drain = remote(dkv_in.at[pl.ds(0, 15)], dkv_in.at[pl.ds(0, 15)], k_send, k_recv, neighbour)
    drain.wait_send()
    drain.wait_recv()


def heads_back(dq4, dkv):
    return pl.pallas_call(
        heads_back_kernel,
        out_shape=[
            jax.ShapeDtypeStruct((4, PAIR, HEAD_Q), BF),
            jax.ShapeDtypeStruct((16, PAIR, 128), BF),
        ],
        in_specs=[ANY] * 2,
        out_specs=[ANY] * 2,
        scratch_shapes=[
            pltpu.SemaphoreType.DMA((2,)),
            pltpu.SemaphoreType.DMA((3,)),
            pltpu.SemaphoreType.DMA((3,)),
            pltpu.SemaphoreType.DMA,
            pltpu.SemaphoreType.DMA,
        ],
        compiler_params=params(3),
        name="heads_back",
    )(dq4, dkv)


def column_swap(blocks, send, recv, out, l_sem):
    y, z, x, c = coords()
    j = z * 2 + c

    def push(k, carry):
        t = (j + k) % 8
        remote(blocks.at[t], out.at[j], send, recv, dev(y, t // 2, x, t % 2)).start()
        return carry

    lax.fori_loop(1, 8, push, 0)
    here = pltpu.make_async_copy(blocks.at[j], out.at[j], l_sem)
    here.start()
    return here


def column_greet():
    y, z, x, c = coords()
    j = z * 2 + c

    def greet(k, carry):
        t = (j + k) % 8
        signal(dev(y, t // 2, x, t % 2))
        return carry

    lax.fori_loop(1, 8, greet, 0)
    pl.semaphore_wait(pltpu.get_barrier_semaphore(), 7)


def column_drain(send, recv, out):
    y, z, x, c = coords()
    drain = remote(out.at[pl.ds(0, 7)], out.at[pl.ds(0, 7)], send, recv, dev(y, z, x, 1 - c))
    drain.wait_send()
    drain.wait_recv()


def attn_return_kernel(blocks, out, l_sem, send, recv):
    column_greet()
    here = column_swap(blocks, send, recv, out, l_sem)
    here.wait()
    column_drain(send, recv, out)


def attn_return(blocks):
    return pl.pallas_call(
        attn_return_kernel,
        out_shape=jax.ShapeDtypeStruct((8, ROWS, HEAD_Q), BF),
        in_specs=[ANY],
        out_specs=ANY,
        scratch_shapes=[pltpu.SemaphoreType.DMA] * 3,
        compiler_params=params(4),
        name="attn_return",
    )(blocks)


def grad_attn_kernel(
    blocks, branch, attn, out, branch_sib, attn_sib, l_sem, send, recv, sib_send, sib_recv
):
    y, z, x, c = coords()
    sibling = dev(y, z, x, 1 - c)
    column_greet()
    here = column_swap(blocks, send, recv, out, l_sem)
    one = remote(branch, branch_sib, sib_send.at[0], sib_recv.at[0], sibling)
    one.start()
    two = remote(attn, attn_sib, sib_send.at[1], sib_recv.at[1], sibling)
    two.start()
    here.wait()
    column_drain(send, recv, out)
    one.wait()
    two.wait()


def grad_attn_out(blocks, branch, attn):
    return pl.pallas_call(
        grad_attn_kernel,
        out_shape=[
            jax.ShapeDtypeStruct((8, ROWS, HEAD_Q), BF),
            jax.ShapeDtypeStruct((ROWS, MODEL_WIDTH), BF),
            jax.ShapeDtypeStruct((ROWS, Q_HALF), BF),
        ],
        in_specs=[ANY] * 3,
        out_specs=[ANY] * 3,
        scratch_shapes=[pltpu.SemaphoreType.DMA] * 3
        + [pltpu.SemaphoreType.DMA((2,)), pltpu.SemaphoreType.DMA((2,))],
        compiler_params=params(5),
        name="grad_attn_out",
    )(blocks, branch, attn)


def dispatch_kernel(xs, gs, x_in, g_in, l_sem, send, recv, f_send, f_recv):
    y, z, x, c = coords()
    me = z * 4 + x
    sibling = dev(y, z, x, 1 - c)
    plane_greet(y, me, c, sibling)
    pairs = ((xs, x_in), (gs, g_in))

    for a, (src, dst) in enumerate(pairs):

        def push(k, carry):
            t = (me + k) % 16
            remote(
                src.at[t], dst.at[c, me], send.at[a, k], recv.at[a, k], dev(y, t // 4, t % 4, c)
            ).start()
            return carry

        lax.fori_loop(1, 16, push, 0)
    here = []
    for a, (src, dst) in enumerate(pairs):
        copy = pltpu.make_async_copy(src.at[me], dst.at[c, me], l_sem.at[a])
        copy.start()
        here.append(copy)
        remote(src.at[me], dst.at[c, me], f_send.at[a], f_recv.at[a], sibling).start()
    for a, (src, dst) in enumerate(pairs):

        def forward(k, carry):
            s = (me + 16 - k) % 16
            t = (me + k) % 16
            arrived = remote(
                src.at[t], dst.at[c, s], send.at[a, k], recv.at[a, k], dev(y, t // 4, t % 4, c)
            )
            arrived.wait_recv()
            remote(dst.at[c, s], dst.at[c, s], f_send.at[a], f_recv.at[a], sibling).start()
            arrived.wait_send()
            return carry

        lax.fori_loop(1, 16, forward, 0)
    for a, (src, dst) in enumerate(pairs):
        here[a].wait()
        drain = remote(dst.at[c], dst.at[1 - c], f_send.at[a], f_recv.at[a], sibling)
        drain.wait_send()
        drain.wait_recv()


def dispatch(xs, gs):
    shape = jax.ShapeDtypeStruct((2, 16, SLOTS, MODEL_WIDTH), BF)
    return pl.pallas_call(
        dispatch_kernel,
        out_shape=[shape, shape],
        in_specs=[ANY] * 2,
        out_specs=[ANY] * 2,
        scratch_shapes=[
            pltpu.SemaphoreType.DMA((2,)),
            pltpu.SemaphoreType.DMA((2, 16)),
            pltpu.SemaphoreType.DMA((2, 16)),
            pltpu.SemaphoreType.DMA((2,)),
            pltpu.SemaphoreType.DMA((2,)),
        ],
        compiler_params=params(6),
        name="dispatch",
    )(xs, gs)


def give_back_kernel(
    po, pg, o_ret, g_ret, own_o, own_g, sib_o, sib_g, l_sem, h_sem, s_send, s_recv, send, recv
):
    y, z, x, c = coords()
    me = z * 4 + x
    sibling = dev(y, z, x, 1 - c)
    plane_greet(y, me, c, sibling)
    arrays = ((po, own_o, sib_o, o_ret), (pg, own_g, sib_g, g_ret))
    loads = []
    for a, (part, own, sib, ret) in enumerate(arrays):
        load = pltpu.make_async_copy(part.at[c], own, l_sem.at[a])
        load.start()
        loads.append(load)

    def swap(k, carry):
        t = (me + k) % 16
        for a, (part, own, sib, ret) in enumerate(arrays):
            remote(part.at[1 - c, t], sib.at[t], s_send.at[a], s_recv.at[a, k % 16], sibling).start()
        return carry

    lax.fori_loop(1, 17, swap, 0)
    for load in loads:
        load.wait()

    def add(k, carry):
        t = (me + k) % 16
        for a, (part, own, sib, ret) in enumerate(arrays):
            remote(
                part.at[1 - c, t], sib.at[t], s_send.at[a], s_recv.at[a, k % 16], sibling
            ).wait_recv()
            own[t] = (own[t].astype(F32) + sib[t].astype(F32)).astype(BF)
        return carry

    def push(k, carry):
        add(k, carry)
        t = (me + k) % 16
        for a, (part, own, sib, ret) in enumerate(arrays):
            remote(own.at[t], ret.at[me], send.at[a], recv.at[a], dev(y, t // 4, t % 4, c)).start()
        return carry

    lax.fori_loop(1, 16, push, 0)
    add(16, 0)
    here = []
    for a, (part, own, sib, ret) in enumerate(arrays):
        copy = pltpu.make_async_copy(own.at[me], ret.at[me], h_sem.at[a])
        copy.start()
        here.append(copy)
    for a, (part, own, sib, ret) in enumerate(arrays):
        here[a].wait()
        remote(part.at[1 - c], sib, s_send.at[a], s_recv.at[a, 0], sibling).wait_send()
        drain = remote(
            own.at[pl.ds(0, 15)], ret.at[pl.ds(0, 15)], send.at[a], recv.at[a], sibling
        )
        drain.wait_send()
        drain.wait_recv()


def give_back(po, pg):
    shape = jax.ShapeDtypeStruct((16, SLOTS, MODEL_WIDTH), BF)
    buffer = pltpu.VMEM((16, SLOTS, MODEL_WIDTH), BF)
    return pl.pallas_call(
        give_back_kernel,
        out_shape=[shape, shape],
        in_specs=[ANY] * 2,
        out_specs=[ANY] * 2,
        scratch_shapes=[buffer] * 4
        + [
            pltpu.SemaphoreType.DMA((2,)),
            pltpu.SemaphoreType.DMA((2,)),
            pltpu.SemaphoreType.DMA((2,)),
            pltpu.SemaphoreType.DMA((2, 16)),
            pltpu.SemaphoreType.DMA((2,)),
            pltpu.SemaphoreType.DMA((2,)),
        ],
        compiler_params=params(7, 32 << 20),
        name="give_back",
    )(po, pg)


def reduce_kernel(
    g0, g1, g2, g3, partial, out, sib_partial,
    a0, a1, a2, a3, b0, b1, b2, b3, c0, c1, c2, c3, s0, s1, s2, s3, t0, t1, t2, t3,
    total, give, send, recv, sib_send, sib_recv,
):
    y, z, x, c = coords()
    place = {"y": y, "z": z, "x": x}
    sibling = dev(y, z, x, 1 - c)
    for axis in ("x", "y", "z"):
        for step in STEPS:
            signal(axis_peer(axis, step))
    signal(sibling)
    pl.semaphore_wait(pltpu.get_barrier_semaphore(), 10)
    other = remote(partial, sib_partial, sib_send.at[0], sib_recv.at[0], sibling)
    other.start()
    held = ((g0, g1, g2, g3), (s0, s1, s2, s3), (t0, t1, t2, t3))
    arrive = ((a0, a1, a2, a3), (b0, b1, b2, b3), (c0, c1, c2, c3))

    def at(phase, part, index):
        order = ORDERS[part][::-1]
        spot = [
            index if axis == order[phase] else slice(None)
            for axis in ("y", "z", "x")
            if axis not in order[:phase]
        ]
        return held[phase][part].at[tuple(spot)]

    for phase in range(3):
        copies = []
        for part in range(PARTS):
            axis = ORDERS[part][::-1][phase]
            for n, step in enumerate(STEPS):
                copy = remote(
                    at(phase, part, (place[axis] + step) % 4),
                    arrive[phase][part].at[n],
                    send.at[phase, part, n],
                    recv.at[phase, part, n],
                    axis_peer(axis, step),
                )
                copy.start()
                copies.append(copy)
        for copy in copies:
            copy.wait()
        for part in range(PARTS):
            axis = ORDERS[part][::-1][phase]
            mine = at(phase, part, place[axis])
            got = arrive[phase][part]
            if phase == 0:

                def add(i, carry):
                    p, q = i // 4, i % 4
                    value = mine[p, q].astype(F32)
                    for n in range(3):
                        value = value + got[n, p, q].astype(F32)
                    held[1][part][p, q] = value.astype(BF)
                    return carry

                lax.fori_loop(0, 16, add, 0)
            elif phase == 1:

                def add(p, carry):
                    value = mine[p].astype(F32)
                    for n in range(3):
                        value = value + got[n, p].astype(F32)
                    held[2][part][p] = value.astype(BF)
                    return carry

                lax.fori_loop(0, 4, add, 0)
            else:
                value = mine[...].astype(F32)
                for n in range(3):
                    value = value + got[n].astype(F32)
                total[:, pl.ds(STARTS[part], WIDTHS[part])] = value
    low, high = total[0:12], total[12:24]
    out[c, 0:12] = jnp.where(c == 0, low, high)
    out[c, 12:16] = jnp.zeros((4, PACK), F32)
    give[0:12] = jnp.where(c == 0, high, low)
    give[12:16] = jnp.zeros((4, PACK), F32)
    last = remote(give, out.at[c], sib_send.at[1], sib_recv.at[1], sibling)
    last.start()
    last.wait()
    other.wait()


def place_blocks(full):
    return full.reshape(4, 4, 4, 24, full.shape[-1])


def reduce_weights(grads, partial):
    scratch = (
        [pltpu.VMEM((3, 4, 4, 24, w), BF) for w in WIDTHS]
        + [pltpu.VMEM((3, 4, 24, w), BF) for w in WIDTHS]
        + [pltpu.VMEM((3, 24, w), BF) for w in WIDTHS]
        + [pltpu.VMEM((4, 4, 24, w), BF) for w in WIDTHS]
        + [pltpu.VMEM((4, 24, w), BF) for w in WIDTHS]
        + [pltpu.VMEM((24, PACK), F32), pltpu.VMEM((16, PACK), F32)]
    )
    return pl.pallas_call(
        reduce_kernel,
        out_shape=[
            jax.ShapeDtypeStruct((2, 16, PACK), F32),
            jax.ShapeDtypeStruct((ROWS, MODEL_WIDTH), F32),
        ],
        in_specs=[IN_VMEM] * PARTS + [ANY],
        out_specs=[IN_VMEM, ANY],
        scratch_shapes=scratch
        + [
            pltpu.SemaphoreType.DMA((3, PARTS, 3)),
            pltpu.SemaphoreType.DMA((3, PARTS, 3)),
            pltpu.SemaphoreType.DMA((2,)),
            pltpu.SemaphoreType.DMA((2,)),
        ],
        compiler_params=params(8, 48 << 20),
        name="reduce_weights",
    )(*[place_blocks(grad) for grad in grads], partial)


def dot(a, b, dims):
    return lax.dot_general(a, b, (dims, ((), ())), preferred_element_type=F32)


def wide(block, head, first):
    part = block[:, 64 * head : 64 * head + 64]
    zero = jnp.zeros_like(part)
    return jnp.concatenate([part, zero] if first else [zero, part], axis=1)


def allowed_keys(kb, first_ref, zq, hi):
    q_pos = hi * 256 + lax.broadcasted_iota(jnp.int32, (256, 256), 1)
    k_pos = kb * 256 + lax.broadcasted_iota(jnp.int32, (256, 256), 0)
    return (k_pos >= first_ref[zq]) & (k_pos <= q_pos)


def attn_forward_kernel(span, q_ref, kv_ref, first_ref, o_ref, ot_ref, lse_ref, qs, top, tot, acc):
    zq = pl.program_id(0)
    lo, hi = span[0, zq], span[1, zq]
    q = q_ref[0] * SCALE_QK
    for h in range(3):
        qs[h] = wide(q, h, True)
    top[...] = jnp.full_like(top, NEGATIVE)
    tot[...] = jnp.zeros_like(tot)
    acc[...] = jnp.zeros_like(acc)

    def step(kb, carry):
        kv = kv_ref[kb]
        ok = allowed_keys(kb, first_ref, zq, hi)
        for h in range(3):
            scores = jnp.where(ok, dot(kv, qs[h], ((1,), (1,))), NEGATIVE)
            old = top[h]
            new = jnp.maximum(old, jnp.max(scores, axis=0, keepdims=True))
            shrink = jnp.exp(old - new)
            probs = jnp.exp(scores - new)
            top[h] = new
            tot[h] = tot[h] * shrink + jnp.sum(probs, axis=0, keepdims=True)
            acc[h] = acc[h] * shrink + dot(kv, probs.astype(BF), ((0,), (0,)))
        return carry

    lax.fori_loop(lo, hi + 1, step, 0)
    heads = []
    for h in range(3):
        mixed = acc[h][64:] / tot[h]
        ot_ref[0, h] = mixed
        lse_ref[0, h] = top[h] + jnp.log(tot[h])
        heads.append(mixed)
    o_ref[0] = jnp.transpose(jnp.concatenate(heads, axis=0)).astype(BF)


def attn_forward(span, q, kv, first):
    return pl.pallas_call(
        attn_forward_kernel,
        out_shape=[
            jax.ShapeDtypeStruct((4, PAIR, HEAD_Q), BF),
            jax.ShapeDtypeStruct((4, 3, HD, PAIR), F32),
            jax.ShapeDtypeStruct((4, 3, 1, PAIR), F32),
        ],
        grid_spec=pltpu.PrefetchScalarGridSpec(
            num_scalar_prefetch=1,
            grid=(4,),
            in_specs=[
                pl.BlockSpec((1, PAIR, HEAD_Q), lambda i, s: (i, 0, 0)),
                pl.BlockSpec((16, PAIR, 128), lambda i, s: (0, 0, 0)),
                pl.BlockSpec((4, 1, PAIR), lambda i, s: (0, 0, 0)),
            ],
            out_specs=[
                pl.BlockSpec((1, PAIR, HEAD_Q), lambda i, s: (i, 0, 0)),
                pl.BlockSpec((1, 3, HD, PAIR), lambda i, s: (i, 0, 0, 0)),
                pl.BlockSpec((1, 3, 1, PAIR), lambda i, s: (i, 0, 0, 0)),
            ],
            scratch_shapes=[
                pltpu.VMEM((3, PAIR, 128), BF),
                pltpu.VMEM((3, 1, PAIR), F32),
                pltpu.VMEM((3, 1, PAIR), F32),
                pltpu.VMEM((3, 128, PAIR), F32),
            ],
        ),
        compiler_params=pltpu.CompilerParams(vmem_limit_bytes=32 << 20),
        name="attn_forward",
    )(span, q, kv, first)


def attn_backward_kernel(
    span, q_ref, kv_ref, first_ref, go_ref, ot_ref, lse_ref, dq_ref, dkv_ref, qs, gs, delta, dq, dkv
):
    zq = pl.program_id(0)
    lo, hi = span[0, zq], span[1, zq]
    q = q_ref[0] * SCALE_QK
    grad = go_ref[0]
    grad_t = jnp.transpose(grad.astype(F32))
    for h in range(3):
        qs[h] = wide(q, h, True)
        gs[h] = wide(grad, h, False)
        delta[h] = jnp.sum(grad_t[64 * h : 64 * h + 64] * ot_ref[0, h], axis=0, keepdims=True)
    dq[...] = jnp.zeros_like(dq)

    @pl.when(zq == 0)
    def _():
        dkv[...] = jnp.zeros_like(dkv)

    def step(kb, carry):
        kv = kv_ref[kb]
        ok = allowed_keys(kb, first_ref, zq, hi)
        total = dkv[kb]
        for h in range(3):
            probs = jnp.where(ok, jnp.exp(dot(kv, qs[h], ((1,), (1,))) - lse_ref[0, h]), 0.0)
            grad_probs = dot(kv, gs[h], ((1,), (1,)))
            grad_scores = (probs * (grad_probs - delta[h])).astype(BF)
            dq[h] = dq[h] + dot(kv, grad_scores, ((0,), (0,)))
            total = total + dot(grad_scores, qs[h], ((1,), (0,)))
            total = total + dot(probs.astype(BF), gs[h], ((1,), (0,)))
        dkv[kb] = total
        return carry

    lax.fori_loop(lo, hi + 1, step, 0)
    heads = jnp.concatenate([dq[h][:64] for h in range(3)], axis=0) * SCALE_QK
    dq_ref[0] = jnp.transpose(heads).astype(BF)

    @pl.when(zq == 3)
    def _():
        dkv_ref[...] = dkv[...].astype(BF)


def attn_backward(span, q, kv, first, grad, ot, lse):
    return pl.pallas_call(
        attn_backward_kernel,
        out_shape=[
            jax.ShapeDtypeStruct((4, PAIR, HEAD_Q), BF),
            jax.ShapeDtypeStruct((16, PAIR, 128), BF),
        ],
        grid_spec=pltpu.PrefetchScalarGridSpec(
            num_scalar_prefetch=1,
            grid=(4,),
            in_specs=[
                pl.BlockSpec((1, PAIR, HEAD_Q), lambda i, s: (i, 0, 0)),
                pl.BlockSpec((16, PAIR, 128), lambda i, s: (0, 0, 0)),
                pl.BlockSpec((4, 1, PAIR), lambda i, s: (0, 0, 0)),
                pl.BlockSpec((1, PAIR, HEAD_Q), lambda i, s: (i, 0, 0)),
                pl.BlockSpec((1, 3, HD, PAIR), lambda i, s: (i, 0, 0, 0)),
                pl.BlockSpec((1, 3, 1, PAIR), lambda i, s: (i, 0, 0, 0)),
            ],
            out_specs=[
                pl.BlockSpec((1, PAIR, HEAD_Q), lambda i, s: (i, 0, 0)),
                pl.BlockSpec((16, PAIR, 128), lambda i, s: (0, 0, 0)),
            ],
            scratch_shapes=[
                pltpu.VMEM((3, PAIR, 128), BF),
                pltpu.VMEM((3, PAIR, 128), BF),
                pltpu.VMEM((3, 1, PAIR), F32),
                pltpu.VMEM((3, 128, PAIR), F32),
                pltpu.VMEM((16, PAIR, 128), F32),
            ],
        ),
        compiler_params=pltpu.CompilerParams(vmem_limit_bytes=32 << 20),
        name="attn_backward",
    )(span, q, kv, first, grad, ot, lse)


def inverse_rms(values):
    return lax.rsqrt(jnp.mean(values * values, axis=-1, keepdims=True) + EPS)


def norm_backward(values, inverse, gain, grad_out):
    scaled = grad_out * gain
    return inverse * scaled - values * inverse**3 * jnp.mean(values * scaled, axis=-1, keepdims=True)


def column_sums(left, right):
    return lax.dot_general(left, right, (((0,), (0,)), ((), ())), precision=HIGH_PRECISION)


def only_column(rows, column):
    return jnp.broadcast_to((jnp.arange(EXTRA) == column).astype(F32), (rows, EXTRA))


def halves(matrix):
    return matrix.reshape(12, 2, Q_HALF).transpose(1, 0, 2)


def local(
    tokens,
    segment_ids,
    expert_ids,
    w_query,
    w_key,
    w_value,
    w_out,
    w_router,
    gain_attn,
    gain_moe,
    w_gate,
    w_up,
    w_down,
    cotangent,
):
    y, z, x, c = coords()
    key_value = jnp.concatenate(
        [w_key.reshape(12, 2, 4, HD), w_value.reshape(12, 2, 4, HD)], axis=3
    ).reshape(12, 2, KV_HALF)
    extra = jnp.concatenate(
        [w_router, gain_attn[:, None], gain_moe[:, None], jnp.zeros((12, EXTRA - 18), BF)], axis=1
    )
    pack = jnp.concatenate(
        [
            halves(w_query),
            key_value.transpose(1, 0, 2),
            halves(w_out.T),
            jnp.broadcast_to(extra[None], (2, 12, EXTRA)),
        ],
        axis=2,
    )
    pack = jnp.pad(pack, ((0, 0), (0, 4), (0, 0)))
    part_q, part_kv, part_out, part_extra, pair, seg_all = gather_weights(
        pack, tokens, segment_ids
    )
    pair, w_gate, w_up, w_down = lax.optimization_barrier((pair, w_gate, w_up, w_down))
    gate_w = lax.all_gather(w_gate, "dp", axis=0, tiled=True)
    up_w = lax.all_gather(w_up, "dp", axis=0, tiled=True)
    down_w = lax.all_gather(w_down, "dp", axis=1, tiled=True)
    full_q = part_q.reshape(MODEL_WIDTH, Q_HALF)
    full_kv = part_kv.reshape(MODEL_WIDTH, KV_HALF)
    half_out = part_out.reshape(MODEL_WIDTH, Q_HALF)
    full_extra = part_extra.reshape(MODEL_WIDTH, EXTRA)
    picks = (jnp.arange(EXTRA)[None, :] == jnp.arange(8)[:, None] + EXPERT_COUNT).astype(BF)
    gains = dot(picks, full_extra, ((1,), (1,)))
    gain_a, gain_m = gains[0:1], gains[1:2]
    router = full_extra[:, :EXPERT_COUNT]

    inputs2 = pair.reshape(PAIR, MODEL_WIDTH).astype(F32)
    inverse_a = inverse_rms(inputs2)
    normed = (inputs2 * inverse_a * gain_a).astype(BF)
    queries = dot(normed, full_q, ((1,), (0,))).astype(BF)
    keys_values = dot(normed, full_kv, ((1,), (0,))).astype(BF)
    q4 = queries.reshape(PAIR, 4, HEAD_Q).transpose(1, 0, 2)
    kv4 = keys_values.reshape(PAIR, 4, 128).transpose(1, 0, 2)
    q_in, kv_in, sib_out = heads_out(q4, kv4, half_out)

    segs = seg_all.reshape(1, 4096)
    counts = jnp.sum((segs < jnp.arange(16)[:, None]).astype(jnp.int32), axis=1)
    row_segs = lax.dynamic_index_in_dim(seg_all.reshape(4, 4, PAIR), x, 1, keepdims=False)
    first = jnp.sum(
        jnp.where(row_segs[:, :, None] == jnp.arange(16), counts, 0), axis=2
    )
    span = jnp.stack([first[:, 0] // PAIR, jnp.arange(4, dtype=jnp.int32) * 4 + x])
    first = first.reshape(4, 1, PAIR)
    attn_low, attn_t, lse = attn_forward(span, q_in, kv_in, first)
    attn = attn_return(attn_low.reshape(8, ROWS, HEAD_Q))
    attn = attn.reshape(4, 2, ROWS, HEAD_Q).transpose(1, 2, 0, 3).reshape(2, ROWS, Q_HALF)

    own_attn = jnp.where(c == 0, attn[0], attn[1])
    other_attn = jnp.where(c == 0, attn[1], attn[0])
    inputs = tokens.astype(F32)
    middle = (
        inputs
        + dot(own_attn, half_out, ((1,), (1,)))
        + dot(other_attn, sib_out, ((1,), (1,)))
    )
    inverse_m = inverse_rms(middle)
    moe_in = (middle * inverse_m * gain_m).astype(BF)
    logits = dot(moe_in, router, ((1,), (0,)))
    chosen = (expert_ids[:, :, None] == jnp.arange(EXPERT_COUNT, dtype=jnp.int32)).astype(F32)
    picked = jnp.sum(chosen * logits[:, None, :], axis=-1)
    gates = jax.nn.softmax(picked, axis=-1)
    used = jnp.sum(chosen, axis=1)
    earlier = (jnp.arange(ROWS)[:, None] > jnp.arange(ROWS)[None, :]).astype(BF)
    before = dot(earlier, used.astype(BF), ((1,), (0,)))
    place = jnp.sum(chosen * before[:, None, :], axis=-1)
    slot = jnp.where(
        place < EXPERT_CAPACITY, expert_ids * SLOTS + place.astype(jnp.int32), -1
    )
    hit = (slot.T[:, :, None] == jnp.arange(EXPERT_COUNT * SLOTS, dtype=jnp.int32)).astype(F32)
    both = (hit[0] + hit[1]).astype(BF)
    slot_gate = jnp.sum(hit * gates.T[:, :, None], axis=(0, 1))
    slots_in = dot(both, moe_in, ((0,), (0,))).astype(BF)
    grad_slots = (dot(both, cotangent, ((0,), (0,))) * slot_gate[:, None]).astype(BF)
    blocks = (EXPERT_COUNT, SLOTS, MODEL_WIDTH)
    x_in, g_in = dispatch(slots_in.reshape(blocks), grad_slots.reshape(blocks))

    expert_in = x_in.reshape(-1, MODEL_WIDTH)
    grad_expert = g_in.reshape(-1, MODEL_WIDTH)
    gate_val = dot(expert_in, gate_w, ((1,), (0,)))
    up_val = dot(expert_in, up_w, ((1,), (0,)))
    sig = jax.nn.sigmoid(gate_val)
    hidden = (gate_val * sig * up_val).astype(BF)
    part_out = dot(hidden, down_w, ((1,), (0,))).astype(BF)
    grad_hidden = dot(grad_expert, down_w, ((1,), (1,)))
    grad_gate = (grad_hidden * up_val * sig * (1.0 + gate_val * (1.0 - sig))).astype(BF)
    grad_up = (grad_hidden * gate_val * sig).astype(BF)
    part_grad = dot(grad_gate, gate_w, ((1,), (1,))) + dot(grad_up, up_w, ((1,), (1,)))
    shape = (2, 16, SLOTS, MODEL_WIDTH)
    out_ret, grad_ret = give_back(part_out.reshape(shape), part_grad.astype(BF).reshape(shape))
    grad_w_gate = dot(expert_in, grad_gate, ((0,), (0,))).astype(BF)
    grad_w_up = dot(expert_in, grad_up, ((0,), (0,))).astype(BF)
    grad_w_down = dot(hidden, grad_expert, ((0,), (0,))).astype(BF)
    expert_grads = (
        lax.psum_scatter(grad_w_gate, "dp", scatter_dimension=0, tiled=True).astype(F32),
        lax.psum_scatter(grad_w_up, "dp", scatter_dimension=0, tiled=True).astype(F32),
        lax.psum_scatter(grad_w_down, "dp", scatter_dimension=1, tiled=True).astype(F32),
    )

    grad_output = cotangent.astype(F32)
    out_ret = out_ret.reshape(EXPERT_COUNT * SLOTS, MODEL_WIDTH)
    grad_ret = grad_ret.reshape(EXPERT_COUNT * SLOTS, MODEL_WIDTH)
    rows_out = [dot(hit[k].astype(BF), out_ret, ((1,), (0,))) for k in range(2)]
    block_out = (middle + gates[:, 0:1] * rows_out[0] + gates[:, 1:2] * rows_out[1]).astype(BF)
    grad_pair = jnp.stack([jnp.sum(grad_output * rows, axis=-1) for rows in rows_out], axis=-1)
    grad_pick = gates * (grad_pair - jnp.sum(gates * grad_pair, axis=-1, keepdims=True))
    grad_logits = jnp.sum(chosen * grad_pick[:, :, None], axis=1)
    grad_moe_in = dot(both, grad_ret, ((1,), (0,))) + lax.dot_general(
        grad_logits, router.astype(F32), (((1,), (1,)), ((), ())), precision=HIGH_PRECISION
    )
    g_router = column_sums(moe_in.astype(F32), jnp.pad(grad_logits, ((0, 0), (0, EXTRA - EXPERT_COUNT))))
    g_gain_m = column_sums(grad_moe_in * middle * inverse_m, only_column(ROWS, EXPERT_COUNT + 1))
    grad_middle = grad_output + norm_backward(middle, inverse_m, gain_m, grad_moe_in)
    branch = grad_middle.astype(BF)
    own_heads = dot(branch, half_out, ((1,), (0,))).astype(BF)
    other_heads = dot(branch, sib_out, ((1,), (0,))).astype(BF)
    grad_heads = jnp.stack(
        [jnp.where(c == 0, own_heads, other_heads), jnp.where(c == 0, other_heads, own_heads)]
    )
    grad_heads = grad_heads.reshape(2, ROWS, 4, HEAD_Q).transpose(2, 0, 1, 3)
    go_in, branch_sib, attn_sib = grad_attn_out(
        grad_heads.reshape(8, ROWS, HEAD_Q), branch, other_attn
    )
    dq_low, dkv_low = attn_backward(
        span, q_in, kv_in, first, go_in.reshape(4, PAIR, HEAD_Q), attn_t, lse
    )
    dq_in, dkv_in = heads_back(dq_low, dkv_low)
    grad_q = dq_in.transpose(1, 0, 2).reshape(PAIR, Q_HALF)
    grad_kv = jnp.sum(dkv_in.reshape(4, 4, PAIR, 128).astype(F32), axis=1).astype(BF)
    grad_kv = grad_kv.transpose(1, 0, 2).reshape(PAIR, KV_HALF)

    part_normed = dot(grad_q, full_q, ((1,), (1,))) + dot(
        grad_kv, full_kv, ((1,), (1,))
    )
    g_gain_a = column_sums(part_normed * inputs2 * inverse_a, only_column(PAIR, EXPERT_COUNT))
    g_query = dot(normed, grad_q, ((0,), (0,))).astype(BF)
    g_kv = dot(normed, grad_kv, ((0,), (0,))).astype(BF)
    g_extra = (g_router + g_gain_m + g_gain_a).astype(BF)
    g_out = (dot(branch, own_attn, ((0,), (0,))) + dot(branch_sib, attn_sib, ((0,), (0,)))).astype(BF)
    by_core = part_normed.reshape(2, ROWS, MODEL_WIDTH)
    own_part = lax.dynamic_index_in_dim(by_core, c, 0, keepdims=False)
    other_part = lax.dynamic_index_in_dim(by_core, 1 - c, 0, keepdims=False)
    reduced, sib_part = reduce_weights((g_query, g_kv, g_out, g_extra), other_part)
    grad_normed = own_part + sib_part
    grad_tokens = grad_middle + norm_backward(
        inputs, inverse_rms(inputs), gain_a, grad_normed
    )
    reduced = reduced[:, :12]
    r_query = reduced[:, :, :Q_HALF].transpose(1, 0, 2).reshape(12, HEADS * HD)
    r_kv = reduced[:, :, Q_HALF : Q_HALF + KV_HALF].transpose(1, 0, 2).reshape(12, KV, 2, HD)
    r_out = reduced[:, :, STARTS[2] : STARTS[3]].transpose(1, 0, 2).reshape(12, HEADS * HD)
    r_extra = jnp.sum(reduced[:, :, STARTS[3] :], axis=0)
    return (
        block_out,
        grad_tokens,
        r_query,
        r_kv[:, :, 0].reshape(12, KV * HD),
        r_kv[:, :, 1].reshape(12, KV * HD),
        r_out.T,
        r_extra[:, :EXPERT_COUNT],
        r_extra[:, EXPERT_COUNT],
        r_extra[:, EXPERT_COUNT + 1],
        expert_grads[0],
        expert_grads[1],
        expert_grads[2],
    )


def solution(mesh):
    rows, flat, dense = P(("dp", "ctx"), None), P(("dp", "ctx")), P("dp", "ctx")
    placed = (
        rows, dense, rows, rows, rows, rows, P(None, ("dp", "ctx")), rows, flat, flat,
        dense, dense, P("ctx", "dp"), rows,
    )
    return jax.shard_map(
        local,
        mesh=mesh,
        in_specs=placed,
        out_specs=(
            rows, rows, rows, rows, rows, P(None, ("dp", "ctx")), rows, flat, flat,
            dense, dense, P("ctx", "dp"),
        ),
        check_vma=False,
    )
```

```python
import functools

import jax
import jax.numpy as jnp
from jax import lax
from jax.experimental import pallas as pl
from jax.experimental.pallas import tpu as pltpu
from jax.sharding import PartitionSpec as P

MODEL_WIDTH = 1536
HEADS = 24
KV = 8
HD = 64
EXPERT_COUNT = 16
FF = 1024
EXPERT_CAPACITY = 20
SLOTS = 24
ROWS = 128
PAIR = 256
HEAD_Q = 192
Q_HALF = 768
KV_HALF = 512
EXTRA = 128
PACK = Q_HALF + KV_HALF + EXTRA + Q_HALF

EPS = 1e-05
SCALE_QK = 0.125
NEGATIVE = -1e30
HIGH_PRECISION = lax.Precision.HIGHEST
MESH = pl.DeviceIdType.MESH
ANY = pl.BlockSpec(memory_space=pl.ANY)
IN_VMEM = pl.BlockSpec(memory_space=pltpu.VMEM)
BF = jnp.bfloat16
F32 = jnp.float32


def dot(a, b, dims):
    return lax.dot_general(a, b, (dims, ((), ())), preferred_element_type=F32)


def coords():
    i = lax.axis_index("ctx")
    return lax.axis_index("dp"), i // 8, (i // 2) % 4, i % 2


def dev(y, z, x, c):
    return (y, z * 8 + x * 2 + c)


def signal(target):
    pl.semaphore_signal(
        pltpu.get_barrier_semaphore(), inc=1, device_id=target, device_id_type=MESH
    )


def remote(src, dst, send, recv, target):
    return pltpu.make_async_remote_copy(
        src_ref=src, dst_ref=dst, send_sem=send, recv_sem=recv, device_id=target, device_id_type=MESH
    )


def params(cid, vmem=None):
    return pltpu.CompilerParams(collective_id=cid, has_side_effects=True, vmem_limit_bytes=vmem)


def axis_peer(axis, step):
    y, z, x, c = coords()
    if axis == "y":
        return dev((y + step) % 4, z, x, c)
    if axis == "z":
        return dev(y, (z + step) % 4, x, c)
    return dev(y, z, (x + step) % 4, c)


ORDERS = (("x", "z", "y"), ("y", "x", "z"), ("z", "y", "x"), ("y", "x", "z"))
WIDTHS = (Q_HALF, KV_HALF, Q_HALF, EXTRA)
STARTS = (0, Q_HALF, Q_HALF + KV_HALF, 2 * Q_HALF + KV_HALF)
PARTS = 4
STEPS = (1, 3, 2)


def slab(ref, done, y, z, x):
    return ref.at[
        slice(None) if "y" in done else y,
        slice(None) if "z" in done else z,
        slice(None) if "x" in done else x,
    ]


def gather_kernel(
    pack, tokens, segs, out0, out1, out2, out3, pair, seg_all,
    sib, block, p_send, p_recv, l_sem, s_send, s_recv, sib_send, sib_recv,
):
    y, z, x, c = coords()
    outs = (out0, out1, out2, out3)
    me = z * 8 + x * 2 + c
    sibling = dev(y, z, x, 1 - c)

    def greet(k, carry):
        signal((y, (me + k) % 32))
        return carry

    lax.fori_loop(1, 32, greet, 0)
    for step in STEPS:
        signal(axis_peer("y", step))
    pl.semaphore_wait(pltpu.get_barrier_semaphore(), 34)

    first = remote(pack.at[1 - c], sib, sib_send.at[0], sib_recv.at[0], sibling)
    first.start()
    second = remote(tokens, pair.at[c], sib_send.at[1], sib_recv.at[1], sibling)
    second.start()
    own_rows = pltpu.make_async_copy(tokens, pair.at[c], l_sem.at[4])
    own_rows.start()
    own_segs = pltpu.make_async_copy(segs, seg_all.at[me], l_sem.at[5])
    own_segs.start()

    def spread(k, carry):
        remote(segs, seg_all.at[me], s_send, s_recv, (y, (me + k) % 32)).start()
        return carry

    lax.fori_loop(1, 32, spread, 0)

    first.wait()
    own = pack[c, :12].astype(F32)
    other = sib[:12].astype(F32)
    low = jnp.where(c == 0, own, other)
    high = jnp.where(c == 0, other, own)
    block[...] = jnp.concatenate([low, high], axis=0).astype(BF)

    locals_ = []
    for part in range(PARTS):
        cols = pl.ds(STARTS[part], WIDTHS[part])
        here = pltpu.make_async_copy(block.at[:, cols], outs[part].at[y, z, x], l_sem.at[part])
        here.start()
        locals_.append(here)
    for phase in range(3):
        copies = []
        for part in range(PARTS):
            axis = ORDERS[part][phase]
            done = ORDERS[part][:phase]
            for n, step in enumerate(STEPS):
                dst = slab(outs[part], done, y, z, x)
                src = block.at[:, pl.ds(STARTS[part], WIDTHS[part])] if phase == 0 else dst
                copy = remote(
                    src, dst, p_send.at[phase, part, n], p_recv.at[phase, part, n], axis_peer(axis, step)
                )
                copy.start()
                copies.append(copy)
        if phase == 0:
            for here in locals_:
                here.wait()
        for copy in copies:
            copy.wait()
    second.wait()
    own_rows.wait()
    own_segs.wait()
    drain = remote(
        seg_all.at[pl.ds(0, 31)], seg_all.at[pl.ds(0, 31)], s_send, s_recv, sibling
    )
    drain.wait_send()
    drain.wait_recv()


def gather_weights(pack, tokens, segs):
    return pl.pallas_call(
        gather_kernel,
        out_shape=[jax.ShapeDtypeStruct((4, 4, 4, 24, width), BF) for width in WIDTHS]
        + [
            jax.ShapeDtypeStruct((2, ROWS, MODEL_WIDTH), BF),
            jax.ShapeDtypeStruct((32, 1, 128), jnp.int32),
        ],
        in_specs=[IN_VMEM, ANY, ANY],
        out_specs=[ANY] * 6,
        scratch_shapes=[
            pltpu.VMEM((16, PACK), BF),
            pltpu.VMEM((24, PACK), BF),
            pltpu.SemaphoreType.DMA((3, PARTS, 3)),
            pltpu.SemaphoreType.DMA((3, PARTS, 3)),
            pltpu.SemaphoreType.DMA((6,)),
            pltpu.SemaphoreType.DMA,
            pltpu.SemaphoreType.DMA,
            pltpu.SemaphoreType.DMA((2,)),
            pltpu.SemaphoreType.DMA((2,)),
        ],
        compiler_params=params(1),
        name="gather_weights",
    )(pack, tokens, segs)


def plane_greet(y, me, c, sibling):
    def greet(k, carry):
        t = (me + k) % 16
        signal(dev(y, t // 4, t % 4, c))
        return carry

    lax.fori_loop(1, 16, greet, 0)
    if sibling is not None:
        signal(sibling)
        pl.semaphore_wait(pltpu.get_barrier_semaphore(), 16)
    else:
        pl.semaphore_wait(pltpu.get_barrier_semaphore(), 15)


def heads_out_kernel(q4, kv4, half, q_in, kv_in, half_sib, l_sem, q_send, q_recv, k_send, k_recv, o_send, o_recv):
    y, z, x, c = coords()
    me = z * 4 + x
    sibling = dev(y, z, x, 1 - c)
    plane_greet(y, me, c, sibling)

    def send_kv(k, carry):
        t = (me + k) % 16
        remote(kv4.at[t // 4], kv_in.at[me], k_send, k_recv, dev(y, t // 4, t % 4, c)).start()
        return carry

    q_copies = []
    for n, step in enumerate(STEPS):
        to = (z + step) % 4
        copy = remote(q4.at[to], q_in.at[z], q_send.at[n], q_recv.at[n], dev(y, to, x, c))
        copy.start()
        q_copies.append(copy)
    lax.fori_loop(1, 16, send_kv, 0)
    swap = remote(half, half_sib, o_send, o_recv, sibling)
    swap.start()
    here = [
        pltpu.make_async_copy(q4.at[z], q_in.at[z], l_sem.at[0]),
        pltpu.make_async_copy(kv4.at[z], kv_in.at[me], l_sem.at[1]),
    ]
    for copy in here:
        copy.start()
    for copy in here:
        copy.wait()
    for copy in q_copies:
        copy.wait()
    drain = remote(kv_in.at[pl.ds(0, 15)], kv_in.at[pl.ds(0, 15)], k_send, k_recv, sibling)
    drain.wait_send()
    drain.wait_recv()
    swap.wait()


def heads_out(q4, kv4, half):
    return pl.pallas_call(
        heads_out_kernel,
        out_shape=[
            jax.ShapeDtypeStruct((4, PAIR, HEAD_Q), BF),
            jax.ShapeDtypeStruct((16, PAIR, 128), BF),
            jax.ShapeDtypeStruct((MODEL_WIDTH, Q_HALF), BF),
        ],
        in_specs=[ANY] * 3,
        out_specs=[ANY] * 3,
        scratch_shapes=[
            pltpu.SemaphoreType.DMA((3,)),
            pltpu.SemaphoreType.DMA((3,)),
            pltpu.SemaphoreType.DMA((3,)),
            pltpu.SemaphoreType.DMA,
            pltpu.SemaphoreType.DMA,
            pltpu.SemaphoreType.DMA,
            pltpu.SemaphoreType.DMA,
        ],
        compiler_params=params(2),
        name="heads_out",
    )(q4, kv4, half)


def heads_back_kernel(dq4, dkv, dq_in, dkv_in, l_sem, q_send, q_recv, k_send, k_recv):
    y, z, x, c = coords()
    me = z * 4 + x
    plane_greet(y, me, c, None)

    def send_kv(k, carry):
        t = (me + k) % 16
        remote(dkv.at[t], dkv_in.at[me], k_send, k_recv, dev(y, t // 4, t % 4, c)).start()
        return carry

    q_copies = []
    for n, step in enumerate(STEPS):
        to = (z + step) % 4
        copy = remote(dq4.at[to], dq_in.at[z], q_send.at[n], q_recv.at[n], dev(y, to, x, c))
        copy.start()
        q_copies.append(copy)
    lax.fori_loop(1, 16, send_kv, 0)
    here = [
        pltpu.make_async_copy(dq4.at[z], dq_in.at[z], l_sem.at[0]),
        pltpu.make_async_copy(dkv.at[me], dkv_in.at[me], l_sem.at[1]),
    ]
    for copy in here:
        copy.start()
    for copy in here:
        copy.wait()
    for copy in q_copies:
        copy.wait()
    neighbour = dev(y, (z + 1) % 4, x, c)
    drain = remote(dkv_in.at[pl.ds(0, 15)], dkv_in.at[pl.ds(0, 15)], k_send, k_recv, neighbour)
    drain.wait_send()
    drain.wait_recv()


def heads_back(dq4, dkv):
    return pl.pallas_call(
        heads_back_kernel,
        out_shape=[
            jax.ShapeDtypeStruct((4, PAIR, HEAD_Q), BF),
            jax.ShapeDtypeStruct((16, PAIR, 128), BF),
        ],
        in_specs=[ANY] * 2,
        out_specs=[ANY] * 2,
        scratch_shapes=[
            pltpu.SemaphoreType.DMA((2,)),
            pltpu.SemaphoreType.DMA((3,)),
            pltpu.SemaphoreType.DMA((3,)),
            pltpu.SemaphoreType.DMA,
            pltpu.SemaphoreType.DMA,
        ],
        compiler_params=params(3),
        name="heads_back",
    )(dq4, dkv)


def column_swap(blocks, send, recv, out, l_sem):
    y, z, x, c = coords()
    j = z * 2 + c

    def push(k, carry):
        t = (j + k) % 8
        remote(blocks.at[t], out.at[j], send, recv, dev(y, t // 2, x, t % 2)).start()
        return carry

    lax.fori_loop(1, 8, push, 0)
    here = pltpu.make_async_copy(blocks.at[j], out.at[j], l_sem)
    here.start()
    return here


def column_greet():
    y, z, x, c = coords()
    j = z * 2 + c

    def greet(k, carry):
        t = (j + k) % 8
        signal(dev(y, t // 2, x, t % 2))
        return carry

    lax.fori_loop(1, 8, greet, 0)
    pl.semaphore_wait(pltpu.get_barrier_semaphore(), 7)


def column_drain(send, recv, out):
    y, z, x, c = coords()
    drain = remote(out.at[pl.ds(0, 7)], out.at[pl.ds(0, 7)], send, recv, dev(y, z, x, 1 - c))
    drain.wait_send()
    drain.wait_recv()


def attn_return_kernel(blocks, out, l_sem, send, recv):
    column_greet()
    here = column_swap(blocks, send, recv, out, l_sem)
    here.wait()
    column_drain(send, recv, out)


def attn_return(blocks):
    return pl.pallas_call(
        attn_return_kernel,
        out_shape=jax.ShapeDtypeStruct((8, ROWS, HEAD_Q), BF),
        in_specs=[ANY],
        out_specs=ANY,
        scratch_shapes=[pltpu.SemaphoreType.DMA] * 3,
        compiler_params=params(4),
        name="attn_return",
    )(blocks)


def grad_attn_kernel(
    blocks, branch, attn, out, branch_sib, attn_sib, l_sem, send, recv, sib_send, sib_recv
):
    y, z, x, c = coords()
    sibling = dev(y, z, x, 1 - c)
    column_greet()
    here = column_swap(blocks, send, recv, out, l_sem)
    one = remote(branch, branch_sib, sib_send.at[0], sib_recv.at[0], sibling)
    one.start()
    two = remote(attn, attn_sib, sib_send.at[1], sib_recv.at[1], sibling)
    two.start()
    here.wait()
    column_drain(send, recv, out)
    one.wait()
    two.wait()


def grad_attn_out(blocks, branch, attn):
    return pl.pallas_call(
        grad_attn_kernel,
        out_shape=[
            jax.ShapeDtypeStruct((8, ROWS, HEAD_Q), BF),
            jax.ShapeDtypeStruct((ROWS, MODEL_WIDTH), BF),
            jax.ShapeDtypeStruct((ROWS, Q_HALF), BF),
        ],
        in_specs=[ANY] * 3,
        out_specs=[ANY] * 3,
        scratch_shapes=[pltpu.SemaphoreType.DMA] * 3
        + [pltpu.SemaphoreType.DMA((2,)), pltpu.SemaphoreType.DMA((2,))],
        compiler_params=params(5),
        name="grad_attn_out",
    )(blocks, branch, attn)


def flat_rows(blocks):
    return blocks.reshape(blocks.shape[0] * SLOTS, blocks.shape[2])


def experts_kernel(
    xs, gs, gate_w, up_w, down_w, out_ret, grad_ret, d_gate, d_up, d_down,
    x_all, g_all, wg, wu, wd, gate_v, up_v, hidden, g_gate, g_up, part_o, part_g, sib_o, sib_g,
    v_gate, v_up, v_down,
    w_sem, l_sem, send, recv, f_send, f_recv, s_send, s_recv, r_send, r_recv, o_sem,
):
    y, z, x, c = coords()
    me = z * 4 + x
    sibling = dev(y, z, x, 1 - c)
    plane_greet(y, me, c, sibling)
    loads = [
        pltpu.make_async_copy(src, dst, w_sem.at[n])
        for n, (src, dst) in enumerate(((gate_w, wg), (up_w, wu), (down_w, wd)))
    ]
    for load in loads:
        load.start()
    arrays = ((xs, x_all), (gs, g_all))

    def scatter(a):
        src, dst = arrays[a]

        def push(k, carry):
            t = (me + k) % 16
            remote(
                src.at[t], dst.at[c * 16 + me], send.at[a, k], recv.at[a, k], dev(y, t // 4, t % 4, c)
            ).start()
            return carry

        lax.fori_loop(1, 16, push, 0)
        pltpu.make_async_copy(src.at[me], dst.at[c * 16 + me], l_sem.at[a]).start()
        remote(src.at[me], dst.at[c * 16 + me], f_send.at[a], f_recv.at[a], sibling).start()

    def hand_over(a):
        src, dst = arrays[a]

        def forward(k, carry):
            s = (me + 16 - k) % 16
            t = (me + k) % 16
            arrived = remote(
                src.at[t], dst.at[c * 16 + s], send.at[a, k], recv.at[a, k], dev(y, t // 4, t % 4, c)
            )
            arrived.wait_recv()
            remote(
                dst.at[c * 16 + s], dst.at[c * 16 + s], f_send.at[a], f_recv.at[a], sibling
            ).start()
            arrived.wait_send()
            return carry

        lax.fori_loop(1, 16, forward, 0)

    def settle(a):
        src, dst = arrays[a]
        pltpu.make_async_copy(src.at[me], dst.at[c * 16 + me], l_sem.at[a]).wait()
        half = pl.ds(0, 16)
        drain = remote(dst.at[half], dst.at[half], f_send.at[a], f_recv.at[a], sibling)
        drain.wait_send()
        drain.wait_recv()

    def swap(part, sib, a):
        rows = pl.ds((1 - c) * 16, 16)
        return remote(part.at[rows], sib, s_send.at[a], s_recv.at[a], sibling)

    def give(part, sib, ret, a):
        def add(t):
            rows = c * 16 + t
            part[rows] = (
                part[rows].astype(F32) + sib[t].astype(F32)
            ).astype(BF)
            return part.at[rows]

        def push(k, carry):
            t = (me + k) % 16
            remote(add(t), ret.at[me], r_send.at[a], r_recv.at[a], dev(y, t // 4, t % 4, c)).start()
            return carry

        lax.fori_loop(1, 16, push, 0)
        pltpu.make_async_copy(add(me), ret.at[me], l_sem.at[2 + a]).start()

    def given(part, ret, a):
        pltpu.make_async_copy(part.at[c * 16 + me], ret.at[me], l_sem.at[2 + a]).wait()
        drain = remote(ret.at[pl.ds(0, 15)], ret.at[pl.ds(0, 15)], r_send.at[a], r_recv.at[a], sibling)
        drain.wait_send()
        drain.wait_recv()

    def tile(n):
        h = 1 - c if n == 0 else c
        rows = 16 * SLOTS
        return pl.ds(h * 16, 16), pl.ds(pl.multiple_of(h * rows, rows), rows)

    scatter(0)
    hand_over(0)
    scatter(1)
    settle(0)
    for load in loads:
        load.wait()
    for n in range(2):
        blocks, rows = tile(n)
        rows_in = flat_rows(x_all[blocks])
        gate_val = dot(rows_in, wg[...], ((1,), (0,)))
        up_val = dot(rows_in, wu[...], ((1,), (0,)))
        gate_v[rows] = gate_val
        up_v[rows] = up_val
        low = (gate_val * jax.nn.sigmoid(gate_val) * up_val).astype(BF)
        hidden[rows] = low
        part_o[blocks] = dot(low, wd[...], ((1,), (0,))).astype(BF).reshape(16, SLOTS, MODEL_WIDTH)
        if n == 0:
            swap(part_o, sib_o, 0).start()
    hand_over(1)
    swap(part_o, sib_o, 0).wait()
    give(part_o, sib_o, out_ret, 0)
    settle(1)
    for n in range(2):
        blocks, rows = tile(n)
        grad_hidden = dot(flat_rows(g_all[blocks]), wd[...], ((1,), (1,)))
        gate_val = gate_v[rows]
        up_val = up_v[rows]
        sig = jax.nn.sigmoid(gate_val)
        grad_gate = (grad_hidden * up_val * sig * (1.0 + gate_val * (1.0 - sig))).astype(BF)
        grad_up = (grad_hidden * gate_val * sig).astype(BF)
        g_gate[rows] = grad_gate
        g_up[rows] = grad_up
        grad_rows = dot(grad_gate, wg[...], ((1,), (1,))) + dot(grad_up, wu[...], ((1,), (1,)))
        part_g[blocks] = grad_rows.astype(BF).reshape(16, SLOTS, MODEL_WIDTH)
        if n == 0:
            swap(part_g, sib_g, 1).start()
    swap(part_g, sib_g, 1).wait()
    give(part_g, sib_g, grad_ret, 1)

    def weights_in(j, carry):
        cols = pl.ds(pl.multiple_of(j * 256, 256), 256)
        left = flat_rows(x_all[:, :, cols])
        v_gate[cols] = dot(left, g_gate[...], ((0,), (0,))).astype(BF)
        v_up[cols] = dot(left, g_up[...], ((0,), (0,))).astype(BF)
        return carry

    lax.fori_loop(0, MODEL_WIDTH // 256, weights_in, 0)
    stores = [
        pltpu.make_async_copy(src, dst, o_sem.at[n])
        for n, (src, dst) in enumerate(((v_gate, d_gate), (v_up, d_up), (v_down, d_down)))
    ]
    stores[0].start()
    stores[1].start()

    def weights_down(j, carry):
        cols = pl.ds(pl.multiple_of(j * 256, 256), 256)
        v_down[cols] = dot(hidden[:, cols], flat_rows(g_all[...]), ((0,), (0,))).astype(BF)
        return carry

    lax.fori_loop(0, 2, weights_down, 0)
    stores[2].start()
    for store in stores:
        store.wait()
    given(part_o, out_ret, 0)
    given(part_g, grad_ret, 1)


def experts(xs, gs, gate_w, up_w, down_w):
    rows = 32 * SLOTS
    width = gate_w.shape[1]
    back = jax.ShapeDtypeStruct((16, SLOTS, MODEL_WIDTH), BF)
    return pl.pallas_call(
        experts_kernel,
        out_shape=[
            back,
            back,
            jax.ShapeDtypeStruct(gate_w.shape, BF),
            jax.ShapeDtypeStruct(up_w.shape, BF),
            jax.ShapeDtypeStruct(down_w.shape, BF),
        ],
        in_specs=[ANY] * 5,
        out_specs=[ANY] * 5,
        scratch_shapes=[
            pltpu.VMEM((32, SLOTS, MODEL_WIDTH), BF),
            pltpu.VMEM((32, SLOTS, MODEL_WIDTH), BF),
            pltpu.VMEM(gate_w.shape, BF),
            pltpu.VMEM(up_w.shape, BF),
            pltpu.VMEM(down_w.shape, BF),
            pltpu.VMEM((rows, width), F32),
            pltpu.VMEM((rows, width), F32),
            pltpu.VMEM((rows, width), BF),
            pltpu.VMEM((rows, width), BF),
            pltpu.VMEM((rows, width), BF),
            pltpu.VMEM((32, SLOTS, MODEL_WIDTH), BF),
            pltpu.VMEM((32, SLOTS, MODEL_WIDTH), BF),
            pltpu.VMEM((16, SLOTS, MODEL_WIDTH), BF),
            pltpu.VMEM((16, SLOTS, MODEL_WIDTH), BF),
            pltpu.VMEM(gate_w.shape, BF),
            pltpu.VMEM(up_w.shape, BF),
            pltpu.VMEM(down_w.shape, BF),
            pltpu.SemaphoreType.DMA((3,)),
            pltpu.SemaphoreType.DMA((4,)),
            pltpu.SemaphoreType.DMA((2, 16)),
            pltpu.SemaphoreType.DMA((2, 16)),
            pltpu.SemaphoreType.DMA((2,)),
            pltpu.SemaphoreType.DMA((2,)),
            pltpu.SemaphoreType.DMA((2,)),
            pltpu.SemaphoreType.DMA((2,)),
            pltpu.SemaphoreType.DMA((2,)),
            pltpu.SemaphoreType.DMA((2,)),
            pltpu.SemaphoreType.DMA((3,)),
        ],
        compiler_params=params(6, 56 << 20),
        name="experts",
    )(xs, gs, gate_w, up_w, down_w)


def reduce_kernel(
    g0, g1, g2, g3, partial, out, sib_partial,
    a0, a1, a2, a3, b0, b1, b2, b3, c0, c1, c2, c3, s0, s1, s2, s3, t0, t1, t2, t3,
    total, give, send, recv, sib_send, sib_recv,
):
    y, z, x, c = coords()
    place = {"y": y, "z": z, "x": x}
    sibling = dev(y, z, x, 1 - c)
    for axis in ("x", "y", "z"):
        for step in STEPS:
            signal(axis_peer(axis, step))
    signal(sibling)
    pl.semaphore_wait(pltpu.get_barrier_semaphore(), 10)
    other = remote(partial, sib_partial, sib_send.at[0], sib_recv.at[0], sibling)
    other.start()
    held = ((g0, g1, g2, g3), (s0, s1, s2, s3), (t0, t1, t2, t3))
    arrive = ((a0, a1, a2, a3), (b0, b1, b2, b3), (c0, c1, c2, c3))

    def at(phase, part, index):
        order = ORDERS[part][::-1]
        spot = [
            index if axis == order[phase] else slice(None)
            for axis in ("y", "z", "x")
            if axis not in order[:phase]
        ]
        return held[phase][part].at[tuple(spot)]

    for phase in range(3):
        copies = []
        for part in range(PARTS):
            axis = ORDERS[part][::-1][phase]
            for n, step in enumerate(STEPS):
                copy = remote(
                    at(phase, part, (place[axis] + step) % 4),
                    arrive[phase][part].at[n],
                    send.at[phase, part, n],
                    recv.at[phase, part, n],
                    axis_peer(axis, step),
                )
                copy.start()
                copies.append(copy)
        for copy in copies:
            copy.wait()
        for part in range(PARTS):
            axis = ORDERS[part][::-1][phase]
            mine = at(phase, part, place[axis])
            got = arrive[phase][part]
            if phase == 0:

                def add(i, carry):
                    p, q = i // 4, i % 4
                    value = mine[p, q].astype(F32)
                    for n in range(3):
                        value = value + got[n, p, q].astype(F32)
                    held[1][part][p, q] = value.astype(BF)
                    return carry

                lax.fori_loop(0, 16, add, 0)
            elif phase == 1:

                def add(p, carry):
                    value = mine[p].astype(F32)
                    for n in range(3):
                        value = value + got[n, p].astype(F32)
                    held[2][part][p] = value.astype(BF)
                    return carry

                lax.fori_loop(0, 4, add, 0)
            else:
                value = mine[...].astype(F32)
                for n in range(3):
                    value = value + got[n].astype(F32)
                total[:, pl.ds(STARTS[part], WIDTHS[part])] = value
    low, high = total[0:12], total[12:24]
    out[c, 0:12] = jnp.where(c == 0, low, high)
    out[c, 12:16] = jnp.zeros((4, PACK), F32)
    give[0:12] = jnp.where(c == 0, high, low)
    give[12:16] = jnp.zeros((4, PACK), F32)
    last = remote(give, out.at[c], sib_send.at[1], sib_recv.at[1], sibling)
    last.start()
    last.wait()
    other.wait()


def place_blocks(full):
    return full.reshape(4, 4, 4, 24, full.shape[-1])


def reduce_weights(grads, partial):
    scratch = (
        [pltpu.VMEM((3, 4, 4, 24, w), BF) for w in WIDTHS]
        + [pltpu.VMEM((3, 4, 24, w), BF) for w in WIDTHS]
        + [pltpu.VMEM((3, 24, w), BF) for w in WIDTHS]
        + [pltpu.VMEM((4, 4, 24, w), BF) for w in WIDTHS]
        + [pltpu.VMEM((4, 24, w), BF) for w in WIDTHS]
        + [pltpu.VMEM((24, PACK), F32), pltpu.VMEM((16, PACK), F32)]
    )
    return pl.pallas_call(
        reduce_kernel,
        out_shape=[
            jax.ShapeDtypeStruct((2, 16, PACK), F32),
            jax.ShapeDtypeStruct((ROWS, MODEL_WIDTH), F32),
        ],
        in_specs=[IN_VMEM] * PARTS + [ANY],
        out_specs=[IN_VMEM, ANY],
        scratch_shapes=scratch
        + [
            pltpu.SemaphoreType.DMA((3, PARTS, 3)),
            pltpu.SemaphoreType.DMA((3, PARTS, 3)),
            pltpu.SemaphoreType.DMA((2,)),
            pltpu.SemaphoreType.DMA((2,)),
        ],
        compiler_params=params(8, 48 << 20),
        name="reduce_weights",
    )(*[place_blocks(grad) for grad in grads], partial)


def wide(block, head, first):
    part = block[:, 64 * head : 64 * head + 64]
    zero = jnp.zeros_like(part)
    return jnp.concatenate([part, zero] if first else [zero, part], axis=1)


def allowed_keys(kb, first_ref, zq, hi):
    q_pos = hi * 256 + lax.broadcasted_iota(jnp.int32, (256, 256), 1)
    k_pos = kb * 256 + lax.broadcasted_iota(jnp.int32, (256, 256), 0)
    return (k_pos >= first_ref[zq]) & (k_pos <= q_pos)


def attn_forward_kernel(span, q_ref, kv_ref, first_ref, o_ref, ot_ref, lse_ref, qs, top, tot, acc):
    zq = pl.program_id(0)
    lo, hi = span[0, zq], span[1, zq]
    q = q_ref[0] * SCALE_QK
    for h in range(3):
        qs[h] = wide(q, h, True)
    top[...] = jnp.full_like(top, NEGATIVE)
    tot[...] = jnp.zeros_like(tot)
    acc[...] = jnp.zeros_like(acc)

    def step(kb, carry):
        kv = kv_ref[kb]
        ok = allowed_keys(kb, first_ref, zq, hi)
        for h in range(3):
            scores = jnp.where(ok, dot(kv, qs[h], ((1,), (1,))), NEGATIVE)
            old = top[h]
            new = jnp.maximum(old, jnp.max(scores, axis=0, keepdims=True))
            shrink = jnp.exp(old - new)
            probs = jnp.exp(scores - new)
            top[h] = new
            tot[h] = tot[h] * shrink + jnp.sum(probs, axis=0, keepdims=True)
            acc[h] = acc[h] * shrink + dot(kv, probs.astype(BF), ((0,), (0,)))
        return carry

    lax.fori_loop(lo, hi + 1, step, 0)
    heads = []
    for h in range(3):
        mixed = acc[h][64:] / tot[h]
        ot_ref[0, h] = mixed
        lse_ref[0, h] = top[h] + jnp.log(tot[h])
        heads.append(mixed)
    o_ref[0] = jnp.transpose(jnp.concatenate(heads, axis=0)).astype(BF)


def attn_forward(span, q, kv, first):
    return pl.pallas_call(
        attn_forward_kernel,
        out_shape=[
            jax.ShapeDtypeStruct((4, PAIR, HEAD_Q), BF),
            jax.ShapeDtypeStruct((4, 3, HD, PAIR), F32),
            jax.ShapeDtypeStruct((4, 3, 1, PAIR), F32),
        ],
        grid_spec=pltpu.PrefetchScalarGridSpec(
            num_scalar_prefetch=1,
            grid=(4,),
            in_specs=[
                pl.BlockSpec((1, PAIR, HEAD_Q), lambda i, s: (i, 0, 0)),
                pl.BlockSpec((16, PAIR, 128), lambda i, s: (0, 0, 0)),
                pl.BlockSpec((4, 1, PAIR), lambda i, s: (0, 0, 0)),
            ],
            out_specs=[
                pl.BlockSpec((1, PAIR, HEAD_Q), lambda i, s: (i, 0, 0)),
                pl.BlockSpec((1, 3, HD, PAIR), lambda i, s: (i, 0, 0, 0)),
                pl.BlockSpec((1, 3, 1, PAIR), lambda i, s: (i, 0, 0, 0)),
            ],
            scratch_shapes=[
                pltpu.VMEM((3, PAIR, 128), BF),
                pltpu.VMEM((3, 1, PAIR), F32),
                pltpu.VMEM((3, 1, PAIR), F32),
                pltpu.VMEM((3, 128, PAIR), F32),
            ],
        ),
        compiler_params=pltpu.CompilerParams(vmem_limit_bytes=32 << 20),
        name="attn_forward",
    )(span, q, kv, first)


def attn_backward_kernel(
    span, q_ref, kv_ref, first_ref, go_ref, ot_ref, lse_ref, dq_ref, dkv_ref, qs, gs, delta, dq, dkv
):
    zq = pl.program_id(0)
    lo, hi = span[0, zq], span[1, zq]
    q = q_ref[0] * SCALE_QK
    grad = go_ref[0]
    grad_t = jnp.transpose(grad.astype(F32))
    for h in range(3):
        qs[h] = wide(q, h, True)
        gs[h] = wide(grad, h, False)
        delta[h] = jnp.sum(grad_t[64 * h : 64 * h + 64] * ot_ref[0, h], axis=0, keepdims=True)
    dq[...] = jnp.zeros_like(dq)

    @pl.when(zq == 0)
    def _():
        dkv[...] = jnp.zeros_like(dkv)

    def step(kb, carry):
        kv = kv_ref[kb]
        ok = allowed_keys(kb, first_ref, zq, hi)
        total = dkv[kb]
        for h in range(3):
            probs = jnp.where(ok, jnp.exp(dot(kv, qs[h], ((1,), (1,))) - lse_ref[0, h]), 0.0)
            grad_probs = dot(kv, gs[h], ((1,), (1,)))
            grad_scores = (probs * (grad_probs - delta[h])).astype(BF)
            dq[h] = dq[h] + dot(kv, grad_scores, ((0,), (0,)))
            total = total + dot(grad_scores, qs[h], ((1,), (0,)))
            total = total + dot(probs.astype(BF), gs[h], ((1,), (0,)))
        dkv[kb] = total
        return carry

    lax.fori_loop(lo, hi + 1, step, 0)
    heads = jnp.concatenate([dq[h][:64] for h in range(3)], axis=0) * SCALE_QK
    dq_ref[0] = jnp.transpose(heads).astype(BF)

    @pl.when(zq == 3)
    def _():
        dkv_ref[...] = dkv[...].astype(BF)


def attn_backward(span, q, kv, first, grad, ot, lse):
    return pl.pallas_call(
        attn_backward_kernel,
        out_shape=[
            jax.ShapeDtypeStruct((4, PAIR, HEAD_Q), BF),
            jax.ShapeDtypeStruct((16, PAIR, 128), BF),
        ],
        grid_spec=pltpu.PrefetchScalarGridSpec(
            num_scalar_prefetch=1,
            grid=(4,),
            in_specs=[
                pl.BlockSpec((1, PAIR, HEAD_Q), lambda i, s: (i, 0, 0)),
                pl.BlockSpec((16, PAIR, 128), lambda i, s: (0, 0, 0)),
                pl.BlockSpec((4, 1, PAIR), lambda i, s: (0, 0, 0)),
                pl.BlockSpec((1, PAIR, HEAD_Q), lambda i, s: (i, 0, 0)),
                pl.BlockSpec((1, 3, HD, PAIR), lambda i, s: (i, 0, 0, 0)),
                pl.BlockSpec((1, 3, 1, PAIR), lambda i, s: (i, 0, 0, 0)),
            ],
            out_specs=[
                pl.BlockSpec((1, PAIR, HEAD_Q), lambda i, s: (i, 0, 0)),
                pl.BlockSpec((16, PAIR, 128), lambda i, s: (0, 0, 0)),
            ],
            scratch_shapes=[
                pltpu.VMEM((3, PAIR, 128), BF),
                pltpu.VMEM((3, PAIR, 128), BF),
                pltpu.VMEM((3, 1, PAIR), F32),
                pltpu.VMEM((3, 128, PAIR), F32),
                pltpu.VMEM((16, PAIR, 128), F32),
            ],
        ),
        compiler_params=pltpu.CompilerParams(vmem_limit_bytes=32 << 20),
        name="attn_backward",
    )(span, q, kv, first, grad, ot, lse)


def inverse_rms(values):
    return lax.rsqrt(jnp.mean(values * values, axis=-1, keepdims=True) + EPS)


def norm_backward(values, inverse, gain, grad_out):
    scaled = grad_out * gain
    return inverse * scaled - values * inverse**3 * jnp.mean(values * scaled, axis=-1, keepdims=True)


def column_sums(left, right):
    return lax.dot_general(left, right, (((0,), (0,)), ((), ())), precision=HIGH_PRECISION)


def only_column(rows, column):
    return jnp.broadcast_to((jnp.arange(EXTRA) == column).astype(F32), (rows, EXTRA))


def halves(matrix):
    return matrix.reshape(12, 2, Q_HALF).transpose(1, 0, 2)


def local(
    tokens,
    segment_ids,
    expert_ids,
    w_query,
    w_key,
    w_value,
    w_out,
    w_router,
    gain_attn,
    gain_moe,
    w_gate,
    w_up,
    w_down,
    cotangent,
):
    y, z, x, c = coords()
    key_value = jnp.concatenate(
        [w_key.reshape(12, 2, 4, HD), w_value.reshape(12, 2, 4, HD)], axis=3
    ).reshape(12, 2, KV_HALF)
    extra = jnp.concatenate(
        [w_router, gain_attn[:, None], gain_moe[:, None], jnp.zeros((12, EXTRA - 18), BF)], axis=1
    )
    pack = jnp.concatenate(
        [
            halves(w_query),
            key_value.transpose(1, 0, 2),
            halves(w_out.T),
            jnp.broadcast_to(extra[None], (2, 12, EXTRA)),
        ],
        axis=2,
    )
    pack = jnp.pad(pack, ((0, 0), (0, 4), (0, 0)))
    part_q, part_kv, part_out, part_extra, pair, seg_all = gather_weights(
        pack, tokens, segment_ids
    )
    pair, w_gate, w_up, w_down = lax.optimization_barrier((pair, w_gate, w_up, w_down))
    gate_w = lax.all_gather(w_gate, "dp", axis=0, tiled=True)
    up_w = lax.all_gather(w_up, "dp", axis=0, tiled=True)
    down_w = lax.all_gather(w_down, "dp", axis=1, tiled=True)
    full_q = part_q.reshape(MODEL_WIDTH, Q_HALF)
    full_kv = part_kv.reshape(MODEL_WIDTH, KV_HALF)
    half_out = part_out.reshape(MODEL_WIDTH, Q_HALF)
    full_extra = part_extra.reshape(MODEL_WIDTH, EXTRA)
    picks = (jnp.arange(EXTRA)[None, :] == jnp.arange(8)[:, None] + EXPERT_COUNT).astype(BF)
    gains = dot(picks, full_extra, ((1,), (1,)))
    gain_a, gain_m = gains[0:1], gains[1:2]
    router = full_extra[:, :EXPERT_COUNT]

    inputs2 = pair.reshape(PAIR, MODEL_WIDTH).astype(F32)
    inverse_a = inverse_rms(inputs2)
    normed = (inputs2 * inverse_a * gain_a).astype(BF)
    queries = dot(normed, full_q, ((1,), (0,))).astype(BF)
    keys_values = dot(normed, full_kv, ((1,), (0,))).astype(BF)
    q4 = queries.reshape(PAIR, 4, HEAD_Q).transpose(1, 0, 2)
    kv4 = keys_values.reshape(PAIR, 4, 128).transpose(1, 0, 2)
    q_in, kv_in, sib_out = heads_out(q4, kv4, half_out)

    segs = seg_all.reshape(1, 4096)
    counts = jnp.sum((segs < jnp.arange(16)[:, None]).astype(jnp.int32), axis=1)
    row_segs = lax.dynamic_index_in_dim(seg_all.reshape(4, 4, PAIR), x, 1, keepdims=False)
    first = jnp.sum(
        jnp.where(row_segs[:, :, None] == jnp.arange(16), counts, 0), axis=2
    )
    span = jnp.stack([first[:, 0] // PAIR, jnp.arange(4, dtype=jnp.int32) * 4 + x])
    first = first.reshape(4, 1, PAIR)
    attn_low, attn_t, lse = attn_forward(span, q_in, kv_in, first)
    attn = attn_return(attn_low.reshape(8, ROWS, HEAD_Q))
    attn = attn.reshape(4, 2, ROWS, HEAD_Q).transpose(1, 2, 0, 3).reshape(2, ROWS, Q_HALF)

    own_attn = jnp.where(c == 0, attn[0], attn[1])
    other_attn = jnp.where(c == 0, attn[1], attn[0])
    inputs = tokens.astype(F32)
    middle = (
        inputs
        + dot(own_attn, half_out, ((1,), (1,)))
        + dot(other_attn, sib_out, ((1,), (1,)))
    )
    inverse_m = inverse_rms(middle)
    moe_in = (middle * inverse_m * gain_m).astype(BF)
    logits = dot(moe_in, router, ((1,), (0,)))
    chosen = (expert_ids[:, :, None] == jnp.arange(EXPERT_COUNT, dtype=jnp.int32)).astype(F32)
    picked = jnp.sum(chosen * logits[:, None, :], axis=-1)
    gates = jax.nn.softmax(picked, axis=-1)
    used = jnp.sum(chosen, axis=1)
    earlier = (jnp.arange(ROWS)[:, None] > jnp.arange(ROWS)[None, :]).astype(BF)
    before = dot(earlier, used.astype(BF), ((1,), (0,)))
    place = jnp.sum(chosen * before[:, None, :], axis=-1)
    slot = jnp.where(
        place < EXPERT_CAPACITY, expert_ids * SLOTS + place.astype(jnp.int32), -1
    )
    hit = (slot.T[:, :, None] == jnp.arange(EXPERT_COUNT * SLOTS, dtype=jnp.int32)).astype(F32)
    both = (hit[0] + hit[1]).astype(BF)
    slot_gate = jnp.sum(hit * gates.T[:, :, None], axis=(0, 1))
    slots_in = dot(both, moe_in, ((0,), (0,))).astype(BF)
    grad_slots = (dot(both, cotangent, ((0,), (0,))) * slot_gate[:, None]).astype(BF)
    blocks = (EXPERT_COUNT, SLOTS, MODEL_WIDTH)
    out_ret, grad_ret, grad_w_gate, grad_w_up, grad_w_down = experts(
        slots_in.reshape(blocks), grad_slots.reshape(blocks), gate_w, up_w, down_w
    )
    expert_grads = (
        lax.psum_scatter(grad_w_gate, "dp", scatter_dimension=0, tiled=True).astype(F32),
        lax.psum_scatter(grad_w_up, "dp", scatter_dimension=0, tiled=True).astype(F32),
        lax.psum_scatter(grad_w_down, "dp", scatter_dimension=1, tiled=True).astype(F32),
    )

    grad_output = cotangent.astype(F32)
    out_ret = out_ret.reshape(EXPERT_COUNT * SLOTS, MODEL_WIDTH)
    grad_ret = grad_ret.reshape(EXPERT_COUNT * SLOTS, MODEL_WIDTH)
    rows_out = [dot(hit[k].astype(BF), out_ret, ((1,), (0,))) for k in range(2)]
    block_out = (middle + gates[:, 0:1] * rows_out[0] + gates[:, 1:2] * rows_out[1]).astype(BF)
    grad_pair = jnp.stack([jnp.sum(grad_output * rows, axis=-1) for rows in rows_out], axis=-1)
    grad_pick = gates * (grad_pair - jnp.sum(gates * grad_pair, axis=-1, keepdims=True))
    grad_logits = jnp.sum(chosen * grad_pick[:, :, None], axis=1)
    grad_moe_in = dot(both, grad_ret, ((1,), (0,))) + lax.dot_general(
        grad_logits, router.astype(F32), (((1,), (1,)), ((), ())), precision=HIGH_PRECISION
    )
    g_router = column_sums(moe_in.astype(F32), jnp.pad(grad_logits, ((0, 0), (0, EXTRA - EXPERT_COUNT))))
    g_gain_m = column_sums(grad_moe_in * middle * inverse_m, only_column(ROWS, EXPERT_COUNT + 1))
    grad_middle = grad_output + norm_backward(middle, inverse_m, gain_m, grad_moe_in)
    branch = grad_middle.astype(BF)
    own_heads = dot(branch, half_out, ((1,), (0,))).astype(BF)
    other_heads = dot(branch, sib_out, ((1,), (0,))).astype(BF)
    grad_heads = jnp.stack(
        [jnp.where(c == 0, own_heads, other_heads), jnp.where(c == 0, other_heads, own_heads)]
    )
    grad_heads = grad_heads.reshape(2, ROWS, 4, HEAD_Q).transpose(2, 0, 1, 3)
    go_in, branch_sib, attn_sib = grad_attn_out(
        grad_heads.reshape(8, ROWS, HEAD_Q), branch, other_attn
    )
    dq_low, dkv_low = attn_backward(
        span, q_in, kv_in, first, go_in.reshape(4, PAIR, HEAD_Q), attn_t, lse
    )
    dq_in, dkv_in = heads_back(dq_low, dkv_low)
    grad_q = dq_in.transpose(1, 0, 2).reshape(PAIR, Q_HALF)
    grad_kv = jnp.sum(dkv_in.reshape(4, 4, PAIR, 128).astype(F32), axis=1).astype(BF)
    grad_kv = grad_kv.transpose(1, 0, 2).reshape(PAIR, KV_HALF)

    part_normed = dot(grad_q, full_q, ((1,), (1,))) + dot(
        grad_kv, full_kv, ((1,), (1,))
    )
    g_gain_a = column_sums(part_normed * inputs2 * inverse_a, only_column(PAIR, EXPERT_COUNT))
    g_query = dot(normed, grad_q, ((0,), (0,))).astype(BF)
    g_kv = dot(normed, grad_kv, ((0,), (0,))).astype(BF)
    g_extra = (g_router + g_gain_m + g_gain_a).astype(BF)
    g_out = (dot(branch, own_attn, ((0,), (0,))) + dot(branch_sib, attn_sib, ((0,), (0,)))).astype(BF)
    by_core = part_normed.reshape(2, ROWS, MODEL_WIDTH)
    own_part = lax.dynamic_index_in_dim(by_core, c, 0, keepdims=False)
    other_part = lax.dynamic_index_in_dim(by_core, 1 - c, 0, keepdims=False)
    reduced, sib_part = reduce_weights((g_query, g_kv, g_out, g_extra), other_part)
    grad_normed = own_part + sib_part
    grad_tokens = grad_middle + norm_backward(
        inputs, inverse_rms(inputs), gain_a, grad_normed
    )
    reduced = reduced[:, :12]
    r_query = reduced[:, :, :Q_HALF].transpose(1, 0, 2).reshape(12, HEADS * HD)
    r_kv = reduced[:, :, Q_HALF : Q_HALF + KV_HALF].transpose(1, 0, 2).reshape(12, KV, 2, HD)
    r_out = reduced[:, :, STARTS[2] : STARTS[3]].transpose(1, 0, 2).reshape(12, HEADS * HD)
    r_extra = jnp.sum(reduced[:, :, STARTS[3] :], axis=0)
    return (
        block_out,
        grad_tokens,
        r_query,
        r_kv[:, :, 0].reshape(12, KV * HD),
        r_kv[:, :, 1].reshape(12, KV * HD),
        r_out.T,
        r_extra[:, :EXPERT_COUNT],
        r_extra[:, EXPERT_COUNT],
        r_extra[:, EXPERT_COUNT + 1],
        expert_grads[0],
        expert_grads[1],
        expert_grads[2],
    )


def solution(mesh):
    rows, flat, dense = P(("dp", "ctx"), None), P(("dp", "ctx")), P("dp", "ctx")
    placed = (
        rows, dense, rows, rows, rows, rows, P(None, ("dp", "ctx")), rows, flat, flat,
        dense, dense, P("ctx", "dp"), rows,
    )
    return jax.shard_map(
        local,
        mesh=mesh,
        in_specs=placed,
        out_specs=(
            rows, rows, rows, rows, rows, P(None, ("dp", "ctx")), rows, flat, flat,
            dense, dense, P("ctx", "dp"),
        ),
        check_vma=False,
    )
```

```python
import functools

import jax
import jax.numpy as jnp
from jax import lax
from jax.experimental import pallas as pl
from jax.experimental.pallas import tpu as pltpu
from jax.sharding import PartitionSpec as P

MODEL_WIDTH = 1536
HEADS = 24
KV = 8
HD = 64
EXPERT_COUNT = 16
FF = 1024
EXPERT_CAPACITY = 20
SLOTS = 24
ROWS = 128
PAIR = 256
HEAD_Q = 192
Q_HALF = 768
KV_HALF = 512
EXTRA = 128
PACK = Q_HALF + KV_HALF + EXTRA + Q_HALF

EPS = 1e-05
SCALE_QK = 0.125
NEGATIVE = -1e30
HIGH_PRECISION = lax.Precision.HIGHEST
MESH = pl.DeviceIdType.MESH
ANY = pl.BlockSpec(memory_space=pl.ANY)
IN_VMEM = pl.BlockSpec(memory_space=pltpu.VMEM)
BF = jnp.bfloat16
F32 = jnp.float32


def dot(a, b, dims):
    return lax.dot_general(a, b, (dims, ((), ())), preferred_element_type=F32)


def coords():
    i = lax.axis_index("ctx")
    return lax.axis_index("dp"), i // 8, (i // 2) % 4, i % 2


def dev(y, z, x, c):
    return (y, z * 8 + x * 2 + c)


def signal(target):
    pl.semaphore_signal(
        pltpu.get_barrier_semaphore(), inc=1, device_id=target, device_id_type=MESH
    )


def remote(src, dst, send, recv, target):
    return pltpu.make_async_remote_copy(
        src_ref=src, dst_ref=dst, send_sem=send, recv_sem=recv, device_id=target, device_id_type=MESH
    )


def params(cid, vmem=None):
    return pltpu.CompilerParams(collective_id=cid, has_side_effects=True, vmem_limit_bytes=vmem)


def axis_peer(axis, step):
    y, z, x, c = coords()
    if axis == "y":
        return dev((y + step) % 4, z, x, c)
    if axis == "z":
        return dev(y, (z + step) % 4, x, c)
    return dev(y, z, (x + step) % 4, c)


WIDTHS = (Q_HALF, KV_HALF, Q_HALF, EXTRA)
STARTS = (0, Q_HALF, Q_HALF + KV_HALF, 2 * Q_HALF + KV_HALF)
STEPS = (1, 3, 2)
FIRST_PARTS = (
    (0, 0, 512, ("x", "z", "y")),
    (1, 0, 512, ("y", "x", "z")),
    (0, 512, 256, ("z", "y", "x")),
    (3, 0, 128, ("z", "y", "x")),
)
OUT_PARTS = (
    (2, 0, 256, ("x", "z", "y")),
    (2, 256, 256, ("y", "x", "z")),
    (2, 512, 256, ("z", "y", "x")),
)
GATHER_PARTS = FIRST_PARTS + OUT_PARTS


def slab(ref, done, y, z, x, cols):
    return ref.at[
        slice(None) if "y" in done else y,
        slice(None) if "z" in done else z,
        slice(None) if "x" in done else x,
        slice(None),
        cols,
    ]


def gather_kernel(
    pack, tokens, segs, out0, out1, out2, out3, pair, seg_all,
    sib, block, p_send, p_recv, l_sem, s_send, s_recv, sib_send, sib_recv,
):
    y, z, x, c = coords()
    outs = (out0, out1, out2, out3)
    me = z * 8 + x * 2 + c
    sibling = dev(y, z, x, 1 - c)

    def greet(k, carry):
        signal((y, (me + k) % 32))
        return carry

    lax.fori_loop(1, 32, greet, 0)
    for step in STEPS:
        signal(axis_peer("y", step))
    pl.semaphore_wait(pltpu.get_barrier_semaphore(), 34)

    first = remote(pack.at[1 - c], sib, sib_send.at[0], sib_recv.at[0], sibling)
    first.start()
    second = remote(tokens, pair.at[c], sib_send.at[1], sib_recv.at[1], sibling)
    second.start()
    own_rows = pltpu.make_async_copy(tokens, pair.at[c], l_sem.at[4])
    own_rows.start()
    own_segs = pltpu.make_async_copy(segs, seg_all.at[me], l_sem.at[5])
    own_segs.start()

    def spread(k, carry):
        remote(segs, seg_all.at[me], s_send, s_recv, (y, (me + k) % 32)).start()
        return carry

    lax.fori_loop(1, 32, spread, 0)

    first.wait()
    own = pack[c, :12].astype(F32)
    other = sib[:12].astype(F32)
    low = jnp.where(c == 0, own, other)
    high = jnp.where(c == 0, other, own)
    block[...] = jnp.concatenate([low, high], axis=0).astype(BF)

    locals_ = []
    for n in range(4):
        cols = pl.ds(STARTS[n], WIDTHS[n])
        here = pltpu.make_async_copy(block.at[:, cols], outs[n].at[y, z, x], l_sem.at[n])
        here.start()
        locals_.append(here)
    for phase in range(3):
        copies = []
        for part, (n, start, width, order) in enumerate(GATHER_PARTS if phase < 2 else FIRST_PARTS):
            for k, step in enumerate(STEPS):
                dst = slab(outs[n], order[:phase], y, z, x, pl.ds(start, width))
                src = block.at[:, pl.ds(STARTS[n] + start, width)] if phase == 0 else dst
                copy = remote(
                    src, dst, p_send.at[phase, part, k], p_recv.at[phase, part, k],
                    axis_peer(order[phase], step),
                )
                copy.start()
                copies.append(copy)
        if phase == 0:
            for here in locals_:
                here.wait()
        for copy in copies:
            copy.wait()
    second.wait()
    own_rows.wait()
    own_segs.wait()
    drain = remote(
        seg_all.at[pl.ds(0, 31)], seg_all.at[pl.ds(0, 31)], s_send, s_recv, sibling
    )
    drain.wait_send()
    drain.wait_recv()


def gather_weights(pack, tokens, segs):
    return pl.pallas_call(
        gather_kernel,
        out_shape=[jax.ShapeDtypeStruct((4, 4, 4, 24, width), BF) for width in WIDTHS]
        + [
            jax.ShapeDtypeStruct((2, ROWS, MODEL_WIDTH), BF),
            jax.ShapeDtypeStruct((32, 1, 128), jnp.int32),
        ],
        in_specs=[IN_VMEM, ANY, ANY],
        out_specs=[ANY] * 6,
        scratch_shapes=[
            pltpu.VMEM((16, PACK), BF),
            pltpu.VMEM((24, PACK), BF),
            pltpu.SemaphoreType.DMA((3, 7, 3)),
            pltpu.SemaphoreType.DMA((3, 7, 3)),
            pltpu.SemaphoreType.DMA((6,)),
            pltpu.SemaphoreType.DMA,
            pltpu.SemaphoreType.DMA,
            pltpu.SemaphoreType.DMA((2,)),
            pltpu.SemaphoreType.DMA((2,)),
        ],
        compiler_params=params(1),
        name="gather_weights",
    )(pack, tokens, segs)


def plane_greet(y, me, c, sibling):
    def greet(k, carry):
        t = (me + k) % 16
        signal(dev(y, t // 4, t % 4, c))
        return carry

    lax.fori_loop(1, 16, greet, 0)
    if sibling is not None:
        signal(sibling)
        pl.semaphore_wait(pltpu.get_barrier_semaphore(), 16)
    else:
        pl.semaphore_wait(pltpu.get_barrier_semaphore(), 15)


def wide(block, head, first):
    part = block[:, 64 * head : 64 * head + 64]
    zero = jnp.zeros_like(part)
    return jnp.concatenate([part, zero] if first else [zero, part], axis=1)


KEYS = 1024


def attend_kernel(
    q4, kv4, half_in, cots, first_ref, q_in, kv_in, attn, ot_ref, lse_ref, half, half_sib, c_all,
    qs, acc, o_buf,
    l_sem, q_send, q_recv, k_send, k_recv, w_send, w_recv, sib_send, sib_recv,
    c_send, c_recv, f_send, f_recv, o_send, o_recv,
):
    y, z, x, c = coords()
    me = z * 4 + x
    sibling = dev(y, z, x, 1 - c)

    wide_greet()

    q_copies = []
    for n, step in enumerate(STEPS):
        to = (z + step) % 4
        copy = remote(q4.at[to], q_in.at[z], q_send.at[n], q_recv.at[n], dev(y, to, x, c))
        copy.start()
        q_copies.append(copy)

    def send_kv(k, carry):
        t = (me + k) % 16
        remote(kv4.at[t // 4], kv_in.at[me], k_send, k_recv, dev(y, t // 4, t % 4, c)).start()
        return carry

    lax.fori_loop(1, 16, send_kv, 0)
    here = [
        pltpu.make_async_copy(q4.at[z], q_in.at[z], l_sem.at[0]),
        pltpu.make_async_copy(kv4.at[z], kv_in.at[me], l_sem.at[1]),
    ]
    for copy in here:
        copy.start()
    for copy in here:
        copy.wait()
    for copy in q_copies:
        copy.wait()
    drain = remote(kv_in.at[pl.ds(0, 15)], kv_in.at[pl.ds(0, 15)], k_send, k_recv, sibling)
    drain.wait_send()
    drain.wait_recv()

    w_copies = []
    for part, (n, start, width, order) in enumerate(OUT_PARTS):
        spot = slab(half, order[:2], y, z, x, pl.ds(start, width))
        for k, step in enumerate(STEPS):
            copy = remote(
                spot, spot, w_send.at[part, k], w_recv.at[part, k], axis_peer(order[2], step)
            )
            copy.start()
            w_copies.append(copy)

    def send_cots(k, carry):
        t = (me + k) % 16
        remote(
            cots.at[t], c_all.at[c * 16 + me], c_send.at[k], c_recv.at[k], dev(y, t // 4, t % 4, c)
        ).start()
        return carry

    lax.fori_loop(1, 16, send_cots, 0)
    own_cots = pltpu.make_async_copy(cots.at[me], c_all.at[c * 16 + me], l_sem.at[2])
    own_cots.start()
    remote(cots.at[me], c_all.at[c * 16 + me], f_send, f_recv, sibling).start()

    def forward_cots(k, carry):
        s = c * 16 + (me + 16 - k) % 16
        t = (me + k) % 16
        arrived = remote(cots.at[t], c_all.at[s], c_send.at[k], c_recv.at[k], dev(y, t // 4, t % 4, c))
        arrived.wait_recv()
        remote(c_all.at[s], c_all.at[s], f_send, f_recv, sibling).start()
        arrived.wait_send()
        return carry

    swap = remote(half, half_sib, sib_send, sib_recv, sibling)
    j = z * 2 + c
    returns = []
    for n in range(4):
        zq = (z + n + 1) % 4
        q = q_in[zq] * SCALE_QK
        for h in range(3):
            qs[256 * h : 256 * h + 256] = wide(q, h, True)
        acc[...] = jnp.zeros_like(acc)
        first = first_ref[zq]
        q_pos = (zq * 4 + x) * PAIR + lax.broadcasted_iota(jnp.int32, (1, PAIR), 1)

        def step(kb, stats):
            kv = kv_in[pl.ds(kb * (KEYS // PAIR), KEYS // PAIR)].reshape(KEYS, 128)
            k_pos = kb * KEYS + lax.broadcasted_iota(jnp.int32, (KEYS, PAIR), 0)
            ok = (k_pos >= first) & (k_pos <= q_pos)
            scores = [dot(kv, qs[256 * h : 256 * h + 256], ((1,), (1,))) for h in range(3)]
            later, probs, shrinks = [], [], []
            for h in range(3):
                top, tot = stats[h]
                masked = jnp.where(ok, scores[h], NEGATIVE)
                new = jnp.maximum(top, jnp.max(masked, axis=0, keepdims=True))
                prob = jnp.exp(masked - new)
                shrink = jnp.exp(top - new)
                later.append((new, tot * shrink + jnp.sum(prob, axis=0, keepdims=True)))
                probs.append(prob.astype(BF))
                shrinks.append(shrink)
            for h in range(3):
                cols = slice(256 * h, 256 * h + 256)
                acc[:, cols] = acc[:, cols] * shrinks[h] + dot(kv, probs[h], ((0,), (0,)))
            return tuple(later)

        none = (jnp.full((1, PAIR), NEGATIVE, F32), jnp.zeros((1, PAIR), F32))
        stats = lax.fori_loop(0, zq + 1, step, (none, none, none))
        heads = []
        for h in range(3):
            cols = slice(256 * h, 256 * h + 256)
            mixed = acc[64:, cols] / stats[h][1]
            ot_ref[zq, :, cols] = mixed
            lse_ref[zq, :, cols] = stats[h][0] + jnp.log(stats[h][1])
            heads.append(mixed)
        heads = jnp.concatenate(heads, axis=0)
        rows = jnp.transpose(heads).astype(BF)
        o_buf[n, 0] = rows[:ROWS]
        o_buf[n, 1] = rows[ROWS:]
        for d in range(2):
            core = c if d == 0 else 1 - c
            if n == 3 and d == 0:
                back = pltpu.make_async_copy(o_buf.at[n, core], attn.at[j], l_sem.at[3])
            else:
                back = remote(
                    o_buf.at[n, core], attn.at[j], o_send.at[n, d], o_recv.at[n, d], dev(y, zq, x, core)
                )
            back.start()
            returns.append(back)
        if n == 1:
            for copy in w_copies:
                copy.wait()
            swap.start()
        if n == 2:
            lax.fori_loop(1, 16, forward_cots, 0)
    own_cots.wait()
    mine = c_all.at[pl.ds(c * 16, 16)]
    drain = remote(mine, mine, f_send, f_recv, sibling)
    drain.wait_send()
    drain.wait_recv()
    swap.wait()
    for back in returns:
        back.wait()


def attend(q4, kv4, half, cots, first):
    blocks = jax.ShapeDtypeStruct((4, 4, 4, 24, Q_HALF), BF)
    return pl.pallas_call(
        attend_kernel,
        out_shape=[
            jax.ShapeDtypeStruct((4, PAIR, HEAD_Q), BF),
            jax.ShapeDtypeStruct((16, PAIR, 128), BF),
            jax.ShapeDtypeStruct((8, ROWS, HEAD_Q), BF),
            jax.ShapeDtypeStruct((4, HD, 3 * PAIR), F32),
            jax.ShapeDtypeStruct((4, 1, 3 * PAIR), F32),
            blocks,
            blocks,
            jax.ShapeDtypeStruct((32, SLOTS, MODEL_WIDTH), BF),
        ],
        in_specs=[ANY, ANY, ANY, ANY, IN_VMEM],
        out_specs=[IN_VMEM, IN_VMEM, ANY, IN_VMEM, IN_VMEM, ANY, ANY, ANY],
        input_output_aliases={2: 5},
        scratch_shapes=[
            pltpu.VMEM((3 * PAIR, 128), BF),
            pltpu.VMEM((128, 3 * PAIR), F32),
            pltpu.VMEM((4, 2, ROWS, HEAD_Q), BF),
            pltpu.SemaphoreType.DMA((4,)),
            pltpu.SemaphoreType.DMA((3,)),
            pltpu.SemaphoreType.DMA((3,)),
            pltpu.SemaphoreType.DMA,
            pltpu.SemaphoreType.DMA,
            pltpu.SemaphoreType.DMA((3, 3)),
            pltpu.SemaphoreType.DMA((3, 3)),
            pltpu.SemaphoreType.DMA,
            pltpu.SemaphoreType.DMA,
            pltpu.SemaphoreType.DMA((16,)),
            pltpu.SemaphoreType.DMA((16,)),
            pltpu.SemaphoreType.DMA,
            pltpu.SemaphoreType.DMA,
            pltpu.SemaphoreType.DMA((4, 2)),
            pltpu.SemaphoreType.DMA((4, 2)),
        ],
        compiler_params=params(2, 56 << 20),
        name="attend",
    )(q4, kv4, half, cots, first)


def flat_rows(blocks):
    return blocks.reshape(blocks.shape[0] * SLOTS, blocks.shape[2])


def experts_kernel(
    xs, gates, cots, weights, out_ret, grad_ret, d_all,
    x_all, t_all, g_all, w_all, gate_v, up_v, hidden, g_both, part_o, part_g, sib_o, sib_g,
    v_all,
    w_sem, l_sem, send, recv, f_send, f_recv, s_send, s_recv, r_send, r_recv, o_sem,
):
    y, z, x, c = coords()
    me = z * 4 + x
    width = hidden.shape[1]
    sibling = dev(y, z, x, 1 - c)
    plane_greet(y, me, c, sibling)
    loads = [
        pltpu.make_async_copy(src, dst, w_sem.at[n])
        for n, (src, dst) in enumerate(((weights, w_all), (cots, g_all)))
    ]
    for load in loads:
        load.start()
    arrays = ((xs, x_all), (gates, t_all))

    def scatter(a):
        src, dst = arrays[a]

        def push(k, carry):
            t = (me + k) % 16
            remote(
                src.at[t], dst.at[c * 16 + me], send.at[a, k], recv.at[a, k], dev(y, t // 4, t % 4, c)
            ).start()
            return carry

        lax.fori_loop(1, 16, push, 0)
        pltpu.make_async_copy(src.at[me], dst.at[c * 16 + me], l_sem.at[a]).start()
        remote(src.at[me], dst.at[c * 16 + me], f_send.at[a], f_recv.at[a], sibling).start()

    def hand_over(a):
        src, dst = arrays[a]

        def forward(k, carry):
            s = (me + 16 - k) % 16
            t = (me + k) % 16
            arrived = remote(
                src.at[t], dst.at[c * 16 + s], send.at[a, k], recv.at[a, k], dev(y, t // 4, t % 4, c)
            )
            arrived.wait_recv()
            remote(
                dst.at[c * 16 + s], dst.at[c * 16 + s], f_send.at[a], f_recv.at[a], sibling
            ).start()
            arrived.wait_send()
            return carry

        lax.fori_loop(1, 16, forward, 0)

    def settle(a):
        src, dst = arrays[a]
        pltpu.make_async_copy(src.at[me], dst.at[c * 16 + me], l_sem.at[a]).wait()
        half = pl.ds(0, 16)
        drain = remote(dst.at[half], dst.at[half], f_send.at[a], f_recv.at[a], sibling)
        drain.wait_send()
        drain.wait_recv()

    def swap(part, sib, a):
        rows = pl.ds((1 - c) * 16, 16)
        return remote(part.at[rows], sib, s_send.at[a], s_recv.at[a], sibling)

    def give(part, sib, ret, a):
        def add(t):
            rows = c * 16 + t
            part[rows] = (
                part[rows].astype(F32) + sib[t].astype(F32)
            ).astype(BF)
            return part.at[rows]

        def push(k, carry):
            t = (me + k) % 16
            remote(add(t), ret.at[me], r_send.at[a], r_recv.at[a], dev(y, t // 4, t % 4, c)).start()
            return carry

        lax.fori_loop(1, 16, push, 0)
        pltpu.make_async_copy(add(me), ret.at[me], l_sem.at[2 + a]).start()

    def given(part, ret, a):
        pltpu.make_async_copy(part.at[c * 16 + me], ret.at[me], l_sem.at[2 + a]).wait()
        drain = remote(ret.at[pl.ds(0, 15)], ret.at[pl.ds(0, 15)], r_send.at[a], r_recv.at[a], sibling)
        drain.wait_send()
        drain.wait_recv()

    def tile(n):
        h = 1 - c if n == 0 else c
        rows = 16 * SLOTS
        return pl.ds(h * 16, 16), pl.ds(pl.multiple_of(h * rows, rows), rows)

    scatter(0)
    scatter(1)
    hand_over(0)
    hand_over(1)
    settle(0)
    settle(1)
    for load in loads:
        load.wait()
    for n in range(2):
        blocks, rows = tile(n)
        rows_in = flat_rows(x_all[blocks])
        both = dot(rows_in, w_all[:, : 2 * width], ((1,), (0,)))
        gate_val, up_val = both[:, :width], both[:, width:]
        gate_v[rows] = gate_val
        up_v[rows] = up_val
        low = (gate_val * jax.nn.sigmoid(gate_val) * up_val).astype(BF)
        hidden[rows] = low
        part_o[blocks] = dot(low, w_all[:, 2 * width :], ((1,), (1,))).astype(BF).reshape(16, SLOTS, MODEL_WIDTH)
        if n == 0:
            swap(part_o, sib_o, 0).start()
    swap(part_o, sib_o, 0).wait()
    give(part_o, sib_o, out_ret, 0)
    for n in range(2):
        blocks, rows = tile(n)
        scale = jnp.concatenate([flat_rows(t_all[blocks])] * (MODEL_WIDTH // 128), axis=1)
        grad_expert = (flat_rows(g_all[blocks]).astype(F32) * scale).astype(BF)
        g_all[blocks] = grad_expert.reshape(16, SLOTS, MODEL_WIDTH)
        grad_hidden = dot(grad_expert, w_all[:, 2 * width :], ((1,), (0,)))
        gate_val = gate_v[rows]
        up_val = up_v[rows]
        sig = jax.nn.sigmoid(gate_val)
        grad_gate = (grad_hidden * up_val * sig * (1.0 + gate_val * (1.0 - sig))).astype(BF)
        grad_up = (grad_hidden * gate_val * sig).astype(BF)
        grads = jnp.concatenate([grad_gate, grad_up], axis=1)
        g_both[rows] = grads
        grad_rows = dot(grads, w_all[:, : 2 * width], ((1,), (1,)))
        part_g[blocks] = grad_rows.astype(BF).reshape(16, SLOTS, MODEL_WIDTH)
        if n == 0:
            swap(part_g, sib_g, 1).start()
    swap(part_g, sib_g, 1).wait()
    give(part_g, sib_g, grad_ret, 1)

    def weight_grads(j, carry):
        cols = pl.ds(pl.multiple_of(j * 256, 256), 256)
        v_all[cols, : 2 * width] = dot(flat_rows(x_all[:, :, cols]), g_both[...], ((0,), (0,))).astype(BF)
        v_all[cols, 2 * width :] = dot(flat_rows(g_all[:, :, cols]), hidden[...], ((0,), (0,))).astype(BF)
        return carry

    lax.fori_loop(0, MODEL_WIDTH // 256, weight_grads, 0)
    store = pltpu.make_async_copy(v_all, d_all, o_sem)
    store.start()
    store.wait()
    given(part_o, out_ret, 0)
    given(part_g, grad_ret, 1)


def experts(xs, gates, cots, weights):
    rows = 32 * SLOTS
    width = weights.shape[1] // 3
    back = jax.ShapeDtypeStruct((16, SLOTS, MODEL_WIDTH), BF)
    return pl.pallas_call(
        experts_kernel,
        out_shape=[back, back, jax.ShapeDtypeStruct(weights.shape, BF)],
        in_specs=[ANY] * 4,
        out_specs=[ANY] * 3,
        scratch_shapes=[
            pltpu.VMEM((32, SLOTS, MODEL_WIDTH), BF),
            pltpu.VMEM((32, SLOTS, 128), F32),
            pltpu.VMEM((32, SLOTS, MODEL_WIDTH), BF),
            pltpu.VMEM(weights.shape, BF),
            pltpu.VMEM((rows, width), F32),
            pltpu.VMEM((rows, width), F32),
            pltpu.VMEM((rows, width), BF),
            pltpu.VMEM((rows, 2 * width), BF),
            pltpu.VMEM((32, SLOTS, MODEL_WIDTH), BF),
            pltpu.VMEM((32, SLOTS, MODEL_WIDTH), BF),
            pltpu.VMEM((16, SLOTS, MODEL_WIDTH), BF),
            pltpu.VMEM((16, SLOTS, MODEL_WIDTH), BF),
            pltpu.VMEM(weights.shape, BF),
            pltpu.SemaphoreType.DMA((2,)),
            pltpu.SemaphoreType.DMA((4,)),
            pltpu.SemaphoreType.DMA((2, 16)),
            pltpu.SemaphoreType.DMA((2, 16)),
            pltpu.SemaphoreType.DMA((2,)),
            pltpu.SemaphoreType.DMA((2,)),
            pltpu.SemaphoreType.DMA((2,)),
            pltpu.SemaphoreType.DMA((2,)),
            pltpu.SemaphoreType.DMA((2,)),
            pltpu.SemaphoreType.DMA((2,)),
            pltpu.SemaphoreType.DMA,
        ],
        compiler_params=params(6, 56 << 20),
        name="experts",
    )(xs, gates, cots, weights)


def reduce_kernel(g_q, g_kv, g_extra, ready, partial, out, sib_partial, *rest):
    parts = len(FIRST_PARTS)
    arrive = [rest[parts * k : parts * k + parts] for k in range(3)]
    held = [None, rest[3 * parts : 4 * parts], rest[4 * parts : 5 * parts]]
    total, give, send, recv, sib_send, sib_recv = rest[5 * parts :]
    grads = (g_q, g_kv, None, g_extra)
    y, z, x, c = coords()
    place = {"y": y, "z": z, "x": x}
    sibling = dev(y, z, x, 1 - c)
    for axis in ("x", "y", "z"):
        for step in STEPS:
            signal(axis_peer(axis, step))
    signal(sibling)
    pl.semaphore_wait(pltpu.get_barrier_semaphore(), 10)
    other = remote(partial, sib_partial, sib_send.at[0], sib_recv.at[0], sibling)
    other.start()

    def at(phase, part, index):
        n, start, width, order = FIRST_PARTS[part]
        order = order[::-1]
        spot = [
            index if axis == order[phase] else slice(None)
            for axis in ("y", "z", "x")
            if axis not in order[:phase]
        ]
        if phase == 0:
            return grads[n].at[tuple(spot) + (slice(None), pl.ds(start, width))]
        return held[phase][part].at[tuple(spot)]

    for phase in range(3):
        copies = []
        for part in range(parts):
            axis = FIRST_PARTS[part][3][::-1][phase]
            for n, step in enumerate(STEPS):
                copy = remote(
                    at(phase, part, (place[axis] + step) % 4),
                    arrive[phase][part].at[n],
                    send.at[phase, part, n],
                    recv.at[phase, part, n],
                    axis_peer(axis, step),
                )
                copy.start()
                copies.append(copy)
        for copy in copies:
            copy.wait()
        for part in range(parts):
            array, start, width, order = FIRST_PARTS[part]
            mine = at(phase, part, place[order[::-1][phase]])
            got = arrive[phase][part]
            if phase < 2:

                def add(p, carry):
                    value = mine[p].astype(F32)
                    for n in range(3):
                        value = value + got[n, p].astype(F32)
                    held[phase + 1][part][p] = value.astype(BF)
                    return carry

                lax.fori_loop(0, 4, add, 0)
            else:
                value = mine[...].astype(F32)
                for n in range(3):
                    value = value + got[n].astype(F32)
                total[:, STARTS[array] + start : STARTS[array] + start + width] = value
    total[:, STARTS[2] : STARTS[3]] = ready[...]
    low, high = total[0:12], total[12:24]
    out[c, 0:12] = jnp.where(c == 0, low, high)
    out[c, 12:16] = jnp.zeros((4, PACK), F32)
    give[0:12] = jnp.where(c == 0, high, low)
    give[12:16] = jnp.zeros((4, PACK), F32)
    last = remote(give, out.at[c], sib_send.at[1], sib_recv.at[1], sibling)
    last.start()
    last.wait()
    other.wait()


def place_blocks(full):
    return full.reshape(4, 4, 4, 24, full.shape[-1])


def reduce_weights(g_q, g_kv, g_extra, ready, partial):
    widths = [part[2] for part in FIRST_PARTS]
    scratch = (
        [pltpu.VMEM((3, 4, 4, 24, w), BF) for w in widths]
        + [pltpu.VMEM((3, 4, 24, w), BF) for w in widths]
        + [pltpu.VMEM((3, 24, w), BF) for w in widths]
        + [pltpu.VMEM((4, 4, 24, w), BF) for w in widths]
        + [pltpu.VMEM((4, 24, w), BF) for w in widths]
        + [pltpu.VMEM((24, PACK), F32), pltpu.VMEM((16, PACK), F32)]
    )
    sems = (3, len(FIRST_PARTS), 3)
    return pl.pallas_call(
        reduce_kernel,
        out_shape=[
            jax.ShapeDtypeStruct((2, 16, PACK), F32),
            jax.ShapeDtypeStruct((ROWS, MODEL_WIDTH), F32),
        ],
        in_specs=[IN_VMEM] * 4 + [ANY],
        out_specs=[IN_VMEM, ANY],
        scratch_shapes=scratch
        + [
            pltpu.SemaphoreType.DMA(sems),
            pltpu.SemaphoreType.DMA(sems),
            pltpu.SemaphoreType.DMA((2,)),
            pltpu.SemaphoreType.DMA((2,)),
        ],
        compiler_params=params(8, 48 << 20),
        name="reduce_weights",
    )(place_blocks(g_q), place_blocks(g_kv), place_blocks(g_extra), ready, partial)


def wide_greet():
    y, z, x, c = coords()
    me = z * 4 + x

    def greet(k, carry):
        t = (me + k) % 16
        signal(dev(y, t // 4, t % 4, c))
        return carry

    lax.fori_loop(1, 16, greet, 0)
    for step in STEPS:
        signal(axis_peer("y", step))
        signal(dev(y, (z + step) % 4, x, 1 - c))
    signal(dev(y, z, x, 1 - c))
    pl.semaphore_wait(pltpu.get_barrier_semaphore(), 22)


def attend_back_kernel(
    heads, branch, own_attn, other_attn, q_in, kv_in, first_ref, ot_ref, lse_ref,
    dq_out, dkv_out, total,
    go, branch_sib, attn_sib, qs, gs, dq, dkv, dkv_low, dq_low,
    g_out, s_out, t_out, a_out, b_out, c_out,
    l_sem, h_send, h_recv, sib_send, sib_recv, q_send, q_recv, k_send, k_recv,
    w_send, w_recv,
):
    y, z, x, c = coords()
    me = z * 4 + x
    j = z * 2 + c
    sibling = dev(y, z, x, 1 - c)
    place = {"y": y, "z": z, "x": x}
    wide_greet()

    def push(k, carry):
        t = (j + k) % 8
        remote(heads.at[t], go.at[j], h_send, h_recv, dev(y, t // 2, x, t % 2)).start()
        return carry

    lax.fori_loop(1, 8, push, 0)
    one = remote(branch, branch_sib, sib_send.at[0], sib_recv.at[0], sibling)
    one.start()
    two = remote(other_attn, attn_sib, sib_send.at[1], sib_recv.at[1], sibling)
    two.start()
    here = pltpu.make_async_copy(heads.at[j], go.at[j], l_sem.at[0])
    here.start()
    here.wait()
    drain = remote(go.at[pl.ds(0, 7)], go.at[pl.ds(0, 7)], h_send, h_recv, sibling)
    drain.wait_send()
    drain.wait_recv()
    one.wait()
    two.wait()

    rows_b = jnp.concatenate([branch[...], branch_sib[...]], axis=0)
    rows_a = jnp.concatenate([own_attn[...], attn_sib[...]], axis=0)
    for n in range(4):
        part = dot(rows_b[:, 384 * n : 384 * n + 384], rows_a, ((0,), (0,)))
        g_out[n] = part.astype(BF).reshape(4, 4, 24, Q_HALF)

    held = (g_out, s_out, t_out)
    arrive = (a_out, b_out, c_out)

    def spot(phase, part, index):
        n, start, width, order = OUT_PARTS[part]
        order = order[::-1]
        cut = [
            index if axis == order[phase] else slice(None)
            for axis in ("y", "z", "x")
            if axis not in order[:phase]
        ]
        if phase == 0:
            return held[0].at[tuple(cut) + (slice(None), pl.ds(start, width))]
        return held[phase].at[(part,) + tuple(cut)]

    def w_copies(phase):
        copies = []
        for part in range(3):
            axis = OUT_PARTS[part][3][::-1][phase]
            for n, step in enumerate(STEPS):
                copies.append(
                    remote(
                        spot(phase, part, (place[axis] + step) % 4), arrive[phase].at[part, n],
                        w_send.at[phase, part, n], w_recv.at[phase, part, n], axis_peer(axis, step),
                    )
                )
        return copies

    def w_sum(phase):
        for copy in w_copies(phase):
            copy.wait()
        for part in range(3):
            n, start, width, order = OUT_PARTS[part]
            mine = spot(phase, part, place[order[::-1][phase]])
            if phase == 2:
                value = mine[...].astype(F32)
                for k in range(3):
                    value = value + arrive[2][part, k].astype(F32)
                total[:, start : start + width] = value
            else:

                def add(p, carry):
                    value = mine[p].astype(F32)
                    for k in range(3):
                        value = value + arrive[phase][part, k, p].astype(F32)
                    held[phase + 1][part, p] = value.astype(BF)
                    return carry

                lax.fori_loop(0, 4, add, 0)

    for copy in w_copies(0):
        copy.start()

    dkv[...] = jnp.zeros_like(dkv)
    for n in range(4):
        zq = 3 - n
        q = q_in[zq] * SCALE_QK
        grad = jnp.concatenate([go[2 * zq], go[2 * zq + 1]], axis=0)
        grad_t = jnp.transpose(grad.astype(F32))
        deltas, sums_log = [], []
        for h in range(3):
            cols = slice(256 * h, 256 * h + 256)
            qs[cols] = wide(q, h, True)
            gs[cols] = wide(grad, h, False)
            deltas.append(
                jnp.sum(grad_t[64 * h : 64 * h + 64] * ot_ref[zq, :, cols], axis=0, keepdims=True)
            )
            sums_log.append(lse_ref[zq, :, cols])
        dq[...] = jnp.zeros_like(dq)
        first = first_ref[zq]
        hi = zq * 4 + x
        q_pos = hi * PAIR + lax.broadcasted_iota(jnp.int32, (1, PAIR), 1)

        def step(kb, carry):
            kv = kv_in[kb]
            k_pos = kb * PAIR + lax.broadcasted_iota(jnp.int32, (PAIR, PAIR), 0)
            ok = (k_pos >= first) & (k_pos <= q_pos)
            scores = [dot(kv, qs[256 * h : 256 * h + 256], ((1,), (1,))) for h in range(3)]
            grad_probs = [dot(kv, gs[256 * h : 256 * h + 256], ((1,), (1,))) for h in range(3)]
            grad_scores, probs = [], []
            for h in range(3):
                prob = jnp.where(ok, jnp.exp(scores[h] - sums_log[h]), 0.0)
                grad_scores.append((prob * (grad_probs[h] - deltas[h])).astype(BF))
                probs.append(prob.astype(BF))
            for h in range(3):
                cols = slice(256 * h, 256 * h + 256)
                dq[:, cols] = dq[:, cols] + dot(kv, grad_scores[h], ((0,), (0,)))
            dkv[kb] = (
                dkv[kb]
                + dot(jnp.concatenate(grad_scores, axis=1), qs[...], ((1,), (0,)))
                + dot(jnp.concatenate(probs, axis=1), gs[...], ((1,), (0,)))
            )
            return carry

        lax.fori_loop(0, hi + 1, step, 0)
        by_head = jnp.concatenate([dq[:64, 256 * h : 256 * h + 256] for h in range(3)], axis=0)
        dq_low[zq] = jnp.transpose(by_head * SCALE_QK).astype(BF)
        away = (zq - z + 4) % 4

        @pl.when(away != 0)
        def _():
            remote(dq_low.at[zq], dq_out.at[z], q_send.at[away], q_recv.at[away], dev(y, zq, x, c)).start()

        @pl.when(away == 0)
        def _():
            pltpu.make_async_copy(dq_low.at[zq], dq_out.at[z], l_sem.at[1]).start()

        for xt in range(4):
            t = zq * 4 + xt
            dkv_low[t] = dkv[t].astype(BF)

            @pl.when(t != me)
            def _():
                remote(dkv_low.at[t], dkv_out.at[me], k_send, k_recv, dev(y, zq, xt, c)).start()

            @pl.when(t == me)
            def _():
                pltpu.make_async_copy(dkv_low.at[t], dkv_out.at[me], l_sem.at[2]).start()

        if n in (1, 2):
            w_sum(n - 1)
            for copy in w_copies(n):
                copy.start()

    w_sum(2)
    pltpu.make_async_copy(dq_low.at[z], dq_out.at[z], l_sem.at[1]).wait()
    pltpu.make_async_copy(dkv_low.at[me], dkv_out.at[me], l_sem.at[2]).wait()
    for k in range(1, 4):
        done = remote(dq_low.at[0], dq_out.at[0], q_send.at[k], q_recv.at[k], sibling)
        done.wait_send()
        done.wait_recv()
    drain = remote(dkv_out.at[pl.ds(0, 15)], dkv_out.at[pl.ds(0, 15)], k_send, k_recv, sibling)
    drain.wait_send()
    drain.wait_recv()


def attend_back(heads, branch, own_attn, other_attn, q_in, kv_in, first, ot, lse):
    return pl.pallas_call(
        attend_back_kernel,
        out_shape=[
            jax.ShapeDtypeStruct((4, PAIR, HEAD_Q), BF),
            jax.ShapeDtypeStruct((16, PAIR, 128), BF),
            jax.ShapeDtypeStruct((24, Q_HALF), F32),
        ],
        in_specs=[ANY] + [IN_VMEM] * 8,
        out_specs=[ANY, ANY, IN_VMEM],
        scratch_shapes=[
            pltpu.VMEM((8, ROWS, HEAD_Q), BF),
            pltpu.VMEM((ROWS, MODEL_WIDTH), BF),
            pltpu.VMEM((ROWS, Q_HALF), BF),
            pltpu.VMEM((3 * PAIR, 128), BF),
            pltpu.VMEM((3 * PAIR, 128), BF),
            pltpu.VMEM((128, 3 * PAIR), F32),
            pltpu.VMEM((16, PAIR, 128), F32),
            pltpu.VMEM((16, PAIR, 128), BF),
            pltpu.VMEM((4, PAIR, HEAD_Q), BF),
            pltpu.VMEM((4, 4, 4, 24, Q_HALF), BF),
            pltpu.VMEM((3, 4, 4, 24, 256), BF),
            pltpu.VMEM((3, 4, 24, 256), BF),
            pltpu.VMEM((3, 3, 4, 4, 24, 256), BF),
            pltpu.VMEM((3, 3, 4, 24, 256), BF),
            pltpu.VMEM((3, 3, 24, 256), BF),
            pltpu.SemaphoreType.DMA((3,)),
            pltpu.SemaphoreType.DMA,
            pltpu.SemaphoreType.DMA,
            pltpu.SemaphoreType.DMA((2,)),
            pltpu.SemaphoreType.DMA((2,)),
            pltpu.SemaphoreType.DMA((4,)),
            pltpu.SemaphoreType.DMA((4,)),
            pltpu.SemaphoreType.DMA,
            pltpu.SemaphoreType.DMA,
            pltpu.SemaphoreType.DMA((3, 3, 3)),
            pltpu.SemaphoreType.DMA((3, 3, 3)),
        ],
        compiler_params=params(4, 58 << 20),
        name="attend_back",
    )(heads, branch, own_attn, other_attn, q_in, kv_in, first, ot, lse)


def inverse_rms(values):
    return lax.rsqrt(jnp.mean(values * values, axis=-1, keepdims=True) + EPS)


def norm_backward(values, inverse, gain, grad_out):
    scaled = grad_out * gain
    return inverse * scaled - values * inverse**3 * jnp.mean(values * scaled, axis=-1, keepdims=True)


def column_sums(left, right):
    return lax.dot_general(left, right, (((0,), (0,)), ((), ())), precision=HIGH_PRECISION)


def only_column(rows, column):
    return jnp.broadcast_to((jnp.arange(EXTRA) == column).astype(F32), (rows, EXTRA))


def halves(matrix):
    return matrix.reshape(12, 2, Q_HALF).transpose(1, 0, 2)


def local(
    tokens,
    segment_ids,
    expert_ids,
    w_query,
    w_key,
    w_value,
    w_out,
    w_router,
    gain_attn,
    gain_moe,
    w_gate,
    w_up,
    w_down,
    cotangent,
):
    y, z, x, c = coords()
    width = w_gate.shape[1]
    key_value = jnp.concatenate(
        [w_key.reshape(12, 2, 4, HD), w_value.reshape(12, 2, 4, HD)], axis=3
    ).reshape(12, 2, KV_HALF)
    extra = jnp.concatenate(
        [w_router, gain_attn[:, None], gain_moe[:, None], jnp.zeros((12, EXTRA - 18), BF)], axis=1
    )
    pack = jnp.concatenate(
        [
            halves(w_query),
            key_value.transpose(1, 0, 2),
            halves(w_out.T),
            jnp.broadcast_to(extra[None], (2, 12, EXTRA)),
        ],
        axis=2,
    )
    pack = jnp.pad(pack, ((0, 0), (0, 4), (0, 0)))
    w_experts = jnp.concatenate([w_gate, w_up, w_down.T], axis=1)
    part_q, part_kv, part_out, part_extra, pair, seg_all = gather_weights(
        pack, tokens, segment_ids
    )
    pair, w_experts = lax.optimization_barrier((pair, w_experts))
    full_experts = lax.all_gather(w_experts, "dp", axis=0, tiled=True)
    full_q = part_q.reshape(MODEL_WIDTH, Q_HALF)
    full_kv = part_kv.reshape(MODEL_WIDTH, KV_HALF)
    full_extra = part_extra.reshape(MODEL_WIDTH, EXTRA)
    picks = (jnp.arange(EXTRA)[None, :] == jnp.arange(8)[:, None] + EXPERT_COUNT).astype(BF)
    gains = dot(picks, full_extra, ((1,), (1,)))
    gain_a, gain_m = gains[0:1], gains[1:2]
    router = full_extra[:, :EXPERT_COUNT]

    inputs2 = pair.reshape(PAIR, MODEL_WIDTH).astype(F32)
    inverse_a = inverse_rms(inputs2)
    normed = (inputs2 * inverse_a * gain_a).astype(BF)
    queries = dot(normed, full_q, ((1,), (0,))).astype(BF)
    keys_values = dot(normed, full_kv, ((1,), (0,))).astype(BF)
    q4 = queries.reshape(PAIR, 4, HEAD_Q).transpose(1, 0, 2)
    kv4 = keys_values.reshape(PAIR, 4, 128).transpose(1, 0, 2)
    segs = seg_all.reshape(1, 4096)
    counts = jnp.sum((segs < jnp.arange(16)[:, None]).astype(jnp.int32), axis=1)
    row_segs = lax.dynamic_index_in_dim(seg_all.reshape(4, 4, PAIR), x, 1, keepdims=False)
    first = jnp.sum(
        jnp.where(row_segs[:, :, None] == jnp.arange(16), counts, 0), axis=2
    )
    first = first.reshape(4, 1, PAIR)
    chosen = (expert_ids[:, :, None] == jnp.arange(EXPERT_COUNT, dtype=jnp.int32)).astype(F32)
    used = jnp.sum(chosen, axis=1)
    earlier = (jnp.arange(ROWS)[:, None] > jnp.arange(ROWS)[None, :]).astype(BF)
    before = dot(earlier, used.astype(BF), ((1,), (0,)))
    place = jnp.sum(chosen * before[:, None, :], axis=-1)
    slot = jnp.where(
        place < EXPERT_CAPACITY, expert_ids * SLOTS + place.astype(jnp.int32), -1
    )
    hit = (slot.T[:, :, None] == jnp.arange(EXPERT_COUNT * SLOTS, dtype=jnp.int32)).astype(F32)
    both = (hit[0] + hit[1]).astype(BF)
    blocks = (EXPERT_COUNT, SLOTS, MODEL_WIDTH)
    cot_slots = dot(both, cotangent, ((0,), (0,))).astype(BF)
    q_in, kv_in, attn, attn_t, lse, half_out, sib_out, cot_all = attend(
        q4, kv4, part_out, cot_slots.reshape(blocks), first
    )
    half_out = half_out.reshape(MODEL_WIDTH, Q_HALF)
    sib_out = sib_out.reshape(MODEL_WIDTH, Q_HALF)
    attn = attn.reshape(4, 2, ROWS, HEAD_Q).transpose(1, 2, 0, 3).reshape(2, ROWS, Q_HALF)

    own_attn = jnp.where(c == 0, attn[0], attn[1])
    other_attn = jnp.where(c == 0, attn[1], attn[0])
    inputs = tokens.astype(F32)
    middle = (
        inputs
        + dot(own_attn, half_out, ((1,), (1,)))
        + dot(other_attn, sib_out, ((1,), (1,)))
    )
    inverse_m = inverse_rms(middle)
    moe_in = (middle * inverse_m * gain_m).astype(BF)
    logits = dot(moe_in, router, ((1,), (0,)))
    picked = jnp.sum(chosen * logits[:, None, :], axis=-1)
    gates = jax.nn.softmax(picked, axis=-1)
    slot_gate = jnp.sum(hit * gates.T[:, :, None], axis=(0, 1))
    slots_in = dot(both, moe_in, ((0,), (0,))).astype(BF)
    slot_gate = jnp.broadcast_to(slot_gate.reshape(EXPERT_COUNT, SLOTS, 1), (EXPERT_COUNT, SLOTS, 128))
    out_ret, grad_ret, grad_experts = experts(
        slots_in.reshape(blocks), slot_gate, cot_all, full_experts
    )
    sum_experts = lax.psum_scatter(grad_experts, "dp", scatter_dimension=0, tiled=True)

    grad_output = cotangent.astype(F32)
    out_ret = out_ret.reshape(EXPERT_COUNT * SLOTS, MODEL_WIDTH)
    grad_ret = grad_ret.reshape(EXPERT_COUNT * SLOTS, MODEL_WIDTH)
    rows_out = [dot(hit[k].astype(BF), out_ret, ((1,), (0,))) for k in range(2)]
    block_out = (middle + gates[:, 0:1] * rows_out[0] + gates[:, 1:2] * rows_out[1]).astype(BF)
    grad_pair = jnp.stack([jnp.sum(grad_output * rows, axis=-1) for rows in rows_out], axis=-1)
    grad_pick = gates * (grad_pair - jnp.sum(gates * grad_pair, axis=-1, keepdims=True))
    grad_logits = jnp.sum(chosen * grad_pick[:, :, None], axis=1)
    grad_moe_in = dot(both, grad_ret, ((1,), (0,))) + lax.dot_general(
        grad_logits, router.astype(F32), (((1,), (1,)), ((), ())), precision=HIGH_PRECISION
    )
    g_router = column_sums(moe_in.astype(F32), jnp.pad(grad_logits, ((0, 0), (0, EXTRA - EXPERT_COUNT))))
    g_gain_m = column_sums(grad_moe_in * middle * inverse_m, only_column(ROWS, EXPERT_COUNT + 1))
    grad_middle = grad_output + norm_backward(middle, inverse_m, gain_m, grad_moe_in)
    branch = grad_middle.astype(BF)
    own_heads = dot(branch, half_out, ((1,), (0,))).astype(BF)
    other_heads = dot(branch, sib_out, ((1,), (0,))).astype(BF)
    grad_heads = jnp.stack(
        [jnp.where(c == 0, own_heads, other_heads), jnp.where(c == 0, other_heads, own_heads)]
    )
    grad_heads = grad_heads.reshape(2, ROWS, 4, HEAD_Q).transpose(2, 0, 1, 3)
    dq_in, dkv_in, sum_out = attend_back(
        grad_heads.reshape(8, ROWS, HEAD_Q), branch, own_attn, other_attn, q_in, kv_in, first,
        attn_t, lse,
    )
    grad_q = dq_in.transpose(1, 0, 2).reshape(PAIR, Q_HALF)
    grad_kv = jnp.sum(dkv_in.reshape(4, 4, PAIR, 128).astype(F32), axis=1).astype(BF)
    grad_kv = grad_kv.transpose(1, 0, 2).reshape(PAIR, KV_HALF)

    part_normed = dot(grad_q, full_q, ((1,), (1,))) + dot(
        grad_kv, full_kv, ((1,), (1,))
    )
    g_gain_a = column_sums(part_normed * inputs2 * inverse_a, only_column(PAIR, EXPERT_COUNT))
    g_query = dot(normed, grad_q, ((0,), (0,))).astype(BF)
    g_kv = dot(normed, grad_kv, ((0,), (0,))).astype(BF)
    g_extra = (g_router + g_gain_m + g_gain_a).astype(BF)
    by_core = part_normed.reshape(2, ROWS, MODEL_WIDTH)
    own_part = lax.dynamic_index_in_dim(by_core, c, 0, keepdims=False)
    other_part = lax.dynamic_index_in_dim(by_core, 1 - c, 0, keepdims=False)
    reduced, sib_part = reduce_weights(g_query, g_kv, g_extra, sum_out, other_part)
    grad_normed = own_part + sib_part
    grad_tokens = grad_middle + norm_backward(
        inputs, inverse_rms(inputs), gain_a, grad_normed
    )
    reduced = reduced[:, :12]
    r_query = reduced[:, :, :Q_HALF].transpose(1, 0, 2).reshape(12, HEADS * HD)
    r_kv = reduced[:, :, Q_HALF : Q_HALF + KV_HALF].transpose(1, 0, 2).reshape(12, KV, 2, HD)
    r_out = reduced[:, :, STARTS[2] : STARTS[3]].transpose(1, 0, 2).reshape(12, HEADS * HD)
    r_extra = jnp.sum(reduced[:, :, STARTS[3] :], axis=0)
    return (
        block_out,
        grad_tokens,
        r_query,
        r_kv[:, :, 0].reshape(12, KV * HD),
        r_kv[:, :, 1].reshape(12, KV * HD),
        r_out.T,
        r_extra[:, :EXPERT_COUNT],
        r_extra[:, EXPERT_COUNT],
        r_extra[:, EXPERT_COUNT + 1],
        sum_experts[:, :width].astype(F32),
        sum_experts[:, width : 2 * width].astype(F32),
        sum_experts[:, 2 * width :].astype(F32).T,
    )


def solution(mesh):
    rows, flat, dense = P(("dp", "ctx"), None), P(("dp", "ctx")), P("dp", "ctx")
    placed = (
        rows, dense, rows, rows, rows, rows, P(None, ("dp", "ctx")), rows, flat, flat,
        dense, dense, P("ctx", "dp"), rows,
    )
    return jax.shard_map(
        local,
        mesh=mesh,
        in_specs=placed,
        out_specs=(
            rows, rows, rows, rows, rows, P(None, ("dp", "ctx")), rows, flat, flat,
            dense, dense, P("ctx", "dp"),
        ),
        check_vma=False,
    )
```

```python
import functools

import jax
import jax.numpy as jnp
from jax import lax
from jax.experimental import pallas as pl
from jax.experimental.pallas import tpu as pltpu
from jax.sharding import PartitionSpec as P

MODEL_WIDTH = 1536
HEADS = 24
KV = 8
HD = 64
EXPERT_COUNT = 16
FF = 1024
EXPERT_CAPACITY = 20
SLOTS = 24
ROWS = 128
PAIR = 256
HEAD_Q = 192
Q_HALF = 768
KV_HALF = 512
EXTRA = 128
PACK = Q_HALF + KV_HALF + EXTRA + Q_HALF

EPS = 1e-05
SCALE_QK = 0.125
NEGATIVE = -1e30
HIGH_PRECISION = lax.Precision.HIGHEST
MESH = pl.DeviceIdType.MESH
ANY = pl.BlockSpec(memory_space=pl.ANY)
IN_VMEM = pl.BlockSpec(memory_space=pltpu.VMEM)
BF = jnp.bfloat16
F32 = jnp.float32


def dot(a, b, dims):
    return lax.dot_general(a, b, (dims, ((), ())), preferred_element_type=F32)


def coords():
    i = lax.axis_index("ctx")
    return lax.axis_index("dp"), i // 8, (i // 2) % 4, i % 2


def dev(y, z, x, c):
    return (y, z * 8 + x * 2 + c)


def signal(target):
    pl.semaphore_signal(
        pltpu.get_barrier_semaphore(), inc=1, device_id=target, device_id_type=MESH
    )


def remote(src, dst, send, recv, target):
    return pltpu.make_async_remote_copy(
        src_ref=src, dst_ref=dst, send_sem=send, recv_sem=recv, device_id=target, device_id_type=MESH
    )


def params(cid, vmem=None):
    return pltpu.CompilerParams(collective_id=cid, has_side_effects=True, vmem_limit_bytes=vmem)


def axis_peer(axis, step):
    y, z, x, c = coords()
    if axis == "y":
        return dev((y + step) % 4, z, x, c)
    if axis == "z":
        return dev(y, (z + step) % 4, x, c)
    return dev(y, z, (x + step) % 4, c)


WIDTHS = (Q_HALF, KV_HALF, Q_HALF, EXTRA)
STARTS = (0, Q_HALF, Q_HALF + KV_HALF, 2 * Q_HALF + KV_HALF)
STEPS = (1, 3, 2)
FIRST_PARTS = (
    (0, 0, 512, ("x", "z", "y")),
    (1, 0, 512, ("y", "x", "z")),
    (0, 512, 256, ("z", "y", "x")),
    (3, 0, 128, ("z", "y", "x")),
)
OUT_PARTS = (
    (2, 0, 128, ("z", "x", "y")),
    (2, 128, 384, ("z", "y", "x")),
    (2, 512, 256, ("y", "x", "z")),
)
OUT_SUMS = ((0, ("x", "y", "z")), (256, ("x", "z", "y")), (512, ("z", "x", "y")))
GATHER_PARTS = FIRST_PARTS + OUT_PARTS


def slab(ref, done, y, z, x, cols):
    return ref.at[
        slice(None) if "y" in done else y,
        slice(None) if "z" in done else z,
        slice(None) if "x" in done else x,
        slice(None),
        cols,
    ]


def gather_kernel(
    pack, tokens, segs, out0, out1, out2, out3, pair, seg_all,
    sib, block, p_send, p_recv, l_sem, s_send, s_recv, sib_send, sib_recv,
):
    y, z, x, c = coords()
    outs = (out0, out1, out2, out3)
    me = z * 8 + x * 2 + c
    sibling = dev(y, z, x, 1 - c)

    def greet(k, carry):
        signal((y, (me + k) % 32))
        return carry

    lax.fori_loop(1, 32, greet, 0)
    for step in STEPS:
        signal(axis_peer("y", step))
    pl.semaphore_wait(pltpu.get_barrier_semaphore(), 34)

    first = remote(pack.at[1 - c], sib, sib_send.at[0], sib_recv.at[0], sibling)
    first.start()
    second = remote(tokens, pair.at[c], sib_send.at[1], sib_recv.at[1], sibling)
    second.start()
    own_rows = pltpu.make_async_copy(tokens, pair.at[c], l_sem.at[4])
    own_rows.start()
    own_segs = pltpu.make_async_copy(segs, seg_all.at[me], l_sem.at[5])
    own_segs.start()

    def spread(k, carry):
        remote(segs, seg_all.at[me], s_send, s_recv, (y, (me + k) % 32)).start()
        return carry

    lax.fori_loop(1, 32, spread, 0)

    first.wait()
    own = pack[c, :12].astype(F32)
    other = sib[:12].astype(F32)
    low = jnp.where(c == 0, own, other)
    high = jnp.where(c == 0, other, own)
    block[...] = jnp.concatenate([low, high], axis=0).astype(BF)

    locals_ = []
    for n in range(4):
        cols = pl.ds(STARTS[n], WIDTHS[n])
        here = pltpu.make_async_copy(block.at[:, cols], outs[n].at[y, z, x], l_sem.at[n])
        here.start()
        locals_.append(here)
    for phase in range(3):
        copies = []
        for part, (n, start, width, order) in enumerate(GATHER_PARTS if phase < 2 else FIRST_PARTS):
            for k, step in enumerate(STEPS):
                dst = slab(outs[n], order[:phase], y, z, x, pl.ds(start, width))
                src = block.at[:, pl.ds(STARTS[n] + start, width)] if phase == 0 else dst
                copy = remote(
                    src, dst, p_send.at[phase, part, k], p_recv.at[phase, part, k],
                    axis_peer(order[phase], step),
                )
                copy.start()
                copies.append(copy)
        if phase == 0:
            for here in locals_:
                here.wait()
        for copy in copies:
            copy.wait()
    second.wait()
    own_rows.wait()
    own_segs.wait()
    drain = remote(
        seg_all.at[pl.ds(0, 31)], seg_all.at[pl.ds(0, 31)], s_send, s_recv, sibling
    )
    drain.wait_send()
    drain.wait_recv()


def gather_weights(pack, tokens, segs):
    return pl.pallas_call(
        gather_kernel,
        out_shape=[jax.ShapeDtypeStruct((4, 4, 4, 24, width), BF) for width in WIDTHS]
        + [
            jax.ShapeDtypeStruct((2, ROWS, MODEL_WIDTH), BF),
            jax.ShapeDtypeStruct((32, 1, 128), jnp.int32),
        ],
        in_specs=[IN_VMEM, ANY, ANY],
        out_specs=[ANY] * 6,
        scratch_shapes=[
            pltpu.VMEM((16, PACK), BF),
            pltpu.VMEM((24, PACK), BF),
            pltpu.SemaphoreType.DMA((3, 7, 3)),
            pltpu.SemaphoreType.DMA((3, 7, 3)),
            pltpu.SemaphoreType.DMA((6,)),
            pltpu.SemaphoreType.DMA,
            pltpu.SemaphoreType.DMA,
            pltpu.SemaphoreType.DMA((2,)),
            pltpu.SemaphoreType.DMA((2,)),
        ],
        compiler_params=params(1),
        name="gather_weights",
    )(pack, tokens, segs)


def plane_greet(y, me, c, sibling):
    def greet(k, carry):
        t = (me + k) % 16
        signal(dev(y, t // 4, t % 4, c))
        return carry

    lax.fori_loop(1, 16, greet, 0)
    if sibling is not None:
        signal(sibling)
        pl.semaphore_wait(pltpu.get_barrier_semaphore(), 16)
    else:
        pl.semaphore_wait(pltpu.get_barrier_semaphore(), 15)


KEYS = 1024


def attend_kernel(
    q4, kv2, half_in, cots, first_ref, q_in, kv_in, attn, ot_ref, lse_ref, half, half_sib, c_all,
    qs, acc, o_buf,
    l_sem, q_send, q_recv, k_send, k_recv, w_send, w_recv, sib_send, sib_recv,
    c_send, c_recv, f_send, f_recv, o_send, o_recv,
):
    y, z, x, c = coords()
    me = z * 4 + x
    sibling = dev(y, z, x, 1 - c)

    wide_greet()

    q_copies = []
    for n, step in enumerate(STEPS):
        to = (z + step) % 4
        copy = remote(q4.at[to], q_in.at[z], q_send.at[n], q_recv.at[n], dev(y, to, x, c))
        copy.start()
        q_copies.append(copy)

    def head(index):
        return kv2.at[:, pl.ds(pl.multiple_of(index * 128, 128), 128)]

    def send_kv(k, carry):
        t = (me + k) % 16
        remote(head(t // 4), kv_in.at[me], k_send, k_recv, dev(y, t // 4, t % 4, c)).start()
        return carry

    lax.fori_loop(1, 16, send_kv, 0)
    here = [
        pltpu.make_async_copy(q4.at[z], q_in.at[z], l_sem.at[0]),
        pltpu.make_async_copy(head(z), kv_in.at[me], l_sem.at[1]),
    ]
    for copy in here:
        copy.start()
    for copy in here:
        copy.wait()
    for copy in q_copies:
        copy.wait()
    drain = remote(kv_in.at[pl.ds(0, 15)], kv_in.at[pl.ds(0, 15)], k_send, k_recv, sibling)
    drain.wait_send()
    drain.wait_recv()

    w_copies = [[], [], []]
    for part, (n, start, width, order) in enumerate(OUT_PARTS):
        spot = slab(half, order[:2], y, z, x, pl.ds(start, width))
        for k, step in enumerate(STEPS):
            copy = remote(
                spot, spot, w_send.at[part, k], w_recv.at[part, k], axis_peer(order[2], step)
            )
            copy.start()
            w_copies[part].append(copy)

    def send_cots(k, carry):
        t = (me + k) % 16
        remote(
            cots.at[t], c_all.at[c * 16 + me], c_send.at[k], c_recv.at[k], dev(y, t // 4, t % 4, c)
        ).start()
        return carry

    lax.fori_loop(1, 16, send_cots, 0)
    own_cots = pltpu.make_async_copy(cots.at[me], c_all.at[c * 16 + me], l_sem.at[2])
    own_cots.start()
    remote(cots.at[me], c_all.at[c * 16 + me], f_send, f_recv, sibling).start()

    def forward_cots(k, carry):
        s = c * 16 + (me + 16 - k) % 16
        t = (me + k) % 16
        arrived = remote(cots.at[t], c_all.at[s], c_send.at[k], c_recv.at[k], dev(y, t // 4, t % 4, c))
        arrived.wait_recv()
        remote(c_all.at[s], c_all.at[s], f_send, f_recv, sibling).start()
        arrived.wait_send()
        return carry

    def swap(part):
        start, width = OUT_PARTS[part][1:3]
        cols = half.at[:, :, :, :, pl.ds(start, width)]
        there = half_sib.at[:, :, :, :, pl.ds(start, width)]
        return remote(cols, there, sib_send.at[part], sib_recv.at[part], sibling)

    j = c * 4 + z
    qs[64:] = jnp.zeros((64, 3 * PAIR), BF)
    returns = []
    for n in range(4):
        zq = (z + n + 1) % 4
        q = q_in[zq] * SCALE_QK
        for h in range(3):
            qs[:64, 256 * h : 256 * h + 256] = q[64 * h : 64 * h + 64]
        acc[...] = jnp.zeros_like(acc)
        first = first_ref[zq]
        q_pos = (zq * 4 + x) * PAIR + lax.broadcasted_iota(jnp.int32, (1, PAIR), 1)

        def step(kb, stats):
            kv = kv_in[pl.ds(kb * (KEYS // PAIR), KEYS // PAIR)].reshape(KEYS, 128)
            k_pos = kb * KEYS + lax.broadcasted_iota(jnp.int32, (KEYS, PAIR), 0)
            ok = (k_pos >= first) & (k_pos <= q_pos)
            scores = [dot(kv, qs[:, 256 * h : 256 * h + 256], ((1,), (0,))) for h in range(3)]
            later, probs, shrinks = [], [], []
            for h in range(3):
                top, tot = stats[h]
                masked = jnp.where(ok, scores[h], NEGATIVE)
                new = jnp.maximum(top, jnp.max(masked, axis=0, keepdims=True))
                prob = jnp.exp(masked - new)
                shrink = jnp.exp(top - new)
                later.append((new, tot * shrink + jnp.sum(prob, axis=0, keepdims=True)))
                probs.append(prob.astype(BF))
                shrinks.append(shrink)
            for h in range(3):
                cols = slice(256 * h, 256 * h + 256)
                acc[:, cols] = acc[:, cols] * shrinks[h] + dot(kv, probs[h], ((0,), (0,)))
            return tuple(later)

        none = (jnp.full((1, PAIR), NEGATIVE, F32), jnp.zeros((1, PAIR), F32))
        stats = lax.fori_loop(0, zq + 1, step, (none, none, none))
        heads = []
        for h in range(3):
            cols = slice(256 * h, 256 * h + 256)
            mixed = acc[64:, cols] / stats[h][1]
            ot_ref[zq, :, cols] = mixed
            lse_ref[zq, :, cols] = stats[h][0] + jnp.log(stats[h][1])
            heads.append(mixed)
        heads = jnp.concatenate(heads, axis=0).astype(BF)
        o_buf[n, 0] = heads[:, :ROWS]
        o_buf[n, 1] = heads[:, ROWS:]
        for d in range(2):
            core = c if d == 0 else 1 - c
            if n == 3 and d == 0:
                back = pltpu.make_async_copy(o_buf.at[n, core], attn.at[j], l_sem.at[3])
            else:
                back = remote(
                    o_buf.at[n, core], attn.at[j], o_send.at[n, d], o_recv.at[n, d], dev(y, zq, x, core)
                )
            back.start()
            returns.append(back)
    for part in range(3):
        for copy in w_copies[part]:
            copy.wait()
        swap(part).start()
        if part == 0:
            lax.fori_loop(1, 16, forward_cots, 0)
    own_cots.wait()
    mine = c_all.at[pl.ds(c * 16, 16)]
    drain = remote(mine, mine, f_send, f_recv, sibling)
    drain.wait_send()
    drain.wait_recv()
    for part in range(3):
        swap(part).wait()
    for back in returns:
        back.wait()


def attend(q4, kv2, half, cots, first):
    blocks = jax.ShapeDtypeStruct((4, 4, 4, 24, Q_HALF), BF)
    return pl.pallas_call(
        attend_kernel,
        out_shape=[
            jax.ShapeDtypeStruct((4, HEAD_Q, PAIR), BF),
            jax.ShapeDtypeStruct((16, PAIR, 128), BF),
            jax.ShapeDtypeStruct((8, HEAD_Q, ROWS), BF),
            jax.ShapeDtypeStruct((4, HD, 3 * PAIR), F32),
            jax.ShapeDtypeStruct((4, 1, 3 * PAIR), F32),
            blocks,
            blocks,
            jax.ShapeDtypeStruct((32, SLOTS, MODEL_WIDTH), BF),
        ],
        in_specs=[ANY, ANY, ANY, ANY, IN_VMEM],
        out_specs=[IN_VMEM, IN_VMEM, ANY, IN_VMEM, IN_VMEM, ANY, ANY, ANY],
        input_output_aliases={2: 5},
        scratch_shapes=[
            pltpu.VMEM((128, 3 * PAIR), BF),
            pltpu.VMEM((128, 3 * PAIR), F32),
            pltpu.VMEM((4, 2, HEAD_Q, ROWS), BF),
            pltpu.SemaphoreType.DMA((4,)),
            pltpu.SemaphoreType.DMA((3,)),
            pltpu.SemaphoreType.DMA((3,)),
            pltpu.SemaphoreType.DMA,
            pltpu.SemaphoreType.DMA,
            pltpu.SemaphoreType.DMA((3, 3)),
            pltpu.SemaphoreType.DMA((3, 3)),
            pltpu.SemaphoreType.DMA((3,)),
            pltpu.SemaphoreType.DMA((3,)),
            pltpu.SemaphoreType.DMA((16,)),
            pltpu.SemaphoreType.DMA((16,)),
            pltpu.SemaphoreType.DMA,
            pltpu.SemaphoreType.DMA,
            pltpu.SemaphoreType.DMA((4, 2)),
            pltpu.SemaphoreType.DMA((4, 2)),
        ],
        compiler_params=params(2, 56 << 20),
        name="attend",
    )(q4, kv2, half, cots, first)


def flat_rows(blocks):
    return blocks.reshape(blocks.shape[0] * SLOTS, blocks.shape[2])


def experts_kernel(
    xs, gates, cots, weights, out_ret, grad_ret, d_all,
    x_all, t_all, g_all, w_all, gate_v, up_v, hidden, g_both, part_o, part_g, sib_o, sib_g,
    v_all,
    w_sem, l_sem, send, recv, f_send, f_recv, s_send, s_recv, r_send, r_recv, o_sem,
):
    y, z, x, c = coords()
    me = z * 4 + x
    width = hidden.shape[1]
    sibling = dev(y, z, x, 1 - c)
    plane_greet(y, me, c, sibling)
    loads = [
        pltpu.make_async_copy(src, dst, w_sem.at[n])
        for n, (src, dst) in enumerate(((weights, w_all), (cots, g_all)))
    ]
    for load in loads:
        load.start()
    arrays = ((xs, x_all), (gates, t_all))

    def scatter(a):
        src, dst = arrays[a]

        def push(k, carry):
            t = (me + k) % 16
            remote(
                src.at[t], dst.at[c * 16 + me], send.at[a, k], recv.at[a, k], dev(y, t // 4, t % 4, c)
            ).start()
            return carry

        lax.fori_loop(1, 16, push, 0)
        pltpu.make_async_copy(src.at[me], dst.at[c * 16 + me], l_sem.at[a]).start()
        remote(src.at[me], dst.at[c * 16 + me], f_send.at[a], f_recv.at[a], sibling).start()

    def hand_over(a):
        src, dst = arrays[a]

        def forward(k, carry):
            s = (me + 16 - k) % 16
            t = (me + k) % 16
            arrived = remote(
                src.at[t], dst.at[c * 16 + s], send.at[a, k], recv.at[a, k], dev(y, t // 4, t % 4, c)
            )
            arrived.wait_recv()
            remote(
                dst.at[c * 16 + s], dst.at[c * 16 + s], f_send.at[a], f_recv.at[a], sibling
            ).start()
            arrived.wait_send()
            return carry

        lax.fori_loop(1, 16, forward, 0)

    def settle(a):
        src, dst = arrays[a]
        pltpu.make_async_copy(src.at[me], dst.at[c * 16 + me], l_sem.at[a]).wait()
        half = pl.ds(0, 16)
        drain = remote(dst.at[half], dst.at[half], f_send.at[a], f_recv.at[a], sibling)
        drain.wait_send()
        drain.wait_recv()

    def swap(part, sib, a):
        rows = pl.ds((1 - c) * 16, 16)
        return remote(part.at[rows], sib, s_send.at[a], s_recv.at[a], sibling)

    def give(part, sib, ret, a):
        def add(t):
            rows = c * 16 + t
            part[rows] = (
                part[rows].astype(F32) + sib[t].astype(F32)
            ).astype(BF)
            return part.at[rows]

        def push(k, carry):
            t = (me + k) % 16
            remote(add(t), ret.at[me], r_send.at[a], r_recv.at[a], dev(y, t // 4, t % 4, c)).start()
            return carry

        lax.fori_loop(1, 16, push, 0)
        pltpu.make_async_copy(add(me), ret.at[me], l_sem.at[2 + a]).start()

    def given(part, ret, a):
        pltpu.make_async_copy(part.at[c * 16 + me], ret.at[me], l_sem.at[2 + a]).wait()
        drain = remote(ret.at[pl.ds(0, 15)], ret.at[pl.ds(0, 15)], r_send.at[a], r_recv.at[a], sibling)
        drain.wait_send()
        drain.wait_recv()

    def tile(n):
        h = 1 - c if n == 0 else c
        rows = 16 * SLOTS
        return pl.ds(h * 16, 16), pl.ds(pl.multiple_of(h * rows, rows), rows)

    scatter(0)
    scatter(1)
    hand_over(0)
    hand_over(1)
    settle(0)
    settle(1)
    for load in loads:
        load.wait()
    for n in range(2):
        blocks, rows = tile(n)
        rows_in = flat_rows(x_all[blocks])
        both = dot(rows_in, w_all[:, : 2 * width], ((1,), (0,)))
        gate_val, up_val = both[:, :width], both[:, width:]
        gate_v[rows] = gate_val
        up_v[rows] = up_val
        low = (gate_val * jax.nn.sigmoid(gate_val) * up_val).astype(BF)
        hidden[rows] = low
        part_o[blocks] = dot(low, w_all[:, 2 * width :], ((1,), (1,))).astype(BF).reshape(16, SLOTS, MODEL_WIDTH)
        if n == 0:
            swap(part_o, sib_o, 0).start()
    swap(part_o, sib_o, 0).wait()
    give(part_o, sib_o, out_ret, 0)
    for n in range(2):
        blocks, rows = tile(n)
        scale = jnp.concatenate([flat_rows(t_all[blocks])] * (MODEL_WIDTH // 128), axis=1)
        grad_expert = (flat_rows(g_all[blocks]).astype(F32) * scale).astype(BF)
        g_all[blocks] = grad_expert.reshape(16, SLOTS, MODEL_WIDTH)
        grad_hidden = dot(grad_expert, w_all[:, 2 * width :], ((1,), (0,)))
        gate_val = gate_v[rows]
        up_val = up_v[rows]
        sig = jax.nn.sigmoid(gate_val)
        grad_gate = (grad_hidden * up_val * sig * (1.0 + gate_val * (1.0 - sig))).astype(BF)
        grad_up = (grad_hidden * gate_val * sig).astype(BF)
        grads = jnp.concatenate([grad_gate, grad_up], axis=1)
        g_both[rows] = grads
        grad_rows = dot(grads, w_all[:, : 2 * width], ((1,), (1,)))
        part_g[blocks] = grad_rows.astype(BF).reshape(16, SLOTS, MODEL_WIDTH)
        if n == 0:
            swap(part_g, sib_g, 1).start()
    swap(part_g, sib_g, 1).wait()
    give(part_g, sib_g, grad_ret, 1)

    def weight_grads(j, carry):
        cols = pl.ds(pl.multiple_of(j * 256, 256), 256)
        v_all[cols, : 2 * width] = dot(flat_rows(x_all[:, :, cols]), g_both[...], ((0,), (0,))).astype(BF)
        v_all[cols, 2 * width :] = dot(flat_rows(g_all[:, :, cols]), hidden[...], ((0,), (0,))).astype(BF)
        return carry

    lax.fori_loop(0, MODEL_WIDTH // 256, weight_grads, 0)
    store = pltpu.make_async_copy(v_all, d_all, o_sem)
    store.start()
    store.wait()
    given(part_o, out_ret, 0)
    given(part_g, grad_ret, 1)


def experts(xs, gates, cots, weights):
    rows = 32 * SLOTS
    width = weights.shape[1] // 3
    back = jax.ShapeDtypeStruct((16, SLOTS, MODEL_WIDTH), BF)
    return pl.pallas_call(
        experts_kernel,
        out_shape=[back, back, jax.ShapeDtypeStruct(weights.shape, BF)],
        in_specs=[ANY] * 4,
        out_specs=[ANY] * 3,
        scratch_shapes=[
            pltpu.VMEM((32, SLOTS, MODEL_WIDTH), BF),
            pltpu.VMEM((32, SLOTS, 128), F32),
            pltpu.VMEM((32, SLOTS, MODEL_WIDTH), BF),
            pltpu.VMEM(weights.shape, BF),
            pltpu.VMEM((rows, width), F32),
            pltpu.VMEM((rows, width), F32),
            pltpu.VMEM((rows, width), BF),
            pltpu.VMEM((rows, 2 * width), BF),
            pltpu.VMEM((32, SLOTS, MODEL_WIDTH), BF),
            pltpu.VMEM((32, SLOTS, MODEL_WIDTH), BF),
            pltpu.VMEM((16, SLOTS, MODEL_WIDTH), BF),
            pltpu.VMEM((16, SLOTS, MODEL_WIDTH), BF),
            pltpu.VMEM(weights.shape, BF),
            pltpu.SemaphoreType.DMA((2,)),
            pltpu.SemaphoreType.DMA((4,)),
            pltpu.SemaphoreType.DMA((2, 16)),
            pltpu.SemaphoreType.DMA((2, 16)),
            pltpu.SemaphoreType.DMA((2,)),
            pltpu.SemaphoreType.DMA((2,)),
            pltpu.SemaphoreType.DMA((2,)),
            pltpu.SemaphoreType.DMA((2,)),
            pltpu.SemaphoreType.DMA((2,)),
            pltpu.SemaphoreType.DMA((2,)),
            pltpu.SemaphoreType.DMA,
        ],
        compiler_params=params(6, 56 << 20),
        name="experts",
    )(xs, gates, cots, weights)


SUMS = tuple((n, start, width, order[::-1]) for n, start, width, order in FIRST_PARTS) + tuple(
    (2, start, 256, order) for start, order in OUT_SUMS
)
LATE = len(FIRST_PARTS)


def reduce_kernel(
    gq_t, dkv, normed, g_moe, s_out, pair, gain, grad_middle, w_q, w_kv,
    o_tokens, o_q, o_k, o_v, o_out, o_extra,
    v_q, v_kv, v_extra, wq, wkv, gkv, mine_part, give_part, sib_part, both, total, give, *rest,
):
    parts = len(SUMS)
    first_in, rest = rest[:LATE], rest[LATE:]
    arrive = [list(first_in) + [None] * 3, rest[:parts], rest[parts : 2 * parts]]
    rest = rest[2 * parts :]
    held = [None, list(rest[:LATE]) + [s_out.at[k] for k in range(3)], rest[LATE : LATE + parts]]
    l_sem, send, recv, sib_send, sib_recv = rest[LATE + parts :]
    grads = (v_q, v_kv, None, v_extra)
    y, z, x, c = coords()
    place = {"y": y, "z": z, "x": x}
    sibling = dev(y, z, x, 1 - c)
    loads = [pltpu.make_async_copy(w_q, wq, l_sem.at[0]), pltpu.make_async_copy(w_kv, wkv, l_sem.at[1])]
    for load in loads:
        load.start()
    for axis in ("x", "y", "z"):
        for step in STEPS:
            signal(axis_peer(axis, step))
    signal(sibling)
    pl.semaphore_wait(pltpu.get_barrier_semaphore(), 10)

    def at(phase, part, index):
        n, start, width, order = SUMS[part]
        spot = [
            index if axis == order[phase] else slice(None)
            for axis in ("y", "z", "x")
            if axis not in order[:phase]
        ]
        if phase == 0:
            return grads[n].at[tuple(spot) + (slice(None), pl.ds(start, width))]
        return held[phase][part].at[tuple(spot)]

    def copies_of(phase, part):
        axis = SUMS[part][3][phase]
        return [
            remote(
                at(phase, part, (place[axis] + step) % 4), arrive[phase][part].at[n],
                send.at[phase, part, n], recv.at[phase, part, n], axis_peer(axis, step),
            )
            for n, step in enumerate(STEPS)
        ]

    def begin(phase, part):
        for copy in copies_of(phase, part):
            copy.start()

    def finish(phase, part):
        for copy in copies_of(phase, part):
            copy.wait()
        array, start, width, order = SUMS[part]
        mine = at(phase, part, place[order[phase]])
        got = arrive[phase][part]
        if phase < 2:

            def add(p, carry):
                value = mine[p].astype(F32)
                for n in range(3):
                    value = value + got[n, p].astype(F32)
                held[phase + 1][part][p] = value.astype(BF)
                return carry

            lax.fori_loop(0, 4, add, 0)
        else:
            value = mine[...].astype(F32)
            for n in range(3):
                value = value + got[n].astype(F32)
            total[:, STARTS[array] + start : STARTS[array] + start + width] = value

    for part in range(LATE, parts):
        begin(1, part)
    for h in range(4):
        value = dkv[4 * h].astype(F32)
        for n in range(1, 4):
            value = value + dkv[4 * h + n].astype(F32)
        gkv[:, 128 * h : 128 * h + 128] = value.astype(BF)
    for n in range(4):
        left = normed[:, 384 * n : 384 * n + 384]
        v_q[n] = dot(left, gq_t[...], ((0,), (1,))).astype(BF).reshape(4, 4, 24, Q_HALF)
        v_kv[n] = dot(left, gkv[...], ((0,), (0,))).astype(BF).reshape(4, 4, 24, KV_HALF)
    for part in range(3):
        begin(0, part)

    for load in loads:
        load.wait()
    gain_sum = jnp.zeros((1, MODEL_WIDTH), F32)
    for n in range(2):
        core = 1 - c if n == 0 else c
        rows = pl.ds(pl.multiple_of(core * ROWS, ROWS), ROWS)
        part = dot(gq_t[:, rows], wq[...], ((0,), (1,))) + dot(gkv[rows], wkv[...], ((1,), (1,)))
        values = pair[rows].astype(F32)
        gain_sum = gain_sum + jnp.sum(part * values * inverse_rms(values), axis=0, keepdims=True)
        if n == 0:
            give_part[...] = part
            remote(give_part, sib_part, sib_send.at[0], sib_recv.at[0], sibling).start()
        else:
            mine_part[...] = part
    column = jnp.transpose(jnp.broadcast_to(gain_sum, (EXTRA, MODEL_WIDTH)))
    lane = lax.broadcasted_iota(jnp.int32, (MODEL_WIDTH, EXTRA), 1)
    extra = g_moe[...] + jnp.where(lane == EXPERT_COUNT, column, 0.0)
    v_extra[...] = extra.astype(BF).reshape(4, 4, 4, 24, EXTRA)
    begin(0, 3)
    remote(give_part, sib_part, sib_send.at[0], sib_recv.at[0], sibling).wait()
    rows = pl.ds(pl.multiple_of(c * ROWS, ROWS), ROWS)
    values = pair[rows].astype(F32)
    o_tokens[...] = grad_middle[...] + norm_backward(
        values, inverse_rms(values), gain[...], mine_part[...] + sib_part[...]
    )

    for part in range(LATE, parts):
        finish(1, part)
        begin(2, part)
    for phase in range(3):
        for part in range(LATE):
            finish(phase, part)
            if phase < 2:
                begin(phase + 1, part)
    for part in range(LATE, parts):
        finish(2, part)
    low, high = total[0:12], total[12:24]
    both[c, 0:12] = jnp.where(c == 0, low, high)
    give[0:12] = jnp.where(c == 0, high, low)
    give[12:16] = jnp.zeros((4, PACK), F32)
    last = remote(give, both.at[c], sib_send.at[1], sib_recv.at[1], sibling)
    last.start()
    last.wait()
    keys, values = [], []
    for k in range(2):
        o_q[:, Q_HALF * k : Q_HALF * k + Q_HALF] = both[k, 0:12, :Q_HALF]
        o_out[:, Q_HALF * k : Q_HALF * k + Q_HALF] = both[k, 0:12, STARTS[2] : STARTS[3]]
        for h in range(4):
            first = STARTS[1] + 128 * h
            keys.append(both[k, 0:12, first : first + HD])
            values.append(both[k, 0:12, first + HD : first + 2 * HD])
    o_k[...] = jnp.concatenate(keys, axis=1)
    o_v[...] = jnp.concatenate(values, axis=1)
    o_extra[...] = both[0, 0:12, STARTS[3] :] + both[1, 0:12, STARTS[3] :]


def reduce_weights(gq_t, dkv, normed, g_moe, s_out, pair, gain, grad_middle, w_q, w_kv):
    widths = [part[2] for part in SUMS]
    full = lambda width: pltpu.VMEM((4, 4, 4, 24, width), BF)
    rows = pltpu.VMEM((ROWS, MODEL_WIDTH), F32)
    scratch = (
        [full(Q_HALF), full(KV_HALF), full(EXTRA)]
        + [pltpu.VMEM((MODEL_WIDTH, Q_HALF), BF), pltpu.VMEM((MODEL_WIDTH, KV_HALF), BF)]
        + [pltpu.VMEM((PAIR, KV_HALF), BF), rows, rows, rows]
        + [pltpu.VMEM((2, 16, PACK), F32), pltpu.VMEM((24, PACK), F32), pltpu.VMEM((16, PACK), F32)]
        + [pltpu.VMEM((3, 4, 4, 24, w), BF) for w in widths[:LATE]]
        + [pltpu.VMEM((3, 4, 24, w), BF) for w in widths]
        + [pltpu.VMEM((3, 24, w), BF) for w in widths]
        + [pltpu.VMEM((4, 4, 24, w), BF) for w in widths[:LATE]]
        + [pltpu.VMEM((4, 24, w), BF) for w in widths]
    )
    sems = (3, len(SUMS), 3)
    shapes = ((ROWS, MODEL_WIDTH), (12, MODEL_WIDTH), (12, KV * HD), (12, KV * HD), (12, MODEL_WIDTH), (12, EXTRA))
    return pl.pallas_call(
        reduce_kernel,
        out_shape=[jax.ShapeDtypeStruct(shape, F32) for shape in shapes],
        in_specs=[IN_VMEM] * 8 + [ANY] * 2,
        out_specs=[IN_VMEM] * 6,
        scratch_shapes=scratch
        + [
            pltpu.SemaphoreType.DMA((2,)),
            pltpu.SemaphoreType.DMA(sems),
            pltpu.SemaphoreType.DMA(sems),
            pltpu.SemaphoreType.DMA((2,)),
            pltpu.SemaphoreType.DMA((2,)),
        ],
        compiler_params=params(8, 58 << 20),
        name="reduce_weights",
    )(gq_t, dkv, normed, g_moe, s_out, pair, gain, grad_middle, w_q, w_kv)


def wide_greet():
    y, z, x, c = coords()
    me = z * 4 + x

    def greet(k, carry):
        t = (me + k) % 16
        signal(dev(y, t // 4, t % 4, c))
        return carry

    lax.fori_loop(1, 16, greet, 0)
    for step in STEPS:
        signal(axis_peer("y", step))
        signal(dev(y, (z + step) % 4, x, 1 - c))
    signal(dev(y, z, x, 1 - c))
    pl.semaphore_wait(pltpu.get_barrier_semaphore(), 22)


def attend_back_kernel(
    heads, branch, own_attn, other_attn, q_in, kv_in, first_ref, ot_ref, lse_ref,
    dq_out, dkv_out, s_out,
    go, branch_sib, attn_sib, qs, gs, dq, dkv, dkv_low, dq_low,
    g_out, a_out,
    l_sem, h_send, h_recv, sib_send, sib_recv, q_send, q_recv, k_send, k_recv,
    w_send, w_recv,
):
    y, z, x, c = coords()
    me = z * 4 + x
    j = c * 4 + z
    sibling = dev(y, z, x, 1 - c)
    place = {"y": y, "z": z, "x": x}
    wide_greet()

    def push(k, carry):
        t = (j + k) % 8
        remote(heads.at[t], go.at[j], h_send, h_recv, dev(y, t % 4, x, t // 4)).start()
        return carry

    lax.fori_loop(1, 8, push, 0)
    one = remote(branch, branch_sib, sib_send.at[0], sib_recv.at[0], sibling)
    one.start()
    two = remote(other_attn, attn_sib, sib_send.at[1], sib_recv.at[1], sibling)
    two.start()
    here = pltpu.make_async_copy(heads.at[j], go.at[j], l_sem.at[0])
    here.start()
    here.wait()
    drain = remote(go.at[pl.ds(0, 7)], go.at[pl.ds(0, 7)], h_send, h_recv, sibling)
    drain.wait_send()
    drain.wait_recv()
    one.wait()
    two.wait()

    rows_b = jnp.concatenate([branch[...], branch_sib[...]], axis=0)
    rows_a = jnp.concatenate([own_attn[...], attn_sib[...]], axis=1)
    for n in range(4):
        part = dot(rows_b[:, 384 * n : 384 * n + 384], rows_a, ((0,), (1,)))
        g_out[n] = part.astype(BF).reshape(4, 4, 24, Q_HALF)

    def spot(part, index):
        start, order = OUT_SUMS[part]
        cut = [index if axis == order[0] else slice(None) for axis in ("y", "z", "x")]
        return g_out.at[tuple(cut) + (slice(None), pl.ds(start, 256))]

    w_copies = []
    for part in range(3):
        axis = OUT_SUMS[part][1][0]
        for n, step in enumerate(STEPS):
            copy = remote(
                spot(part, (place[axis] + step) % 4), a_out.at[part, n],
                w_send.at[part, n], w_recv.at[part, n], axis_peer(axis, step),
            )
            copy.start()
            w_copies.append(copy)

    dkv[...] = jnp.zeros_like(dkv)
    qs[64:] = jnp.zeros((64, 3 * PAIR), BF)
    gs[:64] = jnp.zeros((64, 3 * PAIR), BF)
    for n in range(4):
        zq = 3 - n
        q = q_in[zq] * SCALE_QK
        grad = jnp.concatenate([go[zq], go[4 + zq]], axis=1)
        deltas, sums_log = [], []
        for h in range(3):
            cols = slice(256 * h, 256 * h + 256)
            rows = slice(64 * h, 64 * h + 64)
            qs[:64, cols] = q[rows]
            gs[64:, cols] = grad[rows]
            deltas.append(
                jnp.sum(grad[rows].astype(F32) * ot_ref[zq, :, cols], axis=0, keepdims=True)
            )
            sums_log.append(lse_ref[zq, :, cols])
        dq[...] = jnp.zeros_like(dq)
        first = first_ref[zq]
        hi = zq * 4 + x
        q_pos = hi * PAIR + lax.broadcasted_iota(jnp.int32, (1, PAIR), 1)

        def step(kb, carry):
            kv = kv_in[kb]
            k_pos = kb * PAIR + lax.broadcasted_iota(jnp.int32, (PAIR, PAIR), 0)
            ok = (k_pos >= first) & (k_pos <= q_pos)
            scores = [dot(kv, qs[:, 256 * h : 256 * h + 256], ((1,), (0,))) for h in range(3)]
            grad_probs = [dot(kv, gs[:, 256 * h : 256 * h + 256], ((1,), (0,))) for h in range(3)]
            grad_scores, probs = [], []
            for h in range(3):
                prob = jnp.where(ok, jnp.exp(scores[h] - sums_log[h]), 0.0)
                grad_scores.append((prob * (grad_probs[h] - deltas[h])).astype(BF))
                probs.append(prob.astype(BF))
            for h in range(3):
                cols = slice(256 * h, 256 * h + 256)
                dq[:, cols] = dq[:, cols] + dot(kv, grad_scores[h], ((0,), (0,)))
            dkv[kb] = (
                dkv[kb]
                + dot(jnp.concatenate(grad_scores, axis=1), qs[...], ((1,), (1,)))
                + dot(jnp.concatenate(probs, axis=1), gs[...], ((1,), (1,)))
            )
            return carry

        lax.fori_loop(0, hi + 1, step, 0)
        by_head = jnp.concatenate([dq[:64, 256 * h : 256 * h + 256] for h in range(3)], axis=0)
        dq_low[zq] = (by_head * SCALE_QK).astype(BF)
        away = (zq - z + 4) % 4

        @pl.when(away != 0)
        def _():
            remote(dq_low.at[zq], dq_out.at[z], q_send.at[away], q_recv.at[away], dev(y, zq, x, c)).start()

        @pl.when(away == 0)
        def _():
            pltpu.make_async_copy(dq_low.at[zq], dq_out.at[z], l_sem.at[1]).start()

        for xt in range(4):
            t = zq * 4 + xt
            dkv_low[t] = dkv[t].astype(BF)

            @pl.when(t != me)
            def _():
                remote(dkv_low.at[t], dkv_out.at[me], k_send, k_recv, dev(y, zq, xt, c)).start()

            @pl.when(t == me)
            def _():
                pltpu.make_async_copy(dkv_low.at[t], dkv_out.at[me], l_sem.at[2]).start()


    for copy in w_copies:
        copy.wait()
    for part in range(3):
        mine = spot(part, place[OUT_SUMS[part][1][0]])

        def add(p, carry):
            value = mine[p].astype(F32)
            for k in range(3):
                value = value + a_out[part, k, p].astype(F32)
            s_out[part, p] = value.astype(BF)
            return carry

        lax.fori_loop(0, 4, add, 0)
    pltpu.make_async_copy(dq_low.at[z], dq_out.at[z], l_sem.at[1]).wait()
    pltpu.make_async_copy(dkv_low.at[me], dkv_out.at[me], l_sem.at[2]).wait()
    for k in range(1, 4):
        done = remote(dq_low.at[0], dq_out.at[0], q_send.at[k], q_recv.at[k], sibling)
        done.wait_send()
        done.wait_recv()
    drain = remote(dkv_out.at[pl.ds(0, 15)], dkv_out.at[pl.ds(0, 15)], k_send, k_recv, sibling)
    drain.wait_send()
    drain.wait_recv()


def attend_back(heads, branch, own_attn, other_attn, q_in, kv_in, first, ot, lse):
    return pl.pallas_call(
        attend_back_kernel,
        out_shape=[
            jax.ShapeDtypeStruct((4, HEAD_Q, PAIR), BF),
            jax.ShapeDtypeStruct((16, PAIR, 128), BF),
            jax.ShapeDtypeStruct((3, 4, 4, 24, 256), BF),
        ],
        in_specs=[ANY] + [IN_VMEM] * 8,
        out_specs=[ANY, ANY, IN_VMEM],
        scratch_shapes=[
            pltpu.VMEM((8, HEAD_Q, ROWS), BF),
            pltpu.VMEM((ROWS, MODEL_WIDTH), BF),
            pltpu.VMEM((Q_HALF, ROWS), BF),
            pltpu.VMEM((128, 3 * PAIR), BF),
            pltpu.VMEM((128, 3 * PAIR), BF),
            pltpu.VMEM((128, 3 * PAIR), F32),
            pltpu.VMEM((16, PAIR, 128), F32),
            pltpu.VMEM((16, PAIR, 128), BF),
            pltpu.VMEM((4, HEAD_Q, PAIR), BF),
            pltpu.VMEM((4, 4, 4, 24, Q_HALF), BF),
            pltpu.VMEM((3, 3, 4, 4, 24, 256), BF),
            pltpu.SemaphoreType.DMA((3,)),
            pltpu.SemaphoreType.DMA,
            pltpu.SemaphoreType.DMA,
            pltpu.SemaphoreType.DMA((2,)),
            pltpu.SemaphoreType.DMA((2,)),
            pltpu.SemaphoreType.DMA((4,)),
            pltpu.SemaphoreType.DMA((4,)),
            pltpu.SemaphoreType.DMA,
            pltpu.SemaphoreType.DMA,
            pltpu.SemaphoreType.DMA((3, 3)),
            pltpu.SemaphoreType.DMA((3, 3)),
        ],
        compiler_params=params(4, 58 << 20),
        name="attend_back",
    )(heads, branch, own_attn, other_attn, q_in, kv_in, first, ot, lse)


def inverse_rms(values):
    return lax.rsqrt(jnp.mean(values * values, axis=-1, keepdims=True) + EPS)


def norm_backward(values, inverse, gain, grad_out):
    scaled = grad_out * gain
    return inverse * scaled - values * inverse**3 * jnp.mean(values * scaled, axis=-1, keepdims=True)


def column_sums(left, right):
    return lax.dot_general(left, right, (((0,), (0,)), ((), ())), precision=HIGH_PRECISION)


def only_column(rows, column):
    return jnp.broadcast_to((jnp.arange(EXTRA) == column).astype(F32), (rows, EXTRA))


def halves(matrix):
    return matrix.reshape(12, 2, Q_HALF).transpose(1, 0, 2)


def local(
    tokens,
    segment_ids,
    expert_ids,
    w_query,
    w_key,
    w_value,
    w_out,
    w_router,
    gain_attn,
    gain_moe,
    w_gate,
    w_up,
    w_down,
    cotangent,
):
    y, z, x, c = coords()
    width = w_gate.shape[1]
    key_value = jnp.concatenate(
        [w_key.reshape(12, 2, 4, HD), w_value.reshape(12, 2, 4, HD)], axis=3
    ).reshape(12, 2, KV_HALF)
    extra = jnp.concatenate(
        [w_router, gain_attn[:, None], gain_moe[:, None], jnp.zeros((12, EXTRA - 18), BF)], axis=1
    )
    pack = jnp.concatenate(
        [
            halves(w_query),
            key_value.transpose(1, 0, 2),
            halves(w_out.T),
            jnp.broadcast_to(extra[None], (2, 12, EXTRA)),
        ],
        axis=2,
    )
    pack = jnp.pad(pack, ((0, 0), (0, 4), (0, 0)))
    w_experts = jnp.concatenate([w_gate, w_up, w_down.T], axis=1)
    part_q, part_kv, part_out, part_extra, pair, seg_all = gather_weights(
        pack, tokens, segment_ids
    )
    pair, w_experts = lax.optimization_barrier((pair, w_experts))
    full_experts = lax.all_gather(w_experts, "dp", axis=0, tiled=True)
    full_q = part_q.reshape(MODEL_WIDTH, Q_HALF)
    full_kv = part_kv.reshape(MODEL_WIDTH, KV_HALF)
    full_extra = part_extra.reshape(MODEL_WIDTH, EXTRA)
    picks = (jnp.arange(EXTRA)[None, :] == jnp.arange(8)[:, None] + EXPERT_COUNT).astype(BF)
    gains = dot(picks, full_extra, ((1,), (1,)))
    gain_a, gain_m = gains[0:1], gains[1:2]
    router = full_extra[:, :EXPERT_COUNT]

    inputs2 = pair.reshape(PAIR, MODEL_WIDTH).astype(F32)
    inverse_a = inverse_rms(inputs2)
    normed = (inputs2 * inverse_a * gain_a).astype(BF)
    q4 = dot(full_q, normed, ((0,), (1,))).astype(BF).reshape(4, HEAD_Q, PAIR)
    keys_values = dot(normed, full_kv, ((1,), (0,))).astype(BF)
    segs = seg_all.reshape(1, 4096)
    counts = jnp.sum((segs < jnp.arange(16)[:, None]).astype(jnp.int32), axis=1)
    row_segs = lax.dynamic_index_in_dim(seg_all.reshape(4, 4, PAIR), x, 1, keepdims=False)
    first = jnp.sum(
        jnp.where(row_segs[:, :, None] == jnp.arange(16), counts, 0), axis=2
    )
    first = first.reshape(4, 1, PAIR)
    chosen = (expert_ids[:, :, None] == jnp.arange(EXPERT_COUNT, dtype=jnp.int32)).astype(F32)
    used = jnp.sum(chosen, axis=1)
    earlier = (jnp.arange(ROWS)[:, None] > jnp.arange(ROWS)[None, :]).astype(BF)
    before = dot(earlier, used.astype(BF), ((1,), (0,)))
    place = jnp.sum(chosen * before[:, None, :], axis=-1)
    slot = jnp.where(
        place < EXPERT_CAPACITY, expert_ids * SLOTS + place.astype(jnp.int32), -1
    )
    hit = (slot.T[:, :, None] == jnp.arange(EXPERT_COUNT * SLOTS, dtype=jnp.int32)).astype(F32)
    both = (hit[0] + hit[1]).astype(BF)
    blocks = (EXPERT_COUNT, SLOTS, MODEL_WIDTH)
    cot_slots = dot(both, cotangent, ((0,), (0,))).astype(BF)
    q_in, kv_in, attn, attn_t, lse, half_out, sib_out, cot_all = attend(
        q4, keys_values, part_out, cot_slots.reshape(blocks), first
    )
    half_out = half_out.reshape(MODEL_WIDTH, Q_HALF)
    sib_out = sib_out.reshape(MODEL_WIDTH, Q_HALF)
    attn = attn.reshape(2, Q_HALF, ROWS)

    own_attn = jnp.where(c == 0, attn[0], attn[1])
    other_attn = jnp.where(c == 0, attn[1], attn[0])
    inputs = tokens.astype(F32)
    middle = (
        inputs
        + dot(own_attn, half_out, ((0,), (1,)))
        + dot(other_attn, sib_out, ((0,), (1,)))
    )
    inverse_m = inverse_rms(middle)
    moe_in = (middle * inverse_m * gain_m).astype(BF)
    logits = dot(moe_in, router, ((1,), (0,)))
    picked = jnp.sum(chosen * logits[:, None, :], axis=-1)
    gates = jax.nn.softmax(picked, axis=-1)
    slot_gate = jnp.sum(hit * gates.T[:, :, None], axis=(0, 1))
    slots_in = dot(both, moe_in, ((0,), (0,))).astype(BF)
    slot_gate = jnp.broadcast_to(slot_gate.reshape(EXPERT_COUNT, SLOTS, 1), (EXPERT_COUNT, SLOTS, 128))
    out_ret, grad_ret, grad_experts = experts(
        slots_in.reshape(blocks), slot_gate, cot_all, full_experts
    )
    sum_experts = lax.psum_scatter(grad_experts, "dp", scatter_dimension=0, tiled=True)

    grad_output = cotangent.astype(F32)
    out_ret = out_ret.reshape(EXPERT_COUNT * SLOTS, MODEL_WIDTH)
    grad_ret = grad_ret.reshape(EXPERT_COUNT * SLOTS, MODEL_WIDTH)
    rows_out = [dot(hit[k].astype(BF), out_ret, ((1,), (0,))) for k in range(2)]
    block_out = (middle + gates[:, 0:1] * rows_out[0] + gates[:, 1:2] * rows_out[1]).astype(BF)
    grad_pair = jnp.stack([jnp.sum(grad_output * rows, axis=-1) for rows in rows_out], axis=-1)
    grad_pick = gates * (grad_pair - jnp.sum(gates * grad_pair, axis=-1, keepdims=True))
    grad_logits = jnp.sum(chosen * grad_pick[:, :, None], axis=1)
    grad_moe_in = dot(both, grad_ret, ((1,), (0,))) + lax.dot_general(
        grad_logits, router.astype(F32), (((1,), (1,)), ((), ())), precision=HIGH_PRECISION
    )
    g_router = column_sums(moe_in.astype(F32), jnp.pad(grad_logits, ((0, 0), (0, EXTRA - EXPERT_COUNT))))
    g_gain_m = column_sums(grad_moe_in * middle * inverse_m, only_column(ROWS, EXPERT_COUNT + 1))
    grad_middle = grad_output + norm_backward(middle, inverse_m, gain_m, grad_moe_in)
    branch = grad_middle.astype(BF)
    own_heads = dot(half_out, branch, ((0,), (1,))).astype(BF)
    other_heads = dot(sib_out, branch, ((0,), (1,))).astype(BF)
    grad_heads = jnp.stack(
        [jnp.where(c == 0, own_heads, other_heads), jnp.where(c == 0, other_heads, own_heads)]
    )
    dq_in, dkv_in, sum_out = attend_back(
        grad_heads.reshape(8, HEAD_Q, ROWS), branch, own_attn, other_attn, q_in, kv_in, first,
        attn_t, lse,
    )
    grad_tokens, r_query, r_key, r_value, r_out, r_extra = reduce_weights(
        dq_in.reshape(Q_HALF, PAIR), dkv_in, normed, g_router + g_gain_m, sum_out,
        pair.reshape(PAIR, MODEL_WIDTH), gain_a, grad_middle, full_q, full_kv,
    )
    return (
        block_out,
        grad_tokens,
        r_query,
        r_key,
        r_value,
        r_out.T,
        r_extra[:, :EXPERT_COUNT],
        r_extra[:, EXPERT_COUNT],
        r_extra[:, EXPERT_COUNT + 1],
        sum_experts[:, :width].astype(F32),
        sum_experts[:, width : 2 * width].astype(F32),
        sum_experts[:, 2 * width :].astype(F32).T,
    )


def solution(mesh):
    rows, flat, dense = P(("dp", "ctx"), None), P(("dp", "ctx")), P("dp", "ctx")
    placed = (
        rows, dense, rows, rows, rows, rows, P(None, ("dp", "ctx")), rows, flat, flat,
        dense, dense, P("ctx", "dp"), rows,
    )
    return jax.shard_map(
        local,
        mesh=mesh,
        in_specs=placed,
        out_specs=(
            rows, rows, rows, rows, rows, P(None, ("dp", "ctx")), rows, flat, flat,
            dense, dense, P("ctx", "dp"),
        ),
        check_vma=False,
    )
```

```python
import functools

import jax
import jax.numpy as jnp
from jax import lax
from jax.experimental import pallas as pl
from jax.experimental.pallas import tpu as pltpu
from jax.sharding import PartitionSpec as P

MODEL_WIDTH = 1536
HEADS = 24
KV = 8
HD = 64
EXPERT_COUNT = 16
FF = 1024
EXPERT_CAPACITY = 20
SLOTS = 24
ROWS = 128
PAIR = 256
HEAD_Q = 192
Q_HALF = 768
KV_HALF = 512
EXTRA = 128
PACK = Q_HALF + KV_HALF + EXTRA + Q_HALF

EPS = 1e-05
SCALE_QK = 0.125
NEGATIVE = -1e30
HIGH_PRECISION = lax.Precision.HIGHEST
MESH = pl.DeviceIdType.MESH
ANY = pl.BlockSpec(memory_space=pl.ANY)
IN_VMEM = pl.BlockSpec(memory_space=pltpu.VMEM)
BF = jnp.bfloat16
F32 = jnp.float32


def dot(a, b, dims):
    return lax.dot_general(a, b, (dims, ((), ())), preferred_element_type=F32)


def coords():
    i = lax.axis_index("ctx")
    return lax.axis_index("dp"), i // 8, (i // 2) % 4, i % 2


def dev(y, z, x, c):
    return (y, z * 8 + x * 2 + c)


def signal(target):
    pl.semaphore_signal(
        pltpu.get_barrier_semaphore(), inc=1, device_id=target, device_id_type=MESH
    )


def remote(src, dst, send, recv, target):
    return pltpu.make_async_remote_copy(
        src_ref=src, dst_ref=dst, send_sem=send, recv_sem=recv, device_id=target, device_id_type=MESH
    )


def params(cid, vmem=None):
    return pltpu.CompilerParams(collective_id=cid, has_side_effects=True, vmem_limit_bytes=vmem)


def axis_peer(axis, step):
    y, z, x, c = coords()
    if axis == "y":
        return dev((y + step) % 4, z, x, c)
    if axis == "z":
        return dev(y, (z + step) % 4, x, c)
    return dev(y, z, (x + step) % 4, c)


WIDTHS = (Q_HALF, KV_HALF, Q_HALF, EXTRA)
STARTS = (0, Q_HALF, Q_HALF + KV_HALF, 2 * Q_HALF + KV_HALF)
STEPS = (1, 3, 2)
FIRST_PARTS = (
    (0, 0, 512, ("x", "z", "y")),
    (1, 0, 512, ("y", "x", "z")),
    (0, 512, 256, ("z", "y", "x")),
    (3, 0, 128, ("z", "y", "x")),
)
OUT_PARTS = (
    (2, 0, 128, ("z", "x", "y")),
    (2, 128, 384, ("z", "y", "x")),
    (2, 512, 256, ("y", "x", "z")),
)
OUT_SUMS = ((0, ("x", "y", "z")), (256, ("x", "z", "y")), (512, ("z", "x", "y")))
GATHER_PARTS = FIRST_PARTS + OUT_PARTS


def slab(ref, done, y, z, x, cols):
    return ref.at[
        slice(None) if "y" in done else y,
        slice(None) if "z" in done else z,
        slice(None) if "x" in done else x,
        slice(None),
        cols,
    ]


def gather_kernel(
    w_query, w_key, w_value, w_out, extra, tokens, segs,
    o_q, o_kv, out2, out3, pair, o_normed, q4, kv2, o_first,
    pack, sib, block, w_q, w_kv, w_extra, rows, segments, normed,
    p_send, p_recv, l_sem, s_send, s_recv, sib_send, sib_recv, o_sem,
):
    y, z, x, c = coords()
    outs = (w_q, w_kv, out2, w_extra)
    me = z * 8 + x * 2 + c
    sibling = dev(y, z, x, 1 - c)

    def greet(k, carry):
        signal((y, (me + k) % 32))
        return carry

    lax.fori_loop(1, 32, greet, 0)
    for step in STEPS:
        signal(axis_peer("y", step))
    heads = []
    for h in range(KV):
        cols = slice(HD * h, HD * h + HD)
        heads += [w_key[:, cols].astype(F32), w_value[:, cols].astype(F32)]
    heads = jnp.concatenate(heads, axis=1).astype(BF)
    for k in range(2):
        parts = (
            w_query[:, Q_HALF * k : Q_HALF * k + Q_HALF],
            heads[:, KV_HALF * k : KV_HALF * k + KV_HALF],
            w_out[:, Q_HALF * k : Q_HALF * k + Q_HALF],
            extra[...],
        )
        for start, width, part in zip(STARTS, WIDTHS, parts):
            pack[k, 0:12, start : start + width] = part
            pack[k, 12:16, start : start + width] = jnp.zeros((4, width), BF)
    pl.semaphore_wait(pltpu.get_barrier_semaphore(), 34)

    first = remote(pack.at[1 - c], sib, sib_send.at[0], sib_recv.at[0], sibling)
    first.start()
    second = remote(tokens, rows.at[c], sib_send.at[1], sib_recv.at[1], sibling)
    second.start()
    own_rows = pltpu.make_async_copy(tokens, rows.at[c], l_sem.at[4])
    own_rows.start()
    own_segs = pltpu.make_async_copy(segs, segments.at[me], l_sem.at[5])
    own_segs.start()

    def spread(k, carry):
        remote(segs, segments.at[me], s_send, s_recv, (y, (me + k) % 32)).start()
        return carry

    lax.fori_loop(1, 32, spread, 0)

    first.wait()
    own = pack[c, :12].astype(F32)
    other = sib[:12].astype(F32)
    low = jnp.where(c == 0, own, other)
    high = jnp.where(c == 0, other, own)
    block[...] = jnp.concatenate([low, high], axis=0).astype(BF)

    locals_ = []
    for n in range(4):
        cols = pl.ds(STARTS[n], WIDTHS[n])
        here = pltpu.make_async_copy(block.at[:, cols], outs[n].at[y, z, x], l_sem.at[n])
        here.start()
        locals_.append(here)
    for phase in range(3):
        copies = []
        for part, (n, start, width, order) in enumerate(GATHER_PARTS if phase < 2 else FIRST_PARTS):
            for k, step in enumerate(STEPS):
                dst = slab(outs[n], order[:phase], y, z, x, pl.ds(start, width))
                src = block.at[:, pl.ds(STARTS[n] + start, width)] if phase == 0 else dst
                copy = remote(
                    src, dst, p_send.at[phase, part, k], p_recv.at[phase, part, k],
                    axis_peer(order[phase], step),
                )
                copy.start()
                copies.append(copy)
        if phase == 0:
            for here in locals_:
                here.wait()
        if phase == 2:
            own_segs.wait()
            drain = remote(
                segments.at[pl.ds(0, 31)], segments.at[pl.ds(0, 31)], s_send, s_recv, sibling
            )
            drain.wait_send()
            drain.wait_recv()
            places = segments[...].reshape(32, 128)
            for zq in range(4):
                t = (zq * 4 + x) * 2
                mine = jnp.concatenate([segments[t], segments[t + 1]], axis=1)
                begin = jnp.zeros((1, PAIR), jnp.int32)
                for u in range(15):
                    count = jnp.sum((places == u).astype(jnp.int32))
                    begin = begin + jnp.where(mine > u, count, 0)
                o_first[zq] = begin
            second.wait()
            own_rows.wait()
        for copy in copies:
            copy.wait()
    stores = [
        pltpu.make_async_copy(src, dst, o_sem.at[n])
        for n, (src, dst) in enumerate(((w_q, o_q), (w_kv, o_kv), (w_extra, out3), (rows, pair)))
    ]
    for store in stores:
        store.start()
    gain = jnp.transpose(w_extra[...].reshape(MODEL_WIDTH, EXTRA).astype(F32))[EXPERT_COUNT : EXPERT_COUNT + 1]
    for k in range(2):
        values = rows[k].astype(F32)
        normed[ROWS * k : ROWS * k + ROWS] = (values * inverse_rms(values) * gain).astype(BF)
    last = pltpu.make_async_copy(normed, o_normed, o_sem.at[4])
    last.start()
    queries = dot(w_q[...].reshape(MODEL_WIDTH, Q_HALF), normed[...], ((0,), (1,))).astype(BF)
    q4[...] = queries.reshape(4, HEAD_Q, PAIR)
    kv2[...] = dot(normed[...], w_kv[...].reshape(MODEL_WIDTH, KV_HALF), ((1,), (0,))).astype(BF)
    for store in stores:
        store.wait()
    last.wait()


def gather_weights(w_query, w_key, w_value, w_out, extra, tokens, segs):
    blocks = [(4, 4, 4, 24, width) for width in WIDTHS]
    rows = (2, ROWS, MODEL_WIDTH)
    flat = (PAIR, MODEL_WIDTH)
    return pl.pallas_call(
        gather_kernel,
        out_shape=[jax.ShapeDtypeStruct(shape, BF) for shape in (*blocks, rows, flat)]
        + [
            jax.ShapeDtypeStruct((4, HEAD_Q, PAIR), BF),
            jax.ShapeDtypeStruct((PAIR, KV_HALF), BF),
            jax.ShapeDtypeStruct((4, 1, PAIR), jnp.int32),
        ],
        in_specs=[IN_VMEM] * 5 + [ANY, ANY],
        out_specs=[ANY] * 6 + [IN_VMEM] * 3,
        scratch_shapes=[
            pltpu.VMEM((2, 16, PACK), BF),
            pltpu.VMEM((16, PACK), BF),
            pltpu.VMEM((24, PACK), BF),
            pltpu.VMEM(blocks[0], BF),
            pltpu.VMEM(blocks[1], BF),
            pltpu.VMEM(blocks[3], BF),
            pltpu.VMEM(rows, BF),
            pltpu.VMEM((32, 1, 128), jnp.int32),
            pltpu.VMEM(flat, BF),
            pltpu.SemaphoreType.DMA((3, 7, 3)),
            pltpu.SemaphoreType.DMA((3, 7, 3)),
            pltpu.SemaphoreType.DMA((6,)),
            pltpu.SemaphoreType.DMA,
            pltpu.SemaphoreType.DMA,
            pltpu.SemaphoreType.DMA((2,)),
            pltpu.SemaphoreType.DMA((2,)),
            pltpu.SemaphoreType.DMA((5,)),
        ],
        compiler_params=params(1, 60 << 20),
        name="gather_weights",
    )(w_query, w_key, w_value, w_out, extra, tokens, segs)


def offset(k):
    dz = (k % 8) // 2
    return dz, 2 * (k % 2) + (dz + k // 8) % 2


def chip_to(k):
    y, z, x, c = coords()
    dz, dx = offset(k)
    return (z + dz) % 4, (x + dx) % 4


def chip_from(k):
    y, z, x, c = coords()
    dz, dx = offset(k)
    return (z + 4 - dz) % 4, (x + 4 - dx) % 4


def slot_block(k, core):
    return (k // 8) * 16 + core * 8 + k % 8


def plane_greet(y, me, c, sibling):
    def greet(k, carry):
        t = (me + k) % 16
        signal(dev(y, t // 4, t % 4, c))
        return carry

    lax.fori_loop(1, 16, greet, 0)
    if sibling is not None:
        signal(sibling)
        pl.semaphore_wait(pltpu.get_barrier_semaphore(), 16)
    else:
        pl.semaphore_wait(pltpu.get_barrier_semaphore(), 15)


KEYS = 1024


def attend_kernel(
    q4, kv2, half_in, cots, first_ref, q_in, kv_in, attn, ot_ref, lse_ref, half, half_sib, c_all,
    qs, acc, o_buf,
    l_sem, q_send, q_recv, k_send, k_recv, w_send, w_recv, sib_send, sib_recv,
    c_send, c_recv, f_send, f_recv, o_send, o_recv,
):
    y, z, x, c = coords()
    me = z * 4 + x
    sibling = dev(y, z, x, 1 - c)

    wide_greet()

    q_copies = []
    for n, step in enumerate(STEPS):
        to = (z + step) % 4
        copy = remote(q4.at[to], q_in.at[z], q_send.at[n], q_recv.at[n], dev(y, to, x, c))
        copy.start()
        q_copies.append(copy)

    def head(index):
        return kv2.at[:, pl.ds(pl.multiple_of(index * 128, 128), 128)]

    def send_kv(k, carry):
        t = (me + k) % 16
        remote(head(t // 4), kv_in.at[me], k_send, k_recv, dev(y, t // 4, t % 4, c)).start()
        return carry

    lax.fori_loop(1, 16, send_kv, 0)
    here = [
        pltpu.make_async_copy(q4.at[z], q_in.at[z], l_sem.at[0]),
        pltpu.make_async_copy(head(z), kv_in.at[me], l_sem.at[1]),
    ]
    for copy in here:
        copy.start()
    for copy in here:
        copy.wait()
    for copy in q_copies:
        copy.wait()
    drain = remote(kv_in.at[pl.ds(0, 15)], kv_in.at[pl.ds(0, 15)], k_send, k_recv, sibling)
    drain.wait_send()
    drain.wait_recv()

    w_copies = [[], [], []]
    for part, (n, start, width, order) in enumerate(OUT_PARTS):
        spot = slab(half, order[:2], y, z, x, pl.ds(start, width))
        for k, step in enumerate(STEPS):
            copy = remote(
                spot, spot, w_send.at[part, k], w_recv.at[part, k], axis_peer(order[2], step)
            )
            copy.start()
            w_copies[part].append(copy)

    def cots_copy(k):
        tz, tx = chip_to(k)
        return remote(
            cots.at[tz * 4 + tx], c_all.at[slot_block(k, c)], c_send.at[k], c_recv.at[k], dev(y, tz, tx, c)
        )

    def send_cots(k, carry):
        cots_copy(k).start()
        return carry

    lax.fori_loop(1, 16, send_cots, 0)
    own_cots = pltpu.make_async_copy(cots.at[me], c_all.at[slot_block(0, c)], l_sem.at[2])
    own_cots.start()
    remote(cots.at[me], c_all.at[slot_block(0, c)], f_send, f_recv, sibling).start()

    def forward_cots(k, carry):
        arrived = cots_copy(k)
        arrived.wait_recv()
        remote(c_all.at[slot_block(k, c)], c_all.at[slot_block(k, c)], f_send, f_recv, sibling).start()
        arrived.wait_send()
        return carry

    def swap(part):
        start, width = OUT_PARTS[part][1:3]
        cols = half.at[:, :, :, :, pl.ds(start, width)]
        there = half_sib.at[:, :, :, :, pl.ds(start, width)]
        return remote(cols, there, sib_send.at[part], sib_recv.at[part], sibling)

    j = c * 4 + z
    qs[64:] = jnp.zeros((64, 3 * PAIR), BF)
    returns = []
    for n in range(4):
        zq = (z + n + 1) % 4
        q = q_in[zq] * SCALE_QK
        for h in range(3):
            qs[:64, 256 * h : 256 * h + 256] = q[64 * h : 64 * h + 64]
        acc[...] = jnp.zeros_like(acc)
        first = first_ref[zq]
        q_pos = (zq * 4 + x) * PAIR + lax.broadcasted_iota(jnp.int32, (1, PAIR), 1)

        def step(kb, stats):
            kv = kv_in[pl.ds(kb * (KEYS // PAIR), KEYS // PAIR)].reshape(KEYS, 128)
            k_pos = kb * KEYS + lax.broadcasted_iota(jnp.int32, (KEYS, PAIR), 0)
            ok = (k_pos >= first) & (k_pos <= q_pos)
            scores = [dot(kv, qs[:, 256 * h : 256 * h + 256], ((1,), (0,))) for h in range(3)]
            later, probs, shrinks = [], [], []
            for h in range(3):
                top, tot = stats[h]
                masked = jnp.where(ok, scores[h], NEGATIVE)
                new = jnp.maximum(top, jnp.max(masked, axis=0, keepdims=True))
                prob = jnp.exp(masked - new)
                shrink = jnp.exp(top - new)
                later.append((new, tot * shrink + jnp.sum(prob, axis=0, keepdims=True)))
                probs.append(prob.astype(BF))
                shrinks.append(shrink)
            for h in range(3):
                cols = slice(256 * h, 256 * h + 256)
                acc[:, cols] = acc[:, cols] * shrinks[h] + dot(kv, probs[h], ((0,), (0,)))
            return tuple(later)

        none = (jnp.full((1, PAIR), NEGATIVE, F32), jnp.zeros((1, PAIR), F32))
        stats = lax.fori_loop(0, zq + 1, step, (none, none, none))
        heads = []
        for h in range(3):
            cols = slice(256 * h, 256 * h + 256)
            mixed = acc[64:, cols] / stats[h][1]
            ot_ref[zq, :, cols] = mixed
            lse_ref[zq, :, cols] = stats[h][0] + jnp.log(stats[h][1])
            heads.append(mixed)
        heads = jnp.concatenate(heads, axis=0).astype(BF)
        o_buf[n, 0] = heads[:, :ROWS]
        o_buf[n, 1] = heads[:, ROWS:]
        for d in range(2):
            core = c if d == 0 else 1 - c
            if n == 3 and d == 0:
                back = pltpu.make_async_copy(o_buf.at[n, core], attn.at[j], l_sem.at[3])
            else:
                back = remote(
                    o_buf.at[n, core], attn.at[j], o_send.at[n, d], o_recv.at[n, d], dev(y, zq, x, core)
                )
            back.start()
            returns.append(back)
    for part in range(3):
        for copy in w_copies[part]:
            copy.wait()
        swap(part).start()
        if part == 0:
            lax.fori_loop(1, 16, forward_cots, 0)
    own_cots.wait()
    mine = c_all.at[pl.ds(c * 16, 16)]
    drain = remote(mine, mine, f_send, f_recv, sibling)
    drain.wait_send()
    drain.wait_recv()
    for part in range(3):
        swap(part).wait()
    for back in returns:
        back.wait()


def attend(q4, kv2, half, cots, first):
    blocks = jax.ShapeDtypeStruct((4, 4, 4, 24, Q_HALF), BF)
    return pl.pallas_call(
        attend_kernel,
        out_shape=[
            jax.ShapeDtypeStruct((4, HEAD_Q, PAIR), BF),
            jax.ShapeDtypeStruct((16, PAIR, 128), BF),
            jax.ShapeDtypeStruct((8, HEAD_Q, ROWS), BF),
            jax.ShapeDtypeStruct((4, HD, 3 * PAIR), F32),
            jax.ShapeDtypeStruct((4, 1, 3 * PAIR), F32),
            blocks,
            blocks,
            jax.ShapeDtypeStruct((32, SLOTS, MODEL_WIDTH), BF),
        ],
        in_specs=[ANY, ANY, ANY, ANY, IN_VMEM],
        out_specs=[IN_VMEM, IN_VMEM, ANY, IN_VMEM, IN_VMEM, ANY, ANY, ANY],
        input_output_aliases={2: 5},
        scratch_shapes=[
            pltpu.VMEM((128, 3 * PAIR), BF),
            pltpu.VMEM((128, 3 * PAIR), F32),
            pltpu.VMEM((4, 2, HEAD_Q, ROWS), BF),
            pltpu.SemaphoreType.DMA((4,)),
            pltpu.SemaphoreType.DMA((3,)),
            pltpu.SemaphoreType.DMA((3,)),
            pltpu.SemaphoreType.DMA,
            pltpu.SemaphoreType.DMA,
            pltpu.SemaphoreType.DMA((3, 3)),
            pltpu.SemaphoreType.DMA((3, 3)),
            pltpu.SemaphoreType.DMA((3,)),
            pltpu.SemaphoreType.DMA((3,)),
            pltpu.SemaphoreType.DMA((16,)),
            pltpu.SemaphoreType.DMA((16,)),
            pltpu.SemaphoreType.DMA,
            pltpu.SemaphoreType.DMA,
            pltpu.SemaphoreType.DMA((4, 2)),
            pltpu.SemaphoreType.DMA((4, 2)),
        ],
        compiler_params=params(2, 60 << 20),
        name="attend",
    )(q4, kv2, half, cots, first)


def flat_rows(blocks):
    return blocks.reshape(blocks.shape[0] * SLOTS, blocks.shape[2])


def experts_kernel(
    xs, gates, cots, weights, out_ret, grad_ret, d_all,
    x_all, t_all, g_all, w_all, gate_v, up_v, hidden, g_both, part_o, part_g, sib_o, sib_g,
    v_all,
    w_sem, l_sem, send, recv, f_send, f_recv, s_send, s_recv, r_send, r_recv, o_sem,
):
    y, z, x, c = coords()
    me = z * 4 + x
    width = hidden.shape[1]
    sibling = dev(y, z, x, 1 - c)
    plane_greet(y, me, c, sibling)
    loads = [
        pltpu.make_async_copy(src, dst, w_sem.at[n])
        for n, (src, dst) in enumerate(((weights, w_all), (cots, g_all)))
    ]
    for load in loads:
        load.start()
    arrays = ((xs, x_all), (gates, t_all))

    def arriving(a, k):
        src, dst = arrays[a]
        tz, tx = chip_to(k)
        return remote(
            src.at[tz * 4 + tx], dst.at[slot_block(k, c)], send.at[a, k], recv.at[a, k], dev(y, tz, tx, c)
        )

    def steps_of(part):
        return (1, 8) if part == 0 else (8, 16)

    def scatter(a, part):
        def push(k, carry):
            arriving(a, k).start()
            return carry

        lax.fori_loop(*steps_of(part), push, 0)
        if part == 0:
            src, dst = arrays[a]
            pltpu.make_async_copy(src.at[me], dst.at[slot_block(0, c)], l_sem.at[a]).start()
            remote(src.at[me], dst.at[slot_block(0, c)], f_send.at[a, 0], f_recv.at[a, 0], sibling).start()

    def hand_over(a, part):
        src, dst = arrays[a]

        def forward(k, carry):
            arrived = arriving(a, k)
            arrived.wait_recv()
            block = dst.at[slot_block(k, c)]
            remote(block, block, f_send.at[a, part], f_recv.at[a, part], sibling).start()
            arrived.wait_send()
            return carry

        lax.fori_loop(*steps_of(part), forward, 0)

    def settle(a, part):
        src, dst = arrays[a]
        if part == 0:
            pltpu.make_async_copy(src.at[me], dst.at[slot_block(0, c)], l_sem.at[a]).wait()
        some = dst.at[pl.ds(0, 8)]
        drain = remote(some, some, f_send.at[a, part], f_recv.at[a, part], sibling)
        drain.wait_send()
        drain.wait_recv()

    def swap(mine, sib, a, part):
        return remote(
            mine.at[pl.ds(part * 16 + (1 - c) * 8, 8)], sib.at[pl.ds(part * 8, 8)],
            s_send.at[a, part], s_recv.at[a, part], sibling,
        )

    def give(mine, sib, ret, a, part):
        def add(k):
            block = slot_block(k, c)
            mine[block] = (mine[block].astype(F32) + sib[k].astype(F32)).astype(BF)
            return mine.at[block]

        def push(k, carry):
            sz, sx = chip_from(k)
            remote(add(k), ret.at[me], r_send.at[a], r_recv.at[a], dev(y, sz, sx, c)).start()
            return carry

        lax.fori_loop(*steps_of(part), push, 0)
        if part == 0:
            pltpu.make_async_copy(add(0), ret.at[me], l_sem.at[2 + a]).start()

    def given(mine, ret, a):
        pltpu.make_async_copy(mine.at[slot_block(0, c)], ret.at[me], l_sem.at[2 + a]).wait()
        drain = remote(ret.at[pl.ds(0, 15)], ret.at[pl.ds(0, 15)], r_send.at[a], r_recv.at[a], sibling)
        drain.wait_send()
        drain.wait_recv()

    half = 16 * SLOTS

    def forward_pass(part):
        blocks, rows = pl.ds(part * 16, 16), slice(part * half, part * half + half)
        both = dot(flat_rows(x_all[blocks]), w_all[:, : 2 * width], ((1,), (0,)))
        gate_val, up_val = both[:, :width], both[:, width:]
        gate_v[rows] = gate_val
        up_v[rows] = up_val
        low = (gate_val * jax.nn.sigmoid(gate_val) * up_val).astype(BF)
        hidden[rows] = low
        out = dot(low, w_all[:, 2 * width :], ((1,), (1,))).astype(BF)
        part_o[blocks] = out.reshape(16, SLOTS, MODEL_WIDTH)
        swap(part_o, sib_o, 0, part).start()

    def backward_pass(part):
        blocks, rows = pl.ds(part * 16, 16), slice(part * half, part * half + half)
        scale = jnp.concatenate([flat_rows(t_all[blocks])] * (MODEL_WIDTH // 128), axis=1)
        grad_expert = (flat_rows(g_all[blocks]).astype(F32) * scale).astype(BF)
        g_all[blocks] = grad_expert.reshape(16, SLOTS, MODEL_WIDTH)
        grad_hidden = dot(grad_expert, w_all[:, 2 * width :], ((1,), (0,)))
        gate_val = gate_v[rows]
        up_val = up_v[rows]
        sig = jax.nn.sigmoid(gate_val)
        grad_gate = (grad_hidden * up_val * sig * (1.0 + gate_val * (1.0 - sig))).astype(BF)
        grad_up = (grad_hidden * gate_val * sig).astype(BF)
        grads = jnp.concatenate([grad_gate, grad_up], axis=1)
        g_both[rows] = grads
        grad_rows = dot(grads, w_all[:, : 2 * width], ((1,), (1,))).astype(BF)
        part_g[blocks] = grad_rows.reshape(16, SLOTS, MODEL_WIDTH)
        swap(part_g, sib_g, 1, part).start()

    scatter(0, 0)
    scatter(1, 0)
    scatter(0, 1)
    scatter(1, 1)
    for load in loads:
        load.wait()
    hand_over(0, 0)
    settle(0, 0)
    forward_pass(0)
    hand_over(0, 1)
    swap(part_o, sib_o, 0, 0).wait()
    give(part_o, sib_o, out_ret, 0, 0)
    settle(0, 1)
    forward_pass(1)
    hand_over(1, 0)
    hand_over(1, 1)
    settle(1, 0)
    swap(part_o, sib_o, 0, 1).wait()
    give(part_o, sib_o, out_ret, 0, 1)
    backward_pass(0)
    settle(1, 1)
    swap(part_g, sib_g, 1, 0).wait()
    give(part_g, sib_g, grad_ret, 1, 0)
    backward_pass(1)
    swap(part_g, sib_g, 1, 1).wait()
    give(part_g, sib_g, grad_ret, 1, 1)

    def weight_grads(j, carry):
        cols = pl.ds(pl.multiple_of(j * 256, 256), 256)
        v_all[cols, : 2 * width] = dot(flat_rows(x_all[:, :, cols]), g_both[...], ((0,), (0,))).astype(BF)
        v_all[cols, 2 * width :] = dot(flat_rows(g_all[:, :, cols]), hidden[...], ((0,), (0,))).astype(BF)
        return carry

    lax.fori_loop(0, MODEL_WIDTH // 256, weight_grads, 0)
    store = pltpu.make_async_copy(v_all, d_all, o_sem)
    store.start()
    store.wait()
    given(part_o, out_ret, 0)
    given(part_g, grad_ret, 1)


def experts(xs, gates, cots, weights):
    rows = 32 * SLOTS
    width = weights.shape[1] // 3
    back = jax.ShapeDtypeStruct((16, SLOTS, MODEL_WIDTH), BF)
    return pl.pallas_call(
        experts_kernel,
        out_shape=[back, back, jax.ShapeDtypeStruct(weights.shape, BF)],
        in_specs=[ANY] * 4,
        out_specs=[ANY] * 3,
        scratch_shapes=[
            pltpu.VMEM((32, SLOTS, MODEL_WIDTH), BF),
            pltpu.VMEM((32, SLOTS, 128), F32),
            pltpu.VMEM((32, SLOTS, MODEL_WIDTH), BF),
            pltpu.VMEM(weights.shape, BF),
            pltpu.VMEM((rows, width), F32),
            pltpu.VMEM((rows, width), F32),
            pltpu.VMEM((rows, width), BF),
            pltpu.VMEM((rows, 2 * width), BF),
            pltpu.VMEM((32, SLOTS, MODEL_WIDTH), BF),
            pltpu.VMEM((32, SLOTS, MODEL_WIDTH), BF),
            pltpu.VMEM((16, SLOTS, MODEL_WIDTH), BF),
            pltpu.VMEM((16, SLOTS, MODEL_WIDTH), BF),
            pltpu.VMEM(weights.shape, BF),
            pltpu.SemaphoreType.DMA((2,)),
            pltpu.SemaphoreType.DMA((4,)),
            pltpu.SemaphoreType.DMA((2, 16)),
            pltpu.SemaphoreType.DMA((2, 16)),
            pltpu.SemaphoreType.DMA((2, 2)),
            pltpu.SemaphoreType.DMA((2, 2)),
            pltpu.SemaphoreType.DMA((2, 2)),
            pltpu.SemaphoreType.DMA((2, 2)),
            pltpu.SemaphoreType.DMA((2,)),
            pltpu.SemaphoreType.DMA((2,)),
            pltpu.SemaphoreType.DMA,
        ],
        compiler_params=params(6, 60 << 20),
        name="experts",
    )(xs, gates, cots, weights)


SUMS = tuple((n, start, width, order[::-1]) for n, start, width, order in FIRST_PARTS) + tuple(
    (2, start, 256, order) for start, order in OUT_SUMS
)
LATE = len(FIRST_PARTS)


def reduce_kernel(
    gq_t, dkv, normed, g_moe, s_out, pair, gain, grad_middle, w_q, w_kv,
    o_tokens, o_q, o_k, o_v, o_out, o_extra,
    v_q, v_kv, v_extra, wq, wkv, gkv, mine_part, give_part, sib_part, both, total, give, *rest,
):
    parts = len(SUMS)
    first_in, rest = rest[:LATE], rest[LATE:]
    arrive = [list(first_in) + [None] * 3, rest[:parts], rest[parts : 2 * parts]]
    rest = rest[2 * parts :]
    held = [None, list(rest[:LATE]) + [s_out.at[k] for k in range(3)], rest[LATE : LATE + parts]]
    l_sem, send, recv, sib_send, sib_recv = rest[LATE + parts :]
    grads = (v_q, v_kv, None, v_extra)
    y, z, x, c = coords()
    place = {"y": y, "z": z, "x": x}
    sibling = dev(y, z, x, 1 - c)
    loads = [pltpu.make_async_copy(w_q, wq, l_sem.at[0]), pltpu.make_async_copy(w_kv, wkv, l_sem.at[1])]
    for load in loads:
        load.start()
    for axis in ("x", "y", "z"):
        for step in STEPS:
            signal(axis_peer(axis, step))
    signal(sibling)
    pl.semaphore_wait(pltpu.get_barrier_semaphore(), 10)

    def at(phase, part, index):
        n, start, width, order = SUMS[part]
        spot = [
            index if axis == order[phase] else slice(None)
            for axis in ("y", "z", "x")
            if axis not in order[:phase]
        ]
        if phase == 0:
            return grads[n].at[tuple(spot) + (slice(None), pl.ds(start, width))]
        return held[phase][part].at[tuple(spot)]

    def copies_of(phase, part):
        axis = SUMS[part][3][phase]
        return [
            remote(
                at(phase, part, (place[axis] + step) % 4), arrive[phase][part].at[n],
                send.at[phase, part, n], recv.at[phase, part, n], axis_peer(axis, step),
            )
            for n, step in enumerate(STEPS)
        ]

    def begin(phase, part):
        for copy in copies_of(phase, part):
            copy.start()

    def finish(phase, part):
        for copy in copies_of(phase, part):
            copy.wait()
        array, start, width, order = SUMS[part]
        mine = at(phase, part, place[order[phase]])
        got = arrive[phase][part]
        if phase < 2:

            def add(p, carry):
                value = mine[p].astype(F32)
                for n in range(3):
                    value = value + got[n, p].astype(F32)
                held[phase + 1][part][p] = value.astype(BF)
                return carry

            lax.fori_loop(0, 4, add, 0)
        else:
            value = mine[...].astype(F32)
            for n in range(3):
                value = value + got[n].astype(F32)
            total[:, STARTS[array] + start : STARTS[array] + start + width] = value

    for part in range(LATE, parts):
        begin(1, part)
    for h in range(4):
        value = dkv[4 * h].astype(F32)
        for n in range(1, 4):
            value = value + dkv[4 * h + n].astype(F32)
        gkv[:, 128 * h : 128 * h + 128] = value.astype(BF)
    for n in range(4):
        left = normed[:, 384 * n : 384 * n + 384]
        v_q[n] = dot(left, gq_t[...], ((0,), (1,))).astype(BF).reshape(4, 4, 24, Q_HALF)
        v_kv[n] = dot(left, gkv[...], ((0,), (0,))).astype(BF).reshape(4, 4, 24, KV_HALF)
    for part in range(3):
        begin(0, part)

    for load in loads:
        load.wait()
    gain_sum = jnp.zeros((1, MODEL_WIDTH), F32)
    for n in range(2):
        core = 1 - c if n == 0 else c
        rows = pl.ds(pl.multiple_of(core * ROWS, ROWS), ROWS)
        part = dot(gq_t[:, rows], wq[...], ((0,), (1,))) + dot(gkv[rows], wkv[...], ((1,), (1,)))
        values = pair[rows].astype(F32)
        gain_sum = gain_sum + jnp.sum(part * values * inverse_rms(values), axis=0, keepdims=True)
        if n == 0:
            give_part[...] = part
            remote(give_part, sib_part, sib_send.at[0], sib_recv.at[0], sibling).start()
        else:
            mine_part[...] = part
    column = jnp.transpose(jnp.broadcast_to(gain_sum, (EXTRA, MODEL_WIDTH)))
    lane = lax.broadcasted_iota(jnp.int32, (MODEL_WIDTH, EXTRA), 1)
    extra = g_moe[...] + jnp.where(lane == EXPERT_COUNT, column, 0.0)
    v_extra[...] = extra.astype(BF).reshape(4, 4, 4, 24, EXTRA)
    begin(0, 3)
    remote(give_part, sib_part, sib_send.at[0], sib_recv.at[0], sibling).wait()
    rows = pl.ds(pl.multiple_of(c * ROWS, ROWS), ROWS)
    values = pair[rows].astype(F32)
    o_tokens[...] = grad_middle[...] + norm_backward(
        values, inverse_rms(values), gain[...], mine_part[...] + sib_part[...]
    )

    for part in range(LATE, parts):
        finish(1, part)
        begin(2, part)
    for phase in range(3):
        for part in range(LATE):
            finish(phase, part)
            if phase < 2:
                begin(phase + 1, part)
    for part in range(LATE, parts):
        finish(2, part)
    low, high = total[0:12], total[12:24]
    both[c, 0:12] = jnp.where(c == 0, low, high)
    give[0:12] = jnp.where(c == 0, high, low)
    give[12:16] = jnp.zeros((4, PACK), F32)
    last = remote(give, both.at[c], sib_send.at[1], sib_recv.at[1], sibling)
    last.start()
    last.wait()
    keys, values = [], []
    for k in range(2):
        o_q[:, Q_HALF * k : Q_HALF * k + Q_HALF] = both[k, 0:12, :Q_HALF]
        o_out[:, Q_HALF * k : Q_HALF * k + Q_HALF] = both[k, 0:12, STARTS[2] : STARTS[3]]
        for h in range(4):
            first = STARTS[1] + 128 * h
            keys.append(both[k, 0:12, first : first + HD])
            values.append(both[k, 0:12, first + HD : first + 2 * HD])
    o_k[...] = jnp.concatenate(keys, axis=1)
    o_v[...] = jnp.concatenate(values, axis=1)
    o_extra[...] = both[0, 0:12, STARTS[3] :] + both[1, 0:12, STARTS[3] :]


def reduce_weights(gq_t, dkv, normed, g_moe, s_out, pair, gain, grad_middle, w_q, w_kv):
    widths = [part[2] for part in SUMS]
    full = lambda width: pltpu.VMEM((4, 4, 4, 24, width), BF)
    rows = pltpu.VMEM((ROWS, MODEL_WIDTH), F32)
    scratch = (
        [full(Q_HALF), full(KV_HALF), full(EXTRA)]
        + [pltpu.VMEM((MODEL_WIDTH, Q_HALF), BF), pltpu.VMEM((MODEL_WIDTH, KV_HALF), BF)]
        + [pltpu.VMEM((PAIR, KV_HALF), BF), rows, rows, rows]
        + [pltpu.VMEM((2, 16, PACK), F32), pltpu.VMEM((24, PACK), F32), pltpu.VMEM((16, PACK), F32)]
        + [pltpu.VMEM((3, 4, 4, 24, w), BF) for w in widths[:LATE]]
        + [pltpu.VMEM((3, 4, 24, w), BF) for w in widths]
        + [pltpu.VMEM((3, 24, w), BF) for w in widths]
        + [pltpu.VMEM((4, 4, 24, w), BF) for w in widths[:LATE]]
        + [pltpu.VMEM((4, 24, w), BF) for w in widths]
    )
    sems = (3, len(SUMS), 3)
    shapes = ((ROWS, MODEL_WIDTH), (12, MODEL_WIDTH), (12, KV * HD), (12, KV * HD), (12, MODEL_WIDTH), (12, EXTRA))
    return pl.pallas_call(
        reduce_kernel,
        out_shape=[jax.ShapeDtypeStruct(shape, F32) for shape in shapes],
        in_specs=[IN_VMEM] * 8 + [ANY] * 2,
        out_specs=[IN_VMEM] * 6,
        scratch_shapes=scratch
        + [
            pltpu.SemaphoreType.DMA((2,)),
            pltpu.SemaphoreType.DMA(sems),
            pltpu.SemaphoreType.DMA(sems),
            pltpu.SemaphoreType.DMA((2,)),
            pltpu.SemaphoreType.DMA((2,)),
        ],
        compiler_params=params(8, 60 << 20),
        name="reduce_weights",
    )(gq_t, dkv, normed, g_moe, s_out, pair, gain, grad_middle, w_q, w_kv)


def wide_greet():
    y, z, x, c = coords()
    me = z * 4 + x

    def greet(k, carry):
        t = (me + k) % 16
        signal(dev(y, t // 4, t % 4, c))
        return carry

    lax.fori_loop(1, 16, greet, 0)
    for step in STEPS:
        signal(axis_peer("y", step))
        signal(dev(y, (z + step) % 4, x, 1 - c))
    signal(dev(y, z, x, 1 - c))
    pl.semaphore_wait(pltpu.get_barrier_semaphore(), 22)


def attend_back_kernel(
    heads, branch, own_attn, other_attn, q_in, kv_in, first_ref, ot_ref, lse_ref,
    dq_out, dkv_out, s_out,
    go, branch_sib, attn_sib, qs, gs, dq, dkv, dkv_low, dq_low,
    g_out, a_out,
    l_sem, h_send, h_recv, sib_send, sib_recv, q_send, q_recv, k_send, k_recv,
    w_send, w_recv,
):
    y, z, x, c = coords()
    me = z * 4 + x
    j = c * 4 + z
    sibling = dev(y, z, x, 1 - c)
    place = {"y": y, "z": z, "x": x}
    wide_greet()

    def push(k, carry):
        t = (j + k) % 8
        remote(heads.at[t], go.at[j], h_send, h_recv, dev(y, t % 4, x, t // 4)).start()
        return carry

    lax.fori_loop(1, 8, push, 0)
    one = remote(branch, branch_sib, sib_send.at[0], sib_recv.at[0], sibling)
    one.start()
    two = remote(other_attn, attn_sib, sib_send.at[1], sib_recv.at[1], sibling)
    two.start()
    here = pltpu.make_async_copy(heads.at[j], go.at[j], l_sem.at[0])
    here.start()
    here.wait()
    drain = remote(go.at[pl.ds(0, 7)], go.at[pl.ds(0, 7)], h_send, h_recv, sibling)
    drain.wait_send()
    drain.wait_recv()
    one.wait()
    two.wait()

    rows_b = jnp.concatenate([branch[...], branch_sib[...]], axis=0)
    rows_a = jnp.concatenate([own_attn[...], attn_sib[...]], axis=1)
    for n in range(4):
        part = dot(rows_b[:, 384 * n : 384 * n + 384], rows_a, ((0,), (1,)))
        g_out[n] = part.astype(BF).reshape(4, 4, 24, Q_HALF)

    def spot(part, index):
        start, order = OUT_SUMS[part]
        cut = [index if axis == order[0] else slice(None) for axis in ("y", "z", "x")]
        return g_out.at[tuple(cut) + (slice(None), pl.ds(start, 256))]

    w_copies = []
    for part in range(3):
        axis = OUT_SUMS[part][1][0]
        for n, step in enumerate(STEPS):
            copy = remote(
                spot(part, (place[axis] + step) % 4), a_out.at[part, n],
                w_send.at[part, n], w_recv.at[part, n], axis_peer(axis, step),
            )
            copy.start()
            w_copies.append(copy)

    dkv[...] = jnp.zeros_like(dkv)
    qs[64:] = jnp.zeros((64, 3 * PAIR), BF)
    gs[:64] = jnp.zeros((64, 3 * PAIR), BF)
    for n in range(4):
        zq = 3 - n
        q = q_in[zq] * SCALE_QK
        grad = jnp.concatenate([go[zq], go[4 + zq]], axis=1)
        deltas, sums_log = [], []
        for h in range(3):
            cols = slice(256 * h, 256 * h + 256)
            rows = slice(64 * h, 64 * h + 64)
            qs[:64, cols] = q[rows]
            gs[64:, cols] = grad[rows]
            deltas.append(
                jnp.sum(grad[rows].astype(F32) * ot_ref[zq, :, cols], axis=0, keepdims=True)
            )
            sums_log.append(lse_ref[zq, :, cols])
        dq[...] = jnp.zeros_like(dq)
        first = first_ref[zq]
        hi = zq * 4 + x
        q_pos = hi * PAIR + lax.broadcasted_iota(jnp.int32, (1, PAIR), 1)

        def step(kb, carry):
            kv = kv_in[kb]
            k_pos = kb * PAIR + lax.broadcasted_iota(jnp.int32, (PAIR, PAIR), 0)
            ok = (k_pos >= first) & (k_pos <= q_pos)
            scores = [dot(kv, qs[:, 256 * h : 256 * h + 256], ((1,), (0,))) for h in range(3)]
            grad_probs = [dot(kv, gs[:, 256 * h : 256 * h + 256], ((1,), (0,))) for h in range(3)]
            grad_scores, probs = [], []
            for h in range(3):
                prob = jnp.where(ok, jnp.exp(scores[h] - sums_log[h]), 0.0)
                grad_scores.append((prob * (grad_probs[h] - deltas[h])).astype(BF))
                probs.append(prob.astype(BF))
            for h in range(3):
                cols = slice(256 * h, 256 * h + 256)
                dq[:, cols] = dq[:, cols] + dot(kv, grad_scores[h], ((0,), (0,)))
            dkv[kb] = (
                dkv[kb]
                + dot(jnp.concatenate(grad_scores, axis=1), qs[...], ((1,), (1,)))
                + dot(jnp.concatenate(probs, axis=1), gs[...], ((1,), (1,)))
            )
            return carry

        lax.fori_loop(0, hi + 1, step, 0)
        by_head = jnp.concatenate([dq[:64, 256 * h : 256 * h + 256] for h in range(3)], axis=0)
        dq_low[zq] = (by_head * SCALE_QK).astype(BF)
        away = (zq - z + 4) % 4

        @pl.when(away != 0)
        def _():
            remote(dq_low.at[zq], dq_out.at[z], q_send.at[away], q_recv.at[away], dev(y, zq, x, c)).start()

        @pl.when(away == 0)
        def _():
            pltpu.make_async_copy(dq_low.at[zq], dq_out.at[z], l_sem.at[1]).start()

        for xt in range(4):
            t = zq * 4 + xt
            dkv_low[t] = dkv[t].astype(BF)

            @pl.when(t != me)
            def _():
                remote(dkv_low.at[t], dkv_out.at[me], k_send, k_recv, dev(y, zq, xt, c)).start()

            @pl.when(t == me)
            def _():
                pltpu.make_async_copy(dkv_low.at[t], dkv_out.at[me], l_sem.at[2]).start()


    for copy in w_copies:
        copy.wait()
    for part in range(3):
        mine = spot(part, place[OUT_SUMS[part][1][0]])

        def add(p, carry):
            value = mine[p].astype(F32)
            for k in range(3):
                value = value + a_out[part, k, p].astype(F32)
            s_out[part, p] = value.astype(BF)
            return carry

        lax.fori_loop(0, 4, add, 0)
    pltpu.make_async_copy(dq_low.at[z], dq_out.at[z], l_sem.at[1]).wait()
    pltpu.make_async_copy(dkv_low.at[me], dkv_out.at[me], l_sem.at[2]).wait()
    for k in range(1, 4):
        done = remote(dq_low.at[0], dq_out.at[0], q_send.at[k], q_recv.at[k], sibling)
        done.wait_send()
        done.wait_recv()
    drain = remote(dkv_out.at[pl.ds(0, 15)], dkv_out.at[pl.ds(0, 15)], k_send, k_recv, sibling)
    drain.wait_send()
    drain.wait_recv()


def attend_back(heads, branch, own_attn, other_attn, q_in, kv_in, first, ot, lse):
    return pl.pallas_call(
        attend_back_kernel,
        out_shape=[
            jax.ShapeDtypeStruct((4, HEAD_Q, PAIR), BF),
            jax.ShapeDtypeStruct((16, PAIR, 128), BF),
            jax.ShapeDtypeStruct((3, 4, 4, 24, 256), BF),
        ],
        in_specs=[ANY] + [IN_VMEM] * 8,
        out_specs=[ANY, ANY, IN_VMEM],
        scratch_shapes=[
            pltpu.VMEM((8, HEAD_Q, ROWS), BF),
            pltpu.VMEM((ROWS, MODEL_WIDTH), BF),
            pltpu.VMEM((Q_HALF, ROWS), BF),
            pltpu.VMEM((128, 3 * PAIR), BF),
            pltpu.VMEM((128, 3 * PAIR), BF),
            pltpu.VMEM((128, 3 * PAIR), F32),
            pltpu.VMEM((16, PAIR, 128), F32),
            pltpu.VMEM((16, PAIR, 128), BF),
            pltpu.VMEM((4, HEAD_Q, PAIR), BF),
            pltpu.VMEM((4, 4, 4, 24, Q_HALF), BF),
            pltpu.VMEM((3, 3, 4, 4, 24, 256), BF),
            pltpu.SemaphoreType.DMA((3,)),
            pltpu.SemaphoreType.DMA,
            pltpu.SemaphoreType.DMA,
            pltpu.SemaphoreType.DMA((2,)),
            pltpu.SemaphoreType.DMA((2,)),
            pltpu.SemaphoreType.DMA((4,)),
            pltpu.SemaphoreType.DMA((4,)),
            pltpu.SemaphoreType.DMA,
            pltpu.SemaphoreType.DMA,
            pltpu.SemaphoreType.DMA((3, 3)),
            pltpu.SemaphoreType.DMA((3, 3)),
        ],
        compiler_params=params(4, 60 << 20),
        name="attend_back",
    )(heads, branch, own_attn, other_attn, q_in, kv_in, first, ot, lse)


def inverse_rms(values):
    return lax.rsqrt(jnp.mean(values * values, axis=-1, keepdims=True) + EPS)


def norm_backward(values, inverse, gain, grad_out):
    scaled = grad_out * gain
    return inverse * scaled - values * inverse**3 * jnp.mean(values * scaled, axis=-1, keepdims=True)


def column_sums(left, right):
    return lax.dot_general(left, right, (((0,), (0,)), ((), ())), precision=HIGH_PRECISION)


def only_column(rows, column):
    return jnp.broadcast_to((jnp.arange(EXTRA) == column).astype(F32), (rows, EXTRA))


def local(
    tokens,
    segment_ids,
    expert_ids,
    w_query,
    w_key,
    w_value,
    w_out,
    w_router,
    gain_attn,
    gain_moe,
    w_gate,
    w_up,
    w_down,
    cotangent,
):
    y, z, x, c = coords()
    width = w_gate.shape[1]
    extra = jnp.concatenate(
        [w_router, gain_attn[:, None], gain_moe[:, None], jnp.zeros((12, EXTRA - 18), BF)], axis=1
    )
    part_q, part_kv, part_out, part_extra, pair, normed, q4, keys_values, first = gather_weights(
        w_query, w_key, w_value, w_out.T, extra, tokens, segment_ids
    )
    pair, w_gate, w_up, w_down = lax.optimization_barrier((pair, w_gate, w_up, w_down))
    w_experts = jnp.concatenate([w_gate, w_up, w_down.T], axis=1)
    full_experts = lax.all_gather(w_experts, "dp", axis=0, tiled=True)
    full_q = part_q.reshape(MODEL_WIDTH, Q_HALF)
    full_kv = part_kv.reshape(MODEL_WIDTH, KV_HALF)
    full_extra = part_extra.reshape(MODEL_WIDTH, EXTRA)
    picks = (jnp.arange(EXTRA)[None, :] == jnp.arange(8)[:, None] + EXPERT_COUNT).astype(BF)
    gains = dot(picks, full_extra, ((1,), (1,)))
    gain_a, gain_m = gains[0:1], gains[1:2]
    router = full_extra[:, :EXPERT_COUNT]

    chosen = (expert_ids[:, :, None] == jnp.arange(EXPERT_COUNT, dtype=jnp.int32)).astype(F32)
    used = jnp.sum(chosen, axis=1)
    earlier = (jnp.arange(ROWS)[:, None] > jnp.arange(ROWS)[None, :]).astype(BF)
    before = dot(earlier, used.astype(BF), ((1,), (0,)))
    place = jnp.sum(chosen * before[:, None, :], axis=-1)
    slot = jnp.where(
        place < EXPERT_CAPACITY, expert_ids * SLOTS + place.astype(jnp.int32), -1
    )
    hit = (slot.T[:, :, None] == jnp.arange(EXPERT_COUNT * SLOTS, dtype=jnp.int32)).astype(F32)
    both = (hit[0] + hit[1]).astype(BF)
    blocks = (EXPERT_COUNT, SLOTS, MODEL_WIDTH)
    cot_slots = dot(both, cotangent, ((0,), (0,))).astype(BF)
    q_in, kv_in, attn, attn_t, lse, half_out, sib_out, cot_all = attend(
        q4, keys_values, part_out, cot_slots.reshape(blocks), first
    )
    half_out = half_out.reshape(MODEL_WIDTH, Q_HALF)
    sib_out = sib_out.reshape(MODEL_WIDTH, Q_HALF)
    attn = attn.reshape(2, Q_HALF, ROWS)

    own_attn = jnp.where(c == 0, attn[0], attn[1])
    other_attn = jnp.where(c == 0, attn[1], attn[0])
    inputs = tokens.astype(F32)
    middle = (
        inputs
        + dot(own_attn, half_out, ((0,), (1,)))
        + dot(other_attn, sib_out, ((0,), (1,)))
    )
    inverse_m = inverse_rms(middle)
    moe_in = (middle * inverse_m * gain_m).astype(BF)
    logits = dot(moe_in, router, ((1,), (0,)))
    picked = jnp.sum(chosen * logits[:, None, :], axis=-1)
    gates = jax.nn.softmax(picked, axis=-1)
    slot_gate = jnp.sum(hit * gates.T[:, :, None], axis=(0, 1))
    slots_in = dot(both, moe_in, ((0,), (0,))).astype(BF)
    slot_gate = jnp.broadcast_to(slot_gate.reshape(EXPERT_COUNT, SLOTS, 1), (EXPERT_COUNT, SLOTS, 128))
    out_ret, grad_ret, grad_experts = experts(
        slots_in.reshape(blocks), slot_gate, cot_all, full_experts
    )
    sum_experts = lax.psum_scatter(grad_experts, "dp", scatter_dimension=0, tiled=True)

    grad_output = cotangent.astype(F32)
    out_ret = out_ret.reshape(EXPERT_COUNT * SLOTS, MODEL_WIDTH)
    grad_ret = grad_ret.reshape(EXPERT_COUNT * SLOTS, MODEL_WIDTH)
    rows_out = [dot(hit[k].astype(BF), out_ret, ((1,), (0,))) for k in range(2)]
    block_out = (middle + gates[:, 0:1] * rows_out[0] + gates[:, 1:2] * rows_out[1]).astype(BF)
    grad_pair = jnp.stack([jnp.sum(grad_output * rows, axis=-1) for rows in rows_out], axis=-1)
    grad_pick = gates * (grad_pair - jnp.sum(gates * grad_pair, axis=-1, keepdims=True))
    grad_logits = jnp.sum(chosen * grad_pick[:, :, None], axis=1)
    grad_moe_in = dot(both, grad_ret, ((1,), (0,))) + lax.dot_general(
        grad_logits, router.astype(F32), (((1,), (1,)), ((), ())), precision=HIGH_PRECISION
    )
    g_router = column_sums(moe_in.astype(F32), jnp.pad(grad_logits, ((0, 0), (0, EXTRA - EXPERT_COUNT))))
    g_gain_m = column_sums(grad_moe_in * middle * inverse_m, only_column(ROWS, EXPERT_COUNT + 1))
    grad_middle = grad_output + norm_backward(middle, inverse_m, gain_m, grad_moe_in)
    branch = grad_middle.astype(BF)
    own_heads = dot(half_out, branch, ((0,), (1,))).astype(BF)
    other_heads = dot(sib_out, branch, ((0,), (1,))).astype(BF)
    grad_heads = jnp.stack(
        [jnp.where(c == 0, own_heads, other_heads), jnp.where(c == 0, other_heads, own_heads)]
    )
    dq_in, dkv_in, sum_out = attend_back(
        grad_heads.reshape(8, HEAD_Q, ROWS), branch, own_attn, other_attn, q_in, kv_in, first,
        attn_t, lse,
    )
    grad_tokens, r_query, r_key, r_value, r_out, r_extra = reduce_weights(
        dq_in.reshape(Q_HALF, PAIR), dkv_in, normed, g_router + g_gain_m, sum_out,
        pair.reshape(PAIR, MODEL_WIDTH), gain_a, grad_middle, full_q, full_kv,
    )
    return (
        block_out,
        grad_tokens,
        r_query,
        r_key,
        r_value,
        r_out.T,
        r_extra[:, :EXPERT_COUNT],
        r_extra[:, EXPERT_COUNT],
        r_extra[:, EXPERT_COUNT + 1],
        sum_experts[:, :width].astype(F32),
        sum_experts[:, width : 2 * width].astype(F32),
        sum_experts[:, 2 * width :].astype(F32).T,
    )


def solution(mesh):
    rows, flat, dense = P(("dp", "ctx"), None), P(("dp", "ctx")), P("dp", "ctx")
    placed = (
        rows, dense, rows, rows, rows, rows, P(None, ("dp", "ctx")), rows, flat, flat,
        dense, dense, P("ctx", "dp"), rows,
    )
    return jax.shard_map(
        local,
        mesh=mesh,
        in_specs=placed,
        out_specs=(
            rows, rows, rows, rows, rows, P(None, ("dp", "ctx")), rows, flat, flat,
            dense, dense, P("ctx", "dp"),
        ),
        check_vma=False,
    )
```

```python
import functools

import jax
import jax.numpy as jnp
from jax import lax
from jax.experimental import pallas as pl
from jax.experimental.pallas import tpu as pltpu
from jax.sharding import PartitionSpec as P

MODEL_WIDTH = 1536
KV = 8
HD = 64
EXPERT_COUNT = 16
FF = 1024
EXPERT_CAPACITY = 20
SLOTS = 24
ROWS = 128
PAIR = 256
HEAD_Q = 192
Q_HALF = 768
KV_HALF = 512
EXTRA = 128
PACK = Q_HALF + KV_HALF + EXTRA + Q_HALF

EPS = 1e-05
SCALE_QK = 0.125
NEGATIVE = -1e30
MESH = pl.DeviceIdType.MESH
ANY = pl.BlockSpec(memory_space=pl.ANY)
IN_VMEM = pl.BlockSpec(memory_space=pltpu.VMEM)
BF = jnp.bfloat16
F32 = jnp.float32


def dot(a, b, dims):
    return lax.dot_general(a, b, (dims, ((), ())), preferred_element_type=F32)


def coords():
    i = lax.axis_index("ctx")
    return lax.axis_index("dp"), i // 8, (i // 2) % 4, i % 2


def dev(y, z, x, c):
    return (y, z * 8 + x * 2 + c)


def signal(target):
    pl.semaphore_signal(
        pltpu.get_barrier_semaphore(), inc=1, device_id=target, device_id_type=MESH
    )


def remote(src, dst, send, recv, target):
    return pltpu.make_async_remote_copy(
        src_ref=src, dst_ref=dst, send_sem=send, recv_sem=recv, device_id=target, device_id_type=MESH
    )


def params(cid, vmem=None):
    return pltpu.CompilerParams(collective_id=cid, has_side_effects=True, vmem_limit_bytes=vmem)


def axis_peer(axis, step):
    y, z, x, c = coords()
    if axis == "y":
        return dev((y + step) % 4, z, x, c)
    if axis == "z":
        return dev(y, (z + step) % 4, x, c)
    return dev(y, z, (x + step) % 4, c)


WIDTHS = (Q_HALF, KV_HALF, Q_HALF, EXTRA)
STARTS = (0, Q_HALF, Q_HALF + KV_HALF, 2 * Q_HALF + KV_HALF)
STEPS = (1, 3, 2)
FIRST_PARTS = (
    (0, 0, 512, ("x", "z", "y")),
    (1, 0, 512, ("y", "x", "z")),
    (0, 512, 256, ("z", "y", "x")),
    (3, 0, 128, ("z", "y", "x")),
)
OUT_PARTS = (
    (2, 0, 128, ("z", "x", "y")),
    (2, 128, 384, ("z", "y", "x")),
    (2, 512, 256, ("y", "x", "z")),
)
OUT_SUMS = ((0, ("x", "y", "z")), (256, ("x", "z", "y")), (512, ("z", "x", "y")))
GATHER_PARTS = FIRST_PARTS + OUT_PARTS


def slab(ref, done, y, z, x, cols):
    return ref.at[
        slice(None) if "y" in done else y,
        slice(None) if "z" in done else z,
        slice(None) if "x" in done else x,
        slice(None),
        cols,
    ]


def column_of(row):
    return jnp.transpose(jnp.broadcast_to(row, (128, row.shape[1])))


def slot_hits(ids):
    lane = lax.broadcasted_iota(jnp.int32, (ROWS, 128), 1).astype(F32)
    experts_of = [column_of(ids[k : k + 1].astype(F32)) for k in range(2)]
    chosen = [jnp.where(lane == expert, 1.0, 0.0) for expert in experts_of]
    row = lax.broadcasted_iota(jnp.int32, (ROWS, ROWS), 0)
    earlier = jnp.where(row > lax.broadcasted_iota(jnp.int32, (ROWS, ROWS), 1), 1.0, 0.0).astype(BF)
    before = dot(earlier, (chosen[0] + chosen[1]).astype(BF), ((1,), (0,)))
    slot_lane = lax.broadcasted_iota(jnp.int32, (ROWS, EXPERT_COUNT * SLOTS), 1).astype(F32)
    hits = []
    for k in range(2):
        place = jnp.sum(chosen[k] * before, axis=1, keepdims=True)
        slot = jnp.where(place < EXPERT_CAPACITY, experts_of[k][:, :1] * SLOTS + place, -1.0)
        hits.append(jnp.where(slot_lane == slot, 1.0, 0.0))
    return chosen, hits


def three_parts(values):
    parts = []
    for _ in range(3):
        part = values.astype(BF)
        parts.append(part)
        values = values - part.astype(F32)
    return parts


def gather_kernel(
    w_query, w_key, w_value, w_out, w_router, gain_a, gain_m, ids, cots, tokens, segs, w_gate, w_up, w_down,
    o_q, o_kv, out2, out3, pair, o_normed, w_experts, q4, kv2, o_first, cot_slots,
    pack, sib, block, w_q, w_kv, w_extra, rows, segments, normed, packed, down,
    p_send, p_recv, l_sem, s_send, s_recv, sib_send, sib_recv, o_sem,
):
    y, z, x, c = coords()
    outs = (w_q, w_kv, out2, w_extra)
    me = z * 8 + x * 2 + c
    sibling = dev(y, z, x, 1 - c)

    def greet(k, carry):
        signal((y, (me + k) % 32))
        return carry

    lax.fori_loop(1, 32, greet, 0)
    for step in STEPS:
        signal(axis_peer("y", step))
    expert_loads = [
        pltpu.make_async_copy(w_gate, packed.at[:, 0:FF // 2], o_sem.at[5]),
        pltpu.make_async_copy(w_up, packed.at[:, FF // 2 : FF], o_sem.at[6]),
        pltpu.make_async_copy(w_down, down, o_sem.at[7]),
    ]
    for load in expert_loads:
        load.start()
    lane = lax.broadcasted_iota(jnp.int32, (12, EXTRA), 1)
    square = lax.broadcasted_iota(jnp.int32, (12, 12), 0) == lax.broadcasted_iota(jnp.int32, (12, 12), 1)
    extra = jnp.concatenate(
        [w_router[...].astype(F32), jnp.zeros((12, EXTRA - EXPERT_COUNT), F32)], axis=1
    )
    for k, gain_row in enumerate((gain_a, gain_m)):
        spread_row = jnp.broadcast_to(gain_row[...].astype(F32), (12, 12))
        column = jnp.sum(jnp.where(square, spread_row, 0.0), axis=1, keepdims=True)
        extra = jnp.where(lane == EXPERT_COUNT + k, column, extra)
    extra = extra.astype(BF)
    heads = []
    for h in range(KV):
        cols = slice(HD * h, HD * h + HD)
        heads += [w_key[:, cols].astype(F32), w_value[:, cols].astype(F32)]
    heads = jnp.concatenate(heads, axis=1).astype(BF)
    for k in range(2):
        parts = (
            w_query[:, Q_HALF * k : Q_HALF * k + Q_HALF],
            heads[:, KV_HALF * k : KV_HALF * k + KV_HALF],
            w_out[:, Q_HALF * k : Q_HALF * k + Q_HALF],
            extra,
        )
        for start, width, part in zip(STARTS, WIDTHS, parts):
            pack[k, 0:12, start : start + width] = part
            pack[k, 12:16, start : start + width] = jnp.zeros((4, width), BF)
    pl.semaphore_wait(pltpu.get_barrier_semaphore(), 34)

    first = remote(pack.at[1 - c], sib, sib_send.at[0], sib_recv.at[0], sibling)
    first.start()
    second = remote(tokens, rows.at[c], sib_send.at[1], sib_recv.at[1], sibling)
    second.start()
    own_rows = pltpu.make_async_copy(tokens, rows.at[c], l_sem.at[4])
    own_rows.start()
    own_segs = pltpu.make_async_copy(segs, segments.at[me], l_sem.at[5])
    own_segs.start()

    def spread(k, carry):
        remote(segs, segments.at[me], s_send, s_recv, (y, (me + k) % 32)).start()
        return carry

    lax.fori_loop(1, 32, spread, 0)

    first.wait()
    own = pack[c, :12].astype(F32)
    other = sib[:12].astype(F32)
    low = jnp.where(c == 0, own, other)
    high = jnp.where(c == 0, other, own)
    block[...] = jnp.concatenate([low, high], axis=0).astype(BF)

    locals_ = []
    for n in range(4):
        cols = pl.ds(STARTS[n], WIDTHS[n])
        here = pltpu.make_async_copy(block.at[:, cols], outs[n].at[y, z, x], l_sem.at[n])
        here.start()
        locals_.append(here)
    for phase in range(3):
        copies = []
        for part, (n, start, width, order) in enumerate(GATHER_PARTS if phase < 2 else FIRST_PARTS):
            for k, step in enumerate(STEPS):
                dst = slab(outs[n], order[:phase], y, z, x, pl.ds(start, width))
                src = block.at[:, pl.ds(STARTS[n] + start, width)] if phase == 0 else dst
                copy = remote(
                    src, dst, p_send.at[phase, part, k], p_recv.at[phase, part, k],
                    axis_peer(order[phase], step),
                )
                copy.start()
                copies.append(copy)
        if phase == 0:
            for here in locals_:
                here.wait()
        if phase == 2:
            own_segs.wait()
            drain = remote(
                segments.at[pl.ds(0, 31)], segments.at[pl.ds(0, 31)], s_send, s_recv, sibling
            )
            drain.wait_send()
            drain.wait_recv()
            places = segments[...].reshape(32, 128)
            for zq in range(4):
                t = (zq * 4 + x) * 2
                mine = jnp.concatenate([segments[t], segments[t + 1]], axis=1)
                begin = jnp.zeros((1, PAIR), jnp.int32)
                for u in range(15):
                    count = jnp.sum((places == u).astype(jnp.int32))
                    begin = begin + jnp.where(mine > u, count, 0)
                o_first[zq] = begin
            chosen, hits = slot_hits(ids[...])
            kept = dot((hits[0] + hits[1]).astype(BF), cots[...], ((0,), (0,))).astype(BF)
            cot_slots[...] = kept.reshape(EXPERT_COUNT, SLOTS, MODEL_WIDTH)
            for load in expert_loads:
                load.wait()
            packed[:, FF:] = jnp.transpose(down[...].astype(F32)).astype(BF)
            pltpu.make_async_copy(packed, w_experts, o_sem.at[5]).start()
            second.wait()
            own_rows.wait()
        for copy in copies:
            copy.wait()
    stores = [
        pltpu.make_async_copy(src, dst, o_sem.at[n])
        for n, (src, dst) in enumerate(((w_q, o_q), (w_kv, o_kv), (w_extra, out3), (rows, pair)))
    ]
    for store in stores:
        store.start()
    gain = jnp.transpose(w_extra[...].reshape(MODEL_WIDTH, EXTRA).astype(F32))[EXPERT_COUNT : EXPERT_COUNT + 1]
    for k in range(2):
        values = rows[k].astype(F32)
        normed[ROWS * k : ROWS * k + ROWS] = (values * inverse_rms(values) * gain).astype(BF)
    last = pltpu.make_async_copy(normed, o_normed, o_sem.at[4])
    last.start()
    queries = dot(w_q[...].reshape(MODEL_WIDTH, Q_HALF), normed[...], ((0,), (1,))).astype(BF)
    q4[...] = queries.reshape(4, HEAD_Q, PAIR)
    kv2[...] = dot(normed[...], w_kv[...].reshape(MODEL_WIDTH, KV_HALF), ((1,), (0,))).astype(BF)
    for store in stores:
        store.wait()
    last.wait()
    pltpu.make_async_copy(packed, w_experts, o_sem.at[5]).wait()


def gather_weights(vmem_args, hbm_args):
    blocks = [(4, 4, 4, 24, width) for width in WIDTHS]
    rows = (2, ROWS, MODEL_WIDTH)
    flat = (PAIR, MODEL_WIDTH)
    experts_in = (MODEL_WIDTH // 4, 3 * FF // 2)
    return pl.pallas_call(
        gather_kernel,
        out_shape=[jax.ShapeDtypeStruct(shape, BF) for shape in (*blocks, rows, flat, experts_in)]
        + [
            jax.ShapeDtypeStruct((4, HEAD_Q, PAIR), BF),
            jax.ShapeDtypeStruct((PAIR, KV_HALF), BF),
            jax.ShapeDtypeStruct((4, 1, PAIR), jnp.int32),
            jax.ShapeDtypeStruct((EXPERT_COUNT, SLOTS, MODEL_WIDTH), BF),
        ],
        in_specs=[IN_VMEM] * len(vmem_args) + [ANY] * len(hbm_args),
        out_specs=[ANY] * 7 + [IN_VMEM] * 4,
        scratch_shapes=[
            pltpu.VMEM((2, 16, PACK), BF),
            pltpu.VMEM((16, PACK), BF),
            pltpu.VMEM((24, PACK), BF),
            pltpu.VMEM(blocks[0], BF),
            pltpu.VMEM(blocks[1], BF),
            pltpu.VMEM(blocks[3], BF),
            pltpu.VMEM(rows, BF),
            pltpu.VMEM((32, 1, 128), jnp.int32),
            pltpu.VMEM(flat, BF),
            pltpu.VMEM(experts_in, BF),
            pltpu.VMEM((FF // 2, MODEL_WIDTH // 4), BF),
            pltpu.SemaphoreType.DMA((3, 7, 3)),
            pltpu.SemaphoreType.DMA((3, 7, 3)),
            pltpu.SemaphoreType.DMA((6,)),
            pltpu.SemaphoreType.DMA,
            pltpu.SemaphoreType.DMA,
            pltpu.SemaphoreType.DMA((2,)),
            pltpu.SemaphoreType.DMA((2,)),
            pltpu.SemaphoreType.DMA((8,)),
        ],
        compiler_params=params(1, 60 << 20),
        name="gather_weights",
    )(*vmem_args, *hbm_args)


def offset(k):
    dz = (k % 8) // 2
    return dz, 2 * (k % 2) + (dz + k // 8) % 2


def chip_to(k):
    y, z, x, c = coords()
    dz, dx = offset(k)
    return (z + dz) % 4, (x + dx) % 4


def chip_from(k):
    y, z, x, c = coords()
    dz, dx = offset(k)
    return (z + 4 - dz) % 4, (x + 4 - dx) % 4


def slot_block(k, core):
    return (k // 8) * 16 + core * 8 + k % 8


def plane_greet():
    y, z, x, c = coords()
    me = z * 4 + x

    def greet(k, carry):
        t = (me + k) % 16
        signal(dev(y, t // 4, t % 4, c))
        return carry

    lax.fori_loop(1, 16, greet, 0)
    signal(dev(y, z, x, 1 - c))


KEYS = 1024


def attend_kernel(
    q4, kv2, half_in, cots, first_ref, q_in, kv_in, attn, ot_ref, lse_ref, half, half_sib, c_all,
    qs, acc, o_buf,
    l_sem, q_send, q_recv, k_send, k_recv, w_send, w_recv, sib_send, sib_recv,
    c_send, c_recv, f_send, f_recv, o_send, o_recv,
):
    y, z, x, c = coords()
    me = z * 4 + x
    sibling = dev(y, z, x, 1 - c)

    wide_greet()

    q_copies = []
    for n, step in enumerate(STEPS):
        to = (z + step) % 4
        copy = remote(q4.at[to], q_in.at[z], q_send.at[n], q_recv.at[n], dev(y, to, x, c))
        copy.start()
        q_copies.append(copy)

    def head(index):
        return kv2.at[:, pl.ds(pl.multiple_of(index * 128, 128), 128)]

    def send_kv(k, carry):
        t = (me + k) % 16
        remote(head(t // 4), kv_in.at[me], k_send, k_recv, dev(y, t // 4, t % 4, c)).start()
        return carry

    lax.fori_loop(1, 16, send_kv, 0)
    here = [
        pltpu.make_async_copy(q4.at[z], q_in.at[z], l_sem.at[0]),
        pltpu.make_async_copy(head(z), kv_in.at[me], l_sem.at[1]),
    ]
    for copy in here:
        copy.start()
    for copy in here:
        copy.wait()
    for copy in q_copies:
        copy.wait()
    drain = remote(kv_in.at[pl.ds(0, 15)], kv_in.at[pl.ds(0, 15)], k_send, k_recv, sibling)
    drain.wait_send()
    drain.wait_recv()

    w_copies = [[], [], []]
    for part, (n, start, width, order) in enumerate(OUT_PARTS):
        spot = slab(half, order[:2], y, z, x, pl.ds(start, width))
        for k, step in enumerate(STEPS):
            copy = remote(
                spot, spot, w_send.at[part, k], w_recv.at[part, k], axis_peer(order[2], step)
            )
            copy.start()
            w_copies[part].append(copy)

    def cots_copy(k):
        tz, tx = chip_to(k)
        return remote(
            cots.at[tz * 4 + tx], c_all.at[slot_block(k, c)], c_send.at[k], c_recv.at[k], dev(y, tz, tx, c)
        )

    def send_cots(k, carry):
        cots_copy(k).start()
        return carry

    lax.fori_loop(1, 16, send_cots, 0)
    own_cots = pltpu.make_async_copy(cots.at[me], c_all.at[slot_block(0, c)], l_sem.at[2])
    own_cots.start()
    remote(cots.at[me], c_all.at[slot_block(0, c)], f_send, f_recv, sibling).start()

    def forward_cots(k, carry):
        arrived = cots_copy(k)
        arrived.wait_recv()
        remote(c_all.at[slot_block(k, c)], c_all.at[slot_block(k, c)], f_send, f_recv, sibling).start()
        arrived.wait_send()
        return carry

    def swap(part):
        start, width = OUT_PARTS[part][1:3]
        cols = half.at[:, :, :, :, pl.ds(start, width)]
        there = half_sib.at[:, :, :, :, pl.ds(start, width)]
        return remote(cols, there, sib_send.at[part], sib_recv.at[part], sibling)

    j = c * 4 + z
    qs[64:] = jnp.zeros((64, 3 * PAIR), BF)
    returns = []
    for n in range(4):
        zq = (z + n + 1) % 4
        q = q_in[zq] * SCALE_QK
        for h in range(3):
            qs[:64, 256 * h : 256 * h + 256] = q[64 * h : 64 * h + 64]
        acc[...] = jnp.zeros_like(acc)
        first = first_ref[zq]
        q_pos = (zq * 4 + x) * PAIR + lax.broadcasted_iota(jnp.int32, (1, PAIR), 1)

        def step(kb, stats):
            kv = kv_in[pl.ds(kb * (KEYS // PAIR), KEYS // PAIR)].reshape(KEYS, 128)
            k_pos = kb * KEYS + lax.broadcasted_iota(jnp.int32, (KEYS, PAIR), 0)
            ok = (k_pos >= first) & (k_pos <= q_pos)
            scores = [dot(kv, qs[:, 256 * h : 256 * h + 256], ((1,), (0,))) for h in range(3)]
            later, probs, shrinks = [], [], []
            for h in range(3):
                top, tot = stats[h]
                masked = jnp.where(ok, scores[h], NEGATIVE)
                new = jnp.maximum(top, jnp.max(masked, axis=0, keepdims=True))
                prob = jnp.exp(masked - new)
                shrink = jnp.exp(top - new)
                later.append((new, tot * shrink + jnp.sum(prob, axis=0, keepdims=True)))
                probs.append(prob.astype(BF))
                shrinks.append(shrink)
            for h in range(3):
                cols = slice(256 * h, 256 * h + 256)
                acc[:, cols] = acc[:, cols] * shrinks[h] + dot(kv, probs[h], ((0,), (0,)))
            return tuple(later)

        none = (jnp.full((1, PAIR), NEGATIVE, F32), jnp.zeros((1, PAIR), F32))
        stats = lax.fori_loop(0, zq + 1, step, (none, none, none))
        heads = []
        for h in range(3):
            cols = slice(256 * h, 256 * h + 256)
            mixed = acc[64:, cols] / stats[h][1]
            ot_ref[zq, :, cols] = mixed
            lse_ref[zq, :, cols] = stats[h][0] + jnp.log(stats[h][1])
            heads.append(mixed)
        heads = jnp.concatenate(heads, axis=0).astype(BF)
        o_buf[n, 0] = heads[:, :ROWS]
        o_buf[n, 1] = heads[:, ROWS:]
        for d in range(2):
            core = c if d == 0 else 1 - c
            if n == 3 and d == 0:
                back = pltpu.make_async_copy(o_buf.at[n, core], attn.at[j], l_sem.at[3])
            else:
                back = remote(
                    o_buf.at[n, core], attn.at[j], o_send.at[n, d], o_recv.at[n, d], dev(y, zq, x, core)
                )
            back.start()
            returns.append(back)
    for part in range(3):
        for copy in w_copies[part]:
            copy.wait()
        swap(part).start()
        if part == 0:
            lax.fori_loop(1, 16, forward_cots, 0)
    own_cots.wait()
    mine = c_all.at[pl.ds(c * 16, 16)]
    drain = remote(mine, mine, f_send, f_recv, sibling)
    drain.wait_send()
    drain.wait_recv()
    for part in range(3):
        swap(part).wait()
    for back in returns:
        back.wait()


def attend(q4, kv2, half, cots, first):
    blocks = jax.ShapeDtypeStruct((4, 4, 4, 24, Q_HALF), BF)
    return pl.pallas_call(
        attend_kernel,
        out_shape=[
            jax.ShapeDtypeStruct((4, HEAD_Q, PAIR), BF),
            jax.ShapeDtypeStruct((16, PAIR, 128), BF),
            jax.ShapeDtypeStruct((8, HEAD_Q, ROWS), BF),
            jax.ShapeDtypeStruct((4, HD, 3 * PAIR), F32),
            jax.ShapeDtypeStruct((4, 1, 3 * PAIR), F32),
            blocks,
            blocks,
            jax.ShapeDtypeStruct((32, SLOTS, MODEL_WIDTH), BF),
        ],
        in_specs=[ANY, ANY, ANY, ANY, IN_VMEM],
        out_specs=[IN_VMEM, IN_VMEM, ANY, IN_VMEM, IN_VMEM, ANY, ANY, ANY],
        input_output_aliases={2: 5},
        scratch_shapes=[
            pltpu.VMEM((128, 3 * PAIR), BF),
            pltpu.VMEM((128, 3 * PAIR), F32),
            pltpu.VMEM((4, 2, HEAD_Q, ROWS), BF),
            pltpu.SemaphoreType.DMA((4,)),
            pltpu.SemaphoreType.DMA((3,)),
            pltpu.SemaphoreType.DMA((3,)),
            pltpu.SemaphoreType.DMA,
            pltpu.SemaphoreType.DMA,
            pltpu.SemaphoreType.DMA((3, 3)),
            pltpu.SemaphoreType.DMA((3, 3)),
            pltpu.SemaphoreType.DMA((3,)),
            pltpu.SemaphoreType.DMA((3,)),
            pltpu.SemaphoreType.DMA((16,)),
            pltpu.SemaphoreType.DMA((16,)),
            pltpu.SemaphoreType.DMA,
            pltpu.SemaphoreType.DMA,
            pltpu.SemaphoreType.DMA((4, 2)),
            pltpu.SemaphoreType.DMA((4, 2)),
        ],
        compiler_params=params(2, 60 << 20),
        name="attend",
    )(q4, kv2, half, cots, first)


def flat_rows(blocks):
    return blocks.reshape(blocks.shape[0] * SLOTS, blocks.shape[2])


def experts_kernel(
    attn, tokens, extra, ids, cotangent, half_w, sib_w, cots, weights,
    o_block, o_middle, o_branch, o_heads, o_moe, o_logits, o_gain, d_all,
    x_all, t_all, g_all, w_all, gate_v, up_v, hidden, g_both, part_o, part_g, sib_o, sib_g,
    v_all, wh, ws, xs, gates, out_ret, grad_ret, middle, moe_in,
    w_sem, l_sem, send, recv, f_send, f_recv, s_send, s_recv, r_send, r_recv, o_sem,
):
    y, z, x, c = coords()
    me = z * 4 + x
    width = hidden.shape[1]
    sibling = dev(y, z, x, 1 - c)
    loads = [
        pltpu.make_async_copy(src, dst, w_sem.at[n])
        for n, (src, dst) in enumerate(((half_w, wh), (sib_w, ws), (weights, w_all), (cots, g_all)))
    ]
    plane_greet()
    for load in loads:
        load.start()
    chosen, hits = slot_hits(ids[...])
    both_hits = (hits[0] + hits[1]).astype(BF)
    flat_extra = extra[...].reshape(MODEL_WIDTH, EXTRA)
    gain = jnp.transpose(flat_extra.astype(F32))[EXPERT_COUNT + 1 : EXPERT_COUNT + 2]
    own = attn[pl.ds(c * 4, 4)].reshape(Q_HALF, ROWS)
    other = attn[pl.ds((1 - c) * 4, 4)].reshape(Q_HALF, ROWS)
    loads[0].wait()
    loads[1].wait()
    middle[...] = (
        tokens[...].astype(F32)
        + dot(own, wh[...].reshape(MODEL_WIDTH, Q_HALF), ((0,), (1,)))
        + dot(other, ws[...].reshape(MODEL_WIDTH, Q_HALF), ((0,), (1,)))
    )
    inverse = inverse_rms(middle[...])
    moe_in[...] = (middle[...] * inverse * gain).astype(BF)
    logits = dot(moe_in[...], flat_extra, ((1,), (0,)))
    picked = [jnp.sum(chosen[k] * logits, axis=1, keepdims=True) for k in range(2)]
    most = jnp.maximum(picked[0], picked[1])
    lifted = [jnp.exp(value - most) for value in picked]
    share = [value / (lifted[0] + lifted[1]) for value in lifted]
    slots_in = dot(both_hits, moe_in[...], ((0,), (0,))).astype(BF)
    xs[...] = slots_in.reshape(EXPERT_COUNT, SLOTS, MODEL_WIDTH)
    slot_gate = jnp.sum(hits[0] * share[0] + hits[1] * share[1], axis=0, keepdims=True)
    gates[...] = column_of(slot_gate).reshape(EXPERT_COUNT, SLOTS, 128)
    pl.semaphore_wait(pltpu.get_barrier_semaphore(), 16)
    arrays = ((xs, x_all), (gates, t_all))

    def arriving(a, k):
        src, dst = arrays[a]
        tz, tx = chip_to(k)
        return remote(
            src.at[tz * 4 + tx], dst.at[slot_block(k, c)], send.at[a, k], recv.at[a, k], dev(y, tz, tx, c)
        )

    def steps_of(part):
        return (1, 8) if part == 0 else (8, 16)

    def scatter(a, part):
        def push(k, carry):
            arriving(a, k).start()
            return carry

        lax.fori_loop(*steps_of(part), push, 0)
        if part == 0:
            src, dst = arrays[a]
            pltpu.make_async_copy(src.at[me], dst.at[slot_block(0, c)], l_sem.at[a]).start()
            remote(src.at[me], dst.at[slot_block(0, c)], f_send.at[a, 0], f_recv.at[a, 0], sibling).start()

    def hand_over(a, part):
        src, dst = arrays[a]

        def forward(k, carry):
            arrived = arriving(a, k)
            arrived.wait_recv()
            block = dst.at[slot_block(k, c)]
            remote(block, block, f_send.at[a, part], f_recv.at[a, part], sibling).start()
            arrived.wait_send()
            return carry

        lax.fori_loop(*steps_of(part), forward, 0)

    def settle(a, part):
        src, dst = arrays[a]
        if part == 0:
            pltpu.make_async_copy(src.at[me], dst.at[slot_block(0, c)], l_sem.at[a]).wait()
        some = dst.at[pl.ds(0, 8)]
        drain = remote(some, some, f_send.at[a, part], f_recv.at[a, part], sibling)
        drain.wait_send()
        drain.wait_recv()

    def swap(mine, sib, a, part):
        return remote(
            mine.at[pl.ds(part * 16 + (1 - c) * 8, 8)], sib.at[pl.ds(part * 8, 8)],
            s_send.at[a, part], s_recv.at[a, part], sibling,
        )

    def give(mine, sib, ret, a, part):
        def add(k):
            block = slot_block(k, c)
            mine[block] = (mine[block].astype(F32) + sib[k].astype(F32)).astype(BF)
            return mine.at[block]

        def push(k, carry):
            sz, sx = chip_from(k)
            remote(add(k), ret.at[me], r_send.at[a], r_recv.at[a], dev(y, sz, sx, c)).start()
            return carry

        lax.fori_loop(*steps_of(part), push, 0)
        if part == 0:
            pltpu.make_async_copy(add(0), ret.at[me], l_sem.at[2 + a]).start()

    def given(mine, ret, a):
        pltpu.make_async_copy(mine.at[slot_block(0, c)], ret.at[me], l_sem.at[2 + a]).wait()
        drain = remote(ret.at[pl.ds(0, 15)], ret.at[pl.ds(0, 15)], r_send.at[a], r_recv.at[a], sibling)
        drain.wait_send()
        drain.wait_recv()

    half = 16 * SLOTS

    def forward_pass(part):
        blocks, rows = pl.ds(part * 16, 16), slice(part * half, part * half + half)
        both = dot(flat_rows(x_all[blocks]), w_all[:, : 2 * width], ((1,), (0,)))
        gate_val, up_val = both[:, :width], both[:, width:]
        gate_v[rows] = gate_val
        up_v[rows] = up_val
        low = (gate_val * jax.nn.sigmoid(gate_val) * up_val).astype(BF)
        hidden[rows] = low
        out = dot(low, w_all[:, 2 * width :], ((1,), (1,))).astype(BF)
        part_o[blocks] = out.reshape(16, SLOTS, MODEL_WIDTH)
        swap(part_o, sib_o, 0, part).start()

    def backward_pass(part):
        blocks, rows = pl.ds(part * 16, 16), slice(part * half, part * half + half)
        scale = jnp.concatenate([flat_rows(t_all[blocks])] * (MODEL_WIDTH // 128), axis=1)
        grad_expert = (flat_rows(g_all[blocks]).astype(F32) * scale).astype(BF)
        g_all[blocks] = grad_expert.reshape(16, SLOTS, MODEL_WIDTH)
        grad_hidden = dot(grad_expert, w_all[:, 2 * width :], ((1,), (0,)))
        gate_val = gate_v[rows]
        up_val = up_v[rows]
        sig = jax.nn.sigmoid(gate_val)
        grad_gate = (grad_hidden * up_val * sig * (1.0 + gate_val * (1.0 - sig))).astype(BF)
        grad_up = (grad_hidden * gate_val * sig).astype(BF)
        grads = jnp.concatenate([grad_gate, grad_up], axis=1)
        g_both[rows] = grads
        grad_rows = dot(grads, w_all[:, : 2 * width], ((1,), (1,))).astype(BF)
        part_g[blocks] = grad_rows.reshape(16, SLOTS, MODEL_WIDTH)
        swap(part_g, sib_g, 1, part).start()

    scatter(0, 0)
    scatter(1, 0)
    scatter(0, 1)
    scatter(1, 1)
    loads[2].wait()
    loads[3].wait()
    hand_over(0, 0)
    settle(0, 0)
    forward_pass(0)
    hand_over(0, 1)
    swap(part_o, sib_o, 0, 0).wait()
    give(part_o, sib_o, out_ret, 0, 0)
    settle(0, 1)
    forward_pass(1)
    hand_over(1, 0)
    hand_over(1, 1)
    settle(1, 0)
    swap(part_o, sib_o, 0, 1).wait()
    give(part_o, sib_o, out_ret, 0, 1)
    backward_pass(0)
    settle(1, 1)
    swap(part_g, sib_g, 1, 0).wait()
    give(part_g, sib_g, grad_ret, 1, 0)
    backward_pass(1)
    swap(part_g, sib_g, 1, 1).wait()
    give(part_g, sib_g, grad_ret, 1, 1)

    def weight_grads(j, carry):
        cols = pl.ds(pl.multiple_of(j * 256, 256), 256)
        v_all[cols, : 2 * width] = dot(flat_rows(x_all[:, :, cols]), g_both[...], ((0,), (0,))).astype(BF)
        v_all[cols, 2 * width :] = dot(flat_rows(g_all[:, :, cols]), hidden[...], ((0,), (0,))).astype(BF)
        return carry

    lax.fori_loop(0, MODEL_WIDTH // 256, weight_grads, 0)
    store = pltpu.make_async_copy(v_all, d_all, o_sem)
    store.start()
    given(part_o, out_ret, 0)
    grad_out = cotangent[...].astype(F32)
    rows_out = [dot(hits[k].astype(BF), flat_rows(out_ret[...]), ((1,), (0,))) for k in range(2)]
    o_block[...] = (middle[...] + share[0] * rows_out[0] + share[1] * rows_out[1]).astype(BF)
    pairs = [jnp.sum(grad_out * rows, axis=1, keepdims=True) for rows in rows_out]
    mean = share[0] * pairs[0] + share[1] * pairs[1]
    grad_logits = sum(chosen[k] * (share[k] * (pairs[k] - mean)) for k in range(2))
    o_logits[...] = grad_logits
    o_moe[...] = moe_in[...]
    routed = sum(dot(part, flat_extra, ((1,), (1,))) for part in three_parts(grad_logits))
    given(part_g, grad_ret, 1)
    grad_moe = dot(both_hits, flat_rows(grad_ret[...]), ((1,), (0,))) + routed
    o_gain[...] = jnp.sum(grad_moe * middle[...] * inverse, axis=0, keepdims=True)
    grad_middle = grad_out + norm_backward(middle[...], inverse, gain, grad_moe)
    o_middle[...] = grad_middle
    branch = grad_middle.astype(BF)
    o_branch[...] = branch
    for core, weight in ((c, wh), (1 - c, ws)):
        heads = dot(weight[...].reshape(MODEL_WIDTH, Q_HALF), branch, ((0,), (1,))).astype(BF)
        o_heads[pl.ds(core * 4, 4)] = heads.reshape(4, HEAD_Q, ROWS)
    store.wait()


def experts(attn, tokens, extra, ids, cotangent, half_w, sib_w, cots, weights):
    rows = 32 * SLOTS
    width = weights.shape[1] // 3
    slots = (16, SLOTS, MODEL_WIDTH)
    flat = (ROWS, MODEL_WIDTH)
    low = jax.ShapeDtypeStruct(flat, BF)
    return pl.pallas_call(
        experts_kernel,
        out_shape=[
            low,
            jax.ShapeDtypeStruct(flat, F32),
            low,
            jax.ShapeDtypeStruct((8, HEAD_Q, ROWS), BF),
            low,
            jax.ShapeDtypeStruct((ROWS, 128), F32),
            jax.ShapeDtypeStruct((1, MODEL_WIDTH), F32),
            jax.ShapeDtypeStruct(weights.shape, BF),
        ],
        in_specs=[IN_VMEM] * 5 + [ANY] * 4,
        out_specs=[IN_VMEM] * 7 + [ANY],
        scratch_shapes=[
            pltpu.VMEM((32, SLOTS, MODEL_WIDTH), BF),
            pltpu.VMEM((32, SLOTS, 128), F32),
            pltpu.VMEM((32, SLOTS, MODEL_WIDTH), BF),
            pltpu.VMEM(weights.shape, BF),
            pltpu.VMEM((rows, width), F32),
            pltpu.VMEM((rows, width), F32),
            pltpu.VMEM((rows, width), BF),
            pltpu.VMEM((rows, 2 * width), BF),
            pltpu.VMEM((32, SLOTS, MODEL_WIDTH), BF),
            pltpu.VMEM((32, SLOTS, MODEL_WIDTH), BF),
            pltpu.VMEM((16, SLOTS, MODEL_WIDTH), BF),
            pltpu.VMEM((16, SLOTS, MODEL_WIDTH), BF),
            pltpu.VMEM(weights.shape, BF),
            pltpu.VMEM(half_w.shape, BF),
            pltpu.VMEM(half_w.shape, BF),
            pltpu.VMEM(slots, BF),
            pltpu.VMEM((EXPERT_COUNT, SLOTS, 128), F32),
            pltpu.VMEM(slots, BF),
            pltpu.VMEM(slots, BF),
            pltpu.VMEM(flat, F32),
            pltpu.VMEM(flat, BF),
            pltpu.SemaphoreType.DMA((4,)),
            pltpu.SemaphoreType.DMA((4,)),
            pltpu.SemaphoreType.DMA((2, 16)),
            pltpu.SemaphoreType.DMA((2, 16)),
            pltpu.SemaphoreType.DMA((2, 2)),
            pltpu.SemaphoreType.DMA((2, 2)),
            pltpu.SemaphoreType.DMA((2, 2)),
            pltpu.SemaphoreType.DMA((2, 2)),
            pltpu.SemaphoreType.DMA((2,)),
            pltpu.SemaphoreType.DMA((2,)),
            pltpu.SemaphoreType.DMA,
        ],
        compiler_params=params(6, 60 << 20),
        name="experts",
    )(attn, tokens, extra, ids, cotangent, half_w, sib_w, cots, weights)


SUMS = tuple((n, start, width, order[::-1]) for n, start, width, order in FIRST_PARTS) + tuple(
    (2, start, 256, order) for start, order in OUT_SUMS
)
LATE = len(FIRST_PARTS)


def reduce_kernel(
    gq_t, dkv, normed, moe_in, grad_logits, gain_m, s_out, pair, w_extra, grad_middle, w_q, w_kv,
    o_tokens, o_q, o_k, o_v, o_out, o_extra,
    v_q, v_kv, v_extra, wq, wkv, gkv, mine_part, give_part, sib_part, both, total, give, *rest,
):
    parts = len(SUMS)
    first_in, rest = rest[:LATE], rest[LATE:]
    arrive = [list(first_in) + [None] * 3, rest[:parts], rest[parts : 2 * parts]]
    rest = rest[2 * parts :]
    held = [None, list(rest[:LATE]) + [s_out.at[k] for k in range(3)], rest[LATE : LATE + parts]]
    l_sem, send, recv, sib_send, sib_recv = rest[LATE + parts :]
    grads = (v_q, v_kv, None, v_extra)
    y, z, x, c = coords()
    place = {"y": y, "z": z, "x": x}
    sibling = dev(y, z, x, 1 - c)
    loads = [pltpu.make_async_copy(w_q, wq, l_sem.at[0]), pltpu.make_async_copy(w_kv, wkv, l_sem.at[1])]
    for load in loads:
        load.start()
    for axis in ("x", "y", "z"):
        for step in STEPS:
            signal(axis_peer(axis, step))
    signal(sibling)
    pl.semaphore_wait(pltpu.get_barrier_semaphore(), 10)

    def at(phase, part, index):
        n, start, width, order = SUMS[part]
        spot = [
            index if axis == order[phase] else slice(None)
            for axis in ("y", "z", "x")
            if axis not in order[:phase]
        ]
        if phase == 0:
            return grads[n].at[tuple(spot) + (slice(None), pl.ds(start, width))]
        return held[phase][part].at[tuple(spot)]

    def copies_of(phase, part):
        axis = SUMS[part][3][phase]
        return [
            remote(
                at(phase, part, (place[axis] + step) % 4), arrive[phase][part].at[n],
                send.at[phase, part, n], recv.at[phase, part, n], axis_peer(axis, step),
            )
            for n, step in enumerate(STEPS)
        ]

    def begin(phase, part):
        for copy in copies_of(phase, part):
            copy.start()

    def finish(phase, part):
        for copy in copies_of(phase, part):
            copy.wait()
        array, start, width, order = SUMS[part]
        mine = at(phase, part, place[order[phase]])
        got = arrive[phase][part]
        if phase < 2:

            def add(p, carry):
                value = mine[p].astype(F32)
                for n in range(3):
                    value = value + got[n, p].astype(F32)
                held[phase + 1][part][p] = value.astype(BF)
                return carry

            lax.fori_loop(0, 4, add, 0)
        else:
            value = mine[...].astype(F32)
            for n in range(3):
                value = value + got[n].astype(F32)
            total[:, STARTS[array] + start : STARTS[array] + start + width] = value

    for part in range(LATE, parts):
        begin(1, part)
    for h in range(4):
        value = dkv[4 * h].astype(F32)
        for n in range(1, 4):
            value = value + dkv[4 * h + n].astype(F32)
        gkv[:, 128 * h : 128 * h + 128] = value.astype(BF)
    for n in range(4):
        left = normed[:, 384 * n : 384 * n + 384]
        v_q[n] = dot(left, gq_t[...], ((0,), (1,))).astype(BF).reshape(4, 4, 24, Q_HALF)
        v_kv[n] = dot(left, gkv[...], ((0,), (0,))).astype(BF).reshape(4, 4, 24, KV_HALF)
    for part in range(3):
        begin(0, part)

    for load in loads:
        load.wait()
    gain_sum = jnp.zeros((1, MODEL_WIDTH), F32)
    for n in range(2):
        core = 1 - c if n == 0 else c
        rows = pl.ds(pl.multiple_of(core * ROWS, ROWS), ROWS)
        part = dot(gq_t[:, rows], wq[...], ((0,), (1,))) + dot(gkv[rows], wkv[...], ((1,), (1,)))
        values = pair[rows].astype(F32)
        gain_sum = gain_sum + jnp.sum(part * values * inverse_rms(values), axis=0, keepdims=True)
        if n == 0:
            give_part[...] = part
            remote(give_part, sib_part, sib_send.at[0], sib_recv.at[0], sibling).start()
        else:
            mine_part[...] = part
    lane = lax.broadcasted_iota(jnp.int32, (MODEL_WIDTH, EXTRA), 1)
    extra = sum(dot(moe_in[...], part, ((0,), (0,))) for part in three_parts(grad_logits[...]))
    extra = jnp.where(lane == EXPERT_COUNT, column_of(gain_sum), extra)
    extra = jnp.where(lane == EXPERT_COUNT + 1, column_of(gain_m[...]), extra)
    gain = jnp.transpose(w_extra[...].reshape(MODEL_WIDTH, EXTRA).astype(F32))[EXPERT_COUNT : EXPERT_COUNT + 1]
    v_extra[...] = extra.astype(BF).reshape(4, 4, 4, 24, EXTRA)
    begin(0, 3)
    remote(give_part, sib_part, sib_send.at[0], sib_recv.at[0], sibling).wait()
    rows = pl.ds(pl.multiple_of(c * ROWS, ROWS), ROWS)
    values = pair[rows].astype(F32)
    o_tokens[...] = grad_middle[...] + norm_backward(
        values, inverse_rms(values), gain, mine_part[...] + sib_part[...]
    )

    for part in range(LATE, parts):
        finish(1, part)
        begin(2, part)
    for phase in range(3):
        for part in range(LATE):
            finish(phase, part)
            if phase < 2:
                begin(phase + 1, part)
    for part in range(LATE, parts):
        finish(2, part)
    low, high = total[0:12], total[12:24]
    both[c, 0:12] = jnp.where(c == 0, low, high)
    give[0:12] = jnp.where(c == 0, high, low)
    give[12:16] = jnp.zeros((4, PACK), F32)
    last = remote(give, both.at[c], sib_send.at[1], sib_recv.at[1], sibling)
    last.start()
    last.wait()
    keys, values = [], []
    for k in range(2):
        o_q[:, Q_HALF * k : Q_HALF * k + Q_HALF] = both[k, 0:12, :Q_HALF]
        o_out[:, Q_HALF * k : Q_HALF * k + Q_HALF] = both[k, 0:12, STARTS[2] : STARTS[3]]
        for h in range(4):
            first = STARTS[1] + 128 * h
            keys.append(both[k, 0:12, first : first + HD])
            values.append(both[k, 0:12, first + HD : first + 2 * HD])
    o_k[...] = jnp.concatenate(keys, axis=1)
    o_v[...] = jnp.concatenate(values, axis=1)
    o_extra[...] = both[0, 0:12, STARTS[3] :] + both[1, 0:12, STARTS[3] :]


def reduce_weights(*args):
    widths = [part[2] for part in SUMS]
    full = lambda width: pltpu.VMEM((4, 4, 4, 24, width), BF)
    rows = pltpu.VMEM((ROWS, MODEL_WIDTH), F32)
    scratch = (
        [full(Q_HALF), full(KV_HALF), full(EXTRA)]
        + [pltpu.VMEM((MODEL_WIDTH, Q_HALF), BF), pltpu.VMEM((MODEL_WIDTH, KV_HALF), BF)]
        + [pltpu.VMEM((PAIR, KV_HALF), BF), rows, rows, rows]
        + [pltpu.VMEM((2, 16, PACK), F32), pltpu.VMEM((24, PACK), F32), pltpu.VMEM((16, PACK), F32)]
        + [pltpu.VMEM((3, 4, 4, 24, w), BF) for w in widths[:LATE]]
        + [pltpu.VMEM((3, 4, 24, w), BF) for w in widths]
        + [pltpu.VMEM((3, 24, w), BF) for w in widths]
        + [pltpu.VMEM((4, 4, 24, w), BF) for w in widths[:LATE]]
        + [pltpu.VMEM((4, 24, w), BF) for w in widths]
    )
    sems = (3, len(SUMS), 3)
    shapes = ((ROWS, MODEL_WIDTH), (12, MODEL_WIDTH), (12, KV * HD), (12, KV * HD), (12, MODEL_WIDTH), (12, EXTRA))
    return pl.pallas_call(
        reduce_kernel,
        out_shape=[jax.ShapeDtypeStruct(shape, F32) for shape in shapes],
        in_specs=[IN_VMEM] * 10 + [ANY] * 2,
        out_specs=[IN_VMEM] * 6,
        scratch_shapes=scratch
        + [
            pltpu.SemaphoreType.DMA((2,)),
            pltpu.SemaphoreType.DMA(sems),
            pltpu.SemaphoreType.DMA(sems),
            pltpu.SemaphoreType.DMA((2,)),
            pltpu.SemaphoreType.DMA((2,)),
        ],
        compiler_params=params(8, 60 << 20),
        name="reduce_weights",
    )(*args)


def wide_greet():
    y, z, x, c = coords()
    me = z * 4 + x

    def greet(k, carry):
        t = (me + k) % 16
        signal(dev(y, t // 4, t % 4, c))
        return carry

    lax.fori_loop(1, 16, greet, 0)
    for step in STEPS:
        signal(axis_peer("y", step))
        signal(dev(y, (z + step) % 4, x, 1 - c))
    signal(dev(y, z, x, 1 - c))
    pl.semaphore_wait(pltpu.get_barrier_semaphore(), 22)


def attend_back_kernel(
    heads, branch, attn, q_in, kv_in, first_ref, ot_ref, lse_ref,
    dq_out, dkv_out, s_out,
    go, branch_sib, attn_sib, qs, gs, dq, dkv, dkv_low, dq_low,
    g_out, a_out,
    l_sem, h_send, h_recv, sib_send, sib_recv, q_send, q_recv, k_send, k_recv,
    w_send, w_recv,
):
    y, z, x, c = coords()
    me = z * 4 + x
    j = c * 4 + z
    sibling = dev(y, z, x, 1 - c)
    place = {"y": y, "z": z, "x": x}
    wide_greet()

    def push(k, carry):
        t = (j + k) % 8
        remote(heads.at[t], go.at[j], h_send, h_recv, dev(y, t % 4, x, t // 4)).start()
        return carry

    lax.fori_loop(1, 8, push, 0)
    one = remote(branch, branch_sib, sib_send.at[0], sib_recv.at[0], sibling)
    one.start()
    two = remote(attn.at[pl.ds((1 - c) * 4, 4)], attn_sib, sib_send.at[1], sib_recv.at[1], sibling)
    two.start()
    here = pltpu.make_async_copy(heads.at[j], go.at[j], l_sem.at[0])
    here.start()
    here.wait()
    drain = remote(go.at[pl.ds(0, 7)], go.at[pl.ds(0, 7)], h_send, h_recv, sibling)
    drain.wait_send()
    drain.wait_recv()
    one.wait()
    two.wait()

    rows_b = jnp.concatenate([branch[...], branch_sib[...]], axis=0)
    rows_a = jnp.concatenate(
        [part.reshape(Q_HALF, ROWS) for part in (attn[pl.ds(c * 4, 4)], attn_sib[...])], axis=1
    )
    for n in range(4):
        part = dot(rows_b[:, 384 * n : 384 * n + 384], rows_a, ((0,), (1,)))
        g_out[n] = part.astype(BF).reshape(4, 4, 24, Q_HALF)

    def spot(part, index):
        start, order = OUT_SUMS[part]
        cut = [index if axis == order[0] else slice(None) for axis in ("y", "z", "x")]
        return g_out.at[tuple(cut) + (slice(None), pl.ds(start, 256))]

    w_copies = []
    for part in range(3):
        axis = OUT_SUMS[part][1][0]
        for n, step in enumerate(STEPS):
            copy = remote(
                spot(part, (place[axis] + step) % 4), a_out.at[part, n],
                w_send.at[part, n], w_recv.at[part, n], axis_peer(axis, step),
            )
            copy.start()
            w_copies.append(copy)

    dkv[...] = jnp.zeros_like(dkv)
    qs[64:] = jnp.zeros((64, 3 * PAIR), BF)
    gs[:64] = jnp.zeros((64, 3 * PAIR), BF)
    for n in range(4):
        zq = 3 - n
        q = q_in[zq] * SCALE_QK
        grad = jnp.concatenate([go[zq], go[4 + zq]], axis=1)
        deltas, sums_log = [], []
        for h in range(3):
            cols = slice(256 * h, 256 * h + 256)
            rows = slice(64 * h, 64 * h + 64)
            qs[:64, cols] = q[rows]
            gs[64:, cols] = grad[rows]
            deltas.append(
                jnp.sum(grad[rows].astype(F32) * ot_ref[zq, :, cols], axis=0, keepdims=True)
            )
            sums_log.append(lse_ref[zq, :, cols])
        dq[...] = jnp.zeros_like(dq)
        first = first_ref[zq]
        hi = zq * 4 + x
        q_pos = hi * PAIR + lax.broadcasted_iota(jnp.int32, (1, PAIR), 1)

        def step(kb, carry):
            kv = kv_in[kb]
            k_pos = kb * PAIR + lax.broadcasted_iota(jnp.int32, (PAIR, PAIR), 0)
            ok = (k_pos >= first) & (k_pos <= q_pos)
            scores = [dot(kv, qs[:, 256 * h : 256 * h + 256], ((1,), (0,))) for h in range(3)]
            grad_probs = [dot(kv, gs[:, 256 * h : 256 * h + 256], ((1,), (0,))) for h in range(3)]
            grad_scores, probs = [], []
            for h in range(3):
                prob = jnp.where(ok, jnp.exp(scores[h] - sums_log[h]), 0.0)
                grad_scores.append((prob * (grad_probs[h] - deltas[h])).astype(BF))
                probs.append(prob.astype(BF))
            for h in range(3):
                cols = slice(256 * h, 256 * h + 256)
                dq[:, cols] = dq[:, cols] + dot(kv, grad_scores[h], ((0,), (0,)))
            dkv[kb] = (
                dkv[kb]
                + dot(jnp.concatenate(grad_scores, axis=1), qs[...], ((1,), (1,)))
                + dot(jnp.concatenate(probs, axis=1), gs[...], ((1,), (1,)))
            )
            return carry

        lax.fori_loop(0, hi + 1, step, 0)
        by_head = jnp.concatenate([dq[:64, 256 * h : 256 * h + 256] for h in range(3)], axis=0)
        dq_low[zq] = (by_head * SCALE_QK).astype(BF)
        away = (zq - z + 4) % 4

        @pl.when(away != 0)
        def _():
            remote(dq_low.at[zq], dq_out.at[z], q_send.at[away], q_recv.at[away], dev(y, zq, x, c)).start()

        @pl.when(away == 0)
        def _():
            pltpu.make_async_copy(dq_low.at[zq], dq_out.at[z], l_sem.at[1]).start()

        for xt in range(4):
            t = zq * 4 + xt
            dkv_low[t] = dkv[t].astype(BF)

            @pl.when(t != me)
            def _():
                remote(dkv_low.at[t], dkv_out.at[me], k_send, k_recv, dev(y, zq, xt, c)).start()

            @pl.when(t == me)
            def _():
                pltpu.make_async_copy(dkv_low.at[t], dkv_out.at[me], l_sem.at[2]).start()


    for copy in w_copies:
        copy.wait()
    for part in range(3):
        mine = spot(part, place[OUT_SUMS[part][1][0]])

        def add(p, carry):
            value = mine[p].astype(F32)
            for k in range(3):
                value = value + a_out[part, k, p].astype(F32)
            s_out[part, p] = value.astype(BF)
            return carry

        lax.fori_loop(0, 4, add, 0)
    pltpu.make_async_copy(dq_low.at[z], dq_out.at[z], l_sem.at[1]).wait()
    pltpu.make_async_copy(dkv_low.at[me], dkv_out.at[me], l_sem.at[2]).wait()
    for k in range(1, 4):
        done = remote(dq_low.at[0], dq_out.at[0], q_send.at[k], q_recv.at[k], sibling)
        done.wait_send()
        done.wait_recv()
    drain = remote(dkv_out.at[pl.ds(0, 15)], dkv_out.at[pl.ds(0, 15)], k_send, k_recv, sibling)
    drain.wait_send()
    drain.wait_recv()


def attend_back(heads, branch, attn, q_in, kv_in, first, ot, lse):
    return pl.pallas_call(
        attend_back_kernel,
        out_shape=[
            jax.ShapeDtypeStruct((4, HEAD_Q, PAIR), BF),
            jax.ShapeDtypeStruct((16, PAIR, 128), BF),
            jax.ShapeDtypeStruct((3, 4, 4, 24, 256), BF),
        ],
        in_specs=[ANY] + [IN_VMEM] * 7,
        out_specs=[ANY, ANY, IN_VMEM],
        scratch_shapes=[
            pltpu.VMEM((8, HEAD_Q, ROWS), BF),
            pltpu.VMEM((ROWS, MODEL_WIDTH), BF),
            pltpu.VMEM((4, HEAD_Q, ROWS), BF),
            pltpu.VMEM((128, 3 * PAIR), BF),
            pltpu.VMEM((128, 3 * PAIR), BF),
            pltpu.VMEM((128, 3 * PAIR), F32),
            pltpu.VMEM((16, PAIR, 128), F32),
            pltpu.VMEM((16, PAIR, 128), BF),
            pltpu.VMEM((4, HEAD_Q, PAIR), BF),
            pltpu.VMEM((4, 4, 4, 24, Q_HALF), BF),
            pltpu.VMEM((3, 3, 4, 4, 24, 256), BF),
            pltpu.SemaphoreType.DMA((3,)),
            pltpu.SemaphoreType.DMA,
            pltpu.SemaphoreType.DMA,
            pltpu.SemaphoreType.DMA((2,)),
            pltpu.SemaphoreType.DMA((2,)),
            pltpu.SemaphoreType.DMA((4,)),
            pltpu.SemaphoreType.DMA((4,)),
            pltpu.SemaphoreType.DMA,
            pltpu.SemaphoreType.DMA,
            pltpu.SemaphoreType.DMA((3, 3)),
            pltpu.SemaphoreType.DMA((3, 3)),
        ],
        compiler_params=params(4, 60 << 20),
        name="attend_back",
    )(heads, branch, attn, q_in, kv_in, first, ot, lse)


def inverse_rms(values):
    return lax.rsqrt(jnp.mean(values * values, axis=-1, keepdims=True) + EPS)


def norm_backward(values, inverse, gain, grad_out):
    scaled = grad_out * gain
    return inverse * scaled - values * inverse**3 * jnp.mean(values * scaled, axis=-1, keepdims=True)


def local(
    tokens,
    segment_ids,
    expert_ids,
    w_query,
    w_key,
    w_value,
    w_out,
    w_router,
    gain_attn,
    gain_moe,
    w_gate,
    w_up,
    w_down,
    cotangent,
):
    width = w_gate.shape[1]
    ids = expert_ids.T
    part_q, part_kv, part_out, part_extra, pair, normed, w_experts, q4, keys_values, first, cot_slots = (
        gather_weights(
            (w_query, w_key, w_value, w_out.T, w_router, gain_attn[None], gain_moe[None], ids, cotangent),
            (tokens, segment_ids, w_gate, w_up, w_down),
        )
    )
    full_experts = lax.all_gather(w_experts, "dp", axis=0, tiled=True)
    q_in, kv_in, attn, attn_t, lse, half_out, sib_out, cot_all = attend(
        q4, keys_values, part_out, cot_slots, first
    )
    block_out, grad_middle, branch, grad_heads, moe_in, grad_logits, gain_sum, grad_experts = experts(
        attn, tokens, part_extra, ids, cotangent, half_out, sib_out, cot_all, full_experts
    )
    sum_experts = lax.psum_scatter(grad_experts, "dp", scatter_dimension=0, tiled=True)
    dq_in, dkv_in, sum_out = attend_back(grad_heads, branch, attn, q_in, kv_in, first, attn_t, lse)
    grad_tokens, r_query, r_key, r_value, r_out, r_extra = reduce_weights(
        dq_in.reshape(Q_HALF, PAIR), dkv_in, normed, moe_in, grad_logits, gain_sum, sum_out,
        pair.reshape(PAIR, MODEL_WIDTH), part_extra, grad_middle,
        part_q.reshape(MODEL_WIDTH, Q_HALF), part_kv.reshape(MODEL_WIDTH, KV_HALF),
    )
    return (
        block_out,
        grad_tokens,
        r_query,
        r_key,
        r_value,
        r_out.T,
        r_extra[:, :EXPERT_COUNT],
        r_extra[:, EXPERT_COUNT],
        r_extra[:, EXPERT_COUNT + 1],
        sum_experts[:, :width].astype(F32),
        sum_experts[:, width : 2 * width].astype(F32),
        sum_experts[:, 2 * width :].astype(F32).T,
    )


def solution(mesh):
    rows, flat, dense = P(("dp", "ctx"), None), P(("dp", "ctx")), P("dp", "ctx")
    placed = (
        rows, dense, rows, rows, rows, rows, P(None, ("dp", "ctx")), rows, flat, flat,
        dense, dense, P("ctx", "dp"), rows,
    )
    return jax.shard_map(
        local,
        mesh=mesh,
        in_specs=placed,
        out_specs=(
            rows, rows, rows, rows, rows, P(None, ("dp", "ctx")), rows, flat, flat,
            dense, dense, P("ctx", "dp"),
        ),
        check_vma=False,
    )
```

```python
import functools

import jax
import jax.numpy as jnp
from jax import lax
from jax.experimental import pallas as pl
from jax.experimental.pallas import tpu as pltpu
from jax.sharding import PartitionSpec as P

MODEL_WIDTH = 1536
KV = 8
HD = 64
EXPERT_COUNT = 16
FF = 1024
EXPERT_CAPACITY = 20
SLOTS = 24
ROWS = 128
PAIR = 256
HEAD_Q = 192
Q_HALF = 768
KV_HALF = 512
EXTRA = 128
PACK = Q_HALF + KV_HALF + EXTRA + Q_HALF

EPS = 1e-05
SCALE_QK = 0.125
NEGATIVE = -1e30
MESH = pl.DeviceIdType.MESH
ANY = pl.BlockSpec(memory_space=pl.ANY)
IN_VMEM = pl.BlockSpec(memory_space=pltpu.VMEM)
BF = jnp.bfloat16
F32 = jnp.float32


def dot(a, b, dims):
    return lax.dot_general(a, b, (dims, ((), ())), preferred_element_type=F32)


def coords():
    i = lax.axis_index("ctx")
    return lax.axis_index("dp"), i // 8, (i // 2) % 4, i % 2


def dev(y, z, x, c):
    return (y, z * 8 + x * 2 + c)


def signal(target):
    pl.semaphore_signal(
        pltpu.get_barrier_semaphore(), inc=1, device_id=target, device_id_type=MESH
    )


def remote(src, dst, send, recv, target):
    return pltpu.make_async_remote_copy(
        src_ref=src, dst_ref=dst, send_sem=send, recv_sem=recv, device_id=target, device_id_type=MESH
    )


def params(cid, vmem=None):
    return pltpu.CompilerParams(collective_id=cid, has_side_effects=True, vmem_limit_bytes=vmem)


def axis_peer(axis, step):
    y, z, x, c = coords()
    if axis == "y":
        return dev((y + step) % 4, z, x, c)
    if axis == "z":
        return dev(y, (z + step) % 4, x, c)
    return dev(y, z, (x + step) % 4, c)


WIDTHS = (Q_HALF, KV_HALF, Q_HALF, EXTRA)
STARTS = (0, Q_HALF, Q_HALF + KV_HALF, 2 * Q_HALF + KV_HALF)
STEPS = (1, 3, 2)
FIRST_PARTS = (
    (0, 0, 512, ("x", "z", "y")),
    (1, 0, 512, ("y", "x", "z")),
    (0, 512, 256, ("z", "y", "x")),
    (3, 0, 128, ("z", "y", "x")),
)
OUT_PARTS = (
    (2, 0, 128, ("z", "x", "y")),
    (2, 128, 384, ("z", "y", "x")),
    (2, 512, 256, ("y", "x", "z")),
)
OUT_SUMS = ((0, ("x", "y", "z")), (256, ("x", "z", "y")), (512, ("z", "x", "y")))
GATHER_PARTS = FIRST_PARTS + OUT_PARTS


def slab(ref, done, y, z, x, cols):
    return ref.at[
        slice(None) if "y" in done else y,
        slice(None) if "z" in done else z,
        slice(None) if "x" in done else x,
        slice(None),
        cols,
    ]


def column_of(row):
    return jnp.transpose(jnp.broadcast_to(row, (128, row.shape[1])))


def slot_hits(ids):
    lane = lax.broadcasted_iota(jnp.int32, (ROWS, 128), 1).astype(F32)
    experts_of = [column_of(ids[k : k + 1].astype(F32)) for k in range(2)]
    chosen = [jnp.where(lane == expert, 1.0, 0.0) for expert in experts_of]
    row = lax.broadcasted_iota(jnp.int32, (ROWS, ROWS), 0)
    earlier = jnp.where(row > lax.broadcasted_iota(jnp.int32, (ROWS, ROWS), 1), 1.0, 0.0).astype(BF)
    before = dot(earlier, (chosen[0] + chosen[1]).astype(BF), ((1,), (0,)))
    slot_lane = lax.broadcasted_iota(jnp.int32, (ROWS, EXPERT_COUNT * SLOTS), 1).astype(F32)
    hits = []
    for k in range(2):
        place = jnp.sum(chosen[k] * before, axis=1, keepdims=True)
        slot = jnp.where(place < EXPERT_CAPACITY, experts_of[k][:, :1] * SLOTS + place, -1.0)
        hits.append(jnp.where(slot_lane == slot, 1.0, 0.0))
    return chosen, hits


def three_parts(values):
    parts = []
    for _ in range(3):
        part = values.astype(BF)
        parts.append(part)
        values = values - part.astype(F32)
    return parts


def gather_kernel(
    w_query, w_key, w_value, w_out, w_router, gain_a, gain_m, ids, cots, tokens, segs, w_gate, w_up, w_down,
    o_q, o_kv, out2, out3, pair, o_normed, w_experts, q4, kv2, o_first, cot_slots,
    pack, sib, block, w_q, w_kv, w_extra, rows, segments, normed, packed, down,
    p_send, p_recv, l_sem, s_send, s_recv, sib_send, sib_recv, o_sem,
):
    y, z, x, c = coords()
    outs = (w_q, w_kv, out2, w_extra)
    me = z * 8 + x * 2 + c
    sibling = dev(y, z, x, 1 - c)

    def greet(k, carry):
        signal((y, (me + k) % 32))
        return carry

    lax.fori_loop(1, 32, greet, 0)
    for step in STEPS:
        signal(axis_peer("y", step))
    expert_loads = [
        pltpu.make_async_copy(w_gate, packed.at[:, 0:FF // 2], o_sem.at[5]),
        pltpu.make_async_copy(w_up, packed.at[:, FF // 2 : FF], o_sem.at[6]),
        pltpu.make_async_copy(w_down, down, o_sem.at[7]),
    ]
    for load in expert_loads:
        load.start()
    lane = lax.broadcasted_iota(jnp.int32, (12, EXTRA), 1)
    square = lax.broadcasted_iota(jnp.int32, (12, 12), 0) == lax.broadcasted_iota(jnp.int32, (12, 12), 1)
    extra = jnp.concatenate(
        [w_router[...].astype(F32), jnp.zeros((12, EXTRA - EXPERT_COUNT), F32)], axis=1
    )
    for k, gain_row in enumerate((gain_a, gain_m)):
        spread_row = jnp.broadcast_to(gain_row[...].astype(F32), (12, 12))
        column = jnp.sum(jnp.where(square, spread_row, 0.0), axis=1, keepdims=True)
        extra = jnp.where(lane == EXPERT_COUNT + k, column, extra)
    extra = extra.astype(BF)
    heads = []
    for h in range(KV):
        cols = slice(HD * h, HD * h + HD)
        heads += [w_key[:, cols].astype(F32), w_value[:, cols].astype(F32)]
    heads = jnp.concatenate(heads, axis=1).astype(BF)
    for k in range(2):
        parts = (
            w_query[:, Q_HALF * k : Q_HALF * k + Q_HALF],
            heads[:, KV_HALF * k : KV_HALF * k + KV_HALF],
            w_out[:, Q_HALF * k : Q_HALF * k + Q_HALF],
            extra,
        )
        for start, width, part in zip(STARTS, WIDTHS, parts):
            pack[k, 0:12, start : start + width] = part
            pack[k, 12:16, start : start + width] = jnp.zeros((4, width), BF)
    pl.semaphore_wait(pltpu.get_barrier_semaphore(), 34)

    first = remote(pack.at[1 - c], sib, sib_send.at[0], sib_recv.at[0], sibling)
    first.start()
    second = remote(tokens, rows.at[c], sib_send.at[1], sib_recv.at[1], sibling)
    second.start()
    own_rows = pltpu.make_async_copy(tokens, rows.at[c], l_sem.at[4])
    own_rows.start()
    own_segs = pltpu.make_async_copy(segs, segments.at[me], l_sem.at[5])
    own_segs.start()

    def spread(k, carry):
        remote(segs, segments.at[me], s_send, s_recv, (y, (me + k) % 32)).start()
        return carry

    lax.fori_loop(1, 32, spread, 0)

    first.wait()
    own = pack[c, :12].astype(F32)
    other = sib[:12].astype(F32)
    low = jnp.where(c == 0, own, other)
    high = jnp.where(c == 0, other, own)
    block[...] = jnp.concatenate([low, high], axis=0).astype(BF)

    locals_ = []
    for n in range(4):
        cols = pl.ds(STARTS[n], WIDTHS[n])
        here = pltpu.make_async_copy(block.at[:, cols], outs[n].at[y, z, x], l_sem.at[n])
        here.start()
        locals_.append(here)
    for phase in range(3):
        copies = []
        for part, (n, start, width, order) in enumerate(GATHER_PARTS if phase < 2 else FIRST_PARTS):
            for k, step in enumerate(STEPS):
                dst = slab(outs[n], order[:phase], y, z, x, pl.ds(start, width))
                src = block.at[:, pl.ds(STARTS[n] + start, width)] if phase == 0 else dst
                copy = remote(
                    src, dst, p_send.at[phase, part, k], p_recv.at[phase, part, k],
                    axis_peer(order[phase], step),
                )
                copy.start()
                copies.append(copy)
        if phase == 0:
            for here in locals_:
                here.wait()
        if phase == 2:
            own_segs.wait()
            drain = remote(
                segments.at[pl.ds(0, 31)], segments.at[pl.ds(0, 31)], s_send, s_recv, sibling
            )
            drain.wait_send()
            drain.wait_recv()
            places = segments[...].reshape(32, 128)
            for zq in range(4):
                t = (zq * 4 + x) * 2
                mine = jnp.concatenate([segments[t], segments[t + 1]], axis=1)
                begin = jnp.zeros((1, PAIR), jnp.int32)
                for u in range(15):
                    count = jnp.sum((places == u).astype(jnp.int32))
                    begin = begin + jnp.where(mine > u, count, 0)
                o_first[zq] = begin
            chosen, hits = slot_hits(ids[...])
            kept = dot((hits[0] + hits[1]).astype(BF), cots[...], ((0,), (0,))).astype(BF)
            cot_slots[...] = kept.reshape(EXPERT_COUNT, SLOTS, MODEL_WIDTH)
            for load in expert_loads:
                load.wait()
            packed[:, FF:] = jnp.transpose(down[...].astype(F32)).astype(BF)
            pltpu.make_async_copy(packed, w_experts, o_sem.at[5]).start()
            second.wait()
            own_rows.wait()
        for copy in copies:
            copy.wait()
    stores = [
        pltpu.make_async_copy(src, dst, o_sem.at[n])
        for n, (src, dst) in enumerate(((w_q, o_q), (w_kv, o_kv), (w_extra, out3), (rows, pair)))
    ]
    for store in stores:
        store.start()
    gain = jnp.transpose(w_extra[...].reshape(MODEL_WIDTH, EXTRA).astype(F32))[EXPERT_COUNT : EXPERT_COUNT + 1]
    for k in range(2):
        values = rows[k].astype(F32)
        normed[ROWS * k : ROWS * k + ROWS] = (values * inverse_rms(values) * gain).astype(BF)
    last = pltpu.make_async_copy(normed, o_normed, o_sem.at[4])
    last.start()
    queries = dot(w_q[...].reshape(MODEL_WIDTH, Q_HALF), normed[...], ((0,), (1,))).astype(BF)
    q4[...] = queries.reshape(4, HEAD_Q, PAIR)
    kv2[...] = dot(normed[...], w_kv[...].reshape(MODEL_WIDTH, KV_HALF), ((1,), (0,))).astype(BF)
    for store in stores:
        store.wait()
    last.wait()
    pltpu.make_async_copy(packed, w_experts, o_sem.at[5]).wait()


def gather_weights(vmem_args, hbm_args):
    blocks = [(4, 4, 4, 24, width) for width in WIDTHS]
    rows = (2, ROWS, MODEL_WIDTH)
    flat = (PAIR, MODEL_WIDTH)
    experts_in = (MODEL_WIDTH // 4, 3 * FF // 2)
    return pl.pallas_call(
        gather_kernel,
        out_shape=[jax.ShapeDtypeStruct(shape, BF) for shape in (*blocks, rows, flat, experts_in)]
        + [
            jax.ShapeDtypeStruct((4, HEAD_Q, PAIR), BF),
            jax.ShapeDtypeStruct((PAIR, KV_HALF), BF),
            jax.ShapeDtypeStruct((4, 1, PAIR), jnp.int32),
            jax.ShapeDtypeStruct((EXPERT_COUNT, SLOTS, MODEL_WIDTH), BF),
        ],
        in_specs=[IN_VMEM] * len(vmem_args) + [ANY] * len(hbm_args),
        out_specs=[ANY] * 7 + [IN_VMEM] * 4,
        scratch_shapes=[
            pltpu.VMEM((2, 16, PACK), BF),
            pltpu.VMEM((16, PACK), BF),
            pltpu.VMEM((24, PACK), BF),
            pltpu.VMEM(blocks[0], BF),
            pltpu.VMEM(blocks[1], BF),
            pltpu.VMEM(blocks[3], BF),
            pltpu.VMEM(rows, BF),
            pltpu.VMEM((32, 1, 128), jnp.int32),
            pltpu.VMEM(flat, BF),
            pltpu.VMEM(experts_in, BF),
            pltpu.VMEM((FF // 2, MODEL_WIDTH // 4), BF),
            pltpu.SemaphoreType.DMA((3, 7, 3)),
            pltpu.SemaphoreType.DMA((3, 7, 3)),
            pltpu.SemaphoreType.DMA((6,)),
            pltpu.SemaphoreType.DMA,
            pltpu.SemaphoreType.DMA,
            pltpu.SemaphoreType.DMA((2,)),
            pltpu.SemaphoreType.DMA((2,)),
            pltpu.SemaphoreType.DMA((8,)),
        ],
        compiler_params=params(1, 60 << 20),
        name="gather_weights",
    )(*vmem_args, *hbm_args)


def offset(k):
    dz = (k % 8) // 2
    return dz, 2 * (k % 2) + (dz + k // 8) % 2


def chip_to(k):
    y, z, x, c = coords()
    dz, dx = offset(k)
    return (z + dz) % 4, (x + dx) % 4


def chip_from(k):
    y, z, x, c = coords()
    dz, dx = offset(k)
    return (z + 4 - dz) % 4, (x + 4 - dx) % 4


def slot_block(k, core):
    return (k // 8) * 16 + core * 8 + k % 8


def plane_greet():
    y, z, x, c = coords()
    me = z * 4 + x

    def greet(k, carry):
        t = (me + k) % 16
        signal(dev(y, t // 4, t % 4, c))
        return carry

    lax.fori_loop(1, 16, greet, 0)
    signal(dev(y, z, x, 1 - c))


KEYS = 1024


def attend_kernel(
    q4, kv2, half_in, cots, first_ref, q_out, kv_out, attn, ot_out, lse_ref, half, half_sib, c_all,
    q_in, kv_in, ot_ref, qs, acc, o_buf, keep,
    l_sem, q_send, q_recv, k_send, k_recv, w_send, w_recv, sib_send, sib_recv,
    c_send, c_recv, f_send, f_recv, o_send, o_recv,
):
    y, z, x, c = coords()
    me = z * 4 + x
    sibling = dev(y, z, x, 1 - c)

    wide_greet()

    q_copies = []
    for n, step in enumerate(STEPS):
        to = (z + step) % 4
        copy = remote(q4.at[to], q_in.at[z], q_send.at[n], q_recv.at[n], dev(y, to, x, c))
        copy.start()
        q_copies.append(copy)

    def head(index):
        return kv2.at[:, pl.ds(pl.multiple_of(index * 128, 128), 128)]

    def send_kv(k, carry):
        t = (me + k) % 16
        remote(head(t // 4), kv_in.at[me], k_send, k_recv, dev(y, t // 4, t % 4, c)).start()
        return carry

    lax.fori_loop(1, 16, send_kv, 0)
    here = [
        pltpu.make_async_copy(q4.at[z], q_in.at[z], l_sem.at[0]),
        pltpu.make_async_copy(head(z), kv_in.at[me], l_sem.at[1]),
    ]
    for copy in here:
        copy.start()
    for copy in here:
        copy.wait()
    for copy in q_copies:
        copy.wait()
    drain = remote(kv_in.at[pl.ds(0, 15)], kv_in.at[pl.ds(0, 15)], k_send, k_recv, sibling)
    drain.wait_send()
    drain.wait_recv()

    w_copies = [[], [], []]
    for part, (n, start, width, order) in enumerate(OUT_PARTS):
        spot = slab(half, order[:2], y, z, x, pl.ds(start, width))
        for k, step in enumerate(STEPS):
            copy = remote(
                spot, spot, w_send.at[part, k], w_recv.at[part, k], axis_peer(order[2], step)
            )
            copy.start()
            w_copies[part].append(copy)

    kept = [
        pltpu.make_async_copy(q_in, q_out, keep.at[4]),
        pltpu.make_async_copy(kv_in, kv_out, keep.at[5]),
    ]
    for copy in kept:
        copy.start()

    def cots_copy(k):
        tz, tx = chip_to(k)
        return remote(
            cots.at[tz * 4 + tx], c_all.at[slot_block(k, c)], c_send.at[k], c_recv.at[k], dev(y, tz, tx, c)
        )

    def send_cots(k, carry):
        cots_copy(k).start()
        return carry

    lax.fori_loop(1, 16, send_cots, 0)
    own_cots = pltpu.make_async_copy(cots.at[me], c_all.at[slot_block(0, c)], l_sem.at[2])
    own_cots.start()
    remote(cots.at[me], c_all.at[slot_block(0, c)], f_send, f_recv, sibling).start()

    def forward_cots(k, carry):
        arrived = cots_copy(k)
        arrived.wait_recv()
        remote(c_all.at[slot_block(k, c)], c_all.at[slot_block(k, c)], f_send, f_recv, sibling).start()
        arrived.wait_send()
        return carry

    def swap(part):
        start, width = OUT_PARTS[part][1:3]
        cols = half.at[:, :, :, :, pl.ds(start, width)]
        there = half_sib.at[:, :, :, :, pl.ds(start, width)]
        return remote(cols, there, sib_send.at[part], sib_recv.at[part], sibling)

    j = c * 4 + z
    qs[64:] = jnp.zeros((64, 3 * PAIR), BF)
    returns = []
    for n in range(4):
        zq = (z + n + 1) % 4
        q = q_in[zq] * SCALE_QK
        for h in range(3):
            qs[:64, 256 * h : 256 * h + 256] = q[64 * h : 64 * h + 64]
        acc[...] = jnp.zeros_like(acc)
        first = first_ref[zq]
        q_pos = (zq * 4 + x) * PAIR + lax.broadcasted_iota(jnp.int32, (1, PAIR), 1)

        def step(kb, stats):
            kv = kv_in[pl.ds(kb * (KEYS // PAIR), KEYS // PAIR)].reshape(KEYS, 128)
            k_pos = kb * KEYS + lax.broadcasted_iota(jnp.int32, (KEYS, PAIR), 0)
            ok = (k_pos >= first) & (k_pos <= q_pos)
            scores = [dot(kv, qs[:, 256 * h : 256 * h + 256], ((1,), (0,))) for h in range(3)]
            later, probs, shrinks = [], [], []
            for h in range(3):
                top, tot = stats[h]
                masked = jnp.where(ok, scores[h], NEGATIVE)
                new = jnp.maximum(top, jnp.max(masked, axis=0, keepdims=True))
                prob = jnp.exp(masked - new)
                shrink = jnp.exp(top - new)
                later.append((new, tot * shrink + jnp.sum(prob, axis=0, keepdims=True)))
                probs.append(prob.astype(BF))
                shrinks.append(shrink)
            for h in range(3):
                cols = slice(256 * h, 256 * h + 256)
                acc[:, cols] = acc[:, cols] * shrinks[h] + dot(kv, probs[h], ((0,), (0,)))
            return tuple(later)

        none = (jnp.full((1, PAIR), NEGATIVE, F32), jnp.zeros((1, PAIR), F32))
        stats = lax.fori_loop(0, zq + 1, step, (none, none, none))
        heads = []
        for h in range(3):
            cols = slice(256 * h, 256 * h + 256)
            mixed = acc[64:, cols] / stats[h][1]
            ot_ref[zq, :, cols] = mixed
            lse_ref[zq, :, cols] = stats[h][0] + jnp.log(stats[h][1])
            heads.append(mixed)
        heads = jnp.concatenate(heads, axis=0).astype(BF)
        saved = pltpu.make_async_copy(ot_ref.at[zq], ot_out.at[zq], keep.at[n])
        saved.start()
        kept.append(saved)
        o_buf[n, 0] = heads[:, :ROWS]
        o_buf[n, 1] = heads[:, ROWS:]
        for d in range(2):
            core = c if d == 0 else 1 - c
            if n == 3 and d == 0:
                back = pltpu.make_async_copy(o_buf.at[n, core], attn.at[j], l_sem.at[3])
            else:
                back = remote(
                    o_buf.at[n, core], attn.at[j], o_send.at[n, d], o_recv.at[n, d], dev(y, zq, x, core)
                )
            back.start()
            returns.append(back)
    for part in (0, 2, 1):
        for copy in w_copies[part]:
            copy.wait()
        swap(part).start()
        if part == 0:
            lax.fori_loop(1, 16, forward_cots, 0)
    own_cots.wait()
    mine = c_all.at[pl.ds(c * 16, 16)]
    drain = remote(mine, mine, f_send, f_recv, sibling)
    drain.wait_send()
    drain.wait_recv()
    for part in range(3):
        swap(part).wait()
    for back in returns + kept:
        back.wait()


def attend(q4, kv2, half, cots, first):
    blocks = jax.ShapeDtypeStruct((4, 4, 4, 24, Q_HALF), BF)
    return pl.pallas_call(
        attend_kernel,
        out_shape=[
            jax.ShapeDtypeStruct((4, HEAD_Q, PAIR), BF),
            jax.ShapeDtypeStruct((16, PAIR, 128), BF),
            jax.ShapeDtypeStruct((8, HEAD_Q, ROWS), BF),
            jax.ShapeDtypeStruct((4, HD, 3 * PAIR), F32),
            jax.ShapeDtypeStruct((4, 1, 3 * PAIR), F32),
            blocks,
            blocks,
            jax.ShapeDtypeStruct((32, SLOTS, MODEL_WIDTH), BF),
        ],
        in_specs=[ANY, ANY, ANY, ANY, IN_VMEM],
        out_specs=[ANY, ANY, ANY, ANY, IN_VMEM, ANY, ANY, ANY],
        input_output_aliases={2: 5},
        scratch_shapes=[
            pltpu.VMEM((4, HEAD_Q, PAIR), BF),
            pltpu.VMEM((16, PAIR, 128), BF),
            pltpu.VMEM((4, HD, 3 * PAIR), F32),
            pltpu.VMEM((128, 3 * PAIR), BF),
            pltpu.VMEM((128, 3 * PAIR), F32),
            pltpu.VMEM((4, 2, HEAD_Q, ROWS), BF),
            pltpu.SemaphoreType.DMA((6,)),
            pltpu.SemaphoreType.DMA((4,)),
            pltpu.SemaphoreType.DMA((3,)),
            pltpu.SemaphoreType.DMA((3,)),
            pltpu.SemaphoreType.DMA,
            pltpu.SemaphoreType.DMA,
            pltpu.SemaphoreType.DMA((3, 3)),
            pltpu.SemaphoreType.DMA((3, 3)),
            pltpu.SemaphoreType.DMA((3,)),
            pltpu.SemaphoreType.DMA((3,)),
            pltpu.SemaphoreType.DMA((16,)),
            pltpu.SemaphoreType.DMA((16,)),
            pltpu.SemaphoreType.DMA,
            pltpu.SemaphoreType.DMA,
            pltpu.SemaphoreType.DMA((4, 2)),
            pltpu.SemaphoreType.DMA((4, 2)),
        ],
        compiler_params=params(2, 60 << 20),
        name="attend",
    )(q4, kv2, half, cots, first)


def flat_rows(blocks):
    return blocks.reshape(blocks.shape[0] * SLOTS, blocks.shape[2])


def experts_kernel(
    attn, tokens, extra, ids, cotangent, half_w, sib_w, cots, weights,
    o_block, o_middle, o_branch, o_heads, o_moe, o_logits, o_gain, d_all,
    x_all, t_all, g_all, w_all, gate_v, up_v, hidden, g_both, part_o, part_g, sib_o, sib_g,
    v_all, wh, ws, xs, gates, out_ret, grad_ret, middle, moe_in,
    w_sem, l_sem, send, recv, f_send, f_recv, s_send, s_recv, r_send, r_recv, o_sem,
):
    y, z, x, c = coords()
    me = z * 4 + x
    width = hidden.shape[1]
    sibling = dev(y, z, x, 1 - c)
    loads = [
        pltpu.make_async_copy(src, dst, w_sem.at[n])
        for n, (src, dst) in enumerate(((half_w, wh), (sib_w, ws), (weights, w_all), (cots, g_all)))
    ]
    plane_greet()
    for load in loads:
        load.start()
    chosen, hits = slot_hits(ids[...])
    both_hits = (hits[0] + hits[1]).astype(BF)
    flat_extra = extra[...].reshape(MODEL_WIDTH, EXTRA)
    gain = jnp.transpose(flat_extra.astype(F32))[EXPERT_COUNT + 1 : EXPERT_COUNT + 2]
    own = attn[pl.ds(c * 4, 4)].reshape(Q_HALF, ROWS)
    other = attn[pl.ds((1 - c) * 4, 4)].reshape(Q_HALF, ROWS)
    loads[0].wait()
    loads[1].wait()
    middle[...] = (
        tokens[...].astype(F32)
        + dot(own, wh[...].reshape(MODEL_WIDTH, Q_HALF), ((0,), (1,)))
        + dot(other, ws[...].reshape(MODEL_WIDTH, Q_HALF), ((0,), (1,)))
    )
    inverse = inverse_rms(middle[...])
    moe_in[...] = (middle[...] * inverse * gain).astype(BF)
    logits = dot(moe_in[...], flat_extra, ((1,), (0,)))
    picked = [jnp.sum(chosen[k] * logits, axis=1, keepdims=True) for k in range(2)]
    most = jnp.maximum(picked[0], picked[1])
    lifted = [jnp.exp(value - most) for value in picked]
    share = [value / (lifted[0] + lifted[1]) for value in lifted]
    slots_in = dot(both_hits, moe_in[...], ((0,), (0,))).astype(BF)
    xs[...] = slots_in.reshape(EXPERT_COUNT, SLOTS, MODEL_WIDTH)
    slot_gate = jnp.sum(hits[0] * share[0] + hits[1] * share[1], axis=0, keepdims=True)
    gates[...] = column_of(slot_gate).reshape(EXPERT_COUNT, SLOTS, 128)
    pl.semaphore_wait(pltpu.get_barrier_semaphore(), 16)
    arrays = ((xs, x_all), (gates, t_all))

    def arriving(a, k):
        src, dst = arrays[a]
        tz, tx = chip_to(k)
        return remote(
            src.at[tz * 4 + tx], dst.at[slot_block(k, c)], send.at[a, k], recv.at[a, k], dev(y, tz, tx, c)
        )

    def steps_of(part):
        return (1, 8) if part == 0 else (8, 16)

    def scatter(a, part):
        def push(k, carry):
            arriving(a, k).start()
            return carry

        lax.fori_loop(*steps_of(part), push, 0)
        if part == 0:
            src, dst = arrays[a]
            pltpu.make_async_copy(src.at[me], dst.at[slot_block(0, c)], l_sem.at[a]).start()
            remote(src.at[me], dst.at[slot_block(0, c)], f_send.at[a, 0], f_recv.at[a, 0], sibling).start()

    def hand_over(a, part):
        src, dst = arrays[a]

        def forward(k, carry):
            arrived = arriving(a, k)
            arrived.wait_recv()
            block = dst.at[slot_block(k, c)]
            remote(block, block, f_send.at[a, part], f_recv.at[a, part], sibling).start()
            arrived.wait_send()
            return carry

        lax.fori_loop(*steps_of(part), forward, 0)

    def settle(a, part):
        src, dst = arrays[a]
        if part == 0:
            pltpu.make_async_copy(src.at[me], dst.at[slot_block(0, c)], l_sem.at[a]).wait()
        some = dst.at[pl.ds(0, 8)]
        drain = remote(some, some, f_send.at[a, part], f_recv.at[a, part], sibling)
        drain.wait_send()
        drain.wait_recv()

    def swap(mine, sib, a, part):
        return remote(
            mine.at[pl.ds(part * 16 + (1 - c) * 8, 8)], sib.at[pl.ds(part * 8, 8)],
            s_send.at[a, part], s_recv.at[a, part], sibling,
        )

    def give(mine, sib, ret, a, part):
        def add(k):
            block = slot_block(k, c)
            mine[block] = (mine[block].astype(F32) + sib[k].astype(F32)).astype(BF)
            return mine.at[block]

        def push(k, carry):
            sz, sx = chip_from(k)
            remote(add(k), ret.at[me], r_send.at[a], r_recv.at[a], dev(y, sz, sx, c)).start()
            return carry

        lax.fori_loop(*steps_of(part), push, 0)
        if part == 0:
            pltpu.make_async_copy(add(0), ret.at[me], l_sem.at[2 + a]).start()

    def given(mine, ret, a):
        pltpu.make_async_copy(mine.at[slot_block(0, c)], ret.at[me], l_sem.at[2 + a]).wait()
        drain = remote(ret.at[pl.ds(0, 15)], ret.at[pl.ds(0, 15)], r_send.at[a], r_recv.at[a], sibling)
        drain.wait_send()
        drain.wait_recv()

    half = 16 * SLOTS

    def forward_pass(part):
        blocks, rows = pl.ds(part * 16, 16), slice(part * half, part * half + half)
        both = dot(flat_rows(x_all[blocks]), w_all[:, : 2 * width], ((1,), (0,)))
        gate_val, up_val = both[:, :width], both[:, width:]
        gate_v[rows] = gate_val
        up_v[rows] = up_val
        low = (gate_val * jax.nn.sigmoid(gate_val) * up_val).astype(BF)
        hidden[rows] = low
        out = dot(low, w_all[:, 2 * width :], ((1,), (1,))).astype(BF)
        part_o[blocks] = out.reshape(16, SLOTS, MODEL_WIDTH)
        swap(part_o, sib_o, 0, part).start()

    def backward_pass(part):
        blocks, rows = pl.ds(part * 16, 16), slice(part * half, part * half + half)
        scale = jnp.concatenate([flat_rows(t_all[blocks])] * (MODEL_WIDTH // 128), axis=1)
        grad_expert = (flat_rows(g_all[blocks]).astype(F32) * scale).astype(BF)
        g_all[blocks] = grad_expert.reshape(16, SLOTS, MODEL_WIDTH)
        grad_hidden = dot(grad_expert, w_all[:, 2 * width :], ((1,), (0,)))
        gate_val = gate_v[rows]
        up_val = up_v[rows]
        sig = jax.nn.sigmoid(gate_val)
        grad_gate = (grad_hidden * up_val * sig * (1.0 + gate_val * (1.0 - sig))).astype(BF)
        grad_up = (grad_hidden * gate_val * sig).astype(BF)
        grads = jnp.concatenate([grad_gate, grad_up], axis=1)
        g_both[rows] = grads
        grad_rows = dot(grads, w_all[:, : 2 * width], ((1,), (1,))).astype(BF)
        part_g[blocks] = grad_rows.reshape(16, SLOTS, MODEL_WIDTH)
        swap(part_g, sib_g, 1, part).start()

    scatter(0, 0)
    scatter(1, 0)
    scatter(0, 1)
    scatter(1, 1)
    loads[2].wait()
    loads[3].wait()
    hand_over(0, 0)
    settle(0, 0)
    forward_pass(0)
    hand_over(0, 1)
    swap(part_o, sib_o, 0, 0).wait()
    give(part_o, sib_o, out_ret, 0, 0)
    settle(0, 1)
    forward_pass(1)
    hand_over(1, 0)
    hand_over(1, 1)
    settle(1, 0)
    swap(part_o, sib_o, 0, 1).wait()
    give(part_o, sib_o, out_ret, 0, 1)
    backward_pass(0)
    settle(1, 1)
    swap(part_g, sib_g, 1, 0).wait()
    give(part_g, sib_g, grad_ret, 1, 0)
    backward_pass(1)
    swap(part_g, sib_g, 1, 1).wait()
    give(part_g, sib_g, grad_ret, 1, 1)

    def weight_grads(j, carry):
        cols = pl.ds(pl.multiple_of(j * 256, 256), 256)
        v_all[cols, : 2 * width] = dot(flat_rows(x_all[:, :, cols]), g_both[...], ((0,), (0,))).astype(BF)
        v_all[cols, 2 * width :] = dot(flat_rows(g_all[:, :, cols]), hidden[...], ((0,), (0,))).astype(BF)
        return carry

    lax.fori_loop(0, MODEL_WIDTH // 256, weight_grads, 0)
    store = pltpu.make_async_copy(v_all, d_all, o_sem)
    store.start()
    given(part_o, out_ret, 0)
    grad_out = cotangent[...].astype(F32)
    rows_out = [dot(hits[k].astype(BF), flat_rows(out_ret[...]), ((1,), (0,))) for k in range(2)]
    o_block[...] = (middle[...] + share[0] * rows_out[0] + share[1] * rows_out[1]).astype(BF)
    pairs = [jnp.sum(grad_out * rows, axis=1, keepdims=True) for rows in rows_out]
    mean = share[0] * pairs[0] + share[1] * pairs[1]
    grad_logits = sum(chosen[k] * (share[k] * (pairs[k] - mean)) for k in range(2))
    o_logits[...] = grad_logits
    o_moe[...] = moe_in[...]
    routed = sum(dot(part, flat_extra, ((1,), (1,))) for part in three_parts(grad_logits))
    given(part_g, grad_ret, 1)
    grad_moe = dot(both_hits, flat_rows(grad_ret[...]), ((1,), (0,))) + routed
    o_gain[...] = jnp.sum(grad_moe * middle[...] * inverse, axis=0, keepdims=True)
    grad_middle = grad_out + norm_backward(middle[...], inverse, gain, grad_moe)
    o_middle[...] = grad_middle
    branch = grad_middle.astype(BF)
    o_branch[...] = branch
    for core, weight in ((c, wh), (1 - c, ws)):
        heads = dot(weight[...].reshape(MODEL_WIDTH, Q_HALF), branch, ((0,), (1,))).astype(BF)
        o_heads[pl.ds(core * 4, 4)] = heads.reshape(4, HEAD_Q, ROWS)
    store.wait()


def experts(attn, tokens, extra, ids, cotangent, half_w, sib_w, cots, weights):
    rows = 32 * SLOTS
    width = weights.shape[1] // 3
    slots = (16, SLOTS, MODEL_WIDTH)
    flat = (ROWS, MODEL_WIDTH)
    low = jax.ShapeDtypeStruct(flat, BF)
    return pl.pallas_call(
        experts_kernel,
        out_shape=[
            low,
            jax.ShapeDtypeStruct(flat, F32),
            low,
            jax.ShapeDtypeStruct((8, HEAD_Q, ROWS), BF),
            low,
            jax.ShapeDtypeStruct((ROWS, 128), F32),
            jax.ShapeDtypeStruct((1, MODEL_WIDTH), F32),
            jax.ShapeDtypeStruct(weights.shape, BF),
        ],
        in_specs=[IN_VMEM] * 5 + [ANY] * 4,
        out_specs=[IN_VMEM] * 7 + [ANY],
        scratch_shapes=[
            pltpu.VMEM((32, SLOTS, MODEL_WIDTH), BF),
            pltpu.VMEM((32, SLOTS, 128), F32),
            pltpu.VMEM((32, SLOTS, MODEL_WIDTH), BF),
            pltpu.VMEM(weights.shape, BF),
            pltpu.VMEM((rows, width), F32),
            pltpu.VMEM((rows, width), F32),
            pltpu.VMEM((rows, width), BF),
            pltpu.VMEM((rows, 2 * width), BF),
            pltpu.VMEM((32, SLOTS, MODEL_WIDTH), BF),
            pltpu.VMEM((32, SLOTS, MODEL_WIDTH), BF),
            pltpu.VMEM((16, SLOTS, MODEL_WIDTH), BF),
            pltpu.VMEM((16, SLOTS, MODEL_WIDTH), BF),
            pltpu.VMEM(weights.shape, BF),
            pltpu.VMEM(half_w.shape, BF),
            pltpu.VMEM(half_w.shape, BF),
            pltpu.VMEM(slots, BF),
            pltpu.VMEM((EXPERT_COUNT, SLOTS, 128), F32),
            pltpu.VMEM(slots, BF),
            pltpu.VMEM(slots, BF),
            pltpu.VMEM(flat, F32),
            pltpu.VMEM(flat, BF),
            pltpu.SemaphoreType.DMA((4,)),
            pltpu.SemaphoreType.DMA((4,)),
            pltpu.SemaphoreType.DMA((2, 16)),
            pltpu.SemaphoreType.DMA((2, 16)),
            pltpu.SemaphoreType.DMA((2, 2)),
            pltpu.SemaphoreType.DMA((2, 2)),
            pltpu.SemaphoreType.DMA((2, 2)),
            pltpu.SemaphoreType.DMA((2, 2)),
            pltpu.SemaphoreType.DMA((2,)),
            pltpu.SemaphoreType.DMA((2,)),
            pltpu.SemaphoreType.DMA,
        ],
        compiler_params=params(6, 60 << 20),
        name="experts",
    )(attn, tokens, extra, ids, cotangent, half_w, sib_w, cots, weights)


SUMS = tuple((n, start, width, order[::-1]) for n, start, width, order in FIRST_PARTS) + tuple(
    (2, start, 256, order) for start, order in OUT_SUMS
)
LATE = len(FIRST_PARTS)


def reduce_kernel(
    gq_t, dkv, normed, s_out, grad_logits, gain_m, moe_h, pair_h, extra_h, middle_h, w_q, w_kv, experts_h,
    o_tokens, o_q, o_k, o_v, o_out, o_extra, o_gate, o_up, o_down,
    moe_in, pair, w_extra, grad_middle, summed, f_gate, f_up, f_down, v_q, v_kv, v_extra, wq, wkv, gkv, mine_part, give_part, sib_part, both, total, give, *rest,
):
    parts = len(SUMS)
    first_in, rest = rest[:LATE], rest[LATE:]
    arrive = [list(first_in) + [None] * 3, rest[:parts], rest[parts : 2 * parts]]
    rest = rest[2 * parts :]
    held = [None, list(rest[:LATE]) + [s_out.at[k] for k in range(3)], rest[LATE : LATE + parts]]
    l_sem, send, recv, sib_send, sib_recv = rest[LATE + parts :]
    grads = (v_q, v_kv, None, v_extra)
    y, z, x, c = coords()
    place = {"y": y, "z": z, "x": x}
    sibling = dev(y, z, x, 1 - c)
    loads = [
        pltpu.make_async_copy(src, dst, l_sem.at[n])
        for n, (src, dst) in enumerate(
            (
                (w_q, wq), (w_kv, wkv), (pair_h, pair), (moe_h, moe_in), (extra_h, w_extra),
                (middle_h, grad_middle), (experts_h, summed),
            )
        )
    ]
    for load in loads:
        load.start()
    for axis in ("x", "y", "z"):
        for step in STEPS:
            signal(axis_peer(axis, step))
    signal(sibling)
    pl.semaphore_wait(pltpu.get_barrier_semaphore(), 10)

    def at(phase, part, index):
        n, start, width, order = SUMS[part]
        spot = [
            index if axis == order[phase] else slice(None)
            for axis in ("y", "z", "x")
            if axis not in order[:phase]
        ]
        if phase == 0:
            return grads[n].at[tuple(spot) + (slice(None), pl.ds(start, width))]
        return held[phase][part].at[tuple(spot)]

    def copies_of(phase, part):
        axis = SUMS[part][3][phase]
        return [
            remote(
                at(phase, part, (place[axis] + step) % 4), arrive[phase][part].at[n],
                send.at[phase, part, n], recv.at[phase, part, n], axis_peer(axis, step),
            )
            for n, step in enumerate(STEPS)
        ]

    def begin(phase, part):
        for copy in copies_of(phase, part):
            copy.start()

    def finish(phase, part):
        for copy in copies_of(phase, part):
            copy.wait()
        array, start, width, order = SUMS[part]
        mine = at(phase, part, place[order[phase]])
        got = arrive[phase][part]
        if phase < 2:

            def add(p, carry):
                value = mine[p].astype(F32)
                for n in range(3):
                    value = value + got[n, p].astype(F32)
                held[phase + 1][part][p] = value.astype(BF)
                return carry

            lax.fori_loop(0, 4, add, 0)
        else:
            value = mine[...].astype(F32)
            for n in range(3):
                value = value + got[n].astype(F32)
            total[:, STARTS[array] + start : STARTS[array] + start + width] = value

    for part in range(LATE, parts):
        begin(1, part)
    for h in range(4):
        value = dkv[4 * h].astype(F32)
        for n in range(1, 4):
            value = value + dkv[4 * h + n].astype(F32)
        gkv[128 * h : 128 * h + 128] = value.astype(BF)
    for n in range(4):
        left = normed[:, 384 * n : 384 * n + 384]
        v_kv[n] = dot(left, gkv[...], ((0,), (1,))).astype(BF).reshape(4, 4, 24, KV_HALF)
    begin(0, 1)
    for n in range(4):
        left = normed[:, 384 * n : 384 * n + 384]
        v_q[n] = dot(left, gq_t[...], ((0,), (1,))).astype(BF).reshape(4, 4, 24, Q_HALF)
    begin(0, 0)
    begin(0, 2)

    for load in loads:
        load.wait()
    gain_sum = jnp.zeros((1, MODEL_WIDTH), F32)
    for n in range(2):
        core = 1 - c if n == 0 else c
        rows = pl.ds(pl.multiple_of(core * ROWS, ROWS), ROWS)
        part = dot(gq_t[:, rows], wq[...], ((0,), (1,))) + dot(gkv[:, rows], wkv[...], ((0,), (1,)))
        values = pair[rows].astype(F32)
        gain_sum = gain_sum + jnp.sum(part * values * inverse_rms(values), axis=0, keepdims=True)
        if n == 0:
            give_part[...] = part
            remote(give_part, sib_part, sib_send.at[0], sib_recv.at[0], sibling).start()
        else:
            mine_part[...] = part
    lane = lax.broadcasted_iota(jnp.int32, (MODEL_WIDTH, EXTRA), 1)
    extra = sum(dot(moe_in[...], part, ((0,), (0,))) for part in three_parts(grad_logits[...]))
    extra = jnp.where(lane == EXPERT_COUNT, column_of(gain_sum), extra)
    extra = jnp.where(lane == EXPERT_COUNT + 1, column_of(gain_m[...]), extra)
    gain = jnp.transpose(w_extra[...].reshape(MODEL_WIDTH, EXTRA).astype(F32))[EXPERT_COUNT : EXPERT_COUNT + 1]
    v_extra[...] = extra.astype(BF).reshape(4, 4, 4, 24, EXTRA)
    begin(0, 3)
    remote(give_part, sib_part, sib_send.at[0], sib_recv.at[0], sibling).wait()
    rows = pl.ds(pl.multiple_of(c * ROWS, ROWS), ROWS)
    values = pair[rows].astype(F32)
    o_tokens[...] = grad_middle[...] + norm_backward(
        values, inverse_rms(values), gain, mine_part[...] + sib_part[...]
    )

    third = FF // 2
    f_gate[...] = summed[:, :third].astype(F32)
    f_up[...] = summed[:, third : 2 * third].astype(F32)
    f_down[...] = jnp.transpose(summed[:, 2 * third :].astype(F32))
    stores = [
        pltpu.make_async_copy(src, dst, l_sem.at[n])
        for n, (src, dst) in enumerate(((f_gate, o_gate), (f_up, o_up), (f_down, o_down)))
    ]
    for store in stores:
        store.start()
    for part in range(LATE, parts):
        finish(1, part)
        begin(2, part)
    for phase in range(3):
        for part in range(LATE):
            finish(phase, part)
            if phase < 2:
                begin(phase + 1, part)
    for part in range(LATE, parts):
        finish(2, part)
    low, high = total[0:12], total[12:24]
    both[c, 0:12] = jnp.where(c == 0, low, high)
    give[0:12] = jnp.where(c == 0, high, low)
    give[12:16] = jnp.zeros((4, PACK), F32)
    last = remote(give, both.at[c], sib_send.at[1], sib_recv.at[1], sibling)
    last.start()
    for store in stores:
        store.wait()
    last.wait()
    keys, values = [], []
    for k in range(2):
        o_q[:, Q_HALF * k : Q_HALF * k + Q_HALF] = both[k, 0:12, :Q_HALF]
        o_out[:, Q_HALF * k : Q_HALF * k + Q_HALF] = both[k, 0:12, STARTS[2] : STARTS[3]]
        for h in range(4):
            first = STARTS[1] + 128 * h
            keys.append(both[k, 0:12, first : first + HD])
            values.append(both[k, 0:12, first + HD : first + 2 * HD])
    o_k[...] = jnp.concatenate(keys, axis=1)
    o_v[...] = jnp.concatenate(values, axis=1)
    o_extra[...] = both[0, 0:12, STARTS[3] :] + both[1, 0:12, STARTS[3] :]


def reduce_weights(*args):
    widths = [part[2] for part in SUMS]
    full = lambda width: pltpu.VMEM((4, 4, 4, 24, width), BF)
    rows = pltpu.VMEM((ROWS, MODEL_WIDTH), F32)
    low = pltpu.VMEM((ROWS, MODEL_WIDTH), BF)
    scratch = (
        [low, pltpu.VMEM((PAIR, MODEL_WIDTH), BF), full(EXTRA), rows]
        + [pltpu.VMEM((MODEL_WIDTH // 4, 3 * FF // 2), BF)]
        + [pltpu.VMEM((MODEL_WIDTH // 4, FF // 2), F32)] * 2
        + [pltpu.VMEM((FF // 2, MODEL_WIDTH // 4), F32)]
        + [full(Q_HALF), full(KV_HALF), full(EXTRA)]
        + [pltpu.VMEM((MODEL_WIDTH, Q_HALF), BF), pltpu.VMEM((MODEL_WIDTH, KV_HALF), BF)]
        + [pltpu.VMEM((KV_HALF, PAIR), BF), rows, rows, rows]
        + [pltpu.VMEM((2, 16, PACK), F32), pltpu.VMEM((24, PACK), F32), pltpu.VMEM((16, PACK), F32)]
        + [pltpu.VMEM((3, 4, 4, 24, w), BF) for w in widths[:LATE]]
        + [pltpu.VMEM((3, 4, 24, w), BF) for w in widths]
        + [pltpu.VMEM((3, 24, w), BF) for w in widths]
        + [pltpu.VMEM((4, 4, 24, w), BF) for w in widths[:LATE]]
        + [pltpu.VMEM((4, 24, w), BF) for w in widths]
    )
    sems = (3, len(SUMS), 3)
    shapes = ((ROWS, MODEL_WIDTH), (12, MODEL_WIDTH), (12, KV * HD), (12, KV * HD), (12, MODEL_WIDTH), (12, EXTRA))
    tall, flat = (MODEL_WIDTH // 4, FF // 2), (FF // 2, MODEL_WIDTH // 4)
    shapes = shapes + (tall, tall, flat)
    return pl.pallas_call(
        reduce_kernel,
        out_shape=[jax.ShapeDtypeStruct(shape, F32) for shape in shapes],
        in_specs=[IN_VMEM] * 6 + [ANY] * 7,
        out_specs=[IN_VMEM] * 6 + [ANY] * 3,
        scratch_shapes=scratch
        + [
            pltpu.SemaphoreType.DMA((7,)),
            pltpu.SemaphoreType.DMA(sems),
            pltpu.SemaphoreType.DMA(sems),
            pltpu.SemaphoreType.DMA((2,)),
            pltpu.SemaphoreType.DMA((2,)),
        ],
        compiler_params=params(8, 60 << 20),
        name="reduce_weights",
    )(*args)


def wide_greet():
    y, z, x, c = coords()
    me = z * 4 + x

    def greet(k, carry):
        t = (me + k) % 16
        signal(dev(y, t // 4, t % 4, c))
        return carry

    lax.fori_loop(1, 16, greet, 0)
    for step in STEPS:
        signal(axis_peer("y", step))
        signal(dev(y, (z + step) % 4, x, 1 - c))
    signal(dev(y, z, x, 1 - c))
    pl.semaphore_wait(pltpu.get_barrier_semaphore(), 22)


def attend_back_kernel(
    heads, branch_h, attn_h, q_h, kv_h, first_ref, ot_h, lse_ref,
    dq_out, dkv_out, s_out,
    branch, attn, q_in, kv_in, ot_ref, keep, go, branch_sib, attn_sib, qs, gs, delta, dq, dkv, dkv_low, dq_low,
    g_out, a_out,
    l_sem, h_send, h_recv, sib_send, sib_recv, q_send, q_recv, k_send, k_recv,
    w_send, w_recv,
):
    y, z, x, c = coords()
    me = z * 4 + x
    j = c * 4 + z
    sibling = dev(y, z, x, 1 - c)
    place = {"y": y, "z": z, "x": x}
    loads = [
        pltpu.make_async_copy(src, dst, keep.at[n])
        for n, (src, dst) in enumerate(
            ((branch_h, branch), (attn_h, attn), (q_h, q_in), (kv_h, kv_in), (ot_h, ot_ref))
        )
    ]
    for load in loads:
        load.start()
    wide_greet()

    def push(k, carry):
        t = (j + k) % 8
        remote(heads.at[t], go.at[j], h_send, h_recv, dev(y, t % 4, x, t // 4)).start()
        return carry

    lax.fori_loop(1, 8, push, 0)
    one = remote(branch_h, branch_sib, sib_send.at[0], sib_recv.at[0], sibling)
    one.start()
    two = remote(attn_h.at[pl.ds((1 - c) * 4, 4)], attn_sib, sib_send.at[1], sib_recv.at[1], sibling)
    two.start()
    here = pltpu.make_async_copy(heads.at[j], go.at[j], l_sem.at[0])
    here.start()
    loads[0].wait()
    loads[1].wait()
    one.wait()
    two.wait()

    rows_b = jnp.concatenate([branch[...], branch_sib[...]], axis=0)
    rows_a = jnp.concatenate(
        [part.reshape(Q_HALF, ROWS) for part in (attn[pl.ds(c * 4, 4)], attn_sib[...])], axis=1
    )
    for n in range(4):
        part = dot(rows_b[:, 384 * n : 384 * n + 384], rows_a, ((0,), (1,)))
        g_out[n] = part.astype(BF).reshape(4, 4, 24, Q_HALF)

    def spot(part, index):
        start, order = OUT_SUMS[part]
        cut = [index if axis == order[0] else slice(None) for axis in ("y", "z", "x")]
        return g_out.at[tuple(cut) + (slice(None), pl.ds(start, 256))]

    w_copies = []
    for part in range(3):
        axis = OUT_SUMS[part][1][0]
        for n, step in enumerate(STEPS):
            copy = remote(
                spot(part, (place[axis] + step) % 4), a_out.at[part, n],
                w_send.at[part, n], w_recv.at[part, n], axis_peer(axis, step),
            )
            copy.start()
            w_copies.append(copy)

    for load in loads[2:]:
        load.wait()
    here.wait()
    drain = remote(go.at[pl.ds(0, 7)], go.at[pl.ds(0, 7)], h_send, h_recv, sibling)
    drain.wait_send()
    drain.wait_recv()
    dkv[...] = jnp.zeros_like(dkv)
    dq[...] = jnp.zeros_like(dq)
    for zq in range(4):
        q = q_in[zq] * SCALE_QK
        grad = jnp.concatenate([go[zq], go[4 + zq]], axis=1)
        qs[zq, 64:] = jnp.zeros((64, 3 * PAIR), BF)
        gs[zq, :64] = jnp.zeros((64, 3 * PAIR), BF)
        for h in range(3):
            cols, rows = slice(256 * h, 256 * h + 256), slice(64 * h, 64 * h + 64)
            qs[zq, :64, cols] = q[rows]
            gs[zq, 64:, cols] = grad[rows]
            delta[zq, :, cols] = jnp.sum(
                grad[rows].astype(F32) * ot_ref[zq, :, cols], axis=0, keepdims=True
            )

    for n in range(4):
        group = (z + n + 1) % 4
        for zq in range(4):
            hi = zq * 4 + x
            first = first_ref[zq]
            q_pos = hi * PAIR + lax.broadcasted_iota(jnp.int32, (1, PAIR), 1)

            def step(kb, carry):
                kv = kv_in[kb]
                k_pos = kb * PAIR + lax.broadcasted_iota(jnp.int32, (PAIR, PAIR), 0)
                ok = (k_pos >= first) & (k_pos <= q_pos)
                heads = [slice(256 * h, 256 * h + 256) for h in range(3)]
                scores = [dot(kv, qs[zq, :, cols], ((1,), (0,))) for cols in heads]
                grad_probs = [dot(kv, gs[zq, :, cols], ((1,), (0,))) for cols in heads]
                grad_scores, probs = [], []
                for h in range(3):
                    prob = jnp.where(ok, jnp.exp(scores[h] - lse_ref[zq, :, heads[h]]), 0.0)
                    grad_scores.append((prob * (grad_probs[h] - delta[zq, :, heads[h]])).astype(BF))
                    probs.append(prob.astype(BF))
                for h in range(3):
                    dq[zq, :, heads[h]] = dq[zq, :, heads[h]] + dot(kv, grad_scores[h], ((0,), (0,)))
                grad_scores, probs = jnp.concatenate(grad_scores, axis=1), jnp.concatenate(probs, axis=1)
                dkv[kb, :64] = dkv[kb, :64] + dot(qs[zq, :64], grad_scores, ((1,), (1,)))
                dkv[kb, 64:] = dkv[kb, 64:] + dot(gs[zq, 64:], probs, ((1,), (1,)))
                return carry

            last = jnp.minimum(group * 4 + 3, hi)
            lax.fori_loop(group * 4, jnp.maximum(last + 1, group * 4), step, 0)
        for d in range(4):
            xt = (x + d + 1) % 4
            t = group * 4 + xt
            dkv_low[t] = dkv[t].astype(BF)
            if n == 3 and d == 3:
                own_kv = pltpu.make_async_copy(dkv_low.at[me], dkv_out.at[me], l_sem.at[2])
                own_kv.start()
            else:
                remote(dkv_low.at[t], dkv_out.at[me], k_send, k_recv, dev(y, group, xt, c)).start()
    q_copies = []
    for n in range(4):
        zq = (z + n + 1) % 4
        by_head = jnp.concatenate([dq[zq, :64, 256 * h : 256 * h + 256] for h in range(3)], axis=0)
        dq_low[zq] = (by_head * SCALE_QK).astype(BF)
        if n < 3:
            copy = remote(dq_low.at[zq], dq_out.at[z], q_send.at[n], q_recv.at[n], dev(y, zq, x, c))
        else:
            copy = pltpu.make_async_copy(dq_low.at[zq], dq_out.at[z], l_sem.at[1])
        copy.start()
        q_copies.append(copy)

    for copy in w_copies:
        copy.wait()
    for part in range(3):
        mine = spot(part, place[OUT_SUMS[part][1][0]])

        def add(p, carry):
            value = mine[p].astype(F32)
            for k in range(3):
                value = value + a_out[part, k, p].astype(F32)
            s_out[part, p] = value.astype(BF)
            return carry

        lax.fori_loop(0, 4, add, 0)
    for copy in q_copies:
        copy.wait()
    own_kv.wait()
    drain = remote(dkv_out.at[pl.ds(0, 15)], dkv_out.at[pl.ds(0, 15)], k_send, k_recv, sibling)
    drain.wait_send()
    drain.wait_recv()


def attend_back(heads, branch, attn, q_in, kv_in, first, ot, lse):
    return pl.pallas_call(
        attend_back_kernel,
        out_shape=[
            jax.ShapeDtypeStruct((4, HEAD_Q, PAIR), BF),
            jax.ShapeDtypeStruct((16, 128, PAIR), BF),
            jax.ShapeDtypeStruct((3, 4, 4, 24, 256), BF),
        ],
        in_specs=[ANY] * 5 + [IN_VMEM, ANY, IN_VMEM],
        out_specs=[ANY, ANY, IN_VMEM],
        scratch_shapes=[
            pltpu.VMEM((ROWS, MODEL_WIDTH), BF),
            pltpu.VMEM((8, HEAD_Q, ROWS), BF),
            pltpu.VMEM((4, HEAD_Q, PAIR), BF),
            pltpu.VMEM((16, PAIR, 128), BF),
            pltpu.VMEM((4, HD, 3 * PAIR), F32),
            pltpu.SemaphoreType.DMA((5,)),
            pltpu.VMEM((8, HEAD_Q, ROWS), BF),
            pltpu.VMEM((ROWS, MODEL_WIDTH), BF),
            pltpu.VMEM((4, HEAD_Q, ROWS), BF),
            pltpu.VMEM((4, 128, 3 * PAIR), BF),
            pltpu.VMEM((4, 128, 3 * PAIR), BF),
            pltpu.VMEM((4, 1, 3 * PAIR), F32),
            pltpu.VMEM((4, 128, 3 * PAIR), F32),
            pltpu.VMEM((16, 128, PAIR), F32),
            pltpu.VMEM((16, 128, PAIR), BF),
            pltpu.VMEM((4, HEAD_Q, PAIR), BF),
            pltpu.VMEM((4, 4, 4, 24, Q_HALF), BF),
            pltpu.VMEM((3, 3, 4, 4, 24, 256), BF),
            pltpu.SemaphoreType.DMA((3,)),
            pltpu.SemaphoreType.DMA,
            pltpu.SemaphoreType.DMA,
            pltpu.SemaphoreType.DMA((2,)),
            pltpu.SemaphoreType.DMA((2,)),
            pltpu.SemaphoreType.DMA((4,)),
            pltpu.SemaphoreType.DMA((4,)),
            pltpu.SemaphoreType.DMA,
            pltpu.SemaphoreType.DMA,
            pltpu.SemaphoreType.DMA((3, 3)),
            pltpu.SemaphoreType.DMA((3, 3)),
        ],
        compiler_params=params(4, 60 << 20),
        name="attend_back",
    )(heads, branch, attn, q_in, kv_in, first, ot, lse)


def inverse_rms(values):
    return lax.rsqrt(jnp.mean(values * values, axis=-1, keepdims=True) + EPS)


def norm_backward(values, inverse, gain, grad_out):
    scaled = grad_out * gain
    return inverse * scaled - values * inverse**3 * jnp.mean(values * scaled, axis=-1, keepdims=True)


def local(
    tokens,
    segment_ids,
    expert_ids,
    w_query,
    w_key,
    w_value,
    w_out,
    w_router,
    gain_attn,
    gain_moe,
    w_gate,
    w_up,
    w_down,
    cotangent,
):
    ids = expert_ids.T
    part_q, part_kv, part_out, part_extra, pair, normed, w_experts, q4, keys_values, first, cot_slots = (
        gather_weights(
            (w_query, w_key, w_value, w_out.T, w_router, gain_attn[None], gain_moe[None], ids, cotangent),
            (tokens, segment_ids, w_gate, w_up, w_down),
        )
    )
    full_experts = lax.all_gather(w_experts, "dp", axis=0, tiled=True)
    q_in, kv_in, attn, attn_t, lse, half_out, sib_out, cot_all = attend(
        q4, keys_values, part_out, cot_slots, first
    )
    block_out, grad_middle, branch, grad_heads, moe_in, grad_logits, gain_sum, grad_experts = experts(
        attn, tokens, part_extra, ids, cotangent, half_out, sib_out, cot_all, full_experts
    )
    sum_experts = lax.psum_scatter(grad_experts, "dp", scatter_dimension=0, tiled=True)
    dq_in, dkv_in, sum_out = attend_back(grad_heads, branch, attn, q_in, kv_in, first, attn_t, lse)
    grad_tokens, r_query, r_key, r_value, r_out, r_extra, *expert_grads = reduce_weights(
        dq_in.reshape(Q_HALF, PAIR), dkv_in, normed, sum_out, grad_logits, gain_sum, moe_in,
        pair.reshape(PAIR, MODEL_WIDTH), part_extra, grad_middle,
        part_q.reshape(MODEL_WIDTH, Q_HALF), part_kv.reshape(MODEL_WIDTH, KV_HALF), sum_experts,
    )
    return (
        block_out,
        grad_tokens,
        r_query,
        r_key,
        r_value,
        r_out.T,
        r_extra[:, :EXPERT_COUNT],
        r_extra[:, EXPERT_COUNT],
        r_extra[:, EXPERT_COUNT + 1],
        *expert_grads,
    )


def solution(mesh):
    rows, flat, dense = P(("dp", "ctx"), None), P(("dp", "ctx")), P("dp", "ctx")
    placed = (
        rows, dense, rows, rows, rows, rows, P(None, ("dp", "ctx")), rows, flat, flat,
        dense, dense, P("ctx", "dp"), rows,
    )
    return jax.shard_map(
        local,
        mesh=mesh,
        in_specs=placed,
        out_specs=(
            rows, rows, rows, rows, rows, P(None, ("dp", "ctx")), rows, flat, flat,
            dense, dense, P("ctx", "dp"),
        ),
        check_vma=False,
    )
```

```python
import functools

import jax
import jax.numpy as jnp
from jax import lax
from jax.experimental import pallas as pl
from jax.experimental.pallas import tpu as pltpu
from jax.sharding import PartitionSpec as P

MODEL_WIDTH = 1536
KV = 8
HD = 64
EXPERT_COUNT = 16
FF = 1024
EXPERT_CAPACITY = 20
SLOTS = 24
ROWS = 128
PAIR = 256
HEAD_Q = 192
Q_HALF = 768
KV_HALF = 512
EXTRA = 128
PACK = Q_HALF + KV_HALF + EXTRA + Q_HALF

EPS = 1e-05
SCALE_QK = 0.125
NEGATIVE = -1e30
MESH = pl.DeviceIdType.MESH
ANY = pl.BlockSpec(memory_space=pl.ANY)
IN_VMEM = pl.BlockSpec(memory_space=pltpu.VMEM)
BF = jnp.bfloat16
F32 = jnp.float32


def dot(a, b, dims):
    return lax.dot_general(a, b, (dims, ((), ())), preferred_element_type=F32)


def coords():
    i = lax.axis_index("ctx")
    return lax.axis_index("dp"), i // 8, (i // 2) % 4, i % 2


def dev(y, z, x, c):
    return (y, z * 8 + x * 2 + c)


def signal(target):
    pl.semaphore_signal(
        pltpu.get_barrier_semaphore(), inc=1, device_id=target, device_id_type=MESH
    )


def remote(src, dst, send, recv, target):
    return pltpu.make_async_remote_copy(
        src_ref=src, dst_ref=dst, send_sem=send, recv_sem=recv, device_id=target, device_id_type=MESH
    )


def params(cid, vmem=None):
    return pltpu.CompilerParams(collective_id=cid, has_side_effects=True, vmem_limit_bytes=vmem)


def axis_peer(axis, step):
    y, z, x, c = coords()
    if axis == "y":
        return dev((y + step) % 4, z, x, c)
    if axis == "z":
        return dev(y, (z + step) % 4, x, c)
    return dev(y, z, (x + step) % 4, c)


WIDTHS = (Q_HALF, KV_HALF, Q_HALF, EXTRA)
STARTS = (0, Q_HALF, Q_HALF + KV_HALF, 2 * Q_HALF + KV_HALF)
STEPS = (1, 3, 2)
FIRST_PARTS = (
    (0, 0, 512, ("x", "z", "y")),
    (1, 0, 512, ("y", "x", "z")),
    (0, 512, 256, ("z", "y", "x")),
    (3, 0, 128, ("z", "y", "x")),
)
OUT_PARTS = (
    (2, 0, 128, ("z", "x", "y")),
    (2, 128, 384, ("z", "y", "x")),
    (2, 512, 256, ("y", "x", "z")),
)
OUT_SUMS = ((0, ("x", "y", "z")), (256, ("x", "z", "y")), (512, ("z", "x", "y")))
GATHER_PARTS = FIRST_PARTS + OUT_PARTS


def slab(ref, done, y, z, x, cols):
    return ref.at[
        slice(None) if "y" in done else y,
        slice(None) if "z" in done else z,
        slice(None) if "x" in done else x,
        slice(None),
        cols,
    ]


def column_of(row):
    return jnp.transpose(jnp.broadcast_to(row, (128, row.shape[1])))


def slot_hits(ids):
    lane = lax.broadcasted_iota(jnp.int32, (ROWS, 128), 1).astype(F32)
    experts_of = [column_of(ids[k : k + 1].astype(F32)) for k in range(2)]
    chosen = [jnp.where(lane == expert, 1.0, 0.0) for expert in experts_of]
    row = lax.broadcasted_iota(jnp.int32, (ROWS, ROWS), 0)
    earlier = jnp.where(row > lax.broadcasted_iota(jnp.int32, (ROWS, ROWS), 1), 1.0, 0.0).astype(BF)
    before = dot(earlier, (chosen[0] + chosen[1]).astype(BF), ((1,), (0,)))
    slot_lane = lax.broadcasted_iota(jnp.int32, (ROWS, EXPERT_COUNT * SLOTS), 1).astype(F32)
    hits = []
    for k in range(2):
        place = jnp.sum(chosen[k] * before, axis=1, keepdims=True)
        slot = jnp.where(place < EXPERT_CAPACITY, experts_of[k][:, :1] * SLOTS + place, -1.0)
        hits.append(jnp.where(slot_lane == slot, 1.0, 0.0))
    return chosen, hits


def three_parts(values):
    parts = []
    for _ in range(3):
        part = values.astype(BF)
        parts.append(part)
        values = values - part.astype(F32)
    return parts


def gather_kernel(
    w_query, w_key, w_value, w_out, w_router, gain_a, gain_m, ids, cots, tokens, segs, w_gate, w_up, w_down,
    o_q, o_kv, out2, out3, pair, o_normed, w_experts, q4, kv2, o_first, cot_slots,
    pack, sib, block, w_q, w_kv, w_extra, rows, segments, normed, packed, down,
    p_send, p_recv, l_sem, s_send, s_recv, sib_send, sib_recv, o_sem,
):
    y, z, x, c = coords()
    outs = (w_q, w_kv, out2, w_extra)
    me = z * 8 + x * 2 + c
    sibling = dev(y, z, x, 1 - c)

    def greet(k, carry):
        signal((y, (me + k) % 32))
        return carry

    lax.fori_loop(1, 32, greet, 0)
    for step in STEPS:
        signal(axis_peer("y", step))
    expert_loads = [
        pltpu.make_async_copy(w_gate, packed.at[:, 0:FF // 2], o_sem.at[5]),
        pltpu.make_async_copy(w_up, packed.at[:, FF // 2 : FF], o_sem.at[6]),
        pltpu.make_async_copy(w_down, down, o_sem.at[7]),
    ]
    for load in expert_loads:
        load.start()
    lane = lax.broadcasted_iota(jnp.int32, (12, EXTRA), 1)
    square = lax.broadcasted_iota(jnp.int32, (12, 12), 0) == lax.broadcasted_iota(jnp.int32, (12, 12), 1)
    extra = jnp.concatenate(
        [w_router[...].astype(F32), jnp.zeros((12, EXTRA - EXPERT_COUNT), F32)], axis=1
    )
    for k, gain_row in enumerate((gain_a, gain_m)):
        spread_row = jnp.broadcast_to(gain_row[...].astype(F32), (12, 12))
        column = jnp.sum(jnp.where(square, spread_row, 0.0), axis=1, keepdims=True)
        extra = jnp.where(lane == EXPERT_COUNT + k, column, extra)
    extra = extra.astype(BF)
    heads = []
    for h in range(KV):
        cols = slice(HD * h, HD * h + HD)
        heads += [w_key[:, cols].astype(F32), w_value[:, cols].astype(F32)]
    heads = jnp.concatenate(heads, axis=1).astype(BF)
    for k in range(2):
        parts = (
            w_query[:, Q_HALF * k : Q_HALF * k + Q_HALF],
            heads[:, KV_HALF * k : KV_HALF * k + KV_HALF],
            w_out[:, Q_HALF * k : Q_HALF * k + Q_HALF],
            extra,
        )
        for start, width, part in zip(STARTS, WIDTHS, parts):
            pack[k, 0:12, start : start + width] = part
            pack[k, 12:16, start : start + width] = jnp.zeros((4, width), BF)
    pl.semaphore_wait(pltpu.get_barrier_semaphore(), 34)

    first = remote(pack.at[1 - c], sib, sib_send.at[0], sib_recv.at[0], sibling)
    first.start()
    second = remote(tokens, rows.at[c], sib_send.at[1], sib_recv.at[1], sibling)
    second.start()
    own_rows = pltpu.make_async_copy(tokens, rows.at[c], l_sem.at[4])
    own_rows.start()
    own_segs = pltpu.make_async_copy(segs, segments.at[me], l_sem.at[5])
    own_segs.start()

    def spread(k, carry):
        remote(segs, segments.at[me], s_send, s_recv, (y, (me + k) % 32)).start()
        return carry

    lax.fori_loop(1, 32, spread, 0)

    first.wait()
    own = pack[c, :12].astype(F32)
    other = sib[:12].astype(F32)
    low = jnp.where(c == 0, own, other)
    high = jnp.where(c == 0, other, own)
    block[...] = jnp.concatenate([low, high], axis=0).astype(BF)

    locals_ = []
    for n in range(4):
        cols = pl.ds(STARTS[n], WIDTHS[n])
        here = pltpu.make_async_copy(block.at[:, cols], outs[n].at[y, z, x], l_sem.at[n])
        here.start()
        locals_.append(here)
    for phase in range(3):
        copies = []
        for part, (n, start, width, order) in enumerate(GATHER_PARTS if phase < 2 else FIRST_PARTS):
            for k, step in enumerate(STEPS):
                dst = slab(outs[n], order[:phase], y, z, x, pl.ds(start, width))
                src = block.at[:, pl.ds(STARTS[n] + start, width)] if phase == 0 else dst
                copy = remote(
                    src, dst, p_send.at[phase, part, k], p_recv.at[phase, part, k],
                    axis_peer(order[phase], step),
                )
                copy.start()
                copies.append(copy)
        if phase == 0:
            for here in locals_:
                here.wait()
        if phase == 2:
            own_segs.wait()
            drain = remote(
                segments.at[pl.ds(0, 31)], segments.at[pl.ds(0, 31)], s_send, s_recv, sibling
            )
            drain.wait_send()
            drain.wait_recv()
            places = segments[...].reshape(32, 128)
            for zq in range(4):
                t = (zq * 4 + x) * 2
                mine = jnp.concatenate([segments[t], segments[t + 1]], axis=1)
                begin = jnp.zeros((1, PAIR), jnp.int32)
                for u in range(15):
                    count = jnp.sum((places == u).astype(jnp.int32))
                    begin = begin + jnp.where(mine > u, count, 0)
                o_first[zq] = begin
            chosen, hits = slot_hits(ids[...])
            kept = dot((hits[0] + hits[1]).astype(BF), cots[...], ((0,), (0,))).astype(BF)
            cot_slots[...] = kept.reshape(EXPERT_COUNT, SLOTS, MODEL_WIDTH)
            for load in expert_loads:
                load.wait()
            packed[:, FF:] = jnp.transpose(down[...].astype(F32)).astype(BF)
            pltpu.make_async_copy(packed, w_experts, o_sem.at[5]).start()
            second.wait()
            own_rows.wait()
        for copy in copies:
            copy.wait()
    stores = [
        pltpu.make_async_copy(src, dst, o_sem.at[n])
        for n, (src, dst) in enumerate(((w_q, o_q), (w_kv, o_kv), (w_extra, out3), (rows, pair)))
    ]
    for store in stores:
        store.start()
    gain = jnp.transpose(w_extra[...].reshape(MODEL_WIDTH, EXTRA).astype(F32))[EXPERT_COUNT : EXPERT_COUNT + 1]
    for k in range(2):
        values = rows[k].astype(F32)
        normed[ROWS * k : ROWS * k + ROWS] = (values * inverse_rms(values) * gain).astype(BF)
    last = pltpu.make_async_copy(normed, o_normed, o_sem.at[4])
    last.start()
    queries = dot(w_q[...].reshape(MODEL_WIDTH, Q_HALF), normed[...], ((0,), (1,))).astype(BF)
    q4[...] = queries.reshape(4, HEAD_Q, PAIR)
    kv2[...] = dot(normed[...], w_kv[...].reshape(MODEL_WIDTH, KV_HALF), ((1,), (0,))).astype(BF)
    for store in stores:
        store.wait()
    last.wait()
    pltpu.make_async_copy(packed, w_experts, o_sem.at[5]).wait()


def gather_weights(vmem_args, hbm_args):
    blocks = [(4, 4, 4, 24, width) for width in WIDTHS]
    rows = (2, ROWS, MODEL_WIDTH)
    flat = (PAIR, MODEL_WIDTH)
    experts_in = (MODEL_WIDTH // 4, 3 * FF // 2)
    return pl.pallas_call(
        gather_kernel,
        out_shape=[jax.ShapeDtypeStruct(shape, BF) for shape in (*blocks, rows, flat, experts_in)]
        + [
            jax.ShapeDtypeStruct((4, HEAD_Q, PAIR), BF),
            jax.ShapeDtypeStruct((PAIR, KV_HALF), BF),
            jax.ShapeDtypeStruct((4, 1, PAIR), jnp.int32),
            jax.ShapeDtypeStruct((EXPERT_COUNT, SLOTS, MODEL_WIDTH), BF),
        ],
        in_specs=[IN_VMEM] * len(vmem_args) + [ANY] * len(hbm_args),
        out_specs=[ANY] * 7 + [IN_VMEM] * 4,
        scratch_shapes=[
            pltpu.VMEM((2, 16, PACK), BF),
            pltpu.VMEM((16, PACK), BF),
            pltpu.VMEM((24, PACK), BF),
            pltpu.VMEM(blocks[0], BF),
            pltpu.VMEM(blocks[1], BF),
            pltpu.VMEM(blocks[3], BF),
            pltpu.VMEM(rows, BF),
            pltpu.VMEM((32, 1, 128), jnp.int32),
            pltpu.VMEM(flat, BF),
            pltpu.VMEM(experts_in, BF),
            pltpu.VMEM((FF // 2, MODEL_WIDTH // 4), BF),
            pltpu.SemaphoreType.DMA((3, 7, 3)),
            pltpu.SemaphoreType.DMA((3, 7, 3)),
            pltpu.SemaphoreType.DMA((6,)),
            pltpu.SemaphoreType.DMA,
            pltpu.SemaphoreType.DMA,
            pltpu.SemaphoreType.DMA((2,)),
            pltpu.SemaphoreType.DMA((2,)),
            pltpu.SemaphoreType.DMA((8,)),
        ],
        compiler_params=params(1, 60 << 20),
        name="gather_weights",
    )(*vmem_args, *hbm_args)


def offset(k):
    dz = (k % 8) // 2
    return dz, 2 * (k % 2) + (dz + k // 8) % 2


def chip_to(k):
    y, z, x, c = coords()
    dz, dx = offset(k)
    return (z + dz) % 4, (x + dx) % 4


def chip_from(k):
    y, z, x, c = coords()
    dz, dx = offset(k)
    return (z + 4 - dz) % 4, (x + 4 - dx) % 4


def slot_block(k, core):
    return (k // 8) * 16 + core * 8 + k % 8


def plane_greet():
    y, z, x, c = coords()
    me = z * 4 + x

    def greet(k, carry):
        t = (me + k) % 16
        signal(dev(y, t // 4, t % 4, c))
        return carry

    lax.fori_loop(1, 16, greet, 0)
    signal(dev(y, z, x, 1 - c))


KEYS = 1024


def attend_kernel(
    q4, kv2, half_in, cots, first_ref, q_out, kv_out, attn, ot_out, lse_ref, half, half_sib, c_all,
    q_in, kv_in, ot_ref, qs, acc, o_buf, keep,
    l_sem, q_send, q_recv, k_send, k_recv, w_send, w_recv, sib_send, sib_recv,
    c_send, c_recv, f_send, f_recv, o_send, o_recv,
):
    y, z, x, c = coords()
    me = z * 4 + x
    sibling = dev(y, z, x, 1 - c)

    wide_greet()

    q_copies = []
    for n, step in enumerate(STEPS):
        to = (z + step) % 4
        copy = remote(q4.at[to], q_in.at[z], q_send.at[n], q_recv.at[n], dev(y, to, x, c))
        copy.start()
        q_copies.append(copy)

    def head(index):
        return kv2.at[:, pl.ds(pl.multiple_of(index * 128, 128), 128)]

    def send_kv(k, carry):
        t = (me + k) % 16
        remote(head(t // 4), kv_in.at[me], k_send, k_recv, dev(y, t // 4, t % 4, c)).start()
        return carry

    lax.fori_loop(1, 16, send_kv, 0)
    here = [
        pltpu.make_async_copy(q4.at[z], q_in.at[z], l_sem.at[0]),
        pltpu.make_async_copy(head(z), kv_in.at[me], l_sem.at[1]),
    ]
    for copy in here:
        copy.start()
    for copy in here:
        copy.wait()
    for copy in q_copies:
        copy.wait()
    drain = remote(kv_in.at[pl.ds(0, 15)], kv_in.at[pl.ds(0, 15)], k_send, k_recv, sibling)
    drain.wait_send()
    drain.wait_recv()

    w_copies = [[], [], []]
    for part, (n, start, width, order) in enumerate(OUT_PARTS):
        spot = slab(half, order[:2], y, z, x, pl.ds(start, width))
        for k, step in enumerate(STEPS):
            copy = remote(
                spot, spot, w_send.at[part, k], w_recv.at[part, k], axis_peer(order[2], step)
            )
            copy.start()
            w_copies[part].append(copy)

    kept = [
        pltpu.make_async_copy(q_in, q_out, keep.at[4]),
        pltpu.make_async_copy(kv_in, kv_out, keep.at[5]),
    ]
    for copy in kept:
        copy.start()

    def cots_copy(k):
        tz, tx = chip_to(k)
        return remote(
            cots.at[tz * 4 + tx], c_all.at[slot_block(k, c)], c_send.at[k], c_recv.at[k], dev(y, tz, tx, c)
        )

    def send_cots(k, carry):
        cots_copy(k).start()
        return carry

    lax.fori_loop(1, 16, send_cots, 0)
    own_cots = pltpu.make_async_copy(cots.at[me], c_all.at[slot_block(0, c)], l_sem.at[2])
    own_cots.start()
    remote(cots.at[me], c_all.at[slot_block(0, c)], f_send, f_recv, sibling).start()

    def forward_cots(k, carry):
        arrived = cots_copy(k)
        arrived.wait_recv()
        remote(c_all.at[slot_block(k, c)], c_all.at[slot_block(k, c)], f_send, f_recv, sibling).start()
        arrived.wait_send()
        return carry

    def swap(part):
        start, width = OUT_PARTS[part][1:3]
        cols = half.at[:, :, :, :, pl.ds(start, width)]
        there = half_sib.at[:, :, :, :, pl.ds(start, width)]
        return remote(cols, there, sib_send.at[part], sib_recv.at[part], sibling)

    j = c * 4 + z
    qs[64:] = jnp.zeros((64, 3 * PAIR), BF)
    returns = []
    for n in range(4):
        zq = (z + n + 1) % 4
        q = q_in[zq] * SCALE_QK
        for h in range(3):
            qs[:64, 256 * h : 256 * h + 256] = q[64 * h : 64 * h + 64]
        acc[...] = jnp.zeros_like(acc)
        first = first_ref[zq]
        q_pos = (zq * 4 + x) * PAIR + lax.broadcasted_iota(jnp.int32, (1, PAIR), 1)

        def step(kb, stats):
            kv = kv_in[pl.ds(kb * (KEYS // PAIR), KEYS // PAIR)].reshape(KEYS, 128)
            k_pos = kb * KEYS + lax.broadcasted_iota(jnp.int32, (KEYS, PAIR), 0)
            ok = (k_pos >= first) & (k_pos <= q_pos)
            scores = [dot(kv, qs[:, 256 * h : 256 * h + 256], ((1,), (0,))) for h in range(3)]
            later, probs, shrinks = [], [], []
            for h in range(3):
                top, tot = stats[h]
                masked = jnp.where(ok, scores[h], NEGATIVE)
                new = jnp.maximum(top, jnp.max(masked, axis=0, keepdims=True))
                prob = jnp.exp(masked - new)
                shrink = jnp.exp(top - new)
                later.append((new, tot * shrink + jnp.sum(prob, axis=0, keepdims=True)))
                probs.append(prob.astype(BF))
                shrinks.append(shrink)
            for h in range(3):
                cols = slice(256 * h, 256 * h + 256)
                acc[:, cols] = acc[:, cols] * shrinks[h] + dot(kv, probs[h], ((0,), (0,)))
            return tuple(later)

        none = (jnp.full((1, PAIR), NEGATIVE, F32), jnp.zeros((1, PAIR), F32))
        stats = lax.fori_loop(0, zq + 1, step, (none, none, none))
        heads = []
        for h in range(3):
            cols = slice(256 * h, 256 * h + 256)
            mixed = acc[64:, cols] / stats[h][1]
            ot_ref[zq, :, cols] = mixed
            lse_ref[zq, :, cols] = stats[h][0] + jnp.log(stats[h][1])
            heads.append(mixed)
        heads = jnp.concatenate(heads, axis=0).astype(BF)
        saved = pltpu.make_async_copy(ot_ref.at[zq], ot_out.at[zq], keep.at[n])
        saved.start()
        kept.append(saved)
        o_buf[n, 0] = heads[:, :ROWS]
        o_buf[n, 1] = heads[:, ROWS:]
        for d in range(2):
            core = c if d == 0 else 1 - c
            if n == 3 and d == 0:
                back = pltpu.make_async_copy(o_buf.at[n, core], attn.at[j], l_sem.at[3])
            else:
                back = remote(
                    o_buf.at[n, core], attn.at[j], o_send.at[n, d], o_recv.at[n, d], dev(y, zq, x, core)
                )
            back.start()
            returns.append(back)
    for part in (0, 2, 1):
        for copy in w_copies[part]:
            copy.wait()
        swap(part).start()
        if part == 0:
            lax.fori_loop(1, 16, forward_cots, 0)
    own_cots.wait()
    mine = c_all.at[pl.ds(c * 16, 16)]
    drain = remote(mine, mine, f_send, f_recv, sibling)
    drain.wait_send()
    drain.wait_recv()
    for part in range(3):
        swap(part).wait()
    for back in returns + kept:
        back.wait()


def attend(q4, kv2, half, cots, first):
    blocks = jax.ShapeDtypeStruct((4, 4, 4, 24, Q_HALF), BF)
    return pl.pallas_call(
        attend_kernel,
        out_shape=[
            jax.ShapeDtypeStruct((4, HEAD_Q, PAIR), BF),
            jax.ShapeDtypeStruct((16, PAIR, 128), BF),
            jax.ShapeDtypeStruct((8, HEAD_Q, ROWS), BF),
            jax.ShapeDtypeStruct((4, HD, 3 * PAIR), F32),
            jax.ShapeDtypeStruct((4, 1, 3 * PAIR), F32),
            blocks,
            blocks,
            jax.ShapeDtypeStruct((32, SLOTS, MODEL_WIDTH), BF),
        ],
        in_specs=[ANY, ANY, ANY, ANY, IN_VMEM],
        out_specs=[ANY, ANY, ANY, ANY, IN_VMEM, ANY, ANY, ANY],
        input_output_aliases={2: 5},
        scratch_shapes=[
            pltpu.VMEM((4, HEAD_Q, PAIR), BF),
            pltpu.VMEM((16, PAIR, 128), BF),
            pltpu.VMEM((4, HD, 3 * PAIR), F32),
            pltpu.VMEM((128, 3 * PAIR), BF),
            pltpu.VMEM((128, 3 * PAIR), F32),
            pltpu.VMEM((4, 2, HEAD_Q, ROWS), BF),
            pltpu.SemaphoreType.DMA((6,)),
            pltpu.SemaphoreType.DMA((4,)),
            pltpu.SemaphoreType.DMA((3,)),
            pltpu.SemaphoreType.DMA((3,)),
            pltpu.SemaphoreType.DMA,
            pltpu.SemaphoreType.DMA,
            pltpu.SemaphoreType.DMA((3, 3)),
            pltpu.SemaphoreType.DMA((3, 3)),
            pltpu.SemaphoreType.DMA((3,)),
            pltpu.SemaphoreType.DMA((3,)),
            pltpu.SemaphoreType.DMA((16,)),
            pltpu.SemaphoreType.DMA((16,)),
            pltpu.SemaphoreType.DMA,
            pltpu.SemaphoreType.DMA,
            pltpu.SemaphoreType.DMA((4, 2)),
            pltpu.SemaphoreType.DMA((4, 2)),
        ],
        compiler_params=params(2, 60 << 20),
        name="attend",
    )(q4, kv2, half, cots, first)


def flat_rows(blocks):
    return blocks.reshape(blocks.shape[0] * SLOTS, blocks.shape[2])


def experts_kernel(
    attn, tokens, extra, ids, cotangent, half_w, sib_w, cots, weights,
    o_block, o_middle, o_branch, o_heads, o_moe, o_logits, o_gain, d_all,
    x_all, t_all, g_all, w_all, gate_v, up_v, hidden, g_both, part_o, part_g, sib_o, sib_g,
    v_all, wh, ws, xs, gates, out_ret, grad_ret, middle, moe_in,
    w_sem, l_sem, send, recv, f_send, f_recv, s_send, s_recv, r_send, r_recv, o_sem,
):
    y, z, x, c = coords()
    me = z * 4 + x
    width = hidden.shape[1]
    sibling = dev(y, z, x, 1 - c)
    loads = [
        pltpu.make_async_copy(src, dst, w_sem.at[n])
        for n, (src, dst) in enumerate(((half_w, wh), (sib_w, ws), (weights, w_all), (cots, g_all)))
    ]
    plane_greet()
    for load in loads:
        load.start()
    chosen, hits = slot_hits(ids[...])
    both_hits = (hits[0] + hits[1]).astype(BF)
    flat_extra = extra[...].reshape(MODEL_WIDTH, EXTRA)
    gain = jnp.transpose(flat_extra.astype(F32))[EXPERT_COUNT + 1 : EXPERT_COUNT + 2]
    own = attn[pl.ds(c * 4, 4)].reshape(Q_HALF, ROWS)
    other = attn[pl.ds((1 - c) * 4, 4)].reshape(Q_HALF, ROWS)
    loads[0].wait()
    loads[1].wait()
    middle[...] = (
        tokens[...].astype(F32)
        + dot(own, wh[...].reshape(MODEL_WIDTH, Q_HALF), ((0,), (1,)))
        + dot(other, ws[...].reshape(MODEL_WIDTH, Q_HALF), ((0,), (1,)))
    )
    inverse = inverse_rms(middle[...])
    moe_in[...] = (middle[...] * inverse * gain).astype(BF)
    logits = dot(moe_in[...], flat_extra, ((1,), (0,)))
    picked = [jnp.sum(chosen[k] * logits, axis=1, keepdims=True) for k in range(2)]
    most = jnp.maximum(picked[0], picked[1])
    lifted = [jnp.exp(value - most) for value in picked]
    share = [value / (lifted[0] + lifted[1]) for value in lifted]
    slots_in = dot(both_hits, moe_in[...], ((0,), (0,))).astype(BF)
    xs[...] = slots_in.reshape(EXPERT_COUNT, SLOTS, MODEL_WIDTH)
    slot_gate = jnp.sum(hits[0] * share[0] + hits[1] * share[1], axis=0, keepdims=True)
    gates[...] = column_of(slot_gate).reshape(EXPERT_COUNT, SLOTS, 128)
    pl.semaphore_wait(pltpu.get_barrier_semaphore(), 16)
    arrays = ((xs, x_all), (gates, t_all))

    def arriving(a, k):
        src, dst = arrays[a]
        tz, tx = chip_to(k)
        return remote(
            src.at[tz * 4 + tx], dst.at[slot_block(k, c)], send.at[a, k], recv.at[a, k], dev(y, tz, tx, c)
        )

    def steps_of(part):
        return (1, 8) if part == 0 else (8, 16)

    def scatter(a, part):
        def push(k, carry):
            arriving(a, k).start()
            return carry

        lax.fori_loop(*steps_of(part), push, 0)
        if part == 0:
            src, dst = arrays[a]
            pltpu.make_async_copy(src.at[me], dst.at[slot_block(0, c)], l_sem.at[a]).start()
            remote(src.at[me], dst.at[slot_block(0, c)], f_send.at[a, 0], f_recv.at[a, 0], sibling).start()

    def hand_over(a, part):
        src, dst = arrays[a]

        def forward(k, carry):
            arrived = arriving(a, k)
            arrived.wait_recv()
            block = dst.at[slot_block(k, c)]
            remote(block, block, f_send.at[a, part], f_recv.at[a, part], sibling).start()
            arrived.wait_send()
            return carry

        lax.fori_loop(*steps_of(part), forward, 0)

    def settle(a, part):
        src, dst = arrays[a]
        if part == 0:
            pltpu.make_async_copy(src.at[me], dst.at[slot_block(0, c)], l_sem.at[a]).wait()
        some = dst.at[pl.ds(0, 8)]
        drain = remote(some, some, f_send.at[a, part], f_recv.at[a, part], sibling)
        drain.wait_send()
        drain.wait_recv()

    def swap(mine, sib, a, part):
        return remote(
            mine.at[pl.ds(part * 16 + (1 - c) * 8, 8)], sib.at[pl.ds(part * 8, 8)],
            s_send.at[a, part], s_recv.at[a, part], sibling,
        )

    def give(mine, sib, ret, a, part):
        def add(k):
            block = slot_block(k, c)
            mine[block] = (mine[block].astype(F32) + sib[k].astype(F32)).astype(BF)
            return mine.at[block]

        def push(k, carry):
            sz, sx = chip_from(k)
            remote(add(k), ret.at[me], r_send.at[a], r_recv.at[a], dev(y, sz, sx, c)).start()
            return carry

        lax.fori_loop(*steps_of(part), push, 0)
        if part == 0:
            pltpu.make_async_copy(add(0), ret.at[me], l_sem.at[2 + a]).start()

    def given(mine, ret, a):
        pltpu.make_async_copy(mine.at[slot_block(0, c)], ret.at[me], l_sem.at[2 + a]).wait()
        drain = remote(ret.at[pl.ds(0, 15)], ret.at[pl.ds(0, 15)], r_send.at[a], r_recv.at[a], sibling)
        drain.wait_send()
        drain.wait_recv()

    half = 16 * SLOTS

    def forward_pass(part):
        blocks, rows = pl.ds(part * 16, 16), slice(part * half, part * half + half)
        both = dot(flat_rows(x_all[blocks]), w_all[:, : 2 * width], ((1,), (0,)))
        gate_val, up_val = both[:, :width], both[:, width:]
        gate_v[rows] = gate_val
        up_v[rows] = up_val
        low = (gate_val * jax.nn.sigmoid(gate_val) * up_val).astype(BF)
        hidden[rows] = low
        out = dot(low, w_all[:, 2 * width :], ((1,), (1,))).astype(BF)
        part_o[blocks] = out.reshape(16, SLOTS, MODEL_WIDTH)
        swap(part_o, sib_o, 0, part).start()

    def backward_pass(part):
        blocks, rows = pl.ds(part * 16, 16), slice(part * half, part * half + half)
        scale = jnp.concatenate([flat_rows(t_all[blocks])] * (MODEL_WIDTH // 128), axis=1)
        grad_expert = (flat_rows(g_all[blocks]).astype(F32) * scale).astype(BF)
        g_all[blocks] = grad_expert.reshape(16, SLOTS, MODEL_WIDTH)
        grad_hidden = dot(grad_expert, w_all[:, 2 * width :], ((1,), (0,)))
        gate_val = gate_v[rows]
        up_val = up_v[rows]
        sig = jax.nn.sigmoid(gate_val)
        grad_gate = (grad_hidden * up_val * sig * (1.0 + gate_val * (1.0 - sig))).astype(BF)
        grad_up = (grad_hidden * gate_val * sig).astype(BF)
        grads = jnp.concatenate([grad_gate, grad_up], axis=1)
        g_both[rows] = grads
        grad_rows = dot(grads, w_all[:, : 2 * width], ((1,), (1,))).astype(BF)
        part_g[blocks] = grad_rows.reshape(16, SLOTS, MODEL_WIDTH)
        swap(part_g, sib_g, 1, part).start()

    scatter(0, 0)
    scatter(1, 0)
    scatter(0, 1)
    scatter(1, 1)
    loads[2].wait()
    loads[3].wait()
    hand_over(0, 0)
    settle(0, 0)
    forward_pass(0)
    hand_over(0, 1)
    swap(part_o, sib_o, 0, 0).wait()
    give(part_o, sib_o, out_ret, 0, 0)
    settle(0, 1)
    forward_pass(1)
    hand_over(1, 0)
    hand_over(1, 1)
    settle(1, 0)
    swap(part_o, sib_o, 0, 1).wait()
    give(part_o, sib_o, out_ret, 0, 1)
    backward_pass(0)
    settle(1, 1)
    swap(part_g, sib_g, 1, 0).wait()
    give(part_g, sib_g, grad_ret, 1, 0)
    backward_pass(1)
    swap(part_g, sib_g, 1, 1).wait()
    give(part_g, sib_g, grad_ret, 1, 1)

    def weight_grads(j, carry):
        cols = pl.ds(pl.multiple_of(j * 256, 256), 256)
        v_all[cols, : 2 * width] = dot(flat_rows(x_all[:, :, cols]), g_both[...], ((0,), (0,))).astype(BF)
        v_all[cols, 2 * width :] = dot(flat_rows(g_all[:, :, cols]), hidden[...], ((0,), (0,))).astype(BF)
        return carry

    lax.fori_loop(0, MODEL_WIDTH // 256, weight_grads, 0)
    store = pltpu.make_async_copy(v_all, d_all, o_sem)
    store.start()
    given(part_o, out_ret, 0)
    grad_out = cotangent[...].astype(F32)
    rows_out = [dot(hits[k].astype(BF), flat_rows(out_ret[...]), ((1,), (0,))) for k in range(2)]
    o_block[...] = (middle[...] + share[0] * rows_out[0] + share[1] * rows_out[1]).astype(BF)
    pairs = [jnp.sum(grad_out * rows, axis=1, keepdims=True) for rows in rows_out]
    mean = share[0] * pairs[0] + share[1] * pairs[1]
    grad_logits = sum(chosen[k] * (share[k] * (pairs[k] - mean)) for k in range(2))
    o_logits[...] = grad_logits
    o_moe[...] = moe_in[...]
    routed = sum(dot(part, flat_extra, ((1,), (1,))) for part in three_parts(grad_logits))
    given(part_g, grad_ret, 1)
    grad_moe = dot(both_hits, flat_rows(grad_ret[...]), ((1,), (0,))) + routed
    o_gain[...] = jnp.sum(grad_moe * middle[...] * inverse, axis=0, keepdims=True)
    grad_middle = grad_out + norm_backward(middle[...], inverse, gain, grad_moe)
    o_middle[...] = grad_middle
    branch = grad_middle.astype(BF)
    o_branch[...] = branch
    for core, weight in ((c, wh), (1 - c, ws)):
        heads = dot(weight[...].reshape(MODEL_WIDTH, Q_HALF), branch, ((0,), (1,))).astype(BF)
        o_heads[pl.ds(core * 4, 4)] = heads.reshape(4, HEAD_Q, ROWS)
    store.wait()


def experts(attn, tokens, extra, ids, cotangent, half_w, sib_w, cots, weights):
    rows = 32 * SLOTS
    width = weights.shape[1] // 3
    slots = (16, SLOTS, MODEL_WIDTH)
    flat = (ROWS, MODEL_WIDTH)
    low = jax.ShapeDtypeStruct(flat, BF)
    return pl.pallas_call(
        experts_kernel,
        out_shape=[
            low,
            jax.ShapeDtypeStruct(flat, F32),
            low,
            jax.ShapeDtypeStruct((8, HEAD_Q, ROWS), BF),
            low,
            jax.ShapeDtypeStruct((ROWS, 128), F32),
            jax.ShapeDtypeStruct((1, MODEL_WIDTH), F32),
            jax.ShapeDtypeStruct(weights.shape, BF),
        ],
        in_specs=[IN_VMEM] * 5 + [ANY] * 4,
        out_specs=[IN_VMEM] * 7 + [ANY],
        scratch_shapes=[
            pltpu.VMEM((32, SLOTS, MODEL_WIDTH), BF),
            pltpu.VMEM((32, SLOTS, 128), F32),
            pltpu.VMEM((32, SLOTS, MODEL_WIDTH), BF),
            pltpu.VMEM(weights.shape, BF),
            pltpu.VMEM((rows, width), F32),
            pltpu.VMEM((rows, width), F32),
            pltpu.VMEM((rows, width), BF),
            pltpu.VMEM((rows, 2 * width), BF),
            pltpu.VMEM((32, SLOTS, MODEL_WIDTH), BF),
            pltpu.VMEM((32, SLOTS, MODEL_WIDTH), BF),
            pltpu.VMEM((16, SLOTS, MODEL_WIDTH), BF),
            pltpu.VMEM((16, SLOTS, MODEL_WIDTH), BF),
            pltpu.VMEM(weights.shape, BF),
            pltpu.VMEM(half_w.shape, BF),
            pltpu.VMEM(half_w.shape, BF),
            pltpu.VMEM(slots, BF),
            pltpu.VMEM((EXPERT_COUNT, SLOTS, 128), F32),
            pltpu.VMEM(slots, BF),
            pltpu.VMEM(slots, BF),
            pltpu.VMEM(flat, F32),
            pltpu.VMEM(flat, BF),
            pltpu.SemaphoreType.DMA((4,)),
            pltpu.SemaphoreType.DMA((4,)),
            pltpu.SemaphoreType.DMA((2, 16)),
            pltpu.SemaphoreType.DMA((2, 16)),
            pltpu.SemaphoreType.DMA((2, 2)),
            pltpu.SemaphoreType.DMA((2, 2)),
            pltpu.SemaphoreType.DMA((2, 2)),
            pltpu.SemaphoreType.DMA((2, 2)),
            pltpu.SemaphoreType.DMA((2,)),
            pltpu.SemaphoreType.DMA((2,)),
            pltpu.SemaphoreType.DMA,
        ],
        compiler_params=params(6, 60 << 20),
        name="experts",
    )(attn, tokens, extra, ids, cotangent, half_w, sib_w, cots, weights)


SUMS = tuple((n, start, width, order[::-1]) for n, start, width, order in FIRST_PARTS) + tuple(
    (2, start, 256, order) for start, order in OUT_SUMS
)
LATE = len(FIRST_PARTS)


def reduce_kernel(
    gq_t, dkv, normed, s_out, grad_logits, gain_m, moe_h, pair_h, extra_h, middle_h, w_q, w_kv, experts_h,
    o_tokens, o_q, o_k, o_v, o_out, o_extra, o_gate, o_up, o_down,
    moe_in, pair, w_extra, grad_middle, summed, f_gate, f_up, f_down, v_q, v_kv, v_extra, wq, wkv, gkv, mine_part, give_part, sib_part, both, total, give, *rest,
):
    parts = len(SUMS)
    first_in, rest = rest[:LATE], rest[LATE:]
    arrive = [list(first_in) + [None] * 3, rest[:parts], rest[parts : 2 * parts]]
    rest = rest[2 * parts :]
    held = [None, list(rest[:LATE]) + [s_out.at[k] for k in range(3)], rest[LATE : LATE + parts]]
    l_sem, send, recv, sib_send, sib_recv = rest[LATE + parts :]
    grads = (v_q, v_kv, None, v_extra)
    y, z, x, c = coords()
    place = {"y": y, "z": z, "x": x}
    sibling = dev(y, z, x, 1 - c)
    loads = [
        pltpu.make_async_copy(src, dst, l_sem.at[n])
        for n, (src, dst) in enumerate(
            (
                (w_q, wq), (w_kv, wkv), (pair_h, pair), (moe_h, moe_in), (extra_h, w_extra),
                (middle_h, grad_middle), (experts_h, summed),
            )
        )
    ]
    for load in loads:
        load.start()
    for axis in ("x", "y", "z"):
        for step in STEPS:
            signal(axis_peer(axis, step))
    signal(sibling)
    pl.semaphore_wait(pltpu.get_barrier_semaphore(), 10)

    def at(phase, part, index):
        n, start, width, order = SUMS[part]
        spot = [
            index if axis == order[phase] else slice(None)
            for axis in ("y", "z", "x")
            if axis not in order[:phase]
        ]
        if phase == 0:
            return grads[n].at[tuple(spot) + (slice(None), pl.ds(start, width))]
        return held[phase][part].at[tuple(spot)]

    def copies_of(phase, part):
        axis = SUMS[part][3][phase]
        return [
            remote(
                at(phase, part, (place[axis] + step) % 4), arrive[phase][part].at[n],
                send.at[phase, part, n], recv.at[phase, part, n], axis_peer(axis, step),
            )
            for n, step in enumerate(STEPS)
        ]

    def begin(phase, part):
        for copy in copies_of(phase, part):
            copy.start()

    def finish(phase, part):
        for copy in copies_of(phase, part):
            copy.wait()
        array, start, width, order = SUMS[part]
        mine = at(phase, part, place[order[phase]])
        got = arrive[phase][part]
        if phase < 2:

            def add(p, carry):
                value = mine[p].astype(F32)
                for n in range(3):
                    value = value + got[n, p].astype(F32)
                held[phase + 1][part][p] = value.astype(BF)
                return carry

            lax.fori_loop(0, 4, add, 0)
        else:
            value = mine[...].astype(F32)
            for n in range(3):
                value = value + got[n].astype(F32)
            total[:, STARTS[array] + start : STARTS[array] + start + width] = value

    for part in range(LATE, parts):
        begin(1, part)
    for h in range(4):
        value = dkv[4 * h].astype(F32)
        for n in range(1, 4):
            value = value + dkv[4 * h + n].astype(F32)
        gkv[128 * h : 128 * h + 128] = value.astype(BF)
    for n in range(4):
        left = normed[:, 384 * n : 384 * n + 384]
        v_kv[n] = dot(left, gkv[...], ((0,), (1,))).astype(BF).reshape(4, 4, 24, KV_HALF)
    begin(0, 1)
    for n in range(4):
        left = normed[:, 384 * n : 384 * n + 384]
        v_q[n] = dot(left, gq_t[...], ((0,), (1,))).astype(BF).reshape(4, 4, 24, Q_HALF)
    begin(0, 0)
    begin(0, 2)

    for load in loads:
        load.wait()
    gain_sum = jnp.zeros((1, MODEL_WIDTH), F32)
    for n in range(2):
        core = 1 - c if n == 0 else c
        rows = pl.ds(pl.multiple_of(core * ROWS, ROWS), ROWS)
        part = dot(gq_t[:, rows], wq[...], ((0,), (1,))) + dot(gkv[:, rows], wkv[...], ((0,), (1,)))
        values = pair[rows].astype(F32)
        gain_sum = gain_sum + jnp.sum(part * values * inverse_rms(values), axis=0, keepdims=True)
        if n == 0:
            give_part[...] = part
            remote(give_part, sib_part, sib_send.at[0], sib_recv.at[0], sibling).start()
        else:
            mine_part[...] = part
    lane = lax.broadcasted_iota(jnp.int32, (MODEL_WIDTH, EXTRA), 1)
    extra = sum(dot(moe_in[...], part, ((0,), (0,))) for part in three_parts(grad_logits[...]))
    extra = jnp.where(lane == EXPERT_COUNT, column_of(gain_sum), extra)
    extra = jnp.where(lane == EXPERT_COUNT + 1, column_of(gain_m[...]), extra)
    gain = jnp.transpose(w_extra[...].reshape(MODEL_WIDTH, EXTRA).astype(F32))[EXPERT_COUNT : EXPERT_COUNT + 1]
    v_extra[...] = extra.astype(BF).reshape(4, 4, 4, 24, EXTRA)
    begin(0, 3)
    remote(give_part, sib_part, sib_send.at[0], sib_recv.at[0], sibling).wait()
    rows = pl.ds(pl.multiple_of(c * ROWS, ROWS), ROWS)
    values = pair[rows].astype(F32)
    o_tokens[...] = grad_middle[...] + norm_backward(
        values, inverse_rms(values), gain, mine_part[...] + sib_part[...]
    )

    third = FF // 2
    f_gate[...] = summed[:, :third].astype(F32)
    f_up[...] = summed[:, third : 2 * third].astype(F32)
    f_down[...] = jnp.transpose(summed[:, 2 * third :].astype(F32))
    stores = [
        pltpu.make_async_copy(src, dst, l_sem.at[n])
        for n, (src, dst) in enumerate(((f_gate, o_gate), (f_up, o_up), (f_down, o_down)))
    ]
    for store in stores:
        store.start()
    for part in range(LATE, parts):
        finish(1, part)
        begin(2, part)
    for phase in range(3):
        for part in range(LATE):
            finish(phase, part)
            if phase < 2:
                begin(phase + 1, part)
    for part in range(LATE, parts):
        finish(2, part)
    low, high = total[0:12], total[12:24]
    both[c, 0:12] = jnp.where(c == 0, low, high)
    give[0:12] = jnp.where(c == 0, high, low)
    give[12:16] = jnp.zeros((4, PACK), F32)
    last = remote(give, both.at[c], sib_send.at[1], sib_recv.at[1], sibling)
    last.start()
    for store in stores:
        store.wait()
    last.wait()
    keys, values = [], []
    for k in range(2):
        o_q[:, Q_HALF * k : Q_HALF * k + Q_HALF] = both[k, 0:12, :Q_HALF]
        o_out[:, Q_HALF * k : Q_HALF * k + Q_HALF] = both[k, 0:12, STARTS[2] : STARTS[3]]
        for h in range(4):
            first = STARTS[1] + 128 * h
            keys.append(both[k, 0:12, first : first + HD])
            values.append(both[k, 0:12, first + HD : first + 2 * HD])
    o_k[...] = jnp.concatenate(keys, axis=1)
    o_v[...] = jnp.concatenate(values, axis=1)
    o_extra[...] = both[0, 0:12, STARTS[3] :] + both[1, 0:12, STARTS[3] :]


def reduce_weights(*args):
    widths = [part[2] for part in SUMS]
    full = lambda width: pltpu.VMEM((4, 4, 4, 24, width), BF)
    rows = pltpu.VMEM((ROWS, MODEL_WIDTH), F32)
    low = pltpu.VMEM((ROWS, MODEL_WIDTH), BF)
    scratch = (
        [low, pltpu.VMEM((PAIR, MODEL_WIDTH), BF), full(EXTRA), rows]
        + [pltpu.VMEM((MODEL_WIDTH // 4, 3 * FF // 2), BF)]
        + [pltpu.VMEM((MODEL_WIDTH // 4, FF // 2), F32)] * 2
        + [pltpu.VMEM((FF // 2, MODEL_WIDTH // 4), F32)]
        + [full(Q_HALF), full(KV_HALF), full(EXTRA)]
        + [pltpu.VMEM((MODEL_WIDTH, Q_HALF), BF), pltpu.VMEM((MODEL_WIDTH, KV_HALF), BF)]
        + [pltpu.VMEM((KV_HALF, PAIR), BF), rows, rows, rows]
        + [pltpu.VMEM((2, 16, PACK), F32), pltpu.VMEM((24, PACK), F32), pltpu.VMEM((16, PACK), F32)]
        + [pltpu.VMEM((3, 4, 4, 24, w), BF) for w in widths[:LATE]]
        + [pltpu.VMEM((3, 4, 24, w), BF) for w in widths]
        + [pltpu.VMEM((3, 24, w), BF) for w in widths]
        + [pltpu.VMEM((4, 4, 24, w), BF) for w in widths[:LATE]]
        + [pltpu.VMEM((4, 24, w), BF) for w in widths]
    )
    sems = (3, len(SUMS), 3)
    shapes = ((ROWS, MODEL_WIDTH), (12, MODEL_WIDTH), (12, KV * HD), (12, KV * HD), (12, MODEL_WIDTH), (12, EXTRA))
    tall, flat = (MODEL_WIDTH // 4, FF // 2), (FF // 2, MODEL_WIDTH // 4)
    shapes = shapes + (tall, tall, flat)
    return pl.pallas_call(
        reduce_kernel,
        out_shape=[jax.ShapeDtypeStruct(shape, F32) for shape in shapes],
        in_specs=[IN_VMEM] * 6 + [ANY] * 7,
        out_specs=[IN_VMEM] * 6 + [ANY] * 3,
        scratch_shapes=scratch
        + [
            pltpu.SemaphoreType.DMA((7,)),
            pltpu.SemaphoreType.DMA(sems),
            pltpu.SemaphoreType.DMA(sems),
            pltpu.SemaphoreType.DMA((2,)),
            pltpu.SemaphoreType.DMA((2,)),
        ],
        compiler_params=params(8, 60 << 20),
        name="reduce_weights",
    )(*args)


def wide_greet():
    y, z, x, c = coords()
    me = z * 4 + x

    def greet(k, carry):
        t = (me + k) % 16
        signal(dev(y, t // 4, t % 4, c))
        return carry

    lax.fori_loop(1, 16, greet, 0)
    for step in STEPS:
        signal(axis_peer("y", step))
        signal(dev(y, (z + step) % 4, x, 1 - c))
    signal(dev(y, z, x, 1 - c))
    pl.semaphore_wait(pltpu.get_barrier_semaphore(), 22)


def attend_back_kernel(
    heads, branch_h, attn_h, q_h, kv_h, first_ref, ot_h, lse_ref,
    dq_out, dkv_out, s_out,
    branch, attn, q_in, kv_in, ot_ref, keep, go, branch_sib, attn_sib, qs, gs, delta, dq, dkv, dkv_low, dq_low,
    g_out, a_out,
    l_sem, h_send, h_recv, sib_send, sib_recv, q_send, q_recv, k_send, k_recv,
    w_send, w_recv,
):
    y, z, x, c = coords()
    me = z * 4 + x
    j = c * 4 + z
    sibling = dev(y, z, x, 1 - c)
    place = {"y": y, "z": z, "x": x}
    loads = [
        pltpu.make_async_copy(src, dst, keep.at[n])
        for n, (src, dst) in enumerate(
            ((branch_h, branch), (attn_h, attn), (q_h, q_in), (kv_h, kv_in), (ot_h, ot_ref))
        )
    ]
    for load in loads:
        load.start()
    wide_greet()

    def push(k, carry):
        t = (j + k) % 8
        remote(heads.at[t], go.at[j], h_send, h_recv, dev(y, t % 4, x, t // 4)).start()
        return carry

    lax.fori_loop(1, 8, push, 0)
    one = remote(branch_h, branch_sib, sib_send.at[0], sib_recv.at[0], sibling)
    one.start()
    two = remote(attn_h.at[pl.ds((1 - c) * 4, 4)], attn_sib, sib_send.at[1], sib_recv.at[1], sibling)
    two.start()
    here = pltpu.make_async_copy(heads.at[j], go.at[j], l_sem.at[0])
    here.start()
    loads[0].wait()
    loads[1].wait()
    one.wait()
    two.wait()

    rows_b = jnp.concatenate([branch[...], branch_sib[...]], axis=0)
    rows_a = jnp.concatenate(
        [part.reshape(Q_HALF, ROWS) for part in (attn[pl.ds(c * 4, 4)], attn_sib[...])], axis=1
    )
    for n in range(4):
        part = dot(rows_b[:, 384 * n : 384 * n + 384], rows_a, ((0,), (1,)))
        g_out[n] = part.astype(BF).reshape(4, 4, 24, Q_HALF)

    def spot(part, index):
        start, order = OUT_SUMS[part]
        cut = [index if axis == order[0] else slice(None) for axis in ("y", "z", "x")]
        return g_out.at[tuple(cut) + (slice(None), pl.ds(start, 256))]

    w_copies = []
    for part in range(3):
        axis = OUT_SUMS[part][1][0]
        for n, step in enumerate(STEPS):
            copy = remote(
                spot(part, (place[axis] + step) % 4), a_out.at[part, n],
                w_send.at[part, n], w_recv.at[part, n], axis_peer(axis, step),
            )
            copy.start()
            w_copies.append(copy)

    for load in loads[2:]:
        load.wait()
    here.wait()
    drain = remote(go.at[pl.ds(0, 7)], go.at[pl.ds(0, 7)], h_send, h_recv, sibling)
    drain.wait_send()
    drain.wait_recv()
    dkv[...] = jnp.zeros_like(dkv)
    dq[...] = jnp.zeros_like(dq)
    for zq in range(4):
        q = q_in[zq] * SCALE_QK
        grad = jnp.concatenate([go[zq], go[4 + zq]], axis=1)
        qs[zq, 64:] = jnp.zeros((64, 3 * PAIR), BF)
        gs[zq, :64] = jnp.zeros((64, 3 * PAIR), BF)
        for h in range(3):
            cols, rows = slice(256 * h, 256 * h + 256), slice(64 * h, 64 * h + 64)
            qs[zq, :64, cols] = q[rows]
            gs[zq, 64:, cols] = grad[rows]
            delta[zq, :, cols] = jnp.sum(
                grad[rows].astype(F32) * ot_ref[zq, :, cols], axis=0, keepdims=True
            )

    for n in range(4):
        group = (z + n + 1) % 4
        for zq in range(4):
            hi = zq * 4 + x
            first = first_ref[zq]
            q_pos = hi * PAIR + lax.broadcasted_iota(jnp.int32, (1, PAIR), 1)

            def step(kb, carry):
                kv = kv_in[kb]
                k_pos = kb * PAIR + lax.broadcasted_iota(jnp.int32, (PAIR, PAIR), 0)
                ok = (k_pos >= first) & (k_pos <= q_pos)
                heads = [slice(256 * h, 256 * h + 256) for h in range(3)]
                scores = [dot(kv, qs[zq, :, cols], ((1,), (0,))) for cols in heads]
                grad_probs = [dot(kv, gs[zq, :, cols], ((1,), (0,))) for cols in heads]
                grad_scores, probs = [], []
                for h in range(3):
                    prob = jnp.where(ok, jnp.exp(scores[h] - lse_ref[zq, :, heads[h]]), 0.0)
                    grad_scores.append((prob * (grad_probs[h] - delta[zq, :, heads[h]])).astype(BF))
                    probs.append(prob.astype(BF))
                for h in range(3):
                    dq[zq, :, heads[h]] = dq[zq, :, heads[h]] + dot(kv, grad_scores[h], ((0,), (0,)))
                grad_scores, probs = jnp.concatenate(grad_scores, axis=1), jnp.concatenate(probs, axis=1)
                dkv[kb, :64] = dkv[kb, :64] + dot(qs[zq, :64], grad_scores, ((1,), (1,)))
                dkv[kb, 64:] = dkv[kb, 64:] + dot(gs[zq, 64:], probs, ((1,), (1,)))
                return carry

            last = jnp.minimum(group * 4 + 3, hi)
            lax.fori_loop(group * 4, jnp.maximum(last + 1, group * 4), step, 0)
        for d in range(4):
            xt = (x + d + 1) % 4
            t = group * 4 + xt
            dkv_low[t] = dkv[t].astype(BF)
            if n == 3 and d == 3:
                own_kv = pltpu.make_async_copy(dkv_low.at[me], dkv_out.at[me], l_sem.at[2])
                own_kv.start()
            else:
                remote(dkv_low.at[t], dkv_out.at[me], k_send, k_recv, dev(y, group, xt, c)).start()
    q_copies = []
    for n in range(4):
        zq = (z + n + 1) % 4
        by_head = jnp.concatenate([dq[zq, :64, 256 * h : 256 * h + 256] for h in range(3)], axis=0)
        dq_low[zq] = (by_head * SCALE_QK).astype(BF)
        if n < 3:
            copy = remote(dq_low.at[zq], dq_out.at[z], q_send.at[n], q_recv.at[n], dev(y, zq, x, c))
        else:
            copy = pltpu.make_async_copy(dq_low.at[zq], dq_out.at[z], l_sem.at[1])
        copy.start()
        q_copies.append(copy)

    for copy in w_copies:
        copy.wait()
    for part in range(3):
        mine = spot(part, place[OUT_SUMS[part][1][0]])

        def add(p, carry):
            value = mine[p].astype(F32)
            for k in range(3):
                value = value + a_out[part, k, p].astype(F32)
            s_out[part, p] = value.astype(BF)
            return carry

        lax.fori_loop(0, 4, add, 0)
    for copy in q_copies:
        copy.wait()
    own_kv.wait()
    drain = remote(dkv_out.at[pl.ds(0, 15)], dkv_out.at[pl.ds(0, 15)], k_send, k_recv, sibling)
    drain.wait_send()
    drain.wait_recv()


def attend_back(heads, branch, attn, q_in, kv_in, first, ot, lse):
    return pl.pallas_call(
        attend_back_kernel,
        out_shape=[
            jax.ShapeDtypeStruct((4, HEAD_Q, PAIR), BF),
            jax.ShapeDtypeStruct((16, 128, PAIR), BF),
            jax.ShapeDtypeStruct((3, 4, 4, 24, 256), BF),
        ],
        in_specs=[ANY] * 5 + [IN_VMEM, ANY, IN_VMEM],
        out_specs=[ANY, ANY, IN_VMEM],
        scratch_shapes=[
            pltpu.VMEM((ROWS, MODEL_WIDTH), BF),
            pltpu.VMEM((8, HEAD_Q, ROWS), BF),
            pltpu.VMEM((4, HEAD_Q, PAIR), BF),
            pltpu.VMEM((16, PAIR, 128), BF),
            pltpu.VMEM((4, HD, 3 * PAIR), F32),
            pltpu.SemaphoreType.DMA((5,)),
            pltpu.VMEM((8, HEAD_Q, ROWS), BF),
            pltpu.VMEM((ROWS, MODEL_WIDTH), BF),
            pltpu.VMEM((4, HEAD_Q, ROWS), BF),
            pltpu.VMEM((4, 128, 3 * PAIR), BF),
            pltpu.VMEM((4, 128, 3 * PAIR), BF),
            pltpu.VMEM((4, 1, 3 * PAIR), F32),
            pltpu.VMEM((4, 128, 3 * PAIR), F32),
            pltpu.VMEM((16, 128, PAIR), F32),
            pltpu.VMEM((16, 128, PAIR), BF),
            pltpu.VMEM((4, HEAD_Q, PAIR), BF),
            pltpu.VMEM((4, 4, 4, 24, Q_HALF), BF),
            pltpu.VMEM((3, 3, 4, 4, 24, 256), BF),
            pltpu.SemaphoreType.DMA((3,)),
            pltpu.SemaphoreType.DMA,
            pltpu.SemaphoreType.DMA,
            pltpu.SemaphoreType.DMA((2,)),
            pltpu.SemaphoreType.DMA((2,)),
            pltpu.SemaphoreType.DMA((4,)),
            pltpu.SemaphoreType.DMA((4,)),
            pltpu.SemaphoreType.DMA,
            pltpu.SemaphoreType.DMA,
            pltpu.SemaphoreType.DMA((3, 3)),
            pltpu.SemaphoreType.DMA((3, 3)),
        ],
        compiler_params=params(4, 60 << 20),
        name="attend_back",
    )(heads, branch, attn, q_in, kv_in, first, ot, lse)


def inverse_rms(values):
    return lax.rsqrt(jnp.mean(values * values, axis=-1, keepdims=True) + EPS)


def norm_backward(values, inverse, gain, grad_out):
    scaled = grad_out * gain
    return inverse * scaled - values * inverse**3 * jnp.mean(values * scaled, axis=-1, keepdims=True)


def finish_kernel(extra, *refs):
    n = (len(refs) - 5) // 3
    sources, targets = refs[:n], refs[n : 2 * n]
    o_router, o_gain_a, o_gain_m = refs[2 * n : 2 * n + 3]
    held, (l_sem, s_sem) = refs[2 * n + 3 : 3 * n + 3], refs[3 * n + 3 :]
    loads = [pltpu.make_async_copy(sources[k], held[k], l_sem.at[k]) for k in range(n)]
    stores = [pltpu.make_async_copy(held[k], targets[k], s_sem.at[k]) for k in range(n)]
    for load in loads:
        load.start()
    o_router[...] = extra[:, :EXPERT_COUNT]
    square = lax.broadcasted_iota(jnp.int32, (12, 12), 0) == lax.broadcasted_iota(jnp.int32, (12, 12), 1)
    for k, out in enumerate((o_gain_a, o_gain_m)):
        column = jnp.broadcast_to(extra[:, EXPERT_COUNT + k : EXPERT_COUNT + k + 1], (12, 12))
        out[...] = jnp.sum(jnp.where(square, column, 0.0), axis=0, keepdims=True)
    for k in range(n):
        loads[k].wait()
        stores[k].start()
    for store in stores:
        store.wait()


def finish(extra, arrays):
    n = len(arrays)
    shapes = [jax.ShapeDtypeStruct(array.shape, array.dtype) for array in arrays]
    small = [jax.ShapeDtypeStruct((12, EXPERT_COUNT), F32)] + [jax.ShapeDtypeStruct((1, 12), F32)] * 2
    return pl.pallas_call(
        finish_kernel,
        out_shape=shapes + small,
        in_specs=[IN_VMEM] + [ANY] * n,
        out_specs=[ANY] * n + [IN_VMEM] * 3,
        scratch_shapes=[pltpu.VMEM(shape.shape, shape.dtype) for shape in shapes]
        + [pltpu.SemaphoreType.DMA((n,)), pltpu.SemaphoreType.DMA((n,))],
        compiler_params=pltpu.CompilerParams(vmem_limit_bytes=60 << 20),
        name="finish",
    )(extra, *arrays)


def local(
    tokens,
    segment_ids,
    expert_ids,
    w_query,
    w_key,
    w_value,
    w_out,
    w_router,
    gain_attn,
    gain_moe,
    w_gate,
    w_up,
    w_down,
    cotangent,
):
    ids = expert_ids.T
    part_q, part_kv, part_out, part_extra, pair, normed, w_experts, q4, keys_values, first, cot_slots = (
        gather_weights(
            (w_query, w_key, w_value, w_out.T, w_router, gain_attn[None], gain_moe[None], ids, cotangent),
            (tokens, segment_ids, w_gate, w_up, w_down),
        )
    )
    full_experts = lax.all_gather(w_experts, "dp", axis=0, tiled=True)
    q_in, kv_in, attn, attn_t, lse, half_out, sib_out, cot_all = attend(
        q4, keys_values, part_out, cot_slots, first
    )
    block_out, grad_middle, branch, grad_heads, moe_in, grad_logits, gain_sum, grad_experts = experts(
        attn, tokens, part_extra, ids, cotangent, half_out, sib_out, cot_all, full_experts
    )
    sum_experts = lax.psum_scatter(grad_experts, "dp", scatter_dimension=0, tiled=True)
    dq_in, dkv_in, sum_out = attend_back(grad_heads, branch, attn, q_in, kv_in, first, attn_t, lse)
    grad_tokens, r_query, r_key, r_value, r_out, r_extra, *expert_grads = reduce_weights(
        dq_in.reshape(Q_HALF, PAIR), dkv_in, normed, sum_out, grad_logits, gain_sum, moe_in,
        pair.reshape(PAIR, MODEL_WIDTH), part_extra, grad_middle,
        part_q.reshape(MODEL_WIDTH, Q_HALF), part_kv.reshape(MODEL_WIDTH, KV_HALF), sum_experts,
    )
    *results, r_router, r_gain_a, r_gain_m = finish(
        r_extra,
        (grad_tokens, *expert_grads, block_out, r_query, r_key, r_value, r_out),
    )
    grad_tokens, g_gate, g_up, g_down, block_out, r_query, r_key, r_value, r_out = results
    return (
        block_out,
        grad_tokens,
        r_query,
        r_key,
        r_value,
        r_out.T,
        r_router,
        r_gain_a.reshape(12),
        r_gain_m.reshape(12),
        g_gate,
        g_up,
        g_down,
    )


def solution(mesh):
    rows, flat, dense = P(("dp", "ctx"), None), P(("dp", "ctx")), P("dp", "ctx")
    placed = (
        rows, dense, rows, rows, rows, rows, P(None, ("dp", "ctx")), rows, flat, flat,
        dense, dense, P("ctx", "dp"), rows,
    )
    return jax.shard_map(
        local,
        mesh=mesh,
        in_specs=placed,
        out_specs=(
            rows, rows, rows, rows, rows, P(None, ("dp", "ctx")), rows, flat, flat,
            dense, dense, P("ctx", "dp"),
        ),
        check_vma=False,
    )
```

```python
import functools

import jax
import jax.numpy as jnp
from jax import lax
from jax.experimental import pallas as pl
from jax.experimental.pallas import tpu as pltpu
from jax.sharding import PartitionSpec as P

MODEL_WIDTH = 1536
KV = 8
HD = 64
EXPERT_COUNT = 16
FF = 1024
EXPERT_CAPACITY = 20
SLOTS = 24
ROWS = 128
PAIR = 256
HEAD_Q = 192
Q_HALF = 768
KV_HALF = 512
EXTRA = 128
PACK = Q_HALF + KV_HALF + EXTRA + Q_HALF

EPS = 1e-05
SCALE_QK = 0.125
NEGATIVE = -1e30
MESH = pl.DeviceIdType.MESH
ANY = pl.BlockSpec(memory_space=pl.ANY)
IN_VMEM = pl.BlockSpec(memory_space=pltpu.VMEM)
BF = jnp.bfloat16
F32 = jnp.float32


def dot(a, b, dims):
    return lax.dot_general(a, b, (dims, ((), ())), preferred_element_type=F32)


def coords():
    i = lax.axis_index("ctx")
    return lax.axis_index("dp"), i // 8, (i // 2) % 4, i % 2


def dev(y, z, x, c):
    return (y, z * 8 + x * 2 + c)


def signal(target):
    pl.semaphore_signal(
        pltpu.get_barrier_semaphore(), inc=1, device_id=target, device_id_type=MESH
    )


def remote(src, dst, send, recv, target):
    return pltpu.make_async_remote_copy(
        src_ref=src, dst_ref=dst, send_sem=send, recv_sem=recv, device_id=target, device_id_type=MESH
    )


def params(cid, vmem=None):
    return pltpu.CompilerParams(collective_id=cid, has_side_effects=True, vmem_limit_bytes=vmem)


def axis_peer(axis, step):
    y, z, x, c = coords()
    if axis == "y":
        return dev((y + step) % 4, z, x, c)
    if axis == "z":
        return dev(y, (z + step) % 4, x, c)
    return dev(y, z, (x + step) % 4, c)


WIDTHS = (Q_HALF, KV_HALF, Q_HALF, EXTRA)
STARTS = (0, Q_HALF, Q_HALF + KV_HALF, 2 * Q_HALF + KV_HALF)
STEPS = (1, 3, 2)
FIRST_PARTS = (
    (0, 0, 512, ("x", "z", "y")),
    (1, 0, 512, ("y", "x", "z")),
    (0, 512, 256, ("z", "y", "x")),
    (3, 0, 128, ("z", "y", "x")),
)
OUT_PARTS = (
    (2, 0, 128, ("z", "x", "y")),
    (2, 128, 384, ("z", "y", "x")),
    (2, 512, 256, ("y", "x", "z")),
)
OUT_SUMS = ((0, ("x", "y", "z")), (256, ("x", "z", "y")), (512, ("z", "x", "y")))
GATHER_PARTS = FIRST_PARTS + OUT_PARTS


def slab(ref, done, y, z, x, cols):
    return ref.at[
        slice(None) if "y" in done else y,
        slice(None) if "z" in done else z,
        slice(None) if "x" in done else x,
        slice(None),
        cols,
    ]


def column_of(row):
    return jnp.transpose(jnp.broadcast_to(row, (128, row.shape[1])))


def slot_hits(ids):
    lane = lax.broadcasted_iota(jnp.int32, (ROWS, 128), 1).astype(F32)
    experts_of = [column_of(ids[k : k + 1].astype(F32)) for k in range(2)]
    chosen = [jnp.where(lane == expert, 1.0, 0.0) for expert in experts_of]
    row = lax.broadcasted_iota(jnp.int32, (ROWS, ROWS), 0)
    earlier = jnp.where(row > lax.broadcasted_iota(jnp.int32, (ROWS, ROWS), 1), 1.0, 0.0).astype(BF)
    before = dot(earlier, (chosen[0] + chosen[1]).astype(BF), ((1,), (0,)))
    slot_lane = lax.broadcasted_iota(jnp.int32, (ROWS, EXPERT_COUNT * SLOTS), 1).astype(F32)
    hits = []
    for k in range(2):
        place = jnp.sum(chosen[k] * before, axis=1, keepdims=True)
        slot = jnp.where(place < EXPERT_CAPACITY, experts_of[k][:, :1] * SLOTS + place, -1.0)
        hits.append(jnp.where(slot_lane == slot, 1.0, 0.0))
    return chosen, hits


def three_parts(values):
    parts = []
    for _ in range(3):
        part = values.astype(BF)
        parts.append(part)
        values = values - part.astype(F32)
    return parts


def gather_kernel(
    w_query, w_key, w_value, w_out, w_router, gain_a, gain_m, ids, cots, tokens, segs, w_gate, w_up, w_down,
    o_q, o_kv, out2, out3, pair, o_normed, w_experts, q4, kv2, o_first, cot_slots,
    pack, sib, block, w_q, w_kv, w_extra, rows, segments, normed, packed, down,
    p_send, p_recv, l_sem, s_send, s_recv, sib_send, sib_recv, o_sem,
):
    y, z, x, c = coords()
    outs = (w_q, w_kv, out2, w_extra)
    me = z * 8 + x * 2 + c
    sibling = dev(y, z, x, 1 - c)

    def greet(k, carry):
        signal((y, (me + k) % 32))
        return carry

    lax.fori_loop(1, 32, greet, 0)
    for step in STEPS:
        signal(axis_peer("y", step))
    expert_loads = [
        pltpu.make_async_copy(w_gate, packed.at[:, 0:FF // 2], o_sem.at[5]),
        pltpu.make_async_copy(w_up, packed.at[:, FF // 2 : FF], o_sem.at[6]),
        pltpu.make_async_copy(w_down, down, o_sem.at[7]),
    ]
    for load in expert_loads:
        load.start()
    lane = lax.broadcasted_iota(jnp.int32, (12, EXTRA), 1)
    square = lax.broadcasted_iota(jnp.int32, (12, 12), 0) == lax.broadcasted_iota(jnp.int32, (12, 12), 1)
    extra = jnp.concatenate(
        [w_router[...].astype(F32), jnp.zeros((12, EXTRA - EXPERT_COUNT), F32)], axis=1
    )
    for k, gain_row in enumerate((gain_a, gain_m)):
        spread_row = jnp.broadcast_to(gain_row[...].astype(F32), (12, 12))
        column = jnp.sum(jnp.where(square, spread_row, 0.0), axis=1, keepdims=True)
        extra = jnp.where(lane == EXPERT_COUNT + k, column, extra)
    extra = extra.astype(BF)
    heads = []
    for h in range(KV):
        cols = slice(HD * h, HD * h + HD)
        heads += [w_key[:, cols].astype(F32), w_value[:, cols].astype(F32)]
    heads = jnp.concatenate(heads, axis=1).astype(BF)
    for k in range(2):
        parts = (
            w_query[:, Q_HALF * k : Q_HALF * k + Q_HALF],
            heads[:, KV_HALF * k : KV_HALF * k + KV_HALF],
            w_out[:, Q_HALF * k : Q_HALF * k + Q_HALF],
            extra,
        )
        for start, width, part in zip(STARTS, WIDTHS, parts):
            pack[k, 0:12, start : start + width] = part
            pack[k, 12:16, start : start + width] = jnp.zeros((4, width), BF)
    pl.semaphore_wait(pltpu.get_barrier_semaphore(), 34)

    first = remote(pack.at[1 - c], sib, sib_send.at[0], sib_recv.at[0], sibling)
    first.start()
    second = remote(tokens, rows.at[c], sib_send.at[1], sib_recv.at[1], sibling)
    second.start()
    own_rows = pltpu.make_async_copy(tokens, rows.at[c], l_sem.at[4])
    own_rows.start()
    own_segs = pltpu.make_async_copy(segs, segments.at[me], l_sem.at[5])
    own_segs.start()

    def spread(k, carry):
        remote(segs, segments.at[me], s_send, s_recv, (y, (me + k) % 32)).start()
        return carry

    lax.fori_loop(1, 32, spread, 0)

    first.wait()
    own = pack[c, :12].astype(F32)
    other = sib[:12].astype(F32)
    low = jnp.where(c == 0, own, other)
    high = jnp.where(c == 0, other, own)
    block[...] = jnp.concatenate([low, high], axis=0).astype(BF)

    locals_ = []
    for n in range(4):
        cols = pl.ds(STARTS[n], WIDTHS[n])
        here = pltpu.make_async_copy(block.at[:, cols], outs[n].at[y, z, x], l_sem.at[n])
        here.start()
        locals_.append(here)
    for phase in range(3):
        copies = []
        for part, (n, start, width, order) in enumerate(GATHER_PARTS if phase < 2 else FIRST_PARTS):
            for k, step in enumerate(STEPS):
                dst = slab(outs[n], order[:phase], y, z, x, pl.ds(start, width))
                src = block.at[:, pl.ds(STARTS[n] + start, width)] if phase == 0 else dst
                copy = remote(
                    src, dst, p_send.at[phase, part, k], p_recv.at[phase, part, k],
                    axis_peer(order[phase], step),
                )
                copy.start()
                copies.append(copy)
        if phase == 0:
            for here in locals_:
                here.wait()
        if phase == 2:
            own_segs.wait()
            drain = remote(
                segments.at[pl.ds(0, 31)], segments.at[pl.ds(0, 31)], s_send, s_recv, sibling
            )
            drain.wait_send()
            drain.wait_recv()
            places = segments[...].reshape(32, 128)
            for zq in range(4):
                t = (zq * 4 + x) * 2
                mine = jnp.concatenate([segments[t], segments[t + 1]], axis=1)
                begin = jnp.zeros((1, PAIR), jnp.int32)
                for u in range(15):
                    count = jnp.sum((places == u).astype(jnp.int32))
                    begin = begin + jnp.where(mine > u, count, 0)
                o_first[zq] = begin
            chosen, hits = slot_hits(ids[...])
            kept = dot((hits[0] + hits[1]).astype(BF), cots[...], ((0,), (0,))).astype(BF)
            cot_slots[...] = kept.reshape(EXPERT_COUNT, SLOTS, MODEL_WIDTH)
            for load in expert_loads:
                load.wait()
            packed[:, FF:] = jnp.transpose(down[...].astype(F32)).astype(BF)
            pltpu.make_async_copy(packed, w_experts, o_sem.at[5]).start()
            second.wait()
            own_rows.wait()
        for copy in copies:
            copy.wait()
    stores = [
        pltpu.make_async_copy(src, dst, o_sem.at[n])
        for n, (src, dst) in enumerate(((w_q, o_q), (w_kv, o_kv), (w_extra, out3), (rows, pair)))
    ]
    for store in stores:
        store.start()
    gain = jnp.transpose(w_extra[...].reshape(MODEL_WIDTH, EXTRA).astype(F32))[EXPERT_COUNT : EXPERT_COUNT + 1]
    for k in range(2):
        values = rows[k].astype(F32)
        normed[ROWS * k : ROWS * k + ROWS] = (values * inverse_rms(values) * gain).astype(BF)
    last = pltpu.make_async_copy(normed, o_normed, o_sem.at[4])
    last.start()
    queries = dot(w_q[...].reshape(MODEL_WIDTH, Q_HALF), normed[...], ((0,), (1,))).astype(BF)
    q4[...] = queries.reshape(4, HEAD_Q, PAIR)
    kv2[...] = dot(normed[...], w_kv[...].reshape(MODEL_WIDTH, KV_HALF), ((1,), (0,))).astype(BF)
    for store in stores:
        store.wait()
    last.wait()
    pltpu.make_async_copy(packed, w_experts, o_sem.at[5]).wait()


def gather_weights(vmem_args, hbm_args):
    blocks = [(4, 4, 4, 24, width) for width in WIDTHS]
    rows = (2, ROWS, MODEL_WIDTH)
    flat = (PAIR, MODEL_WIDTH)
    experts_in = (MODEL_WIDTH // 4, 3 * FF // 2)
    return pl.pallas_call(
        gather_kernel,
        out_shape=[jax.ShapeDtypeStruct(shape, BF) for shape in (*blocks, rows, flat, experts_in)]
        + [
            jax.ShapeDtypeStruct((4, HEAD_Q, PAIR), BF),
            jax.ShapeDtypeStruct((PAIR, KV_HALF), BF),
            jax.ShapeDtypeStruct((4, 1, PAIR), jnp.int32),
            jax.ShapeDtypeStruct((EXPERT_COUNT, SLOTS, MODEL_WIDTH), BF),
        ],
        in_specs=[IN_VMEM] * len(vmem_args) + [ANY] * len(hbm_args),
        out_specs=[ANY] * 7 + [IN_VMEM] * 4,
        scratch_shapes=[
            pltpu.VMEM((2, 16, PACK), BF),
            pltpu.VMEM((16, PACK), BF),
            pltpu.VMEM((24, PACK), BF),
            pltpu.VMEM(blocks[0], BF),
            pltpu.VMEM(blocks[1], BF),
            pltpu.VMEM(blocks[3], BF),
            pltpu.VMEM(rows, BF),
            pltpu.VMEM((32, 1, 128), jnp.int32),
            pltpu.VMEM(flat, BF),
            pltpu.VMEM(experts_in, BF),
            pltpu.VMEM((FF // 2, MODEL_WIDTH // 4), BF),
            pltpu.SemaphoreType.DMA((3, 7, 3)),
            pltpu.SemaphoreType.DMA((3, 7, 3)),
            pltpu.SemaphoreType.DMA((6,)),
            pltpu.SemaphoreType.DMA,
            pltpu.SemaphoreType.DMA,
            pltpu.SemaphoreType.DMA((2,)),
            pltpu.SemaphoreType.DMA((2,)),
            pltpu.SemaphoreType.DMA((8,)),
        ],
        compiler_params=params(1, 60 << 20),
        name="gather_weights",
    )(*vmem_args, *hbm_args)


def offset(k):
    dz = (k % 8) // 2
    return dz, 2 * (k % 2) + (dz + k // 8) % 2


def chip_to(k):
    y, z, x, c = coords()
    dz, dx = offset(k)
    return (z + dz) % 4, (x + dx) % 4


def chip_from(k):
    y, z, x, c = coords()
    dz, dx = offset(k)
    return (z + 4 - dz) % 4, (x + 4 - dx) % 4


def slot_block(k, core):
    return (k // 8) * 16 + core * 8 + k % 8


def plane_greet():
    y, z, x, c = coords()
    me = z * 4 + x

    def greet(k, carry):
        t = (me + k) % 16
        signal(dev(y, t // 4, t % 4, c))
        return carry

    lax.fori_loop(1, 16, greet, 0)
    signal(dev(y, z, x, 1 - c))


KEYS = 1024


def attend_kernel(
    q4, kv2, half_in, cots, first_ref, q_out, kv_out, attn, ot_out, lse_ref, half, half_sib, c_all,
    q_in, kv_in, ot_ref, qs, acc, o_buf, keep,
    l_sem, q_send, q_recv, k_send, k_recv, w_send, w_recv, sib_send, sib_recv,
    c_send, c_recv, f_send, f_recv, o_send, o_recv,
):
    y, z, x, c = coords()
    me = z * 4 + x
    sibling = dev(y, z, x, 1 - c)

    wide_greet()

    q_copies = []
    for n, step in enumerate(STEPS):
        to = (z + step) % 4
        copy = remote(q4.at[to], q_in.at[z], q_send.at[n], q_recv.at[n], dev(y, to, x, c))
        copy.start()
        q_copies.append(copy)

    def head(index):
        return kv2.at[:, pl.ds(pl.multiple_of(index * 128, 128), 128)]

    def send_kv(k, carry):
        tz, tx = chip_to(k)
        remote(head(tz), kv_in.at[me], k_send, k_recv, dev(y, tz, tx, c)).start()
        return carry

    lax.fori_loop(1, 16, send_kv, 0)
    here = [
        pltpu.make_async_copy(q4.at[z], q_in.at[z], l_sem.at[0]),
        pltpu.make_async_copy(head(z), kv_in.at[me], l_sem.at[1]),
    ]
    for copy in here:
        copy.start()
    for copy in here:
        copy.wait()
    for copy in q_copies:
        copy.wait()
    drain = remote(kv_in.at[pl.ds(0, 15)], kv_in.at[pl.ds(0, 15)], k_send, k_recv, sibling)
    drain.wait_send()
    drain.wait_recv()

    w_copies = [[], [], []]
    for part, (n, start, width, order) in enumerate(OUT_PARTS):
        spot = slab(half, order[:2], y, z, x, pl.ds(start, width))
        for k, step in enumerate(STEPS):
            copy = remote(
                spot, spot, w_send.at[part, k], w_recv.at[part, k], axis_peer(order[2], step)
            )
            copy.start()
            w_copies[part].append(copy)

    kept = [
        pltpu.make_async_copy(q_in, q_out, keep.at[4]),
        pltpu.make_async_copy(kv_in, kv_out, keep.at[5]),
    ]
    for copy in kept:
        copy.start()

    def cots_copy(k):
        tz, tx = chip_to(k)
        return remote(
            cots.at[tz * 4 + tx], c_all.at[slot_block(k, c)], c_send.at[k], c_recv.at[k], dev(y, tz, tx, c)
        )

    def send_cots(k, carry):
        cots_copy(k).start()
        return carry

    lax.fori_loop(1, 16, send_cots, 0)
    own_cots = pltpu.make_async_copy(cots.at[me], c_all.at[slot_block(0, c)], l_sem.at[2])
    own_cots.start()
    remote(cots.at[me], c_all.at[slot_block(0, c)], f_send, f_recv, sibling).start()

    def forward_cots(k, carry):
        arrived = cots_copy(k)
        arrived.wait_recv()
        remote(c_all.at[slot_block(k, c)], c_all.at[slot_block(k, c)], f_send, f_recv, sibling).start()
        arrived.wait_send()
        return carry

    def swap(part):
        start, width = OUT_PARTS[part][1:3]
        cols = half.at[:, :, :, :, pl.ds(start, width)]
        there = half_sib.at[:, :, :, :, pl.ds(start, width)]
        return remote(cols, there, sib_send.at[part], sib_recv.at[part], sibling)

    j = c * 4 + z
    qs[64:] = jnp.zeros((64, 3 * PAIR), BF)
    returns = []
    for n in range(4):
        zq = (z + n + 1) % 4
        q = q_in[zq] * SCALE_QK
        for h in range(3):
            qs[:64, 256 * h : 256 * h + 256] = q[64 * h : 64 * h + 64]
        acc[...] = jnp.zeros_like(acc)
        first = first_ref[zq]
        q_pos = (zq * 4 + x) * PAIR + lax.broadcasted_iota(jnp.int32, (1, PAIR), 1)

        def step(kb, stats):
            kv = kv_in[pl.ds(kb * (KEYS // PAIR), KEYS // PAIR)].reshape(KEYS, 128)
            k_pos = kb * KEYS + lax.broadcasted_iota(jnp.int32, (KEYS, PAIR), 0)
            ok = (k_pos >= first) & (k_pos <= q_pos)
            scores = [dot(kv, qs[:, 256 * h : 256 * h + 256], ((1,), (0,))) for h in range(3)]
            later, probs, shrinks = [], [], []
            for h in range(3):
                top, tot = stats[h]
                masked = jnp.where(ok, scores[h], NEGATIVE)
                new = jnp.maximum(top, jnp.max(masked, axis=0, keepdims=True))
                prob = jnp.exp(masked - new)
                shrink = jnp.exp(top - new)
                later.append((new, tot * shrink + jnp.sum(prob, axis=0, keepdims=True)))
                probs.append(prob.astype(BF))
                shrinks.append(shrink)
            for h in range(3):
                cols = slice(256 * h, 256 * h + 256)
                acc[:, cols] = acc[:, cols] * shrinks[h] + dot(kv, probs[h], ((0,), (0,)))
            return tuple(later)

        none = (jnp.full((1, PAIR), NEGATIVE, F32), jnp.zeros((1, PAIR), F32))
        stats = lax.fori_loop(0, zq + 1, step, (none, none, none))
        heads = []
        for h in range(3):
            cols = slice(256 * h, 256 * h + 256)
            mixed = acc[64:, cols] / stats[h][1]
            ot_ref[zq, :, cols] = mixed
            lse_ref[zq, :, cols] = stats[h][0] + jnp.log(stats[h][1])
            heads.append(mixed)
        heads = jnp.concatenate(heads, axis=0).astype(BF)
        saved = pltpu.make_async_copy(ot_ref.at[zq], ot_out.at[zq], keep.at[n])
        saved.start()
        kept.append(saved)
        o_buf[n, 0] = heads[:, :ROWS]
        o_buf[n, 1] = heads[:, ROWS:]
        for d in range(2):
            core = c if d == 0 else 1 - c
            if n == 3 and d == 0:
                back = pltpu.make_async_copy(o_buf.at[n, core], attn.at[j], l_sem.at[3])
            else:
                back = remote(
                    o_buf.at[n, core], attn.at[j], o_send.at[n, d], o_recv.at[n, d], dev(y, zq, x, core)
                )
            back.start()
            returns.append(back)
    for part in (0, 2, 1):
        for copy in w_copies[part]:
            copy.wait()
        swap(part).start()
        if part == 0:
            lax.fori_loop(1, 16, forward_cots, 0)
    own_cots.wait()
    mine = c_all.at[pl.ds(c * 16, 16)]
    drain = remote(mine, mine, f_send, f_recv, sibling)
    drain.wait_send()
    drain.wait_recv()
    for part in range(3):
        swap(part).wait()
    for back in returns + kept:
        back.wait()


def attend(q4, kv2, half, cots, first):
    blocks = jax.ShapeDtypeStruct((4, 4, 4, 24, Q_HALF), BF)
    return pl.pallas_call(
        attend_kernel,
        out_shape=[
            jax.ShapeDtypeStruct((4, HEAD_Q, PAIR), BF),
            jax.ShapeDtypeStruct((16, PAIR, 128), BF),
            jax.ShapeDtypeStruct((8, HEAD_Q, ROWS), BF),
            jax.ShapeDtypeStruct((4, HD, 3 * PAIR), F32),
            jax.ShapeDtypeStruct((4, 1, 3 * PAIR), F32),
            blocks,
            blocks,
            jax.ShapeDtypeStruct((32, SLOTS, MODEL_WIDTH), BF),
        ],
        in_specs=[ANY, ANY, ANY, ANY, IN_VMEM],
        out_specs=[ANY, ANY, ANY, ANY, IN_VMEM, ANY, ANY, ANY],
        input_output_aliases={2: 5},
        scratch_shapes=[
            pltpu.VMEM((4, HEAD_Q, PAIR), BF),
            pltpu.VMEM((16, PAIR, 128), BF),
            pltpu.VMEM((4, HD, 3 * PAIR), F32),
            pltpu.VMEM((128, 3 * PAIR), BF),
            pltpu.VMEM((128, 3 * PAIR), F32),
            pltpu.VMEM((4, 2, HEAD_Q, ROWS), BF),
            pltpu.SemaphoreType.DMA((6,)),
            pltpu.SemaphoreType.DMA((4,)),
            pltpu.SemaphoreType.DMA((3,)),
            pltpu.SemaphoreType.DMA((3,)),
            pltpu.SemaphoreType.DMA,
            pltpu.SemaphoreType.DMA,
            pltpu.SemaphoreType.DMA((3, 3)),
            pltpu.SemaphoreType.DMA((3, 3)),
            pltpu.SemaphoreType.DMA((3,)),
            pltpu.SemaphoreType.DMA((3,)),
            pltpu.SemaphoreType.DMA((16,)),
            pltpu.SemaphoreType.DMA((16,)),
            pltpu.SemaphoreType.DMA,
            pltpu.SemaphoreType.DMA,
            pltpu.SemaphoreType.DMA((4, 2)),
            pltpu.SemaphoreType.DMA((4, 2)),
        ],
        compiler_params=params(2, 60 << 20),
        name="attend",
    )(q4, kv2, half, cots, first)


def flat_rows(blocks):
    return blocks.reshape(blocks.shape[0] * SLOTS, blocks.shape[2])


def experts_kernel(
    attn, tokens, extra, ids, cotangent, half_w, sib_w, cots, weights,
    o_block, o_middle, o_branch, o_heads, o_moe, o_logits, o_gain, d_all,
    x_all, t_all, g_all, w_all, gate_v, up_v, hidden, g_both, part_o, part_g, sib_o, sib_g,
    v_all, wh, ws, xs, gates, out_ret, grad_ret, middle, moe_in,
    w_sem, l_sem, send, recv, f_send, f_recv, s_send, s_recv, r_send, r_recv, o_sem,
):
    y, z, x, c = coords()
    me = z * 4 + x
    width = hidden.shape[1]
    sibling = dev(y, z, x, 1 - c)
    loads = [
        pltpu.make_async_copy(src, dst, w_sem.at[n])
        for n, (src, dst) in enumerate(((half_w, wh), (sib_w, ws), (weights, w_all), (cots, g_all)))
    ]
    plane_greet()
    for load in loads:
        load.start()
    chosen, hits = slot_hits(ids[...])
    both_hits = (hits[0] + hits[1]).astype(BF)
    flat_extra = extra[...].reshape(MODEL_WIDTH, EXTRA)
    gain = jnp.transpose(flat_extra.astype(F32))[EXPERT_COUNT + 1 : EXPERT_COUNT + 2]
    own = attn[pl.ds(c * 4, 4)].reshape(Q_HALF, ROWS)
    other = attn[pl.ds((1 - c) * 4, 4)].reshape(Q_HALF, ROWS)
    loads[0].wait()
    loads[1].wait()
    middle[...] = (
        tokens[...].astype(F32)
        + dot(own, wh[...].reshape(MODEL_WIDTH, Q_HALF), ((0,), (1,)))
        + dot(other, ws[...].reshape(MODEL_WIDTH, Q_HALF), ((0,), (1,)))
    )
    inverse = inverse_rms(middle[...])
    moe_in[...] = (middle[...] * inverse * gain).astype(BF)
    logits = dot(moe_in[...], flat_extra, ((1,), (0,)))
    picked = [jnp.sum(chosen[k] * logits, axis=1, keepdims=True) for k in range(2)]
    most = jnp.maximum(picked[0], picked[1])
    lifted = [jnp.exp(value - most) for value in picked]
    share = [value / (lifted[0] + lifted[1]) for value in lifted]
    slots_in = dot(both_hits, moe_in[...], ((0,), (0,))).astype(BF)
    xs[...] = slots_in.reshape(EXPERT_COUNT, SLOTS, MODEL_WIDTH)
    slot_gate = jnp.sum(hits[0] * share[0] + hits[1] * share[1], axis=0, keepdims=True)
    gates[...] = column_of(slot_gate).reshape(EXPERT_COUNT, SLOTS, 128)
    pl.semaphore_wait(pltpu.get_barrier_semaphore(), 16)
    arrays = ((xs, x_all), (gates, t_all))

    def arriving(a, k):
        src, dst = arrays[a]
        tz, tx = chip_to(k)
        return remote(
            src.at[tz * 4 + tx], dst.at[slot_block(k, c)], send.at[a, k], recv.at[a, k], dev(y, tz, tx, c)
        )

    def steps_of(part):
        return (1, 8) if part == 0 else (8, 16)

    def scatter(a, part):
        def push(k, carry):
            arriving(a, k).start()
            return carry

        lax.fori_loop(*steps_of(part), push, 0)
        if part == 0:
            src, dst = arrays[a]
            pltpu.make_async_copy(src.at[me], dst.at[slot_block(0, c)], l_sem.at[a]).start()
            remote(src.at[me], dst.at[slot_block(0, c)], f_send.at[a, 0], f_recv.at[a, 0], sibling).start()

    def hand_over(a, part):
        src, dst = arrays[a]

        def forward(k, carry):
            arrived = arriving(a, k)
            arrived.wait_recv()
            block = dst.at[slot_block(k, c)]
            remote(block, block, f_send.at[a, part], f_recv.at[a, part], sibling).start()
            arrived.wait_send()
            return carry

        lax.fori_loop(*steps_of(part), forward, 0)

    def settle(a, part):
        src, dst = arrays[a]
        if part == 0:
            pltpu.make_async_copy(src.at[me], dst.at[slot_block(0, c)], l_sem.at[a]).wait()
        some = dst.at[pl.ds(0, 8)]
        drain = remote(some, some, f_send.at[a, part], f_recv.at[a, part], sibling)
        drain.wait_send()
        drain.wait_recv()

    def swap(mine, sib, a, part):
        return remote(
            mine.at[pl.ds(part * 16 + (1 - c) * 8, 8)], sib.at[pl.ds(part * 8, 8)],
            s_send.at[a, part], s_recv.at[a, part], sibling,
        )

    def give(mine, sib, ret, a, part):
        def add(k):
            block = slot_block(k, c)
            mine[block] = (mine[block].astype(F32) + sib[k].astype(F32)).astype(BF)
            return mine.at[block]

        def push(k, carry):
            sz, sx = chip_from(k)
            remote(add(k), ret.at[me], r_send.at[a], r_recv.at[a], dev(y, sz, sx, c)).start()
            return carry

        lax.fori_loop(*steps_of(part), push, 0)
        if part == 0:
            pltpu.make_async_copy(add(0), ret.at[me], l_sem.at[2 + a]).start()

    def given(mine, ret, a):
        pltpu.make_async_copy(mine.at[slot_block(0, c)], ret.at[me], l_sem.at[2 + a]).wait()
        drain = remote(ret.at[pl.ds(0, 15)], ret.at[pl.ds(0, 15)], r_send.at[a], r_recv.at[a], sibling)
        drain.wait_send()
        drain.wait_recv()

    half = 16 * SLOTS

    def forward_pass(part):
        blocks, rows = pl.ds(part * 16, 16), slice(part * half, part * half + half)
        both = dot(flat_rows(x_all[blocks]), w_all[:, : 2 * width], ((1,), (0,)))
        gate_val, up_val = both[:, :width], both[:, width:]
        gate_v[rows] = gate_val
        up_v[rows] = up_val
        low = (gate_val * jax.nn.sigmoid(gate_val) * up_val).astype(BF)
        hidden[rows] = low
        out = dot(low, w_all[:, 2 * width :], ((1,), (1,))).astype(BF)
        part_o[blocks] = out.reshape(16, SLOTS, MODEL_WIDTH)
        swap(part_o, sib_o, 0, part).start()

    def backward_pass(part):
        blocks, rows = pl.ds(part * 16, 16), slice(part * half, part * half + half)
        scale = jnp.concatenate([flat_rows(t_all[blocks])] * (MODEL_WIDTH // 128), axis=1)
        grad_expert = (flat_rows(g_all[blocks]).astype(F32) * scale).astype(BF)
        g_all[blocks] = grad_expert.reshape(16, SLOTS, MODEL_WIDTH)
        grad_hidden = dot(grad_expert, w_all[:, 2 * width :], ((1,), (0,)))
        gate_val = gate_v[rows]
        up_val = up_v[rows]
        sig = jax.nn.sigmoid(gate_val)
        grad_gate = (grad_hidden * up_val * sig * (1.0 + gate_val * (1.0 - sig))).astype(BF)
        grad_up = (grad_hidden * gate_val * sig).astype(BF)
        grads = jnp.concatenate([grad_gate, grad_up], axis=1)
        g_both[rows] = grads
        grad_rows = dot(grads, w_all[:, : 2 * width], ((1,), (1,))).astype(BF)
        part_g[blocks] = grad_rows.reshape(16, SLOTS, MODEL_WIDTH)
        swap(part_g, sib_g, 1, part).start()

    scatter(0, 0)
    scatter(1, 0)
    scatter(0, 1)
    scatter(1, 1)
    loads[2].wait()
    loads[3].wait()
    hand_over(0, 0)
    settle(0, 0)
    forward_pass(0)
    hand_over(0, 1)
    swap(part_o, sib_o, 0, 0).wait()
    give(part_o, sib_o, out_ret, 0, 0)
    settle(0, 1)
    forward_pass(1)
    hand_over(1, 0)
    hand_over(1, 1)
    settle(1, 0)
    swap(part_o, sib_o, 0, 1).wait()
    give(part_o, sib_o, out_ret, 0, 1)
    backward_pass(0)
    settle(1, 1)
    swap(part_g, sib_g, 1, 0).wait()
    give(part_g, sib_g, grad_ret, 1, 0)
    backward_pass(1)
    swap(part_g, sib_g, 1, 1).wait()
    give(part_g, sib_g, grad_ret, 1, 1)

    def weight_grads(j, carry):
        cols = pl.ds(pl.multiple_of(j * 256, 256), 256)
        v_all[cols, : 2 * width] = dot(flat_rows(x_all[:, :, cols]), g_both[...], ((0,), (0,))).astype(BF)
        v_all[cols, 2 * width :] = dot(flat_rows(g_all[:, :, cols]), hidden[...], ((0,), (0,))).astype(BF)
        return carry

    lax.fori_loop(0, MODEL_WIDTH // 256, weight_grads, 0)
    store = pltpu.make_async_copy(v_all, d_all, o_sem)
    store.start()
    given(part_o, out_ret, 0)
    grad_out = cotangent[...].astype(F32)
    rows_out = [dot(hits[k].astype(BF), flat_rows(out_ret[...]), ((1,), (0,))) for k in range(2)]
    o_block[...] = (middle[...] + share[0] * rows_out[0] + share[1] * rows_out[1]).astype(BF)
    pairs = [jnp.sum(grad_out * rows, axis=1, keepdims=True) for rows in rows_out]
    mean = share[0] * pairs[0] + share[1] * pairs[1]
    grad_logits = sum(chosen[k] * (share[k] * (pairs[k] - mean)) for k in range(2))
    o_logits[...] = grad_logits
    o_moe[...] = moe_in[...]
    routed = sum(dot(part, flat_extra, ((1,), (1,))) for part in three_parts(grad_logits))
    given(part_g, grad_ret, 1)
    grad_moe = dot(both_hits, flat_rows(grad_ret[...]), ((1,), (0,))) + routed
    o_gain[...] = jnp.sum(grad_moe * middle[...] * inverse, axis=0, keepdims=True)
    grad_middle = grad_out + norm_backward(middle[...], inverse, gain, grad_moe)
    o_middle[...] = grad_middle
    branch = grad_middle.astype(BF)
    o_branch[...] = branch
    for core, weight in ((c, wh), (1 - c, ws)):
        heads = dot(weight[...].reshape(MODEL_WIDTH, Q_HALF), branch, ((0,), (1,))).astype(BF)
        o_heads[pl.ds(core * 4, 4)] = heads.reshape(4, HEAD_Q, ROWS)
    store.wait()


def experts(attn, tokens, extra, ids, cotangent, half_w, sib_w, cots, weights):
    rows = 32 * SLOTS
    width = weights.shape[1] // 3
    slots = (16, SLOTS, MODEL_WIDTH)
    flat = (ROWS, MODEL_WIDTH)
    low = jax.ShapeDtypeStruct(flat, BF)
    return pl.pallas_call(
        experts_kernel,
        out_shape=[
            low,
            jax.ShapeDtypeStruct(flat, F32),
            low,
            jax.ShapeDtypeStruct((8, HEAD_Q, ROWS), BF),
            low,
            jax.ShapeDtypeStruct((ROWS, 128), F32),
            jax.ShapeDtypeStruct((1, MODEL_WIDTH), F32),
            jax.ShapeDtypeStruct(weights.shape, BF),
        ],
        in_specs=[IN_VMEM] * 5 + [ANY] * 4,
        out_specs=[IN_VMEM] * 7 + [ANY],
        scratch_shapes=[
            pltpu.VMEM((32, SLOTS, MODEL_WIDTH), BF),
            pltpu.VMEM((32, SLOTS, 128), F32),
            pltpu.VMEM((32, SLOTS, MODEL_WIDTH), BF),
            pltpu.VMEM(weights.shape, BF),
            pltpu.VMEM((rows, width), F32),
            pltpu.VMEM((rows, width), F32),
            pltpu.VMEM((rows, width), BF),
            pltpu.VMEM((rows, 2 * width), BF),
            pltpu.VMEM((32, SLOTS, MODEL_WIDTH), BF),
            pltpu.VMEM((32, SLOTS, MODEL_WIDTH), BF),
            pltpu.VMEM((16, SLOTS, MODEL_WIDTH), BF),
            pltpu.VMEM((16, SLOTS, MODEL_WIDTH), BF),
            pltpu.VMEM(weights.shape, BF),
            pltpu.VMEM(half_w.shape, BF),
            pltpu.VMEM(half_w.shape, BF),
            pltpu.VMEM(slots, BF),
            pltpu.VMEM((EXPERT_COUNT, SLOTS, 128), F32),
            pltpu.VMEM(slots, BF),
            pltpu.VMEM(slots, BF),
            pltpu.VMEM(flat, F32),
            pltpu.VMEM(flat, BF),
            pltpu.SemaphoreType.DMA((4,)),
            pltpu.SemaphoreType.DMA((4,)),
            pltpu.SemaphoreType.DMA((2, 16)),
            pltpu.SemaphoreType.DMA((2, 16)),
            pltpu.SemaphoreType.DMA((2, 2)),
            pltpu.SemaphoreType.DMA((2, 2)),
            pltpu.SemaphoreType.DMA((2, 2)),
            pltpu.SemaphoreType.DMA((2, 2)),
            pltpu.SemaphoreType.DMA((2,)),
            pltpu.SemaphoreType.DMA((2,)),
            pltpu.SemaphoreType.DMA,
        ],
        compiler_params=params(6, 60 << 20),
        name="experts",
    )(attn, tokens, extra, ids, cotangent, half_w, sib_w, cots, weights)


SUMS = tuple((n, start, width, order[::-1]) for n, start, width, order in FIRST_PARTS) + tuple(
    (2, start, 256, order) for start, order in OUT_SUMS
)
LATE = len(FIRST_PARTS)


def reduce_kernel(
    gq_t, dkv, normed, s_out, grad_logits, gain_m, moe_h, pair_h, extra_h, middle_h, w_q, w_kv, experts_h,
    o_tokens, o_q, o_k, o_v, o_out, o_extra, o_gate, o_up, o_down,
    moe_in, pair, w_extra, grad_middle, summed, f_gate, f_up, f_down, v_q, v_kv, v_extra, wq, wkv, gkv, mine_part, give_part, sib_part, both, total, give, *rest,
):
    parts = len(SUMS)
    first_in, rest = rest[:LATE], rest[LATE:]
    arrive = [list(first_in) + [None] * 3, rest[:parts], rest[parts : 2 * parts]]
    rest = rest[2 * parts :]
    held = [None, list(rest[:LATE]) + [s_out.at[k] for k in range(3)], rest[LATE : LATE + parts]]
    l_sem, send, recv, sib_send, sib_recv = rest[LATE + parts :]
    grads = (v_q, v_kv, None, v_extra)
    y, z, x, c = coords()
    place = {"y": y, "z": z, "x": x}
    sibling = dev(y, z, x, 1 - c)
    loads = [
        pltpu.make_async_copy(src, dst, l_sem.at[n])
        for n, (src, dst) in enumerate(
            (
                (w_q, wq), (w_kv, wkv), (pair_h, pair), (moe_h, moe_in), (extra_h, w_extra),
                (middle_h, grad_middle), (experts_h, summed),
            )
        )
    ]
    for load in loads:
        load.start()
    for axis in ("x", "y", "z"):
        for step in STEPS:
            signal(axis_peer(axis, step))
    signal(sibling)
    pl.semaphore_wait(pltpu.get_barrier_semaphore(), 10)

    def at(phase, part, index):
        n, start, width, order = SUMS[part]
        spot = [
            index if axis == order[phase] else slice(None)
            for axis in ("y", "z", "x")
            if axis not in order[:phase]
        ]
        if phase == 0:
            return grads[n].at[tuple(spot) + (slice(None), pl.ds(start, width))]
        return held[phase][part].at[tuple(spot)]

    def copies_of(phase, part):
        axis = SUMS[part][3][phase]
        return [
            remote(
                at(phase, part, (place[axis] + step) % 4), arrive[phase][part].at[n],
                send.at[phase, part, n], recv.at[phase, part, n], axis_peer(axis, step),
            )
            for n, step in enumerate(STEPS)
        ]

    def begin(phase, part):
        for copy in copies_of(phase, part):
            copy.start()

    def finish(phase, part):
        for copy in copies_of(phase, part):
            copy.wait()
        array, start, width, order = SUMS[part]
        mine = at(phase, part, place[order[phase]])
        got = arrive[phase][part]
        if phase < 2:

            def add(p, carry):
                value = mine[p].astype(F32)
                for n in range(3):
                    value = value + got[n, p].astype(F32)
                held[phase + 1][part][p] = value.astype(BF)
                return carry

            lax.fori_loop(0, 4, add, 0)
        else:
            value = mine[...].astype(F32)
            for n in range(3):
                value = value + got[n].astype(F32)
            total[:, STARTS[array] + start : STARTS[array] + start + width] = value

    for part in range(LATE, parts):
        begin(1, part)
    for h in range(4):
        value = dkv[4 * h].astype(F32)
        for n in range(1, 4):
            value = value + dkv[4 * h + n].astype(F32)
        gkv[128 * h : 128 * h + 128] = value.astype(BF)
    for n in range(4):
        left = normed[:, 384 * n : 384 * n + 384]
        v_kv[n] = dot(left, gkv[...], ((0,), (1,))).astype(BF).reshape(4, 4, 24, KV_HALF)
    begin(0, 1)
    for n in range(4):
        left = normed[:, 384 * n : 384 * n + 384]
        v_q[n] = dot(left, gq_t[...], ((0,), (1,))).astype(BF).reshape(4, 4, 24, Q_HALF)
    begin(0, 0)
    begin(0, 2)

    for load in loads:
        load.wait()
    gain_sum = jnp.zeros((1, MODEL_WIDTH), F32)
    for n in range(2):
        core = 1 - c if n == 0 else c
        rows = pl.ds(pl.multiple_of(core * ROWS, ROWS), ROWS)
        part = dot(gq_t[:, rows], wq[...], ((0,), (1,))) + dot(gkv[:, rows], wkv[...], ((0,), (1,)))
        values = pair[rows].astype(F32)
        gain_sum = gain_sum + jnp.sum(part * values * inverse_rms(values), axis=0, keepdims=True)
        if n == 0:
            give_part[...] = part
            remote(give_part, sib_part, sib_send.at[0], sib_recv.at[0], sibling).start()
        else:
            mine_part[...] = part
    lane = lax.broadcasted_iota(jnp.int32, (MODEL_WIDTH, EXTRA), 1)
    extra = sum(dot(moe_in[...], part, ((0,), (0,))) for part in three_parts(grad_logits[...]))
    extra = jnp.where(lane == EXPERT_COUNT, column_of(gain_sum), extra)
    extra = jnp.where(lane == EXPERT_COUNT + 1, column_of(gain_m[...]), extra)
    gain = jnp.transpose(w_extra[...].reshape(MODEL_WIDTH, EXTRA).astype(F32))[EXPERT_COUNT : EXPERT_COUNT + 1]
    v_extra[...] = extra.astype(BF).reshape(4, 4, 4, 24, EXTRA)
    begin(0, 3)
    remote(give_part, sib_part, sib_send.at[0], sib_recv.at[0], sibling).wait()
    rows = pl.ds(pl.multiple_of(c * ROWS, ROWS), ROWS)
    values = pair[rows].astype(F32)
    o_tokens[...] = grad_middle[...] + norm_backward(
        values, inverse_rms(values), gain, mine_part[...] + sib_part[...]
    )

    third = FF // 2
    f_gate[...] = summed[:, :third].astype(F32)
    f_up[...] = summed[:, third : 2 * third].astype(F32)
    f_down[...] = jnp.transpose(summed[:, 2 * third :].astype(F32))
    stores = [
        pltpu.make_async_copy(src, dst, l_sem.at[n])
        for n, (src, dst) in enumerate(((f_gate, o_gate), (f_up, o_up), (f_down, o_down)))
    ]
    for store in stores:
        store.start()
    for part in range(LATE, parts):
        finish(1, part)
        begin(2, part)
    for phase in range(3):
        for part in range(LATE):
            finish(phase, part)
            if phase < 2:
                begin(phase + 1, part)
    for part in range(LATE, parts):
        finish(2, part)
    low, high = total[0:12], total[12:24]
    both[c, 0:12] = jnp.where(c == 0, low, high)
    give[0:12] = jnp.where(c == 0, high, low)
    give[12:16] = jnp.zeros((4, PACK), F32)
    last = remote(give, both.at[c], sib_send.at[1], sib_recv.at[1], sibling)
    last.start()
    for store in stores:
        store.wait()
    last.wait()
    keys, values = [], []
    for k in range(2):
        o_q[:, Q_HALF * k : Q_HALF * k + Q_HALF] = both[k, 0:12, :Q_HALF]
        o_out[:, Q_HALF * k : Q_HALF * k + Q_HALF] = both[k, 0:12, STARTS[2] : STARTS[3]]
        for h in range(4):
            first = STARTS[1] + 128 * h
            keys.append(both[k, 0:12, first : first + HD])
            values.append(both[k, 0:12, first + HD : first + 2 * HD])
    o_k[...] = jnp.concatenate(keys, axis=1)
    o_v[...] = jnp.concatenate(values, axis=1)
    o_extra[...] = both[0, 0:12, STARTS[3] :] + both[1, 0:12, STARTS[3] :]


def reduce_weights(*args):
    widths = [part[2] for part in SUMS]
    full = lambda width: pltpu.VMEM((4, 4, 4, 24, width), BF)
    rows = pltpu.VMEM((ROWS, MODEL_WIDTH), F32)
    low = pltpu.VMEM((ROWS, MODEL_WIDTH), BF)
    scratch = (
        [low, pltpu.VMEM((PAIR, MODEL_WIDTH), BF), full(EXTRA), rows]
        + [pltpu.VMEM((MODEL_WIDTH // 4, 3 * FF // 2), BF)]
        + [pltpu.VMEM((MODEL_WIDTH // 4, FF // 2), F32)] * 2
        + [pltpu.VMEM((FF // 2, MODEL_WIDTH // 4), F32)]
        + [full(Q_HALF), full(KV_HALF), full(EXTRA)]
        + [pltpu.VMEM((MODEL_WIDTH, Q_HALF), BF), pltpu.VMEM((MODEL_WIDTH, KV_HALF), BF)]
        + [pltpu.VMEM((KV_HALF, PAIR), BF), rows, rows, rows]
        + [pltpu.VMEM((2, 16, PACK), F32), pltpu.VMEM((24, PACK), F32), pltpu.VMEM((16, PACK), F32)]
        + [pltpu.VMEM((3, 4, 4, 24, w), BF) for w in widths[:LATE]]
        + [pltpu.VMEM((3, 4, 24, w), BF) for w in widths]
        + [pltpu.VMEM((3, 24, w), BF) for w in widths]
        + [pltpu.VMEM((4, 4, 24, w), BF) for w in widths[:LATE]]
        + [pltpu.VMEM((4, 24, w), BF) for w in widths]
    )
    sems = (3, len(SUMS), 3)
    shapes = ((ROWS, MODEL_WIDTH), (12, MODEL_WIDTH), (12, KV * HD), (12, KV * HD), (12, MODEL_WIDTH), (12, EXTRA))
    tall, flat = (MODEL_WIDTH // 4, FF // 2), (FF // 2, MODEL_WIDTH // 4)
    shapes = shapes + (tall, tall, flat)
    return pl.pallas_call(
        reduce_kernel,
        out_shape=[jax.ShapeDtypeStruct(shape, F32) for shape in shapes],
        in_specs=[IN_VMEM] * 6 + [ANY] * 7,
        out_specs=[IN_VMEM] * 6 + [ANY] * 3,
        scratch_shapes=scratch
        + [
            pltpu.SemaphoreType.DMA((7,)),
            pltpu.SemaphoreType.DMA(sems),
            pltpu.SemaphoreType.DMA(sems),
            pltpu.SemaphoreType.DMA((2,)),
            pltpu.SemaphoreType.DMA((2,)),
        ],
        compiler_params=params(8, 60 << 20),
        name="reduce_weights",
    )(*args)


def wide_greet():
    y, z, x, c = coords()
    me = z * 4 + x

    def greet(k, carry):
        t = (me + k) % 16
        signal(dev(y, t // 4, t % 4, c))
        return carry

    lax.fori_loop(1, 16, greet, 0)
    for step in STEPS:
        signal(axis_peer("y", step))
        signal(dev(y, (z + step) % 4, x, 1 - c))
    signal(dev(y, z, x, 1 - c))
    pl.semaphore_wait(pltpu.get_barrier_semaphore(), 22)


def attend_back_kernel(
    heads, branch_h, attn_h, q_h, kv_h, first_ref, ot_h, lse_ref,
    dq_out, dkv_out, s_out,
    branch, attn, q_in, kv_in, ot_ref, keep, go, branch_sib, attn_sib, qs, gs, delta, dq, dkv, dkv_low, dq_low,
    g_out, a_out,
    l_sem, h_send, h_recv, sib_send, sib_recv, q_send, q_recv, k_send, k_recv,
    w_send, w_recv,
):
    y, z, x, c = coords()
    me = z * 4 + x
    j = c * 4 + z
    sibling = dev(y, z, x, 1 - c)
    place = {"y": y, "z": z, "x": x}
    loads = [
        pltpu.make_async_copy(src, dst, keep.at[n])
        for n, (src, dst) in enumerate(
            ((branch_h, branch), (attn_h, attn), (q_h, q_in), (kv_h, kv_in), (ot_h, ot_ref))
        )
    ]
    for load in loads:
        load.start()
    wide_greet()

    def push(k, carry):
        t = (j + k) % 8
        remote(heads.at[t], go.at[j], h_send, h_recv, dev(y, t % 4, x, t // 4)).start()
        return carry

    lax.fori_loop(1, 8, push, 0)
    one = remote(branch_h, branch_sib, sib_send.at[0], sib_recv.at[0], sibling)
    one.start()
    two = remote(attn_h.at[pl.ds((1 - c) * 4, 4)], attn_sib, sib_send.at[1], sib_recv.at[1], sibling)
    two.start()
    here = pltpu.make_async_copy(heads.at[j], go.at[j], l_sem.at[0])
    here.start()
    loads[0].wait()
    loads[1].wait()
    one.wait()
    two.wait()

    rows_b = jnp.concatenate([branch[...], branch_sib[...]], axis=0)
    rows_a = jnp.concatenate(
        [part.reshape(Q_HALF, ROWS) for part in (attn[pl.ds(c * 4, 4)], attn_sib[...])], axis=1
    )
    for n in range(4):
        part = dot(rows_b[:, 384 * n : 384 * n + 384], rows_a, ((0,), (1,)))
        g_out[n] = part.astype(BF).reshape(4, 4, 24, Q_HALF)

    def spot(part, index):
        start, order = OUT_SUMS[part]
        cut = [index if axis == order[0] else slice(None) for axis in ("y", "z", "x")]
        return g_out.at[tuple(cut) + (slice(None), pl.ds(start, 256))]

    w_copies = []
    for part in range(3):
        axis = OUT_SUMS[part][1][0]
        for n, step in enumerate(STEPS):
            copy = remote(
                spot(part, (place[axis] + step) % 4), a_out.at[part, n],
                w_send.at[part, n], w_recv.at[part, n], axis_peer(axis, step),
            )
            copy.start()
            w_copies.append(copy)

    for load in loads[2:]:
        load.wait()
    here.wait()
    drain = remote(go.at[pl.ds(0, 7)], go.at[pl.ds(0, 7)], h_send, h_recv, sibling)
    drain.wait_send()
    drain.wait_recv()
    dkv[...] = jnp.zeros_like(dkv)
    dq[...] = jnp.zeros_like(dq)
    for zq in range(4):
        q = q_in[zq] * SCALE_QK
        grad = jnp.concatenate([go[zq], go[4 + zq]], axis=1)
        qs[zq, 64:] = jnp.zeros((64, 3 * PAIR), BF)
        gs[zq, :64] = jnp.zeros((64, 3 * PAIR), BF)
        for h in range(3):
            cols, rows = slice(256 * h, 256 * h + 256), slice(64 * h, 64 * h + 64)
            qs[zq, :64, cols] = q[rows]
            gs[zq, 64:, cols] = grad[rows]
            delta[zq, :, cols] = jnp.sum(
                grad[rows].astype(F32) * ot_ref[zq, :, cols], axis=0, keepdims=True
            )

    for n in range(4):
        group = (z + n + 1) % 4
        for zq in range(4):
            hi = zq * 4 + x
            first = first_ref[zq]
            q_pos = hi * PAIR + lax.broadcasted_iota(jnp.int32, (1, PAIR), 1)

            def step(kb, carry):
                kv = kv_in[kb]
                k_pos = kb * PAIR + lax.broadcasted_iota(jnp.int32, (PAIR, PAIR), 0)
                ok = (k_pos >= first) & (k_pos <= q_pos)
                heads = [slice(256 * h, 256 * h + 256) for h in range(3)]
                scores = [dot(kv, qs[zq, :, cols], ((1,), (0,))) for cols in heads]
                grad_probs = [dot(kv, gs[zq, :, cols], ((1,), (0,))) for cols in heads]
                grad_scores, probs = [], []
                for h in range(3):
                    prob = jnp.where(ok, jnp.exp(scores[h] - lse_ref[zq, :, heads[h]]), 0.0)
                    grad_scores.append((prob * (grad_probs[h] - delta[zq, :, heads[h]])).astype(BF))
                    probs.append(prob.astype(BF))
                for h in range(3):
                    dq[zq, :, heads[h]] = dq[zq, :, heads[h]] + dot(kv, grad_scores[h], ((0,), (0,)))
                grad_scores, probs = jnp.concatenate(grad_scores, axis=1), jnp.concatenate(probs, axis=1)
                dkv[kb, :64] = dkv[kb, :64] + dot(qs[zq, :64], grad_scores, ((1,), (1,)))
                dkv[kb, 64:] = dkv[kb, 64:] + dot(gs[zq, 64:], probs, ((1,), (1,)))
                return carry

            last = jnp.minimum(group * 4 + 3, hi)
            lax.fori_loop(group * 4, jnp.maximum(last + 1, group * 4), step, 0)
        for d in range(4):
            xt = (x + d + 1) % 4
            t = group * 4 + xt
            dkv_low[t] = dkv[t].astype(BF)
            if n == 3 and d == 3:
                own_kv = pltpu.make_async_copy(dkv_low.at[me], dkv_out.at[me], l_sem.at[2])
                own_kv.start()
            else:
                remote(dkv_low.at[t], dkv_out.at[me], k_send, k_recv, dev(y, group, xt, c)).start()
    q_copies = []
    for n in range(4):
        zq = (z + n + 1) % 4
        by_head = jnp.concatenate([dq[zq, :64, 256 * h : 256 * h + 256] for h in range(3)], axis=0)
        dq_low[zq] = (by_head * SCALE_QK).astype(BF)
        if n < 3:
            copy = remote(dq_low.at[zq], dq_out.at[z], q_send.at[n], q_recv.at[n], dev(y, zq, x, c))
        else:
            copy = pltpu.make_async_copy(dq_low.at[zq], dq_out.at[z], l_sem.at[1])
        copy.start()
        q_copies.append(copy)

    for copy in w_copies:
        copy.wait()
    for part in range(3):
        mine = spot(part, place[OUT_SUMS[part][1][0]])

        def add(p, carry):
            value = mine[p].astype(F32)
            for k in range(3):
                value = value + a_out[part, k, p].astype(F32)
            s_out[part, p] = value.astype(BF)
            return carry

        lax.fori_loop(0, 4, add, 0)
    for copy in q_copies:
        copy.wait()
    own_kv.wait()
    drain = remote(dkv_out.at[pl.ds(0, 15)], dkv_out.at[pl.ds(0, 15)], k_send, k_recv, sibling)
    drain.wait_send()
    drain.wait_recv()


def attend_back(heads, branch, attn, q_in, kv_in, first, ot, lse):
    return pl.pallas_call(
        attend_back_kernel,
        out_shape=[
            jax.ShapeDtypeStruct((4, HEAD_Q, PAIR), BF),
            jax.ShapeDtypeStruct((16, 128, PAIR), BF),
            jax.ShapeDtypeStruct((3, 4, 4, 24, 256), BF),
        ],
        in_specs=[ANY] * 5 + [IN_VMEM, ANY, IN_VMEM],
        out_specs=[ANY, ANY, IN_VMEM],
        scratch_shapes=[
            pltpu.VMEM((ROWS, MODEL_WIDTH), BF),
            pltpu.VMEM((8, HEAD_Q, ROWS), BF),
            pltpu.VMEM((4, HEAD_Q, PAIR), BF),
            pltpu.VMEM((16, PAIR, 128), BF),
            pltpu.VMEM((4, HD, 3 * PAIR), F32),
            pltpu.SemaphoreType.DMA((5,)),
            pltpu.VMEM((8, HEAD_Q, ROWS), BF),
            pltpu.VMEM((ROWS, MODEL_WIDTH), BF),
            pltpu.VMEM((4, HEAD_Q, ROWS), BF),
            pltpu.VMEM((4, 128, 3 * PAIR), BF),
            pltpu.VMEM((4, 128, 3 * PAIR), BF),
            pltpu.VMEM((4, 1, 3 * PAIR), F32),
            pltpu.VMEM((4, 128, 3 * PAIR), F32),
            pltpu.VMEM((16, 128, PAIR), F32),
            pltpu.VMEM((16, 128, PAIR), BF),
            pltpu.VMEM((4, HEAD_Q, PAIR), BF),
            pltpu.VMEM((4, 4, 4, 24, Q_HALF), BF),
            pltpu.VMEM((3, 3, 4, 4, 24, 256), BF),
            pltpu.SemaphoreType.DMA((3,)),
            pltpu.SemaphoreType.DMA,
            pltpu.SemaphoreType.DMA,
            pltpu.SemaphoreType.DMA((2,)),
            pltpu.SemaphoreType.DMA((2,)),
            pltpu.SemaphoreType.DMA((4,)),
            pltpu.SemaphoreType.DMA((4,)),
            pltpu.SemaphoreType.DMA,
            pltpu.SemaphoreType.DMA,
            pltpu.SemaphoreType.DMA((3, 3)),
            pltpu.SemaphoreType.DMA((3, 3)),
        ],
        compiler_params=params(4, 60 << 20),
        name="attend_back",
    )(heads, branch, attn, q_in, kv_in, first, ot, lse)


def inverse_rms(values):
    return lax.rsqrt(jnp.mean(values * values, axis=-1, keepdims=True) + EPS)


def norm_backward(values, inverse, gain, grad_out):
    scaled = grad_out * gain
    return inverse * scaled - values * inverse**3 * jnp.mean(values * scaled, axis=-1, keepdims=True)


def finish_kernel(extra, *refs):
    n = (len(refs) - 5) // 3
    sources, targets = refs[:n], refs[n : 2 * n]
    o_router, o_gain_a, o_gain_m = refs[2 * n : 2 * n + 3]
    held, (l_sem, s_sem) = refs[2 * n + 3 : 3 * n + 3], refs[3 * n + 3 :]
    loads = [pltpu.make_async_copy(sources[k], held[k], l_sem.at[k]) for k in range(n)]
    stores = [pltpu.make_async_copy(held[k], targets[k], s_sem.at[k]) for k in range(n)]
    for load in loads:
        load.start()
    o_router[...] = extra[:, :EXPERT_COUNT]
    square = lax.broadcasted_iota(jnp.int32, (12, 12), 0) == lax.broadcasted_iota(jnp.int32, (12, 12), 1)
    for k, out in enumerate((o_gain_a, o_gain_m)):
        column = jnp.broadcast_to(extra[:, EXPERT_COUNT + k : EXPERT_COUNT + k + 1], (12, 12))
        out[...] = jnp.sum(jnp.where(square, column, 0.0), axis=0, keepdims=True)
    for k in range(n):
        loads[k].wait()
        stores[k].start()
    for store in stores:
        store.wait()


def finish(extra, arrays):
    n = len(arrays)
    shapes = [jax.ShapeDtypeStruct(array.shape, array.dtype) for array in arrays]
    small = [jax.ShapeDtypeStruct((12, EXPERT_COUNT), F32)] + [jax.ShapeDtypeStruct((1, 12), F32)] * 2
    return pl.pallas_call(
        finish_kernel,
        out_shape=shapes + small,
        in_specs=[IN_VMEM] + [ANY] * n,
        out_specs=[ANY] * n + [IN_VMEM] * 3,
        scratch_shapes=[pltpu.VMEM(shape.shape, shape.dtype) for shape in shapes]
        + [pltpu.SemaphoreType.DMA((n,)), pltpu.SemaphoreType.DMA((n,))],
        compiler_params=pltpu.CompilerParams(vmem_limit_bytes=60 << 20),
        name="finish",
    )(extra, *arrays)


def local(
    tokens,
    segment_ids,
    expert_ids,
    w_query,
    w_key,
    w_value,
    w_out,
    w_router,
    gain_attn,
    gain_moe,
    w_gate,
    w_up,
    w_down,
    cotangent,
):
    ids = expert_ids.T
    part_q, part_kv, part_out, part_extra, pair, normed, w_experts, q4, keys_values, first, cot_slots = (
        gather_weights(
            (w_query, w_key, w_value, w_out.T, w_router, gain_attn[None], gain_moe[None], ids, cotangent),
            (tokens, segment_ids, w_gate, w_up, w_down),
        )
    )
    full_experts = lax.all_gather(w_experts, "dp", axis=0, tiled=True)
    q_in, kv_in, attn, attn_t, lse, half_out, sib_out, cot_all = attend(
        q4, keys_values, part_out, cot_slots, first
    )
    block_out, grad_middle, branch, grad_heads, moe_in, grad_logits, gain_sum, grad_experts = experts(
        attn, tokens, part_extra, ids, cotangent, half_out, sib_out, cot_all, full_experts
    )
    sum_experts = lax.psum_scatter(grad_experts, "dp", scatter_dimension=0, tiled=True)
    dq_in, dkv_in, sum_out = attend_back(grad_heads, branch, attn, q_in, kv_in, first, attn_t, lse)
    grad_tokens, r_query, r_key, r_value, r_out, r_extra, *expert_grads = reduce_weights(
        dq_in.reshape(Q_HALF, PAIR), dkv_in, normed, sum_out, grad_logits, gain_sum, moe_in,
        pair.reshape(PAIR, MODEL_WIDTH), part_extra, grad_middle,
        part_q.reshape(MODEL_WIDTH, Q_HALF), part_kv.reshape(MODEL_WIDTH, KV_HALF), sum_experts,
    )
    *results, r_router, r_gain_a, r_gain_m = finish(
        r_extra,
        (grad_tokens, *expert_grads, block_out, r_query, r_key, r_value, r_out),
    )
    grad_tokens, g_gate, g_up, g_down, block_out, r_query, r_key, r_value, r_out = results
    return (
        block_out,
        grad_tokens,
        r_query,
        r_key,
        r_value,
        r_out.T,
        r_router,
        r_gain_a.reshape(12),
        r_gain_m.reshape(12),
        g_gate,
        g_up,
        g_down,
    )


def solution(mesh):
    rows, flat, dense = P(("dp", "ctx"), None), P(("dp", "ctx")), P("dp", "ctx")
    placed = (
        rows, dense, rows, rows, rows, rows, P(None, ("dp", "ctx")), rows, flat, flat,
        dense, dense, P("ctx", "dp"), rows,
    )
    return jax.shard_map(
        local,
        mesh=mesh,
        in_specs=placed,
        out_specs=(
            rows, rows, rows, rows, rows, P(None, ("dp", "ctx")), rows, flat, flat,
            dense, dense, P("ctx", "dp"),
        ),
        check_vma=False,
    )
```

```python
import functools

import jax
import jax.numpy as jnp
from jax import lax
from jax.experimental import pallas as pl
from jax.experimental.pallas import tpu as pltpu
from jax.sharding import PartitionSpec as P

MODEL_WIDTH = 1536
KV = 8
HD = 64
EXPERT_COUNT = 16
FF = 1024
EXPERT_CAPACITY = 20
SLOTS = 24
ROWS = 128
PAIR = 256
HEAD_Q = 192
Q_HALF = 768
KV_HALF = 512
EXTRA = 128
PACK = Q_HALF + KV_HALF + EXTRA + Q_HALF

EPS = 1e-05
SCALE_QK = 0.125
NEGATIVE = -1e30
MESH = pl.DeviceIdType.MESH
ANY = pl.BlockSpec(memory_space=pl.ANY)
IN_VMEM = pl.BlockSpec(memory_space=pltpu.VMEM)
BF = jnp.bfloat16
F32 = jnp.float32


def dot(a, b, dims):
    return lax.dot_general(a, b, (dims, ((), ())), preferred_element_type=F32)


def coords():
    i = lax.axis_index("ctx")
    return lax.axis_index("dp"), i // 8, (i // 2) % 4, i % 2


def dev(y, z, x, c):
    return (y, z * 8 + x * 2 + c)


def signal(target):
    pl.semaphore_signal(
        pltpu.get_barrier_semaphore(), inc=1, device_id=target, device_id_type=MESH
    )


def remote(src, dst, send, recv, target):
    return pltpu.make_async_remote_copy(
        src_ref=src, dst_ref=dst, send_sem=send, recv_sem=recv, device_id=target, device_id_type=MESH
    )


def params(cid, vmem=None):
    return pltpu.CompilerParams(collective_id=cid, has_side_effects=True, vmem_limit_bytes=vmem)


def axis_peer(axis, step):
    y, z, x, c = coords()
    if axis == "y":
        return dev((y + step) % 4, z, x, c)
    if axis == "z":
        return dev(y, (z + step) % 4, x, c)
    return dev(y, z, (x + step) % 4, c)


WIDTHS = (Q_HALF, KV_HALF, Q_HALF, EXTRA)
STARTS = (0, Q_HALF, Q_HALF + KV_HALF, 2 * Q_HALF + KV_HALF)
STEPS = (1, 3, 2)
FIRST_PARTS = (
    (0, 0, 512, ("x", "z", "y")),
    (1, 0, 512, ("y", "x", "z")),
    (0, 512, 256, ("z", "y", "x")),
    (3, 0, 128, ("z", "y", "x")),
)
OUT_PARTS = (
    (2, 0, 128, ("z", "x", "y")),
    (2, 128, 384, ("z", "y", "x")),
    (2, 512, 256, ("y", "x", "z")),
)
OUT_SUMS = ((0, ("x", "y", "z")), (256, ("x", "z", "y")), (512, ("z", "x", "y")))
GATHER_PARTS = FIRST_PARTS + OUT_PARTS


def slab(ref, done, y, z, x, cols):
    return ref.at[
        slice(None) if "y" in done else y,
        slice(None) if "z" in done else z,
        slice(None) if "x" in done else x,
        slice(None),
        cols,
    ]


def column_of(row):
    return jnp.transpose(jnp.broadcast_to(row, (128, row.shape[1])))


def slot_hits(ids):
    lane = lax.broadcasted_iota(jnp.int32, (ROWS, 128), 1).astype(F32)
    experts_of = [column_of(ids[k : k + 1].astype(F32)) for k in range(2)]
    chosen = [jnp.where(lane == expert, 1.0, 0.0) for expert in experts_of]
    row = lax.broadcasted_iota(jnp.int32, (ROWS, ROWS), 0)
    earlier = jnp.where(row > lax.broadcasted_iota(jnp.int32, (ROWS, ROWS), 1), 1.0, 0.0).astype(BF)
    before = dot(earlier, (chosen[0] + chosen[1]).astype(BF), ((1,), (0,)))
    slot_lane = lax.broadcasted_iota(jnp.int32, (ROWS, EXPERT_COUNT * SLOTS), 1).astype(F32)
    hits = []
    for k in range(2):
        place = jnp.sum(chosen[k] * before, axis=1, keepdims=True)
        slot = jnp.where(place < EXPERT_CAPACITY, experts_of[k][:, :1] * SLOTS + place, -1.0)
        hits.append(jnp.where(slot_lane == slot, 1.0, 0.0))
    return chosen, hits


def three_parts(values):
    parts = []
    for _ in range(3):
        part = values.astype(BF)
        parts.append(part)
        values = values - part.astype(F32)
    return parts


def gather_kernel(
    w_query, w_key, w_value, w_out, w_router, gain_a, gain_m, ids, cots, tokens, segs, w_gate, w_up, w_down,
    o_q, o_kv, out2, out3, pair, o_normed, w_experts, q4, kv2, o_first, cot_slots,
    pack, sib, block, w_q, w_kv, w_extra, rows, segments, normed, packed, down,
    p_send, p_recv, l_sem, s_send, s_recv, sib_send, sib_recv, o_sem,
):
    y, z, x, c = coords()
    outs = (w_q, w_kv, out2, w_extra)
    me = z * 8 + x * 2 + c
    sibling = dev(y, z, x, 1 - c)

    def greet(k, carry):
        signal((y, (me + k) % 32))
        return carry

    lax.fori_loop(1, 32, greet, 0)
    for step in STEPS:
        signal(axis_peer("y", step))
    expert_loads = [
        pltpu.make_async_copy(w_gate, packed.at[:, 0:FF // 2], o_sem.at[5]),
        pltpu.make_async_copy(w_up, packed.at[:, FF // 2 : FF], o_sem.at[6]),
        pltpu.make_async_copy(w_down, down, o_sem.at[7]),
    ]
    for load in expert_loads:
        load.start()
    lane = lax.broadcasted_iota(jnp.int32, (12, EXTRA), 1)
    square = lax.broadcasted_iota(jnp.int32, (12, 12), 0) == lax.broadcasted_iota(jnp.int32, (12, 12), 1)
    extra = jnp.concatenate(
        [w_router[...].astype(F32), jnp.zeros((12, EXTRA - EXPERT_COUNT), F32)], axis=1
    )
    for k, gain_row in enumerate((gain_a, gain_m)):
        spread_row = jnp.broadcast_to(gain_row[...].astype(F32), (12, 12))
        column = jnp.sum(jnp.where(square, spread_row, 0.0), axis=1, keepdims=True)
        extra = jnp.where(lane == EXPERT_COUNT + k, column, extra)
    extra = extra.astype(BF)
    heads = []
    for h in range(KV):
        cols = slice(HD * h, HD * h + HD)
        heads += [w_key[:, cols].astype(F32), w_value[:, cols].astype(F32)]
    heads = jnp.concatenate(heads, axis=1).astype(BF)
    for k in range(2):
        parts = (
            w_query[:, Q_HALF * k : Q_HALF * k + Q_HALF],
            heads[:, KV_HALF * k : KV_HALF * k + KV_HALF],
            w_out[:, Q_HALF * k : Q_HALF * k + Q_HALF],
            extra,
        )
        for start, width, part in zip(STARTS, WIDTHS, parts):
            pack[k, 0:12, start : start + width] = part
            pack[k, 12:16, start : start + width] = jnp.zeros((4, width), BF)
    pl.semaphore_wait(pltpu.get_barrier_semaphore(), 34)

    first = remote(pack.at[1 - c], sib, sib_send.at[0], sib_recv.at[0], sibling)
    first.start()
    second = remote(tokens, rows.at[c], sib_send.at[1], sib_recv.at[1], sibling)
    second.start()
    own_rows = pltpu.make_async_copy(tokens, rows.at[c], l_sem.at[4])
    own_rows.start()
    own_segs = pltpu.make_async_copy(segs, segments.at[me], l_sem.at[5])
    own_segs.start()

    def spread(k, carry):
        remote(segs, segments.at[me], s_send, s_recv, (y, (me + k) % 32)).start()
        return carry

    lax.fori_loop(1, 32, spread, 0)

    first.wait()
    own = pack[c, :12].astype(F32)
    other = sib[:12].astype(F32)
    low = jnp.where(c == 0, own, other)
    high = jnp.where(c == 0, other, own)
    block[...] = jnp.concatenate([low, high], axis=0).astype(BF)

    locals_ = []
    for n in range(4):
        cols = pl.ds(STARTS[n], WIDTHS[n])
        here = pltpu.make_async_copy(block.at[:, cols], outs[n].at[y, z, x], l_sem.at[n])
        here.start()
        locals_.append(here)
    for phase in range(3):
        copies = []
        for part, (n, start, width, order) in enumerate(GATHER_PARTS if phase < 2 else FIRST_PARTS):
            for k, step in enumerate(STEPS):
                dst = slab(outs[n], order[:phase], y, z, x, pl.ds(start, width))
                src = block.at[:, pl.ds(STARTS[n] + start, width)] if phase == 0 else dst
                copy = remote(
                    src, dst, p_send.at[phase, part, k], p_recv.at[phase, part, k],
                    axis_peer(order[phase], step),
                )
                copy.start()
                copies.append(copy)
        if phase == 0:
            for here in locals_:
                here.wait()
        if phase == 2:
            own_segs.wait()
            drain = remote(
                segments.at[pl.ds(0, 31)], segments.at[pl.ds(0, 31)], s_send, s_recv, sibling
            )
            drain.wait_send()
            drain.wait_recv()
            places = segments[...].reshape(32, 128)
            for zq in range(4):
                t = (zq * 4 + x) * 2
                mine = jnp.concatenate([segments[t], segments[t + 1]], axis=1)
                begin = jnp.zeros((1, PAIR), jnp.int32)
                for u in range(15):
                    count = jnp.sum((places == u).astype(jnp.int32))
                    begin = begin + jnp.where(mine > u, count, 0)
                o_first[zq] = begin
            chosen, hits = slot_hits(ids[...])
            kept = dot((hits[0] + hits[1]).astype(BF), cots[...], ((0,), (0,))).astype(BF)
            cot_slots[...] = kept.reshape(EXPERT_COUNT, SLOTS, MODEL_WIDTH)
            for load in expert_loads:
                load.wait()
            packed[:, FF:] = jnp.transpose(down[...].astype(F32)).astype(BF)
            pltpu.make_async_copy(packed, w_experts, o_sem.at[5]).start()
            second.wait()
            own_rows.wait()
        for copy in copies:
            copy.wait()
    stores = [
        pltpu.make_async_copy(src, dst, o_sem.at[n])
        for n, (src, dst) in enumerate(((w_q, o_q), (w_kv, o_kv), (w_extra, out3), (rows, pair)))
    ]
    for store in stores:
        store.start()
    gain = jnp.transpose(w_extra[...].reshape(MODEL_WIDTH, EXTRA).astype(F32))[EXPERT_COUNT : EXPERT_COUNT + 1]
    for k in range(2):
        values = rows[k].astype(F32)
        normed[ROWS * k : ROWS * k + ROWS] = (values * inverse_rms(values) * gain).astype(BF)
    last = pltpu.make_async_copy(normed, o_normed, o_sem.at[4])
    last.start()
    queries = dot(w_q[...].reshape(MODEL_WIDTH, Q_HALF), normed[...], ((0,), (1,))).astype(BF)
    q4[...] = queries.reshape(4, HEAD_Q, PAIR)
    kv2[...] = dot(normed[...], w_kv[...].reshape(MODEL_WIDTH, KV_HALF), ((1,), (0,))).astype(BF)
    for store in stores:
        store.wait()
    last.wait()
    pltpu.make_async_copy(packed, w_experts, o_sem.at[5]).wait()


def gather_weights(vmem_args, hbm_args):
    blocks = [(4, 4, 4, 24, width) for width in WIDTHS]
    rows = (2, ROWS, MODEL_WIDTH)
    flat = (PAIR, MODEL_WIDTH)
    experts_in = (MODEL_WIDTH // 4, 3 * FF // 2)
    return pl.pallas_call(
        gather_kernel,
        out_shape=[jax.ShapeDtypeStruct(shape, BF) for shape in (*blocks, rows, flat, experts_in)]
        + [
            jax.ShapeDtypeStruct((4, HEAD_Q, PAIR), BF),
            jax.ShapeDtypeStruct((PAIR, KV_HALF), BF),
            jax.ShapeDtypeStruct((4, 1, PAIR), jnp.int32),
            jax.ShapeDtypeStruct((EXPERT_COUNT, SLOTS, MODEL_WIDTH), BF),
        ],
        in_specs=[IN_VMEM] * len(vmem_args) + [ANY] * len(hbm_args),
        out_specs=[ANY] * 7 + [IN_VMEM] * 4,
        scratch_shapes=[
            pltpu.VMEM((2, 16, PACK), BF),
            pltpu.VMEM((16, PACK), BF),
            pltpu.VMEM((24, PACK), BF),
            pltpu.VMEM(blocks[0], BF),
            pltpu.VMEM(blocks[1], BF),
            pltpu.VMEM(blocks[3], BF),
            pltpu.VMEM(rows, BF),
            pltpu.VMEM((32, 1, 128), jnp.int32),
            pltpu.VMEM(flat, BF),
            pltpu.VMEM(experts_in, BF),
            pltpu.VMEM((FF // 2, MODEL_WIDTH // 4), BF),
            pltpu.SemaphoreType.DMA((3, 7, 3)),
            pltpu.SemaphoreType.DMA((3, 7, 3)),
            pltpu.SemaphoreType.DMA((6,)),
            pltpu.SemaphoreType.DMA,
            pltpu.SemaphoreType.DMA,
            pltpu.SemaphoreType.DMA((2,)),
            pltpu.SemaphoreType.DMA((2,)),
            pltpu.SemaphoreType.DMA((8,)),
        ],
        compiler_params=params(1, 60 << 20),
        name="gather_weights",
    )(*vmem_args, *hbm_args)


def offset(k):
    dz = (k % 8) // 2
    return dz, 2 * (k % 2) + (dz + k // 8) % 2


def chip_to(k):
    y, z, x, c = coords()
    dz, dx = offset(k)
    return (z + dz) % 4, (x + dx) % 4


def chip_from(k):
    y, z, x, c = coords()
    dz, dx = offset(k)
    return (z + 4 - dz) % 4, (x + 4 - dx) % 4


def slot_block(k, core):
    return (k // 8) * 16 + core * 8 + k % 8


def plane_greet():
    y, z, x, c = coords()
    me = z * 4 + x

    def greet(k, carry):
        t = (me + k) % 16
        signal(dev(y, t // 4, t % 4, c))
        return carry

    lax.fori_loop(1, 16, greet, 0)
    signal(dev(y, z, x, 1 - c))


KEYS = 1024


def attend_kernel(
    q4, kv2, half_in, cots, first_ref, q_out, kv_out, attn, ot_out, lse_ref, half, half_sib, c_all,
    q_in, kv_in, ot_ref, qs, acc, o_buf, keep,
    l_sem, q_send, q_recv, k_send, k_recv, w_send, w_recv, sib_send, sib_recv,
    c_send, c_recv, f_send, f_recv, o_send, o_recv,
):
    y, z, x, c = coords()
    me = z * 4 + x
    sibling = dev(y, z, x, 1 - c)

    wide_greet()

    q_copies = []
    for n, step in enumerate(STEPS):
        to = (z + step) % 4
        copy = remote(q4.at[to], q_in.at[z], q_send.at[n], q_recv.at[n], dev(y, to, x, c))
        copy.start()
        q_copies.append(copy)

    def head(index):
        return kv2.at[:, pl.ds(pl.multiple_of(index * 128, 128), 128)]

    def send_kv(k, carry):
        tz, tx = chip_to(k)
        remote(head(tz), kv_in.at[me], k_send, k_recv, dev(y, tz, tx, c)).start()
        return carry

    lax.fori_loop(1, 16, send_kv, 0)
    here = [
        pltpu.make_async_copy(q4.at[z], q_in.at[z], l_sem.at[0]),
        pltpu.make_async_copy(head(z), kv_in.at[me], l_sem.at[1]),
    ]
    for copy in here:
        copy.start()
    for copy in here:
        copy.wait()
    for copy in q_copies:
        copy.wait()
    drain = remote(kv_in.at[pl.ds(0, 15)], kv_in.at[pl.ds(0, 15)], k_send, k_recv, sibling)
    drain.wait_send()
    drain.wait_recv()

    w_copies = [[], [], []]
    for part, (n, start, width, order) in enumerate(OUT_PARTS):
        spot = slab(half, order[:2], y, z, x, pl.ds(start, width))
        for k, step in enumerate(STEPS):
            copy = remote(
                spot, spot, w_send.at[part, k], w_recv.at[part, k], axis_peer(order[2], step)
            )
            copy.start()
            w_copies[part].append(copy)

    kept = [
        pltpu.make_async_copy(q_in, q_out, keep.at[4]),
        pltpu.make_async_copy(kv_in, kv_out, keep.at[5]),
    ]
    for copy in kept:
        copy.start()

    def cots_copy(k):
        tz, tx = chip_to(k)
        return remote(
            cots.at[tz * 4 + tx], c_all.at[slot_block(k, c)], c_send.at[k], c_recv.at[k], dev(y, tz, tx, c)
        )

    def send_cots(k, carry):
        cots_copy(k).start()
        return carry

    lax.fori_loop(1, 16, send_cots, 0)
    own_cots = pltpu.make_async_copy(cots.at[me], c_all.at[slot_block(0, c)], l_sem.at[2])
    own_cots.start()
    remote(cots.at[me], c_all.at[slot_block(0, c)], f_send, f_recv, sibling).start()

    def forward_cots(k, carry):
        arrived = cots_copy(k)
        arrived.wait_recv()
        remote(c_all.at[slot_block(k, c)], c_all.at[slot_block(k, c)], f_send, f_recv, sibling).start()
        arrived.wait_send()
        return carry

    def swap(part):
        start, width = OUT_PARTS[part][1:3]
        cols = half.at[:, :, :, :, pl.ds(start, width)]
        there = half_sib.at[:, :, :, :, pl.ds(start, width)]
        return remote(cols, there, sib_send.at[part], sib_recv.at[part], sibling)

    j = c * 4 + z
    qs[64:] = jnp.zeros((64, 3 * PAIR), BF)
    returns = []
    for n in range(4):
        zq = (z + n + 1) % 4
        q = q_in[zq] * SCALE_QK
        for h in range(3):
            qs[:64, 256 * h : 256 * h + 256] = q[64 * h : 64 * h + 64]
        acc[...] = jnp.zeros_like(acc)
        first = first_ref[zq]
        q_pos = (zq * 4 + x) * PAIR + lax.broadcasted_iota(jnp.int32, (1, PAIR), 1)

        def step(kb, stats):
            kv = kv_in[pl.ds(kb * (KEYS // PAIR), KEYS // PAIR)].reshape(KEYS, 128)
            k_pos = kb * KEYS + lax.broadcasted_iota(jnp.int32, (KEYS, PAIR), 0)
            ok = (k_pos >= first) & (k_pos <= q_pos)
            scores = [dot(kv, qs[:, 256 * h : 256 * h + 256], ((1,), (0,))) for h in range(3)]
            later, probs, shrinks = [], [], []
            for h in range(3):
                top, tot = stats[h]
                masked = jnp.where(ok, scores[h], NEGATIVE)
                new = jnp.maximum(top, jnp.max(masked, axis=0, keepdims=True))
                prob = jnp.exp(masked - new)
                shrink = jnp.exp(top - new)
                later.append((new, tot * shrink + jnp.sum(prob, axis=0, keepdims=True)))
                probs.append(prob.astype(BF))
                shrinks.append(shrink)
            for h in range(3):
                cols = slice(256 * h, 256 * h + 256)
                acc[:, cols] = acc[:, cols] * shrinks[h] + dot(kv, probs[h], ((0,), (0,)))
            return tuple(later)

        none = (jnp.full((1, PAIR), NEGATIVE, F32), jnp.zeros((1, PAIR), F32))
        stats = lax.fori_loop(0, zq + 1, step, (none, none, none))
        heads = []
        for h in range(3):
            cols = slice(256 * h, 256 * h + 256)
            mixed = acc[64:, cols] / stats[h][1]
            ot_ref[zq, :, cols] = mixed
            lse_ref[zq, :, cols] = stats[h][0] + jnp.log(stats[h][1])
            heads.append(mixed)
        heads = jnp.concatenate(heads, axis=0).astype(BF)
        saved = pltpu.make_async_copy(ot_ref.at[zq], ot_out.at[zq], keep.at[n])
        saved.start()
        kept.append(saved)
        o_buf[n, 0] = heads[:, :ROWS]
        o_buf[n, 1] = heads[:, ROWS:]
        for d in range(2):
            core = c if d == 0 else 1 - c
            if n == 3 and d == 0:
                back = pltpu.make_async_copy(o_buf.at[n, core], attn.at[j], l_sem.at[3])
            else:
                back = remote(
                    o_buf.at[n, core], attn.at[j], o_send.at[n, d], o_recv.at[n, d], dev(y, zq, x, core)
                )
            back.start()
            returns.append(back)
    for part in (0, 2, 1):
        for copy in w_copies[part]:
            copy.wait()
        swap(part).start()
        if part == 0:
            lax.fori_loop(1, 16, forward_cots, 0)
    own_cots.wait()
    mine = c_all.at[pl.ds(c * 16, 16)]
    drain = remote(mine, mine, f_send, f_recv, sibling)
    drain.wait_send()
    drain.wait_recv()
    for part in range(3):
        swap(part).wait()
    for back in returns + kept:
        back.wait()


def attend(q4, kv2, half, cots, first):
    blocks = jax.ShapeDtypeStruct((4, 4, 4, 24, Q_HALF), BF)
    return pl.pallas_call(
        attend_kernel,
        out_shape=[
            jax.ShapeDtypeStruct((4, HEAD_Q, PAIR), BF),
            jax.ShapeDtypeStruct((16, PAIR, 128), BF),
            jax.ShapeDtypeStruct((8, HEAD_Q, ROWS), BF),
            jax.ShapeDtypeStruct((4, HD, 3 * PAIR), F32),
            jax.ShapeDtypeStruct((4, 1, 3 * PAIR), F32),
            blocks,
            blocks,
            jax.ShapeDtypeStruct((32, SLOTS, MODEL_WIDTH), BF),
        ],
        in_specs=[ANY, ANY, ANY, ANY, IN_VMEM],
        out_specs=[ANY, ANY, ANY, ANY, IN_VMEM, ANY, ANY, ANY],
        input_output_aliases={2: 5},
        scratch_shapes=[
            pltpu.VMEM((4, HEAD_Q, PAIR), BF),
            pltpu.VMEM((16, PAIR, 128), BF),
            pltpu.VMEM((4, HD, 3 * PAIR), F32),
            pltpu.VMEM((128, 3 * PAIR), BF),
            pltpu.VMEM((128, 3 * PAIR), F32),
            pltpu.VMEM((4, 2, HEAD_Q, ROWS), BF),
            pltpu.SemaphoreType.DMA((6,)),
            pltpu.SemaphoreType.DMA((4,)),
            pltpu.SemaphoreType.DMA((3,)),
            pltpu.SemaphoreType.DMA((3,)),
            pltpu.SemaphoreType.DMA,
            pltpu.SemaphoreType.DMA,
            pltpu.SemaphoreType.DMA((3, 3)),
            pltpu.SemaphoreType.DMA((3, 3)),
            pltpu.SemaphoreType.DMA((3,)),
            pltpu.SemaphoreType.DMA((3,)),
            pltpu.SemaphoreType.DMA((16,)),
            pltpu.SemaphoreType.DMA((16,)),
            pltpu.SemaphoreType.DMA,
            pltpu.SemaphoreType.DMA,
            pltpu.SemaphoreType.DMA((4, 2)),
            pltpu.SemaphoreType.DMA((4, 2)),
        ],
        compiler_params=params(2, 60 << 20),
        name="attend",
    )(q4, kv2, half, cots, first)


def flat_rows(blocks):
    return blocks.reshape(blocks.shape[0] * SLOTS, blocks.shape[2])


def experts_kernel(
    attn, tokens, extra, ids, cotangent, half_w, sib_w, cots, weights,
    o_block, o_middle, o_branch, o_heads, o_moe, o_logits, o_gain, d_all,
    x_all, t_all, g_all, w_all, gate_v, up_v, hidden, g_both, part_o, part_g, sib_o, sib_g,
    v_all, wh, ws, xs, gates, out_ret, grad_ret, middle, moe_in,
    w_sem, l_sem, send, recv, f_send, f_recv, s_send, s_recv, r_send, r_recv, o_sem,
):
    y, z, x, c = coords()
    me = z * 4 + x
    width = hidden.shape[1]
    sibling = dev(y, z, x, 1 - c)
    loads = [
        pltpu.make_async_copy(src, dst, w_sem.at[n])
        for n, (src, dst) in enumerate(((half_w, wh), (sib_w, ws), (weights, w_all), (cots, g_all)))
    ]
    plane_greet()
    for load in loads:
        load.start()
    chosen, hits = slot_hits(ids[...])
    both_hits = (hits[0] + hits[1]).astype(BF)
    flat_extra = extra[...].reshape(MODEL_WIDTH, EXTRA)
    gain = jnp.transpose(flat_extra.astype(F32))[EXPERT_COUNT + 1 : EXPERT_COUNT + 2]
    own = attn[pl.ds(c * 4, 4)].reshape(Q_HALF, ROWS)
    other = attn[pl.ds((1 - c) * 4, 4)].reshape(Q_HALF, ROWS)
    loads[0].wait()
    loads[1].wait()
    middle[...] = (
        tokens[...].astype(F32)
        + dot(own, wh[...].reshape(MODEL_WIDTH, Q_HALF), ((0,), (1,)))
        + dot(other, ws[...].reshape(MODEL_WIDTH, Q_HALF), ((0,), (1,)))
    )
    inverse = inverse_rms(middle[...])
    moe_in[...] = (middle[...] * inverse * gain).astype(BF)
    logits = dot(moe_in[...], flat_extra, ((1,), (0,)))
    picked = [jnp.sum(chosen[k] * logits, axis=1, keepdims=True) for k in range(2)]
    most = jnp.maximum(picked[0], picked[1])
    lifted = [jnp.exp(value - most) for value in picked]
    share = [value / (lifted[0] + lifted[1]) for value in lifted]
    slots_in = dot(both_hits, moe_in[...], ((0,), (0,))).astype(BF)
    xs[...] = slots_in.reshape(EXPERT_COUNT, SLOTS, MODEL_WIDTH)
    slot_gate = jnp.sum(hits[0] * share[0] + hits[1] * share[1], axis=0, keepdims=True)
    gates[...] = column_of(slot_gate).reshape(EXPERT_COUNT, SLOTS, 128)
    pl.semaphore_wait(pltpu.get_barrier_semaphore(), 16)
    arrays = ((xs, x_all), (gates, t_all))

    def arriving(a, k):
        src, dst = arrays[a]
        tz, tx = chip_to(k)
        return remote(
            src.at[tz * 4 + tx], dst.at[slot_block(k, c)], send.at[a, k], recv.at[a, k], dev(y, tz, tx, c)
        )

    def steps_of(part):
        return (1, 8) if part == 0 else (8, 16)

    def scatter(a, part):
        def push(k, carry):
            arriving(a, k).start()
            return carry

        lax.fori_loop(*steps_of(part), push, 0)
        if part == 0:
            src, dst = arrays[a]
            pltpu.make_async_copy(src.at[me], dst.at[slot_block(0, c)], l_sem.at[a]).start()
            remote(src.at[me], dst.at[slot_block(0, c)], f_send.at[a, 0], f_recv.at[a, 0], sibling).start()

    def hand_over(a, part, steps=None):
        src, dst = arrays[a]

        def forward(k, carry):
            arrived = arriving(a, k)
            arrived.wait_recv()
            block = dst.at[slot_block(k, c)]
            remote(block, block, f_send.at[a, part], f_recv.at[a, part], sibling).start()
            arrived.wait_send()
            return carry

        lax.fori_loop(*(steps or steps_of(part)), forward, 0)

    def settle(a, part):
        src, dst = arrays[a]
        if part == 0:
            pltpu.make_async_copy(src.at[me], dst.at[slot_block(0, c)], l_sem.at[a]).wait()
        some = dst.at[pl.ds(0, 8)]
        drain = remote(some, some, f_send.at[a, part], f_recv.at[a, part], sibling)
        drain.wait_send()
        drain.wait_recv()

    def swap(mine, sib, a, part):
        return remote(
            mine.at[pl.ds(part * 16 + (1 - c) * 8, 8)], sib.at[pl.ds(part * 8, 8)],
            s_send.at[a, part], s_recv.at[a, part], sibling,
        )

    def give(mine, sib, ret, a, part):
        def add(k):
            block = slot_block(k, c)
            mine[block] = (mine[block].astype(F32) + sib[k].astype(F32)).astype(BF)
            return mine.at[block]

        def push(k, carry):
            sz, sx = chip_from(k)
            remote(add(k), ret.at[me], r_send.at[a], r_recv.at[a], dev(y, sz, sx, c)).start()
            return carry

        lax.fori_loop(*steps_of(part), push, 0)
        if part == 0:
            pltpu.make_async_copy(add(0), ret.at[me], l_sem.at[2 + a]).start()

    def given(mine, ret, a):
        pltpu.make_async_copy(mine.at[slot_block(0, c)], ret.at[me], l_sem.at[2 + a]).wait()
        drain = remote(ret.at[pl.ds(0, 15)], ret.at[pl.ds(0, 15)], r_send.at[a], r_recv.at[a], sibling)
        drain.wait_send()
        drain.wait_recv()

    half = 16 * SLOTS

    def forward_pass(part):
        blocks, rows = pl.ds(part * 16, 16), slice(part * half, part * half + half)
        both = dot(flat_rows(x_all[blocks]), w_all[:, : 2 * width], ((1,), (0,)))
        gate_val, up_val = both[:, :width], both[:, width:]
        gate_v[rows] = gate_val
        up_v[rows] = up_val
        low = (gate_val * jax.nn.sigmoid(gate_val) * up_val).astype(BF)
        hidden[rows] = low
        out = dot(low, w_all[:, 2 * width :], ((1,), (1,))).astype(BF)
        part_o[blocks] = out.reshape(16, SLOTS, MODEL_WIDTH)
        swap(part_o, sib_o, 0, part).start()

    def backward_pass(part):
        blocks, rows = pl.ds(part * 16, 16), slice(part * half, part * half + half)
        scale = jnp.concatenate([flat_rows(t_all[blocks])] * (MODEL_WIDTH // 128), axis=1)
        grad_expert = (flat_rows(g_all[blocks]).astype(F32) * scale).astype(BF)
        g_all[blocks] = grad_expert.reshape(16, SLOTS, MODEL_WIDTH)
        grad_hidden = dot(grad_expert, w_all[:, 2 * width :], ((1,), (0,)))
        gate_val = gate_v[rows]
        up_val = up_v[rows]
        sig = jax.nn.sigmoid(gate_val)
        grad_gate = (grad_hidden * up_val * sig * (1.0 + gate_val * (1.0 - sig))).astype(BF)
        grad_up = (grad_hidden * gate_val * sig).astype(BF)
        grads = jnp.concatenate([grad_gate, grad_up], axis=1)
        g_both[rows] = grads
        grad_rows = dot(grads, w_all[:, : 2 * width], ((1,), (1,))).astype(BF)
        part_g[blocks] = grad_rows.reshape(16, SLOTS, MODEL_WIDTH)
        swap(part_g, sib_g, 1, part).start()

    scatter(0, 0)
    scatter(1, 0)
    hand_over(0, 0, (1, 4))
    scatter(0, 1)
    scatter(1, 1)
    hand_over(0, 0, (4, 8))
    loads[2].wait()
    loads[3].wait()
    settle(0, 0)
    forward_pass(0)
    hand_over(0, 1)
    swap(part_o, sib_o, 0, 0).wait()
    give(part_o, sib_o, out_ret, 0, 0)
    settle(0, 1)
    forward_pass(1)
    hand_over(1, 0)
    hand_over(1, 1)
    settle(1, 0)
    swap(part_o, sib_o, 0, 1).wait()
    give(part_o, sib_o, out_ret, 0, 1)
    backward_pass(0)
    settle(1, 1)
    swap(part_g, sib_g, 1, 0).wait()
    give(part_g, sib_g, grad_ret, 1, 0)
    backward_pass(1)
    swap(part_g, sib_g, 1, 1).wait()
    give(part_g, sib_g, grad_ret, 1, 1)

    def weight_grads(j, carry):
        cols = pl.ds(pl.multiple_of(j * 256, 256), 256)
        v_all[cols, : 2 * width] = dot(flat_rows(x_all[:, :, cols]), g_both[...], ((0,), (0,))).astype(BF)
        v_all[cols, 2 * width :] = dot(flat_rows(g_all[:, :, cols]), hidden[...], ((0,), (0,))).astype(BF)
        return carry

    lax.fori_loop(0, MODEL_WIDTH // 256, weight_grads, 0)
    store = pltpu.make_async_copy(v_all, d_all, o_sem)
    store.start()
    given(part_o, out_ret, 0)
    grad_out = cotangent[...].astype(F32)
    rows_out = [dot(hits[k].astype(BF), flat_rows(out_ret[...]), ((1,), (0,))) for k in range(2)]
    o_block[...] = (middle[...] + share[0] * rows_out[0] + share[1] * rows_out[1]).astype(BF)
    pairs = [jnp.sum(grad_out * rows, axis=1, keepdims=True) for rows in rows_out]
    mean = share[0] * pairs[0] + share[1] * pairs[1]
    grad_logits = sum(chosen[k] * (share[k] * (pairs[k] - mean)) for k in range(2))
    o_logits[...] = grad_logits
    o_moe[...] = moe_in[...]
    routed = sum(dot(part, flat_extra, ((1,), (1,))) for part in three_parts(grad_logits))
    given(part_g, grad_ret, 1)
    grad_moe = dot(both_hits, flat_rows(grad_ret[...]), ((1,), (0,))) + routed
    o_gain[...] = jnp.sum(grad_moe * middle[...] * inverse, axis=0, keepdims=True)
    grad_middle = grad_out + norm_backward(middle[...], inverse, gain, grad_moe)
    o_middle[...] = grad_middle
    branch = grad_middle.astype(BF)
    o_branch[...] = branch
    for core, weight in ((c, wh), (1 - c, ws)):
        heads = dot(weight[...].reshape(MODEL_WIDTH, Q_HALF), branch, ((0,), (1,))).astype(BF)
        o_heads[pl.ds(core * 4, 4)] = heads.reshape(4, HEAD_Q, ROWS)
    store.wait()


def experts(attn, tokens, extra, ids, cotangent, half_w, sib_w, cots, weights):
    rows = 32 * SLOTS
    width = weights.shape[1] // 3
    slots = (16, SLOTS, MODEL_WIDTH)
    flat = (ROWS, MODEL_WIDTH)
    low = jax.ShapeDtypeStruct(flat, BF)
    return pl.pallas_call(
        experts_kernel,
        out_shape=[
            low,
            jax.ShapeDtypeStruct(flat, F32),
            low,
            jax.ShapeDtypeStruct((8, HEAD_Q, ROWS), BF),
            low,
            jax.ShapeDtypeStruct((ROWS, 128), F32),
            jax.ShapeDtypeStruct((1, MODEL_WIDTH), F32),
            jax.ShapeDtypeStruct(weights.shape, BF),
        ],
        in_specs=[IN_VMEM] * 5 + [ANY] * 4,
        out_specs=[IN_VMEM] * 7 + [ANY],
        scratch_shapes=[
            pltpu.VMEM((32, SLOTS, MODEL_WIDTH), BF),
            pltpu.VMEM((32, SLOTS, 128), F32),
            pltpu.VMEM((32, SLOTS, MODEL_WIDTH), BF),
            pltpu.VMEM(weights.shape, BF),
            pltpu.VMEM((rows, width), F32),
            pltpu.VMEM((rows, width), F32),
            pltpu.VMEM((rows, width), BF),
            pltpu.VMEM((rows, 2 * width), BF),
            pltpu.VMEM((32, SLOTS, MODEL_WIDTH), BF),
            pltpu.VMEM((32, SLOTS, MODEL_WIDTH), BF),
            pltpu.VMEM((16, SLOTS, MODEL_WIDTH), BF),
            pltpu.VMEM((16, SLOTS, MODEL_WIDTH), BF),
            pltpu.VMEM(weights.shape, BF),
            pltpu.VMEM(half_w.shape, BF),
            pltpu.VMEM(half_w.shape, BF),
            pltpu.VMEM(slots, BF),
            pltpu.VMEM((EXPERT_COUNT, SLOTS, 128), F32),
            pltpu.VMEM(slots, BF),
            pltpu.VMEM(slots, BF),
            pltpu.VMEM(flat, F32),
            pltpu.VMEM(flat, BF),
            pltpu.SemaphoreType.DMA((4,)),
            pltpu.SemaphoreType.DMA((4,)),
            pltpu.SemaphoreType.DMA((2, 16)),
            pltpu.SemaphoreType.DMA((2, 16)),
            pltpu.SemaphoreType.DMA((2, 2)),
            pltpu.SemaphoreType.DMA((2, 2)),
            pltpu.SemaphoreType.DMA((2, 2)),
            pltpu.SemaphoreType.DMA((2, 2)),
            pltpu.SemaphoreType.DMA((2,)),
            pltpu.SemaphoreType.DMA((2,)),
            pltpu.SemaphoreType.DMA,
        ],
        compiler_params=params(6, 60 << 20),
        name="experts",
    )(attn, tokens, extra, ids, cotangent, half_w, sib_w, cots, weights)


SUMS = tuple((n, start, width, order[::-1]) for n, start, width, order in FIRST_PARTS) + tuple(
    (2, start, 256, order) for start, order in OUT_SUMS
)
LATE = len(FIRST_PARTS)


def reduce_kernel(
    gq_t, dkv, normed, s_out, grad_logits, gain_m, moe_h, pair_h, extra_h, middle_h, w_q, w_kv, experts_h,
    o_tokens, o_q, o_k, o_v, o_out, o_extra, o_gate, o_up, o_down,
    moe_in, pair, w_extra, grad_middle, summed, f_gate, f_up, f_down, v_q, v_kv, v_extra, wq, wkv, gkv, mine_part, give_part, sib_part, both, total, give, *rest,
):
    parts = len(SUMS)
    first_in, rest = rest[:LATE], rest[LATE:]
    arrive = [list(first_in) + [None] * 3, rest[:parts], rest[parts : 2 * parts]]
    rest = rest[2 * parts :]
    held = [None, list(rest[:LATE]) + [s_out.at[k] for k in range(3)], rest[LATE : LATE + parts]]
    l_sem, send, recv, sib_send, sib_recv = rest[LATE + parts :]
    grads = (v_q, v_kv, None, v_extra)
    y, z, x, c = coords()
    place = {"y": y, "z": z, "x": x}
    sibling = dev(y, z, x, 1 - c)
    loads = [
        pltpu.make_async_copy(src, dst, l_sem.at[n])
        for n, (src, dst) in enumerate(
            (
                (w_q, wq), (w_kv, wkv), (pair_h, pair), (moe_h, moe_in), (extra_h, w_extra),
                (middle_h, grad_middle), (experts_h, summed),
            )
        )
    ]
    for load in loads:
        load.start()
    for axis in ("x", "y", "z"):
        for step in STEPS:
            signal(axis_peer(axis, step))
    signal(sibling)
    pl.semaphore_wait(pltpu.get_barrier_semaphore(), 10)

    def at(phase, part, index):
        n, start, width, order = SUMS[part]
        spot = [
            index if axis == order[phase] else slice(None)
            for axis in ("y", "z", "x")
            if axis not in order[:phase]
        ]
        if phase == 0:
            return grads[n].at[tuple(spot) + (slice(None), pl.ds(start, width))]
        return held[phase][part].at[tuple(spot)]

    def copies_of(phase, part):
        axis = SUMS[part][3][phase]
        return [
            remote(
                at(phase, part, (place[axis] + step) % 4), arrive[phase][part].at[n],
                send.at[phase, part, n], recv.at[phase, part, n], axis_peer(axis, step),
            )
            for n, step in enumerate(STEPS)
        ]

    def begin(phase, part):
        for copy in copies_of(phase, part):
            copy.start()

    def finish(phase, part):
        for copy in copies_of(phase, part):
            copy.wait()
        array, start, width, order = SUMS[part]
        mine = at(phase, part, place[order[phase]])
        got = arrive[phase][part]
        if phase < 2:

            def add(p, carry):
                value = mine[p].astype(F32)
                for n in range(3):
                    value = value + got[n, p].astype(F32)
                held[phase + 1][part][p] = value.astype(BF)
                return carry

            lax.fori_loop(0, 4, add, 0)
        else:
            value = mine[...].astype(F32)
            for n in range(3):
                value = value + got[n].astype(F32)
            total[:, STARTS[array] + start : STARTS[array] + start + width] = value

    for part in range(LATE, parts):
        begin(1, part)
    for h in range(4):
        value = dkv[4 * h].astype(F32)
        for n in range(1, 4):
            value = value + dkv[4 * h + n].astype(F32)
        gkv[128 * h : 128 * h + 128] = value.astype(BF)
    for n in range(4):
        left = normed[:, 384 * n : 384 * n + 384]
        v_kv[n] = dot(left, gkv[...], ((0,), (1,))).astype(BF).reshape(4, 4, 24, KV_HALF)
    begin(0, 1)
    for n in range(4):
        left = normed[:, 384 * n : 384 * n + 384]
        v_q[n] = dot(left, gq_t[...], ((0,), (1,))).astype(BF).reshape(4, 4, 24, Q_HALF)
    begin(0, 0)
    begin(0, 2)

    for load in loads:
        load.wait()
    gain_sum = jnp.zeros((1, MODEL_WIDTH), F32)
    for n in range(2):
        core = 1 - c if n == 0 else c
        rows = pl.ds(pl.multiple_of(core * ROWS, ROWS), ROWS)
        part = dot(gq_t[:, rows], wq[...], ((0,), (1,))) + dot(gkv[:, rows], wkv[...], ((0,), (1,)))
        values = pair[rows].astype(F32)
        gain_sum = gain_sum + jnp.sum(part * values * inverse_rms(values), axis=0, keepdims=True)
        if n == 0:
            give_part[...] = part
            remote(give_part, sib_part, sib_send.at[0], sib_recv.at[0], sibling).start()
        else:
            mine_part[...] = part
    lane = lax.broadcasted_iota(jnp.int32, (MODEL_WIDTH, EXTRA), 1)
    extra = sum(dot(moe_in[...], part, ((0,), (0,))) for part in three_parts(grad_logits[...]))
    extra = jnp.where(lane == EXPERT_COUNT, column_of(gain_sum), extra)
    extra = jnp.where(lane == EXPERT_COUNT + 1, column_of(gain_m[...]), extra)
    gain = jnp.transpose(w_extra[...].reshape(MODEL_WIDTH, EXTRA).astype(F32))[EXPERT_COUNT : EXPERT_COUNT + 1]
    v_extra[...] = extra.astype(BF).reshape(4, 4, 4, 24, EXTRA)
    begin(0, 3)
    remote(give_part, sib_part, sib_send.at[0], sib_recv.at[0], sibling).wait()
    rows = pl.ds(pl.multiple_of(c * ROWS, ROWS), ROWS)
    values = pair[rows].astype(F32)
    o_tokens[...] = grad_middle[...] + norm_backward(
        values, inverse_rms(values), gain, mine_part[...] + sib_part[...]
    )

    third = FF // 2
    f_gate[...] = summed[:, :third].astype(F32)
    f_up[...] = summed[:, third : 2 * third].astype(F32)
    f_down[...] = jnp.transpose(summed[:, 2 * third :].astype(F32))
    stores = [
        pltpu.make_async_copy(src, dst, l_sem.at[n])
        for n, (src, dst) in enumerate(((f_gate, o_gate), (f_up, o_up), (f_down, o_down)))
    ]
    for store in stores:
        store.start()
    for part in range(LATE, parts):
        finish(1, part)
        begin(2, part)
    for phase in range(3):
        for part in range(LATE):
            finish(phase, part)
            if phase < 2:
                begin(phase + 1, part)
    for part in range(LATE, parts):
        finish(2, part)
    low, high = total[0:12], total[12:24]
    both[c, 0:12] = jnp.where(c == 0, low, high)
    give[0:12] = jnp.where(c == 0, high, low)
    give[12:16] = jnp.zeros((4, PACK), F32)
    last = remote(give, both.at[c], sib_send.at[1], sib_recv.at[1], sibling)
    last.start()
    for store in stores:
        store.wait()
    last.wait()
    keys, values = [], []
    for k in range(2):
        o_q[:, Q_HALF * k : Q_HALF * k + Q_HALF] = both[k, 0:12, :Q_HALF]
        o_out[:, Q_HALF * k : Q_HALF * k + Q_HALF] = both[k, 0:12, STARTS[2] : STARTS[3]]
        for h in range(4):
            first = STARTS[1] + 128 * h
            keys.append(both[k, 0:12, first : first + HD])
            values.append(both[k, 0:12, first + HD : first + 2 * HD])
    o_k[...] = jnp.concatenate(keys, axis=1)
    o_v[...] = jnp.concatenate(values, axis=1)
    o_extra[...] = both[0, 0:12, STARTS[3] :] + both[1, 0:12, STARTS[3] :]


def reduce_weights(*args):
    widths = [part[2] for part in SUMS]
    full = lambda width: pltpu.VMEM((4, 4, 4, 24, width), BF)
    rows = pltpu.VMEM((ROWS, MODEL_WIDTH), F32)
    low = pltpu.VMEM((ROWS, MODEL_WIDTH), BF)
    scratch = (
        [low, pltpu.VMEM((PAIR, MODEL_WIDTH), BF), full(EXTRA), rows]
        + [pltpu.VMEM((MODEL_WIDTH // 4, 3 * FF // 2), BF)]
        + [pltpu.VMEM((MODEL_WIDTH // 4, FF // 2), F32)] * 2
        + [pltpu.VMEM((FF // 2, MODEL_WIDTH // 4), F32)]
        + [full(Q_HALF), full(KV_HALF), full(EXTRA)]
        + [pltpu.VMEM((MODEL_WIDTH, Q_HALF), BF), pltpu.VMEM((MODEL_WIDTH, KV_HALF), BF)]
        + [pltpu.VMEM((KV_HALF, PAIR), BF), rows, rows, rows]
        + [pltpu.VMEM((2, 16, PACK), F32), pltpu.VMEM((24, PACK), F32), pltpu.VMEM((16, PACK), F32)]
        + [pltpu.VMEM((3, 4, 4, 24, w), BF) for w in widths[:LATE]]
        + [pltpu.VMEM((3, 4, 24, w), BF) for w in widths]
        + [pltpu.VMEM((3, 24, w), BF) for w in widths]
        + [pltpu.VMEM((4, 4, 24, w), BF) for w in widths[:LATE]]
        + [pltpu.VMEM((4, 24, w), BF) for w in widths]
    )
    sems = (3, len(SUMS), 3)
    shapes = ((ROWS, MODEL_WIDTH), (12, MODEL_WIDTH), (12, KV * HD), (12, KV * HD), (12, MODEL_WIDTH), (12, EXTRA))
    tall, flat = (MODEL_WIDTH // 4, FF // 2), (FF // 2, MODEL_WIDTH // 4)
    shapes = shapes + (tall, tall, flat)
    return pl.pallas_call(
        reduce_kernel,
        out_shape=[jax.ShapeDtypeStruct(shape, F32) for shape in shapes],
        in_specs=[IN_VMEM] * 6 + [ANY] * 7,
        out_specs=[IN_VMEM] * 6 + [ANY] * 3,
        scratch_shapes=scratch
        + [
            pltpu.SemaphoreType.DMA((7,)),
            pltpu.SemaphoreType.DMA(sems),
            pltpu.SemaphoreType.DMA(sems),
            pltpu.SemaphoreType.DMA((2,)),
            pltpu.SemaphoreType.DMA((2,)),
        ],
        compiler_params=params(8, 60 << 20),
        name="reduce_weights",
    )(*args)


def wide_greet():
    y, z, x, c = coords()
    me = z * 4 + x

    def greet(k, carry):
        t = (me + k) % 16
        signal(dev(y, t // 4, t % 4, c))
        return carry

    lax.fori_loop(1, 16, greet, 0)
    for step in STEPS:
        signal(axis_peer("y", step))
        signal(dev(y, (z + step) % 4, x, 1 - c))
    signal(dev(y, z, x, 1 - c))
    pl.semaphore_wait(pltpu.get_barrier_semaphore(), 22)


def attend_back_kernel(
    heads, branch_h, attn_h, q_h, kv_h, first_ref, ot_h, lse_ref,
    dq_out, dkv_out, s_out,
    branch, attn, q_in, kv_in, ot_ref, keep, go, branch_sib, attn_sib, qs, gs, delta, dq, dkv, dkv_low, dq_low,
    g_out, a_out,
    l_sem, h_send, h_recv, sib_send, sib_recv, q_send, q_recv, k_send, k_recv,
    w_send, w_recv,
):
    y, z, x, c = coords()
    me = z * 4 + x
    j = c * 4 + z
    sibling = dev(y, z, x, 1 - c)
    place = {"y": y, "z": z, "x": x}
    loads = [
        pltpu.make_async_copy(src, dst, keep.at[n])
        for n, (src, dst) in enumerate(
            ((branch_h, branch), (attn_h, attn), (q_h, q_in), (kv_h, kv_in), (ot_h, ot_ref))
        )
    ]
    for load in loads:
        load.start()
    wide_greet()

    def push(k, carry):
        t = (j + k) % 8
        remote(heads.at[t], go.at[j], h_send, h_recv, dev(y, t % 4, x, t // 4)).start()
        return carry

    lax.fori_loop(1, 8, push, 0)
    one = remote(branch_h, branch_sib, sib_send.at[0], sib_recv.at[0], sibling)
    one.start()
    two = remote(attn_h.at[pl.ds((1 - c) * 4, 4)], attn_sib, sib_send.at[1], sib_recv.at[1], sibling)
    two.start()
    here = pltpu.make_async_copy(heads.at[j], go.at[j], l_sem.at[0])
    here.start()
    loads[0].wait()
    loads[1].wait()
    one.wait()
    two.wait()

    rows_b = jnp.concatenate([branch[...], branch_sib[...]], axis=0)
    rows_a = jnp.concatenate(
        [part.reshape(Q_HALF, ROWS) for part in (attn[pl.ds(c * 4, 4)], attn_sib[...])], axis=1
    )
    for n in range(4):
        part = dot(rows_b[:, 384 * n : 384 * n + 384], rows_a, ((0,), (1,)))
        g_out[n] = part.astype(BF).reshape(4, 4, 24, Q_HALF)

    def spot(part, index):
        start, order = OUT_SUMS[part]
        cut = [index if axis == order[0] else slice(None) for axis in ("y", "z", "x")]
        return g_out.at[tuple(cut) + (slice(None), pl.ds(start, 256))]

    w_copies = []
    for part in range(3):
        axis = OUT_SUMS[part][1][0]
        for n, step in enumerate(STEPS):
            copy = remote(
                spot(part, (place[axis] + step) % 4), a_out.at[part, n],
                w_send.at[part, n], w_recv.at[part, n], axis_peer(axis, step),
            )
            copy.start()
            w_copies.append(copy)

    for load in loads[2:]:
        load.wait()
    here.wait()
    drain = remote(go.at[pl.ds(0, 7)], go.at[pl.ds(0, 7)], h_send, h_recv, sibling)
    drain.wait_send()
    drain.wait_recv()
    dkv[...] = jnp.zeros_like(dkv)
    dq[...] = jnp.zeros_like(dq)
    for zq in range(4):
        q = q_in[zq] * SCALE_QK
        grad = jnp.concatenate([go[zq], go[4 + zq]], axis=1)
        qs[zq, 64:] = jnp.zeros((64, 3 * PAIR), BF)
        gs[zq, :64] = jnp.zeros((64, 3 * PAIR), BF)
        for h in range(3):
            cols, rows = slice(256 * h, 256 * h + 256), slice(64 * h, 64 * h + 64)
            qs[zq, :64, cols] = q[rows]
            gs[zq, 64:, cols] = grad[rows]
            delta[zq, :, cols] = jnp.sum(
                grad[rows].astype(F32) * ot_ref[zq, :, cols], axis=0, keepdims=True
            )

    for n in range(4):
        group = (z + n + 1) % 4
        for zq in range(4):
            hi = zq * 4 + x
            first = first_ref[zq]
            q_pos = hi * PAIR + lax.broadcasted_iota(jnp.int32, (1, PAIR), 1)

            def step(kb, carry):
                kv = kv_in[kb]
                k_pos = kb * PAIR + lax.broadcasted_iota(jnp.int32, (PAIR, PAIR), 0)
                ok = (k_pos >= first) & (k_pos <= q_pos)
                heads = [slice(256 * h, 256 * h + 256) for h in range(3)]
                scores = [dot(kv, qs[zq, :, cols], ((1,), (0,))) for cols in heads]
                grad_probs = [dot(kv, gs[zq, :, cols], ((1,), (0,))) for cols in heads]
                grad_scores, probs = [], []
                for h in range(3):
                    prob = jnp.where(ok, jnp.exp(scores[h] - lse_ref[zq, :, heads[h]]), 0.0)
                    grad_scores.append((prob * (grad_probs[h] - delta[zq, :, heads[h]])).astype(BF))
                    probs.append(prob.astype(BF))
                for h in range(3):
                    dq[zq, :, heads[h]] = dq[zq, :, heads[h]] + dot(kv, grad_scores[h], ((0,), (0,)))
                grad_scores, probs = jnp.concatenate(grad_scores, axis=1), jnp.concatenate(probs, axis=1)
                dkv[kb, :64] = dkv[kb, :64] + dot(qs[zq, :64], grad_scores, ((1,), (1,)))
                dkv[kb, 64:] = dkv[kb, 64:] + dot(gs[zq, 64:], probs, ((1,), (1,)))
                return carry

            last = jnp.minimum(group * 4 + 3, hi)
            lax.fori_loop(group * 4, jnp.maximum(last + 1, group * 4), step, 0)
        for d in range(4):
            xt = (x + d + 1) % 4
            t = group * 4 + xt
            dkv_low[t] = dkv[t].astype(BF)
            if n == 3 and d == 3:
                own_kv = pltpu.make_async_copy(dkv_low.at[me], dkv_out.at[me], l_sem.at[2])
                own_kv.start()
            else:
                remote(dkv_low.at[t], dkv_out.at[me], k_send, k_recv, dev(y, group, xt, c)).start()
    q_copies = []
    for n in range(4):
        zq = (z + n + 1) % 4
        by_head = jnp.concatenate([dq[zq, :64, 256 * h : 256 * h + 256] for h in range(3)], axis=0)
        dq_low[zq] = (by_head * SCALE_QK).astype(BF)
        if n < 3:
            copy = remote(dq_low.at[zq], dq_out.at[z], q_send.at[n], q_recv.at[n], dev(y, zq, x, c))
        else:
            copy = pltpu.make_async_copy(dq_low.at[zq], dq_out.at[z], l_sem.at[1])
        copy.start()
        q_copies.append(copy)

    for copy in w_copies:
        copy.wait()
    for part in range(3):
        mine = spot(part, place[OUT_SUMS[part][1][0]])

        def add(p, carry):
            value = mine[p].astype(F32)
            for k in range(3):
                value = value + a_out[part, k, p].astype(F32)
            s_out[part, p] = value.astype(BF)
            return carry

        lax.fori_loop(0, 4, add, 0)
    for copy in q_copies:
        copy.wait()
    own_kv.wait()
    drain = remote(dkv_out.at[pl.ds(0, 15)], dkv_out.at[pl.ds(0, 15)], k_send, k_recv, sibling)
    drain.wait_send()
    drain.wait_recv()


def attend_back(heads, branch, attn, q_in, kv_in, first, ot, lse):
    return pl.pallas_call(
        attend_back_kernel,
        out_shape=[
            jax.ShapeDtypeStruct((4, HEAD_Q, PAIR), BF),
            jax.ShapeDtypeStruct((16, 128, PAIR), BF),
            jax.ShapeDtypeStruct((3, 4, 4, 24, 256), BF),
        ],
        in_specs=[ANY] * 5 + [IN_VMEM, ANY, IN_VMEM],
        out_specs=[ANY, ANY, IN_VMEM],
        scratch_shapes=[
            pltpu.VMEM((ROWS, MODEL_WIDTH), BF),
            pltpu.VMEM((8, HEAD_Q, ROWS), BF),
            pltpu.VMEM((4, HEAD_Q, PAIR), BF),
            pltpu.VMEM((16, PAIR, 128), BF),
            pltpu.VMEM((4, HD, 3 * PAIR), F32),
            pltpu.SemaphoreType.DMA((5,)),
            pltpu.VMEM((8, HEAD_Q, ROWS), BF),
            pltpu.VMEM((ROWS, MODEL_WIDTH), BF),
            pltpu.VMEM((4, HEAD_Q, ROWS), BF),
            pltpu.VMEM((4, 128, 3 * PAIR), BF),
            pltpu.VMEM((4, 128, 3 * PAIR), BF),
            pltpu.VMEM((4, 1, 3 * PAIR), F32),
            pltpu.VMEM((4, 128, 3 * PAIR), F32),
            pltpu.VMEM((16, 128, PAIR), F32),
            pltpu.VMEM((16, 128, PAIR), BF),
            pltpu.VMEM((4, HEAD_Q, PAIR), BF),
            pltpu.VMEM((4, 4, 4, 24, Q_HALF), BF),
            pltpu.VMEM((3, 3, 4, 4, 24, 256), BF),
            pltpu.SemaphoreType.DMA((3,)),
            pltpu.SemaphoreType.DMA,
            pltpu.SemaphoreType.DMA,
            pltpu.SemaphoreType.DMA((2,)),
            pltpu.SemaphoreType.DMA((2,)),
            pltpu.SemaphoreType.DMA((4,)),
            pltpu.SemaphoreType.DMA((4,)),
            pltpu.SemaphoreType.DMA,
            pltpu.SemaphoreType.DMA,
            pltpu.SemaphoreType.DMA((3, 3)),
            pltpu.SemaphoreType.DMA((3, 3)),
        ],
        compiler_params=params(4, 60 << 20),
        name="attend_back",
    )(heads, branch, attn, q_in, kv_in, first, ot, lse)


def inverse_rms(values):
    return lax.rsqrt(jnp.mean(values * values, axis=-1, keepdims=True) + EPS)


def norm_backward(values, inverse, gain, grad_out):
    scaled = grad_out * gain
    return inverse * scaled - values * inverse**3 * jnp.mean(values * scaled, axis=-1, keepdims=True)


def finish_kernel(extra, *refs):
    n = (len(refs) - 5) // 3
    sources, targets = refs[:n], refs[n : 2 * n]
    o_router, o_gain_a, o_gain_m = refs[2 * n : 2 * n + 3]
    held, (l_sem, s_sem) = refs[2 * n + 3 : 3 * n + 3], refs[3 * n + 3 :]
    loads = [pltpu.make_async_copy(sources[k], held[k], l_sem.at[k]) for k in range(n)]
    stores = [pltpu.make_async_copy(held[k], targets[k], s_sem.at[k]) for k in range(n)]
    for load in loads:
        load.start()
    o_router[...] = extra[:, :EXPERT_COUNT]
    square = lax.broadcasted_iota(jnp.int32, (12, 12), 0) == lax.broadcasted_iota(jnp.int32, (12, 12), 1)
    for k, out in enumerate((o_gain_a, o_gain_m)):
        column = jnp.broadcast_to(extra[:, EXPERT_COUNT + k : EXPERT_COUNT + k + 1], (12, 12))
        out[...] = jnp.sum(jnp.where(square, column, 0.0), axis=0, keepdims=True)
    for k in range(n):
        loads[k].wait()
        stores[k].start()
    for store in stores:
        store.wait()


def finish(extra, arrays):
    n = len(arrays)
    shapes = [jax.ShapeDtypeStruct(array.shape, array.dtype) for array in arrays]
    small = [jax.ShapeDtypeStruct((12, EXPERT_COUNT), F32)] + [jax.ShapeDtypeStruct((1, 12), F32)] * 2
    return pl.pallas_call(
        finish_kernel,
        out_shape=shapes + small,
        in_specs=[IN_VMEM] + [ANY] * n,
        out_specs=[ANY] * n + [IN_VMEM] * 3,
        scratch_shapes=[pltpu.VMEM(shape.shape, shape.dtype) for shape in shapes]
        + [pltpu.SemaphoreType.DMA((n,)), pltpu.SemaphoreType.DMA((n,))],
        compiler_params=pltpu.CompilerParams(vmem_limit_bytes=60 << 20),
        name="finish",
    )(extra, *arrays)


def local(
    tokens,
    segment_ids,
    expert_ids,
    w_query,
    w_key,
    w_value,
    w_out,
    w_router,
    gain_attn,
    gain_moe,
    w_gate,
    w_up,
    w_down,
    cotangent,
):
    ids = expert_ids.T
    part_q, part_kv, part_out, part_extra, pair, normed, w_experts, q4, keys_values, first, cot_slots = (
        gather_weights(
            (w_query, w_key, w_value, w_out.T, w_router, gain_attn[None], gain_moe[None], ids, cotangent),
            (tokens, segment_ids, w_gate, w_up, w_down),
        )
    )
    full_experts = lax.all_gather(w_experts, "dp", axis=0, tiled=True)
    q_in, kv_in, attn, attn_t, lse, half_out, sib_out, cot_all = attend(
        q4, keys_values, part_out, cot_slots, first
    )
    block_out, grad_middle, branch, grad_heads, moe_in, grad_logits, gain_sum, grad_experts = experts(
        attn, tokens, part_extra, ids, cotangent, half_out, sib_out, cot_all, full_experts
    )
    sum_experts = lax.psum_scatter(grad_experts, "dp", scatter_dimension=0, tiled=True)
    dq_in, dkv_in, sum_out = attend_back(grad_heads, branch, attn, q_in, kv_in, first, attn_t, lse)
    grad_tokens, r_query, r_key, r_value, r_out, r_extra, *expert_grads = reduce_weights(
        dq_in.reshape(Q_HALF, PAIR), dkv_in, normed, sum_out, grad_logits, gain_sum, moe_in,
        pair.reshape(PAIR, MODEL_WIDTH), part_extra, grad_middle,
        part_q.reshape(MODEL_WIDTH, Q_HALF), part_kv.reshape(MODEL_WIDTH, KV_HALF), sum_experts,
    )
    *results, r_router, r_gain_a, r_gain_m = finish(
        r_extra,
        (grad_tokens, *expert_grads, block_out, r_query, r_key, r_value, r_out),
    )
    grad_tokens, g_gate, g_up, g_down, block_out, r_query, r_key, r_value, r_out = results
    return (
        block_out,
        grad_tokens,
        r_query,
        r_key,
        r_value,
        r_out.T,
        r_router,
        r_gain_a.reshape(12),
        r_gain_m.reshape(12),
        g_gate,
        g_up,
        g_down,
    )


def solution(mesh):
    rows, flat, dense = P(("dp", "ctx"), None), P(("dp", "ctx")), P("dp", "ctx")
    placed = (
        rows, dense, rows, rows, rows, rows, P(None, ("dp", "ctx")), rows, flat, flat,
        dense, dense, P("ctx", "dp"), rows,
    )
    return jax.shard_map(
        local,
        mesh=mesh,
        in_specs=placed,
        out_specs=(
            rows, rows, rows, rows, rows, P(None, ("dp", "ctx")), rows, flat, flat,
            dense, dense, P("ctx", "dp"),
        ),
        check_vma=False,
    )
```
